32 devices in a mesh: wide: 8 (over z, x), narrow: 4 (over y, core).
Axes of the slice: x: 2, y: 2, z: 4, core: 2. Of those that a mesh axis runs over, the one named last changes fastest.
Arguments:
- tokens: bfloat16 [20480, 1024], P(('wide', 'narrow')), may hold values from -6 to 6
- cotangent: bfloat16 [20480, 1024], P(('wide', 'narrow')), may hold values from -6 to 6
- flags: int32 [8], P('wide'), may hold values from 0 to 1
- norm_gain: bfloat16 [1024], replicated, may hold values from 0.5 to 1.5
- query_weight: bfloat16 [1024, 512], P(None, 'narrow'), may hold values from -0.1875 to 0.1875
- key_weight: bfloat16 [1024, 512], P(None, 'narrow'), may hold values from -0.1875 to 0.1875
- value_weight: bfloat16 [1024, 1024], P(None, 'narrow'), may hold values from -0.1875 to 0.1875
- swish_weight: bfloat16 [1024, 1024], P(None, 'narrow'), may hold values from -0.1875 to 0.1875
- rank_down: bfloat16 [1024, 16], replicated, may hold values from -0.1875 to 0.1875
- rank_up: bfloat16 [16, 512], replicated, may hold values from -0.375 to 0.375
- decay_bias: bfloat16 [512], replicated, may hold values from 0 to 10
- group_gain: bfloat16 [256], replicated, may hold values from 0.5 to 1.5
- output_weight: bfloat16 [1024, 1024], P('narrow'), may hold values from -0.1875 to 0.1875
- mlp_gain: bfloat16 [1024], replicated, may hold values from 0.5 to 1.5
- mlp_gate: bfloat16 [1024, 2816], P(None, 'narrow'), may hold values from -0.1875 to 0.1875
- mlp_up: bfloat16 [1024, 2816], P(None, 'narrow'), may hold values from -0.1875 to 0.1875
- mlp_down: bfloat16 [2816, 1024], P('narrow'), may hold values from -0.109375 to 0.109375
Outputs:
- result: bfloat16 [20480, 1024], P(('wide', 'narrow'))
- input_grad: float32 [20480, 1024], P(('wide', 'narrow'))
- norm_gain_grad: float32 [1024], replicated
- query_grad: float32 [1024, 512], P('wide', 'narrow')
- key_grad: float32 [1024, 512], P('wide', 'narrow')
- value_grad: float32 [1024, 1024], P('wide', 'narrow')
- swish_grad: float32 [1024, 1024], P('wide', 'narrow')
- rank_down_grad: float32 [1024, 16], replicated
- rank_up_grad: float32 [16, 512], replicated
- decay_bias_grad: float32 [512], replicated
- group_gain_grad: float32 [256], replicated
- output_grad: float32 [1024, 1024], P('narrow', 'wide')
- mlp_gain_grad: float32 [1024], replicated
- mlp_gate_grad: float32 [1024, 2816], P('wide', 'narrow')
- mlp_up_grad: float32 [1024, 2816], P('wide', 'narrow')
- mlp_down_grad: float32 [2816, 1024], P('narrow', 'wide')
The draws below stay inside these ranges and needn't reach their ends.
All inputs are finite; a program needn't handle non-finite values.
Results may differ from the reference program's by a relative error of at most 0.03.
Values may be sent and summed in bfloat16 or wider, within the bound.
A program may use at most 192 MiB of HBM per device.

```python
import jax
import jax.numpy as jnp
from jax import lax

D = 1024
NH = 4
DK = 128
DV = 256
RANK = 16
FF = 2816
SPAN = 64
SEG = 2560
TOKENS = 20480
QK = 512
VD = 1024
N_WIDE = 8


def draw_flags(key, part):
    picks = jax.random.randint(key, (N_WIDE,), 0, 8)
    first_one = jnp.arange(N_WIDE) == 0
    return jnp.where(first_one | (picks == 0), 1, 0).astype(jnp.int32)


def spiked(drawn, own_key, source, target, parts, factor):
    owner, partner = [(jnp.arange(drawn.shape[axis_at]) // (drawn.shape[axis_at] // parts)).reshape([-1 if axis == axis_at else 1 for axis in range(drawn.ndim)]) for axis_at in (source, target)]
    chosen = jax.random.permutation(own_key, parts)[partner]
    strong = (owner == chosen) | (owner == (partner + parts // 2) % parts)
    return jnp.where(strong, factor * drawn, drawn)


def level_of(key, extent, pieces, low, top_value):
    factor_of, own = 1.0, jax.random.fold_in(key, 6)
    for dim, shards_of in pieces:
        heights = jnp.exp(jax.random.uniform(jax.random.fold_in(own, dim), (shards_of,), jnp.float32, low / len(pieces), top_value / len(pieces)))
        factor_of = factor_of * jnp.repeat(heights, extent[dim] // shards_of).reshape([-1 if axis == dim else 1 for axis in range(len(extent))])
    return factor_of


def bell_draw(stream_key, dims, scale, most, split=(), dtype=jnp.bfloat16):
    gain = level_of(stream_key, dims, split, -0.22, 0.18) if split else 1.0
    values = jax.random.normal(stream_key, dims, jnp.float32) * scale * gain
    return jnp.minimum(jnp.maximum(values, -most), most).astype(dtype)


def bell_draw_with(own_key, extent, scale, reach, shards, heavy, dtype=jnp.bfloat16):
    entries = scale * jax.random.normal(own_key, extent, jnp.float32)
    if shards:
        entries = entries * level_of(own_key, extent, shards, -0.22, 0.18)
    return jnp.clip(spiked(entries, jax.random.fold_in(own_key, 3), *heavy), -reach, reach).astype(dtype)


def setup_inputs(seed: int = 0) -> dict:
    arg_keys = jax.random.split(jax.random.key(seed), 18)
    tokens = bell_draw_with(arg_keys[0], (TOKENS, D), 1.0, 6.0, ((0, 32),), (0, 1, 32, 2.75))
    cotangent = bell_draw_with(arg_keys[1], (TOKENS, D), 1.0, 6.0, ((0, 32),), (0, 1, 32, 2.75))
    flags = draw_flags(jax.random.fold_in(arg_keys[17], 71), 0)
    norm_gain = jnp.clip(1.0 + 0.1 * jax.random.normal(arg_keys[3], (D,), jnp.float32), 0.5, 1.5).astype(jnp.bfloat16)
    query_weight = bell_draw(arg_keys[4], (D, QK), D ** -0.5, 0.1875, ((1, 4),))
    key_weight = bell_draw(arg_keys[5], (D, QK), D ** -0.5, 0.1875, ((1, 4),))
    value_weight = bell_draw(arg_keys[6], (D, VD), D ** -0.5, 0.1875, ((1, 4),))
    swish_weight = bell_draw(arg_keys[7], (D, VD), D ** -0.5, 0.1875, ((1, 4),))
    rank_down = bell_draw(arg_keys[8], (D, RANK), D ** -0.5, 0.1875)
    rank_up = bell_draw(arg_keys[9], (RANK, QK), (16 * RANK) ** -0.5, 0.375)
    decay_bias = jnp.clip(jax.random.uniform(arg_keys[10], (QK,), jnp.float32, 0.0, 10.0), 0.0, 10.0).astype(jnp.bfloat16)
    group_gain = jnp.clip(1.0 + 0.1 * jax.random.normal(arg_keys[11], (DV,), jnp.float32), 0.5, 1.5).astype(jnp.bfloat16)
    output_weight = bell_draw(arg_keys[12], (VD, D), VD ** -0.5, 0.1875, ((0, 4),))
    mlp_gain = jnp.clip(1.0 + 0.1 * jax.random.normal(arg_keys[13], (D,), jnp.float32), 0.5, 1.5).astype(jnp.bfloat16)
    mlp_gate = bell_draw(arg_keys[14], (D, FF), D ** -0.5, 0.1875, ((1, 4),))
    mlp_up = bell_draw(arg_keys[15], (D, FF), D ** -0.5, 0.1875, ((1, 4),))
    mlp_down = bell_draw(arg_keys[16], (FF, D), FF ** -0.5, 0.109375, ((0, 4),))
    return dict(tokens=tokens, cotangent=cotangent, flags=flags, norm_gain=norm_gain, query_weight=query_weight, key_weight=key_weight, value_weight=value_weight, swish_weight=swish_weight, rank_down=rank_down, rank_up=rank_up, decay_bias=decay_bias, group_gain=group_gain, output_weight=output_weight, mlp_gain=mlp_gain, mlp_gate=mlp_gate, mlp_up=mlp_up, mlp_down=mlp_down)


NORM_EPS = 1e-06
GROUP_EPS = 1e-05
GATE_NORM = 16.0
HIGHEST_PREC = lax.Precision.HIGHEST

@jax.custom_vjp
def low(v):
    return lax.optimization_barrier(v.astype(jnp.bfloat16)).astype(jnp.float32)

@jax.custom_vjp
def low_back(v):
    return v

def low_keep(v):
    return (low(v), None)

def low_pass(kept, grad):
    return (grad,)

def back_keep(v):
    return (v, None)

def back_low(kept, grad):
    return (low(grad),)
low.defvjp(low_keep, low_pass)
low_back.defvjp(back_keep, back_low)

def dense(left_mat, right_mat):
    return jnp.dot(left_mat, right_mat, precision=HIGHEST_PREC)

def rms_rows(values, gain_vec, eps_value):
    return values * lax.rsqrt(lax.optimization_barrier(jnp.mean(values * values, axis=-1, keepdims=True)) + eps_value) * gain_vec

def segment_mix(query_rows, key_rows, value_rows, decay_rows, start_state):
    seg_len = query_rows.shape[0]
    blocks = seg_len // SPAN
    key_dim = query_rows.shape[1]
    query_blk = query_rows.reshape(blocks, SPAN, key_dim) * key_dim ** (-0.5)
    key_blk = key_rows.reshape(blocks, SPAN, key_dim)
    value_blk = value_rows.reshape(blocks, SPAN, -1)
    inner_cum = jnp.cumsum(decay_rows.reshape(blocks, SPAN, key_dim), axis=1)
    block_end = inner_cum[:, -1:, :]
    query_dec = query_blk * jnp.exp(inner_cum)
    key_dec = key_blk * jnp.exp(-inner_cum)
    key_end = key_blk * jnp.exp(block_end - inner_cum)
    causal_mask = jnp.arange(SPAN)[:, None] >= jnp.arange(SPAN)[None, :]
    scores = jnp.einsum('bik,bjk->bij', query_dec, key_dec, precision=HIGHEST_PREC)
    scores = jnp.where(causal_mask[None], scores, 0.0)
    in_block = jnp.einsum('bij,bjv->biv', scores, value_blk, precision=HIGHEST_PREC)
    block_states = jnp.einsum('bjk,bjv->bkv', key_end, value_blk, precision=HIGHEST_PREC)
    block_rates = jnp.exp(block_end[:, 0, :])

    def advance(carried, step_item):
        decay_rate, increment = step_item
        return (decay_rate[:, None] * carried + increment, carried)
    last_state, entering = lax.scan(advance, start_state, (block_rates, block_states))
    from_state = jnp.einsum('bik,bkv->biv', query_dec, entering, precision=HIGHEST_PREC)
    return ((in_block + from_state).reshape(seg_len, -1), last_state)

def split_heads(matrix, width):
    return matrix.reshape(SEG, NH, width).transpose(1, 0, 2)

def layer_segment(weights, carried, seg_item):
    norm_gain, query_weight, key_weight, value_weight, swish_weight, rank_down, rank_up, decay_bias, group_gain, output_weight, mlp_gain, mlp_gate, mlp_up, mlp_down = weights
    seg_tokens, flag_value = seg_item
    enter_state = carried * (1.0 - flag_value)
    normed = low(rms_rows(seg_tokens, norm_gain, NORM_EPS))
    query_rows = low(low_back(dense(normed, query_weight)))
    key_rows = low(low_back(dense(normed, key_weight)))
    value_rows = low(low_back(dense(normed, value_weight)))
    swish_pre = low_back(dense(normed, swish_weight))
    rank_pre = low_back(dense(normed, rank_down))
    decay_log = jax.nn.log_sigmoid(dense(rank_pre, rank_up) + decay_bias) / GATE_NORM
    mixed, last_state = jax.vmap(segment_mix)(split_heads(query_rows, DK), split_heads(key_rows, DK), split_heads(value_rows, DV), split_heads(decay_log, DK), enter_state)
    mixed = mixed.transpose(1, 0, 2)
    normed_mix = rms_rows(mixed, group_gain, GROUP_EPS).reshape(SEG, VD)
    gated = low(normed_mix * jax.nn.silu(swish_pre))
    middle = seg_tokens + low_back(dense(gated, output_weight))
    normed_two = low(rms_rows(middle, mlp_gain, NORM_EPS))
    gate_pre = low_back(dense(normed_two, mlp_gate))
    up_pre = low_back(dense(normed_two, mlp_up))
    hidden = low(jax.nn.silu(gate_pre) * up_pre)
    result = middle + low_back(dense(hidden, mlp_down))
    return (last_state, result)

def forward(tokens, norm_gain, query_weight, key_weight, value_weight, swish_weight, rank_down, rank_up, decay_bias, group_gain, output_weight, mlp_gain, mlp_gate, mlp_up, mlp_down, flag_values):
    weights = (norm_gain, query_weight, key_weight, value_weight, swish_weight, rank_down, rank_up, decay_bias, group_gain, output_weight, mlp_gain, mlp_gate, mlp_up, mlp_down)

    def seg_step(carried, seg_item):
        return layer_segment(weights, carried, seg_item)
    start_state = jnp.zeros((NH, DK, DV), jnp.float32)
    _, outputs = lax.scan(jax.checkpoint(seg_step), start_state, (tokens.reshape(N_WIDE, SEG, D), flag_values))
    return outputs.reshape(TOKENS, D)

def reference(tokens, cotangent, flags, norm_gain, query_weight, key_weight, value_weight, swish_weight, rank_down, rank_up, decay_bias, group_gain, output_weight, mlp_gain, mlp_gate, mlp_up, mlp_down):
    flag_values = flags.astype(jnp.float32)
    floats = [arr.astype(jnp.float32) for arr in (tokens, norm_gain, query_weight, key_weight, value_weight, swish_weight, rank_down, rank_up, decay_bias, group_gain, output_weight, mlp_gain, mlp_gate, mlp_up, mlp_down)]

    def wrapped(*values):
        return forward(*values, flag_values)
    outcome, pullback = jax.vjp(wrapped, *floats)
    grads = pullback(cotangent.astype(jnp.float32))
    return (outcome.astype(jnp.bfloat16), grads[0], grads[1], grads[2], grads[3], grads[4], grads[5], grads[6], grads[7], grads[8], grads[9], grads[10], grads[11], grads[12], grads[13], grads[14])
```

```python
import functools

import jax
import jax.numpy as jnp
from jax import lax
from jax.experimental import pallas as pl
from jax.experimental.pallas import tpu as pltpu
from jax.sharding import PartitionSpec as P

NORM_EPS = 1e-06
GROUP_EPS = 1e-05
GATE_NORM = 16.0
HIGHEST_PREC = lax.Precision.HIGHEST
CHUNK = 128
HALF = CHUNK // 2
BLOCK = 256
F32 = jnp.float32
BF16 = jnp.bfloat16


def dot(a, b):
    return lax.dot_general(a, b, (((1,), (0,)), ((), ())), preferred_element_type=F32)


def dot_nt(a, b):
    return lax.dot_general(a, b, (((1,), (1,)), ((), ())), preferred_element_type=F32)


def dot_tn(a, b):
    return lax.dot_general(a, b, (((0,), (0,)), ((), ())), preferred_element_type=F32)


def exact(a, b, dims):
    return lax.dot_general(
        a, b, (dims, ((), ())), precision=HIGHEST_PREC, preferred_element_type=F32
    )


def sds(shape, dtype):
    return jax.ShapeDtypeStruct(shape, dtype)


def params(mib=48):
    return pltpu.CompilerParams(vmem_limit_bytes=mib << 20)


def cost(flops, nbytes, trans=0):
    return pl.CostEstimate(flops=int(flops), bytes_accessed=int(nbytes), transcendentals=int(trans))


def whole(shape):
    return pl.BlockSpec(shape, lambda i: (0,) * len(shape), pipeline_mode=pl.Buffered(1))


def rows_spec(rows, cols):
    return pl.BlockSpec((rows, cols), lambda i: (i, 0))


def triangle(lower):
    r = lax.broadcasted_iota(jnp.int32, (CHUNK, CHUNK), 0)
    c = lax.broadcasted_iota(jnp.int32, (CHUNK, CHUNK), 1)
    return r >= c if lower else r <= c


def forward_head_kernel(
    x_ref, w_ref, rd_ref, ru_ref, bias_ref,
    q_ref, k_ref, v_ref, s_ref, cum_ref, dpre_ref, rank_ref, base_ref, reach_ref, sin_ref, off_ref,
    state_ref, mult_ref,
    st, off,
):
    i = pl.program_id(0)
    dk = q_ref.shape[1]
    dv = v_ref.shape[1]

    @pl.when(i == 0)
    def _():
        st[...] = jnp.zeros_like(st)
        off[...] = jnp.zeros_like(off)

    x = x_ref[...]
    proj = dot(x, w_ref[...])
    rank = dot(x, rd_ref[...])
    dpre = exact(rank, ru_ref[...], ((1,), (0,))) + bias_ref[...]
    dlog = jax.nn.log_sigmoid(dpre) * (1.0 / GATE_NORM)
    q_low = proj[:, :dk].astype(BF16)
    k_low = proj[:, dk : 2 * dk].astype(BF16)
    v_low = proj[:, 2 * dk : 2 * dk + dv].astype(BF16)
    q_ref[...] = q_low
    k_ref[...] = k_low
    v_ref[...] = v_low
    s_ref[...] = proj[:, 2 * dk + dv :]
    rank_ref[...] = rank
    dpre_ref[...] = dpre
    mask = triangle(True)
    ones = mask.astype(F32)
    scale = dk**-0.5
    for j in range(BLOCK // CHUNK):
        rows = slice(j * CHUNK, (j + 1) * CHUNK)
        cum = exact(ones, dlog[rows], ((1,), (0,)))
        mid = cum[HALF - 1 : HALF]
        end = cum[CHUNK - 1 :]
        qf = q_low[rows].astype(F32) * scale
        kf = k_low[rows].astype(F32)
        v = v_low[rows]
        qd = (qf * jnp.exp(cum - mid)).astype(BF16)
        kd = (kf * jnp.exp(mid - cum)).astype(BF16)
        qi = (qf * jnp.exp(cum)).astype(BF16)
        ke = (kf * jnp.exp(end - cum)).astype(BF16)
        scores = jnp.where(mask, dot_nt(qd, kd), 0.0).astype(BF16)
        state = st[...]
        state_low = state.astype(BF16)
        offset = off[...]
        base_ref[rows, :] = dot(scores, v) + dot_nt(qi, state_low)
        reach_ref[rows, :] = (qf * jnp.exp(cum + offset)).astype(BF16)
        cum_ref[rows, :] = cum
        sin_ref[j] = state_low
        off_ref[j] = offset
        st[...] = state * jnp.exp(end) + dot_tn(v, ke)
        off[...] = offset + end
    state_ref[...] = st[...]
    mult_ref[...] = jnp.exp(off[...])


def forward_head(x, w, rank_down, rank_cols, bias_cols, dk, dv):
    n, d = x.shape
    rank = rank_down.shape[1]
    per = BLOCK // CHUNK
    return pl.pallas_call(
        forward_head_kernel,
        name="forward_head",
        grid=(n // BLOCK,),
        in_specs=[
            rows_spec(BLOCK, d), whole(w.shape), whole(rank_down.shape), whole(rank_cols.shape), whole(bias_cols.shape),
        ],
        out_specs=[
            rows_spec(BLOCK, dk), rows_spec(BLOCK, dk), rows_spec(BLOCK, dv), rows_spec(BLOCK, dv),
            rows_spec(BLOCK, dk), rows_spec(BLOCK, dk), rows_spec(BLOCK, rank), rows_spec(BLOCK, dv), rows_spec(BLOCK, dk),
            pl.BlockSpec((per, dv, dk), lambda i: (i, 0, 0)), pl.BlockSpec((per, 1, dk), lambda i: (i, 0, 0)),
            whole((dv, dk)), whole((1, dk)),
        ],
        out_shape=[
            sds((n, dk), BF16), sds((n, dk), BF16), sds((n, dv), BF16), sds((n, dv), F32),
            sds((n, dk), F32), sds((n, dk), F32), sds((n, rank), F32), sds((n, dv), F32), sds((n, dk), BF16),
            sds((n // CHUNK, dv, dk), BF16), sds((n // CHUNK, 1, dk), F32),
            sds((dv, dk), F32), sds((1, dk), F32),
        ],
        scratch_shapes=[pltpu.VMEM((dv, dk), F32), pltpu.VMEM((1, dk), F32)],
        compiler_params=params(),
        cost_estimate=cost(2 * n * d * (2 * dk + 2 * dv) * 1.5, n * d * 2 + n * 4000, n * dk * 6),
    )(x, w, rank_down, rank_cols, bias_cols)


def gate_out_kernel(b0, b1, r0, r1, s0, s1, e0, e1, gain_ref, w0, w1, m0, m1, g0, g1, out_ref):
    total = None
    gain = gain_ref[...]
    for b, r, s, e, w, m, g in ((b0, r0, s0, e0, w0, m0, g0), (b1, r1, s1, e1, w1, m1, g1)):
        mixed = b[...] + dot_nt(r[...], e[...])
        inv = lax.rsqrt(jnp.mean(mixed * mixed, axis=-1, keepdims=True) + GROUP_EPS)
        sw = s[...]
        gated = (mixed * inv * gain * (sw * jax.nn.sigmoid(sw))).astype(BF16)
        m[...] = mixed
        g[...] = gated
        part = dot(gated, w[...])
        total = part if total is None else total + part
    out_ref[...] = total.astype(BF16)


def gate_out(bases, reaches, swishes, enters, gain, weights):
    n, dv = bases[0].shape
    dk = reaches[0].shape[1]
    d = weights[0].shape[1]
    row = rows_spec(BLOCK, dv)
    return pl.pallas_call(
        gate_out_kernel,
        name="gate_out",
        grid=(n // BLOCK,),
        in_specs=[row, row, rows_spec(BLOCK, dk), rows_spec(BLOCK, dk), row, row]
        + [whole((dv, dk))] * 2 + [whole((1, dv))] + [whole((dv, d))] * 2,
        out_specs=[row, row, row, row, rows_spec(BLOCK, d)],
        out_shape=[sds((n, dv), F32)] * 2 + [sds((n, dv), BF16)] * 2 + [sds((n, d), BF16)],
        compiler_params=params(),
        cost_estimate=cost(2 * n * dv * (d + dk) * 2, n * (dv * 28 + d * 2), n * dv * 2),
    )(*bases, *reaches, *swishes, *enters, gain, *weights)


def mlp_kernel(x_ref, c_ref, wg_ref, wu_ref, wd_ref, h_ref, gg_ref, gu_ref, dn_ref, gn_ref):
    x = x_ref[...]
    gate = dot(x, wg_ref[...])
    up = dot(x, wu_ref[...])
    gh = dot_nt(c_ref[...], wd_ref[...])
    sig = jax.nn.sigmoid(gate)
    act = gate * sig
    hidden = (act * up).astype(BF16)
    g_up = (gh * act).astype(BF16)
    g_gate = (gh * up * sig * (1.0 + gate * (1.0 - sig))).astype(BF16)
    h_ref[...] = hidden
    gg_ref[...] = g_gate
    gu_ref[...] = g_up
    gn_ref[...] = (dot_nt(g_gate, wg_ref[...]) + dot_nt(g_up, wu_ref[...])).astype(BF16)
    dn_ref[...] = dot(hidden, wd_ref[...]).astype(BF16)


def mlp(x, cot, wg, wu, wd):
    n, d = x.shape
    ff = wg.shape[1]
    blk = 320 if n % 320 == 0 else n
    return pl.pallas_call(
        mlp_kernel,
        name="mlp",
        grid=(n // blk,),
        in_specs=[rows_spec(blk, d), rows_spec(blk, d), whole((d, ff)), whole((d, ff)), whole((ff, d))],
        out_specs=[rows_spec(blk, ff)] * 3 + [rows_spec(blk, d)] * 2,
        out_shape=[sds((n, ff), BF16)] * 3 + [sds((n, d), BF16)] * 2,
        compiler_params=params(),
        cost_estimate=cost(12 * n * d * ff, n * d * 8 + n * ff * 6 + d * ff * 6, n * ff),
    )(x, cot, wg, wu, wd)


def mlp_grads_kernel(pieces, *refs):
    xs, cs, hs, ggs, gus = [refs[i * pieces : (i + 1) * pieces] for i in range(5)]
    out_ref = refs[5 * pieces]
    ff = hs[0].shape[1]
    for at, lefts, rights in ((0, xs, ggs), (ff, xs, gus), (2 * ff, cs, hs)):
        acc = dot_tn(lefts[0][...], rights[0][...])
        for left, right in zip(lefts[1:], rights[1:]):
            acc = acc + dot_tn(left[...], right[...])
        out_ref[:, at : at + ff] = acc.astype(BF16)


def mlp_grads(xs, cs, hs, ggs, gus):
    pieces = len(xs)
    n, d = xs[0].shape
    ff = hs[0].shape[1]
    blk = 256
    cols = pl.BlockSpec((n, blk), lambda i: (0, i))
    return pl.pallas_call(
        functools.partial(mlp_grads_kernel, pieces),
        name="mlp_grads",
        grid=(d // blk,),
        in_specs=[cols] * (2 * pieces) + [whole((n, ff))] * (3 * pieces),
        out_specs=rows_spec(blk, 3 * ff),
        out_shape=sds((d, 3 * ff), BF16),
        compiler_params=params(),
        cost_estimate=cost(6 * pieces * n * d * ff, pieces * n * (d * 4 + ff * 6) + d * ff * 6),
    )(*xs, *cs, *hs, *ggs, *gus)


def gate_back_kernel(
    gm_ref, m0, m1, s0, s1, r0, r1, gain_ref, w0, w1, gx0, gx1, gs0, gs1, lb0, lb1, gp_ref
):
    i = pl.program_id(0)

    @pl.when(i == 0)
    def _():
        lb0[...] = jnp.zeros_like(lb0)
        lb1[...] = jnp.zeros_like(lb1)
        gp_ref[...] = jnp.zeros_like(gp_ref)

    gm = gm_ref[...]
    gain = gain_ref[...]
    for m, s, r, w, gx, gs, lb in ((m0, s0, r0, w0, gx0, gs0, lb0), (m1, s1, r1, w1, gx1, gs1, lb1)):
        grad = dot_nt(gm, w[...])
        mixed = m[...]
        inv = lax.rsqrt(jnp.mean(mixed * mixed, axis=-1, keepdims=True) + GROUP_EPS)
        unit = mixed * inv
        sw = s[...]
        sig = jax.nn.sigmoid(sw)
        gs[...] = (grad * unit * gain * (sig * (1.0 + sw * (1.0 - sig)))).astype(BF16)
        dn = grad * (sw * sig)
        gp_ref[...] += jnp.sum(dn * unit, axis=0, keepdims=True)
        weighted = dn * gain
        gmix = (inv * (weighted - unit * jnp.mean(weighted * unit, axis=-1, keepdims=True))).astype(BF16)
        gx[...] = gmix
        lb[...] += dot_tn(gmix, r[...])


def gate_back(gm, mixeds, swishes, reaches, gain, weights):
    n, d = gm.shape
    dv = mixeds[0].shape[1]
    dk = reaches[0].shape[1]
    row = rows_spec(BLOCK, dv)
    return pl.pallas_call(
        gate_back_kernel,
        name="gate_back",
        grid=(n // BLOCK,),
        in_specs=[rows_spec(BLOCK, d), row, row, row, row, rows_spec(BLOCK, dk), rows_spec(BLOCK, dk)]
        + [whole((1, dv))] + [whole((dv, d))] * 2,
        out_specs=[row] * 4 + [whole((dv, dk))] * 2 + [whole((1, dv))],
        out_shape=[sds((n, dv), BF16)] * 4 + [sds((dv, dk), F32)] * 2 + [sds((1, dv), F32)],
        compiler_params=params(),
        cost_estimate=cost(2 * n * dv * (d + dk) * 2, n * (dv * 28 + d * 2), n * dv * 2),
    )(gm, *mixeds, *swishes, *reaches, gain, *weights)


def back_head_kernel(
    q_ref, k_ref, v_ref, cum_ref, dpre_ref, rank_ref, sin_ref, off_ref, gx_ref, gs_ref, enter_ref, later_ref, ru_ref,
    all_ref, grank_ref, rup_ref, bias_ref,
    ds,
):
    i = pl.program_id(0)
    dk = q_ref.shape[1]
    dv = v_ref.shape[1]

    @pl.when(i == 0)
    def _():
        ds[...] = later_ref[...]
        rup_ref[...] = jnp.zeros_like(rup_ref)
        bias_ref[...] = jnp.zeros_like(bias_ref)

    mask = triangle(True)
    ones = triangle(False).astype(F32)
    scale = dk**-0.5
    enter = enter_ref[...]
    for j in reversed(range(BLOCK // CHUNK)):
        rows = slice(j * CHUNK, (j + 1) * CHUNK)
        cum = cum_ref[rows, :]
        mid = cum[HALF - 1 : HALF]
        end = cum[CHUNK - 1 :]
        e_qd, e_kd, e_qi, e_ke = jnp.exp(cum - mid), jnp.exp(mid - cum), jnp.exp(cum), jnp.exp(end - cum)
        e_end = jnp.exp(end)
        qf = q_ref[rows, :].astype(F32) * scale
        kf = k_ref[rows, :].astype(F32)
        v = v_ref[rows, :]
        qd = (qf * e_qd).astype(BF16)
        kd = (kf * e_kd).astype(BF16)
        qi = (qf * e_qi).astype(BF16)
        ke = (kf * e_ke).astype(BF16)
        go = gx_ref[rows, :]
        state = sin_ref[j].astype(F32) + enter * jnp.exp(off_ref[j])
        state_low = state.astype(BF16)
        dstate = ds[...]
        dstate_low = dstate.astype(BF16)
        scores = jnp.where(mask, dot_nt(qd, kd), 0.0).astype(BF16)
        dscores = jnp.where(mask, dot_nt(go, v), 0.0).astype(BF16)
        d_v = dot_tn(scores, go) + dot_nt(ke, dstate_low)
        d_qd = dot(dscores, kd)
        d_qi = dot(go, state_low)
        d_kd = dot_tn(dscores, qd)
        d_ke = dot(v, dstate_low)
        d_q = scale * (d_qd * e_qd + d_qi * e_qi)
        d_k = d_kd * e_kd + d_ke * e_ke
        tail = ke.astype(F32) * d_ke
        d_cum = qd.astype(F32) * d_qd + qi.astype(F32) * d_qi - kd.astype(F32) * d_kd - tail
        d_end = jnp.sum(tail, axis=0, keepdims=True) + e_end * jnp.sum(dstate * state, axis=0, keepdims=True)
        grad_decay = exact(ones, d_cum, ((1,), (0,))) + d_end
        g_pre = grad_decay * jax.nn.sigmoid(-dpre_ref[rows, :]) * (1.0 / GATE_NORM)
        all_ref[rows, :dk] = d_q.astype(BF16)
        all_ref[rows, dk : 2 * dk] = d_k.astype(BF16)
        all_ref[rows, 2 * dk : 2 * dk + dv] = d_v.astype(BF16)
        all_ref[rows, 2 * dk + dv :] = gs_ref[rows, :]
        grank_ref[rows, :] = exact(g_pre, ru_ref[...], ((1,), (1,)))
        rup_ref[...] += exact(rank_ref[rows, :], g_pre, ((0,), (0,)))
        bias_ref[...] += jnp.sum(g_pre, axis=0, keepdims=True)
        ds[...] = dstate * e_end + dot_tn(go, qi)


def back_head(q, k, v, cum, dpre, rank, sin, off, gx, gs, enter, later, rank_cols):
    n, dk = q.shape
    dv = v.shape[1]
    rk = rank.shape[1]
    per = BLOCK // CHUNK
    last = n // BLOCK - 1

    def rev(rows, cols):
        return pl.BlockSpec((rows, cols), lambda i: (last - i, 0))

    return pl.pallas_call(
        back_head_kernel,
        name="back_head",
        grid=(n // BLOCK,),
        in_specs=[
            rev(BLOCK, dk), rev(BLOCK, dk), rev(BLOCK, dv), rev(BLOCK, dk), rev(BLOCK, dk), rev(BLOCK, rk),
            pl.BlockSpec((per, dv, dk), lambda i: (last - i, 0, 0)), pl.BlockSpec((per, 1, dk), lambda i: (last - i, 0, 0)),
            rev(BLOCK, dv), rev(BLOCK, dv), whole((dv, dk)), whole((dv, dk)), whole((rk, dk)),
        ],
        out_specs=[rev(BLOCK, 2 * dk + 2 * dv), rev(BLOCK, rk), whole((rk, dk)), whole((1, dk))],
        out_shape=[sds((n, 2 * dk + 2 * dv), BF16), sds((n, rk), F32), sds((rk, dk), F32), sds((1, dk), F32)],
        scratch_shapes=[pltpu.VMEM((dv, dk), F32)],
        compiler_params=params(),
        cost_estimate=cost(n * 128 * 128 * 40, n * 6000, n * dk * 6),
    )(q, k, v, cum, dpre, rank, sin, off, gx, gs, enter, later, rank_cols)


def hop(value, axis, bit):
    return lax.ppermute(value, axis, [(i, i ^ bit) for i in range(lax.axis_size(axis))])


def wide_bits():
    count, bits, bit = lax.axis_size("wide"), [], 1
    while bit < count:
        bits.append(bit)
        bit *= 2
    return bits


def scan_states(mult, state, backward):
    place = {"narrow": lax.axis_index("narrow"), "wide": lax.axis_index("wide")}
    heads, dv, dk = state.shape
    pre_m, pre_s = jnp.ones_like(mult), jnp.zeros_like(state)
    tot_m, tot_s = mult, state
    for axis, bit in [("narrow", 2)] + [("wide", b) for b in wide_bits()]:
        packed = jnp.concatenate(
            [tot_s, jnp.broadcast_to(tot_m, (heads, 16, dk))], axis=1
        ).astype(BF16)
        other = hop(packed, axis, bit).astype(F32)
        if axis == "narrow":
            other = other[::-1]
        oth_s, oth_m = other[:, :dv], other[:, dv : dv + 1]
        is_set = (place[axis] & bit) != 0
        mine_later = jnp.logical_not(is_set) if backward else is_set
        new_s = oth_s * pre_m + pre_s
        new_m = oth_m * pre_m
        sum_later = oth_s * tot_m + tot_s
        sum_first = tot_s * oth_m + oth_s
        pre_s = jnp.where(mine_later, new_s, pre_s)
        pre_m = jnp.where(mine_later, new_m, pre_m)
        tot_s = jnp.where(mine_later, sum_later, sum_first)
        tot_m = tot_m * oth_m
    return pre_s


def scatter_rows(value, bits):
    count = lax.axis_size("wide")
    place = lax.axis_index("wide")
    rows, cols = value.shape[0] // count, value.shape[1]
    order = sorted(bits, reverse=True)
    value = value.reshape((2,) * len(bits) + (rows, cols))
    left = list(order)
    for bit in bits:
        dim = left.index(bit)
        mine = jnp.where((place & bit) != 0, 1, 0)
        keep = lax.dynamic_index_in_dim(value, mine, dim, False)
        send = lax.dynamic_index_in_dim(value, 1 - mine, dim, False)
        got = hop(send.astype(BF16), "wide", bit)
        value = keep.astype(F32) + got.astype(F32)
        left.pop(dim)
        if left:
            value = value.astype(BF16)
    return value


def sum_everywhere(value):
    for axis, bit in [("narrow", 1), ("narrow", 2)] + [("wide", b) for b in wide_bits()]:
        value = value + hop(value, axis, bit)
    return value


def norm_back(grad, values, inv, gain):
    unit = values * inv
    weighted = grad * gain
    part = jnp.sum(grad * unit, axis=0, keepdims=True)
    return inv * (weighted - unit * jnp.mean(weighted * unit, axis=-1, keepdims=True)), part


def shards(
    tokens, cotangent, flags, norm_gain, query_weight, key_weight, value_weight, swish_weight, rank_down, rank_up,
    decay_bias, group_gain, output_weight, mlp_gain, mlp_gate, mlp_up, mlp_down,
):
    own_rows = tokens.shape[0]
    place = lax.axis_index("narrow")
    core = place & 1
    second = (place & 2) != 0
    wide_odd = (lax.axis_index("wide") & 1) != 0
    dk = query_weight.shape[1]
    dv = value_weight.shape[1]
    d = tokens.shape[1]

    def in_order(mine, other):
        return jnp.where(
            core == 0, jnp.concatenate([mine, other]), jnp.concatenate([other, mine])
        )

    def from_row_partner(value):
        half = value.shape[0] // 2
        piece = lax.dynamic_slice_in_dim(value, jnp.where(wide_odd, half, 0), half, 0)
        first = hop(piece, "narrow", 2)
        relayed = hop(first, "wide", 1)
        return jnp.where(
            wide_odd, jnp.concatenate([relayed, first]), jnp.concatenate([first, relayed])
        )

    def head_cols(index):
        ru = lax.dynamic_slice_in_dim(rank_up, index * dk, dk, 1).astype(F32)
        bias = lax.dynamic_slice_in_dim(decay_bias, index * dk, dk, 0).astype(F32)
        return ru, bias.reshape(1, dk)

    restart = 1.0 - flags[0].astype(F32)
    restart = jnp.where(second, 1.0, restart)
    norm_gain_f = norm_gain.astype(F32)
    mlp_gain_f = mlp_gain.astype(F32)
    gain_row = group_gain.astype(F32).reshape(1, dv)

    inputs = tokens.astype(F32)
    inv_one = lax.rsqrt(jnp.mean(inputs * inputs, axis=-1, keepdims=True) + NORM_EPS)
    normed = (inputs * inv_one * norm_gain_f).astype(BF16)
    normed_two = hop(normed, "narrow", 1)
    rows_all = in_order(normed, normed_two)

    w_own = jnp.concatenate([query_weight, key_weight, value_weight, swish_weight], axis=1)
    w_other = from_row_partner(w_own)
    out_other = from_row_partner(output_weight)
    cot_late, w_other, out_other = lax.optimization_barrier((cotangent, w_other, out_other))
    cot_y = hop(cot_late, "narrow", 2)
    cot_c = hop(cotangent, "narrow", 1)
    cot_d = hop(cot_y, "narrow", 1)

    ru_own, bias_own = head_cols(place)
    ru_oth, bias_oth = head_cols(place ^ 2)
    weights_out = (output_weight, out_other)
    one = forward_head(rows_all, w_own, rank_down, ru_own, bias_own, dk, dv)
    two = forward_head(rows_all, w_other, rank_down, ru_oth, bias_oth, dk, dv)
    (q, k, v, s, cum, dpre, rank_pre, base, reach, sin, off, state, mult) = zip(one, two)
    rank_pre = rank_pre[0]
    mults = restart * jnp.stack(mult)
    enter = restart * scan_states(mults, jnp.stack(state), False)
    enter_low = enter.astype(BF16)
    mixed0, mixed1, gated0, gated1, term = gate_out(
        base, reach, s, (enter_low[0], enter_low[1]), gain_row, weights_out
    )
    own_term = lax.dynamic_slice_in_dim(term, core * own_rows, own_rows, 0)
    send_term = lax.dynamic_slice_in_dim(term, (1 - core) * own_rows, own_rows, 0)
    middle = inputs + (own_term.astype(F32) + hop(send_term, "narrow", 1).astype(F32))
    inv_two = lax.rsqrt(jnp.mean(middle * middle, axis=-1, keepdims=True) + NORM_EPS)
    x_own = (middle * inv_two * mlp_gain_f).astype(BF16)

    x_y = hop(x_own, "narrow", 2)
    x_c = hop(x_own, "narrow", 1)
    x_d = hop(x_y, "narrow", 1)
    xs, cs = (x_own, x_c, x_y, x_d), (cotangent, cot_c, cot_y, cot_d)
    hs, ggs, gus, dns, gns = zip(*[mlp(x, c, mlp_gate, mlp_up, mlp_down) for x, c in zip(xs, cs)])

    def gather_sum(parts):
        own, by_core, by_y, by_both = parts
        across = by_y.astype(F32) + hop(by_both, "narrow", 1).astype(F32)
        near = own.astype(F32) + hop(by_core, "narrow", 1).astype(F32)
        return near + hop(across.astype(BF16), "narrow", 2).astype(F32)

    grad_two = gather_sum(gns)
    mlp_w_grads = mlp_grads(xs, cs, hs, ggs, gus)
    bits = wide_bits()
    mlp_w = scatter_rows(mlp_w_grads, bits)

    grad_norm, mlp_gain_part = norm_back(grad_two, middle, inv_two, mlp_gain_f)
    grad_middle = cotangent.astype(F32) + grad_norm
    middle_low = grad_middle.astype(BF16)
    gm_all = in_order(middle_low, hop(middle_low, "narrow", 1))
    gx0, gx1, gs0, gs1, lb0, lb1, group_part = gate_back(
        gm_all, (mixed0, mixed1), s, reach, gain_row, weights_out
    )
    later = scan_states(mults, restart * jnp.stack([lb0, lb1]), True)
    dns_y, _ = lax.optimization_barrier((dns, gm_all))
    result = (middle + gather_sum(dns_y)).astype(BF16)

    all0, gr0, rup0, gb0 = back_head(
        q[0], k[0], v[0], cum[0], dpre[0], rank_pre, sin[0], off[0], gx0, gs0, enter[0], later[0], ru_own
    )
    all1, gr1, rup1, gb1 = back_head(
        q[1], k[1], v[1], cum[1], dpre[1], rank_pre, sin[1], off[1], gx1, gs1, enter[1], later[1], ru_oth
    )
    grad_rank = (gr0 + gr1).astype(BF16)
    total = dot_nt(all0, w_own) + dot_nt(all1, w_other) + dot_nt(grad_rank, rank_down)
    total = total.astype(BF16)
    own_total = lax.dynamic_slice_in_dim(total, core * own_rows, own_rows, 0)
    send_total = lax.dynamic_slice_in_dim(total, (1 - core) * own_rows, own_rows, 0)
    grad_normed = own_total.astype(F32) + hop(send_total, "narrow", 1).astype(F32)
    grad_input, norm_gain_part = norm_back(grad_normed, inputs, inv_one, norm_gain_f)
    input_grad = grad_middle + grad_input

    def over_y(mine, other):
        return (mine + hop(other.astype(BF16), "narrow", 2).astype(F32)).astype(BF16)

    qkvs = over_y(dot_tn(rows_all, all0), dot_tn(rows_all, all1))
    outs = over_y(dot_tn(gm_all, gated0), dot_tn(gm_all, gated1))
    qkvs = scatter_rows(qkvs, bits)
    outs = scatter_rows(outs, bits)
    grad_rank_down = dot_tn(rows_all, grad_rank)

    def spread(mine, other, width):
        zero = jnp.zeros((mine.shape[0], width), F32)
        zero = lax.dynamic_update_slice_in_dim(zero, mine, place * dk, 1)
        return lax.dynamic_update_slice_in_dim(zero, other, (place ^ 2) * dk, 1)

    qk = rank_up.shape[1]
    rank = rank_up.shape[0]
    small = [
        norm_gain_part,
        mlp_gain_part,
        group_part,
        grad_rank_down.T,
        spread(rup0, rup1, qk),
        spread(gb0, gb1, qk),
    ]
    flat = jnp.concatenate([jnp.reshape(part, (-1, dk)) for part in small])
    flat = sum_everywhere(flat)
    parts, at = [], 0
    for part in small:
        size = part.size // dk
        parts.append(flat[at : at + size].reshape(part.shape))
        at += size
    ff = mlp_gate.shape[1]
    return (
        result,
        input_grad,
        parts[0].reshape(d),
        qkvs[:, :dk],
        qkvs[:, dk : 2 * dk],
        qkvs[:, 2 * dk : 2 * dk + dv],
        qkvs[:, 2 * dk + dv :],
        parts[3].reshape(rank, d).T,
        parts[4].reshape(rank, qk),
        parts[5].reshape(qk),
        parts[2].reshape(dv),
        outs.T,
        parts[1].reshape(d),
        mlp_w[:, :ff],
        mlp_w[:, ff : 2 * ff],
        mlp_w[:, 2 * ff :].T,
    )


def solution(mesh):
    rows, cols = P(("wide", "narrow"), None), P(None, "narrow")
    both = P("wide", "narrow")
    in_specs = (
        rows, rows, P("wide"), P(), cols, cols, cols, cols, P(), P(), P(), P(), P("narrow", None), P(), cols, cols,
        P("narrow", None),
    )
    out_specs = (
        rows, rows, P(), both, both, both, both, P(), P(), P(), P(), P("narrow", "wide"), P(), both, both,
        P("narrow", "wide"),
    )
    return jax.shard_map(shards, mesh=mesh, in_specs=in_specs, out_specs=out_specs, check_vma=False)
```

```python
import functools

import jax
import jax.numpy as jnp
from jax import lax
from jax.experimental import pallas as pl
from jax.experimental.pallas import tpu as pltpu
from jax.sharding import PartitionSpec as P

NORM_EPS = 1e-06
GROUP_EPS = 1e-05
GATE_NORM = 16.0
HIGHEST_PREC = lax.Precision.HIGHEST
MESH = pl.DeviceIdType.MESH
CHUNK = 128
HALF = CHUNK // 2
BLOCK = 256
F32 = jnp.float32
BF16 = jnp.bfloat16


def dot(a, b):
    return lax.dot_general(a, b, (((1,), (0,)), ((), ())), preferred_element_type=F32)


def dot_nt(a, b):
    return lax.dot_general(a, b, (((1,), (1,)), ((), ())), preferred_element_type=F32)


def dot_tn(a, b):
    return lax.dot_general(a, b, (((0,), (0,)), ((), ())), preferred_element_type=F32)


def exact(a, b, dims):
    return lax.dot_general(
        a, b, (dims, ((), ())), precision=HIGHEST_PREC, preferred_element_type=F32
    )


def sds(shape, dtype):
    return jax.ShapeDtypeStruct(shape, dtype)


def params(mib=48):
    return pltpu.CompilerParams(vmem_limit_bytes=mib << 20)


def cost(flops, nbytes, trans=0):
    return pl.CostEstimate(flops=int(flops), bytes_accessed=int(nbytes), transcendentals=int(trans))


def whole(shape):
    return pl.BlockSpec(shape, lambda i: (0,) * len(shape), pipeline_mode=pl.Buffered(1))


def rows_spec(rows, cols):
    return pl.BlockSpec((rows, cols), lambda i: (i, 0))


def triangle(lower):
    r = lax.broadcasted_iota(jnp.int32, (CHUNK, CHUNK), 0)
    c = lax.broadcasted_iota(jnp.int32, (CHUNK, CHUNK), 1)
    return r >= c if lower else r <= c


def forward_head_kernel(
    x_ref, w_ref, rd_ref, ru_ref, bias_ref,
    q_ref, k_ref, v_ref, s_ref, cum_ref, dpre_ref, rank_ref, base_ref, reach_ref, sin_ref, off_ref,
    state_ref, mult_ref,
    st, off,
):
    i = pl.program_id(0)
    dk = q_ref.shape[1]
    dv = v_ref.shape[1]

    @pl.when(i == 0)
    def _():
        st[...] = jnp.zeros_like(st)
        off[...] = jnp.zeros_like(off)

    x = x_ref[...]
    proj = dot(x, w_ref[...])
    rank = dot(x, rd_ref[...])
    dpre = exact(rank, ru_ref[...], ((1,), (0,))) + bias_ref[...]
    dlog = jax.nn.log_sigmoid(dpre) * (1.0 / GATE_NORM)
    q_low = proj[:, :dk].astype(BF16)
    k_low = proj[:, dk : 2 * dk].astype(BF16)
    v_low = proj[:, 2 * dk : 2 * dk + dv].astype(BF16)
    q_ref[...] = q_low
    k_ref[...] = k_low
    v_ref[...] = v_low
    s_ref[...] = proj[:, 2 * dk + dv :]
    rank_ref[...] = rank
    dpre_ref[...] = dpre
    mask = triangle(True)
    ones = mask.astype(F32)
    scale = dk**-0.5
    for j in range(BLOCK // CHUNK):
        rows = slice(j * CHUNK, (j + 1) * CHUNK)
        cum = exact(ones, dlog[rows], ((1,), (0,)))
        mid = cum[HALF - 1 : HALF]
        end = cum[CHUNK - 1 :]
        qf = q_low[rows].astype(F32) * scale
        kf = k_low[rows].astype(F32)
        v = v_low[rows]
        qd = (qf * jnp.exp(cum - mid)).astype(BF16)
        kd = (kf * jnp.exp(mid - cum)).astype(BF16)
        qi = (qf * jnp.exp(cum)).astype(BF16)
        ke = (kf * jnp.exp(end - cum)).astype(BF16)
        scores = jnp.where(mask, dot_nt(qd, kd), 0.0).astype(BF16)
        state = st[...]
        state_low = state.astype(BF16)
        offset = off[...]
        base_ref[rows, :] = dot(scores, v) + dot_nt(qi, state_low)
        reach_ref[rows, :] = (qf * jnp.exp(cum + offset)).astype(BF16)
        cum_ref[rows, :] = cum
        sin_ref[j] = state_low
        off_ref[j] = offset
        st[...] = state * jnp.exp(end) + dot_tn(v, ke)
        off[...] = offset + end
    state_ref[...] = st[...]
    mult_ref[...] = jnp.exp(off[...])


def forward_head(x, w, rank_down, rank_cols, bias_cols, dk, dv):
    n, d = x.shape
    rank = rank_down.shape[1]
    per = BLOCK // CHUNK
    return pl.pallas_call(
        forward_head_kernel,
        name="forward_head",
        grid=(n // BLOCK,),
        in_specs=[
            rows_spec(BLOCK, d), whole(w.shape), whole(rank_down.shape), whole(rank_cols.shape), whole(bias_cols.shape),
        ],
        out_specs=[
            rows_spec(BLOCK, dk), rows_spec(BLOCK, dk), rows_spec(BLOCK, dv), rows_spec(BLOCK, dv),
            rows_spec(BLOCK, dk), rows_spec(BLOCK, dk), rows_spec(BLOCK, rank), rows_spec(BLOCK, dv), rows_spec(BLOCK, dk),
            pl.BlockSpec((per, dv, dk), lambda i: (i, 0, 0)), pl.BlockSpec((per, 1, dk), lambda i: (i, 0, 0)),
            whole((dv, dk)), whole((1, dk)),
        ],
        out_shape=[
            sds((n, dk), BF16), sds((n, dk), BF16), sds((n, dv), BF16), sds((n, dv), F32),
            sds((n, dk), F32), sds((n, dk), F32), sds((n, rank), F32), sds((n, dv), F32), sds((n, dk), BF16),
            sds((n // CHUNK, dv, dk), BF16), sds((n // CHUNK, 1, dk), F32),
            sds((dv, dk), F32), sds((1, dk), F32),
        ],
        scratch_shapes=[pltpu.VMEM((dv, dk), F32), pltpu.VMEM((1, dk), F32)],
        compiler_params=params(),
        cost_estimate=cost(2 * n * d * (2 * dk + 2 * dv) * 1.5, n * d * 2 + n * 4000, n * dk * 6),
    )(x, w, rank_down, rank_cols, bias_cols)


def gate_out_kernel(b0, b1, r0, r1, s0, s1, e0, e1, gain_ref, w0, w1, m0, m1, g0, g1, out_ref):
    total = None
    gain = gain_ref[...]
    for b, r, s, e, w, m, g in ((b0, r0, s0, e0, w0, m0, g0), (b1, r1, s1, e1, w1, m1, g1)):
        mixed = b[...] + dot_nt(r[...], e[...])
        inv = lax.rsqrt(jnp.mean(mixed * mixed, axis=-1, keepdims=True) + GROUP_EPS)
        sw = s[...]
        gated = (mixed * inv * gain * (sw * jax.nn.sigmoid(sw))).astype(BF16)
        m[...] = mixed
        g[...] = gated
        part = dot(gated, w[...])
        total = part if total is None else total + part
    out_ref[...] = total.astype(BF16)


def gate_out(bases, reaches, swishes, enters, gain, weights):
    n, dv = bases[0].shape
    dk = reaches[0].shape[1]
    d = weights[0].shape[1]
    row = rows_spec(BLOCK, dv)
    return pl.pallas_call(
        gate_out_kernel,
        name="gate_out",
        grid=(n // BLOCK,),
        in_specs=[row, row, rows_spec(BLOCK, dk), rows_spec(BLOCK, dk), row, row]
        + [whole((dv, dk))] * 2 + [whole((1, dv))] + [whole((dv, d))] * 2,
        out_specs=[row, row, row, row, rows_spec(BLOCK, d)],
        out_shape=[sds((n, dv), F32)] * 2 + [sds((n, dv), BF16)] * 2 + [sds((n, d), BF16)],
        compiler_params=params(),
        cost_estimate=cost(2 * n * dv * (d + dk) * 2, n * (dv * 28 + d * 2), n * dv * 2),
    )(*bases, *reaches, *swishes, *enters, gain, *weights)


def tile_of(step):
    return jnp.where((step == 5) | (step == 6), 11 - step, step)


def mlp_phase_kernel(
    mid_h, c0_h, c1_h, c2_h, c3_h, wg_h, wu_h, wd_h, gain_ref,
    gmid_h, gm_h, part_ref, grads_h, dn_h,
    mid, xs, cs, wg, wu, wd, hs, ggs, gus, gn, rc, rd, ac, ry, dn_st, gr_st, gmb,
    load_sem, send_sem, recv_sem, dn_sem, gr_sem, out_sem,
):
    tile = xs.shape[1]
    rows = 2 * tile
    d = xs.shape[2]
    ff = hs.shape[2]
    wide, place = lax.axis_index("wide"), lax.axis_index("narrow")
    core = place % 2
    by_core = (wide, place + 1 - 2 * core)
    by_row = (wide, (place + 2) % 4)

    loads = [pltpu.make_async_copy(mid_h, mid, load_sem.at[0])]
    for i, (src, dst) in enumerate(((wg_h, wg), (wu_h, wu), (wd_h, wd))):
        loads.append(pltpu.make_async_copy(src, dst, load_sem.at[1 + i]))
    for i, src in enumerate((c0_h, c1_h, c2_h, c3_h)):
        for j in range(2):
            loads.append(
                pltpu.make_async_copy(src.at[pl.ds(j * tile, tile)], cs.at[2 * i + j], load_sem.at[4 + 2 * i + j])
            )
    for load in loads:
        load.start()

    barrier = pltpu.get_barrier_semaphore()
    for other in (by_core, by_row):
        pl.semaphore_signal(barrier, 1, device_id=other, device_id_type=MESH)
    pl.semaphore_wait(barrier, 2)

    def remote(src, dst, index, target):
        return pltpu.make_async_remote_copy(
            src, dst, send_sem.at[index], recv_sem.at[index], device_id=target, device_id_type=MESH
        )

    x_row = [remote(xs.at[j], xs.at[4 + j], j, by_row) for j in range(2)]
    x_core = [remote(xs.at[j], xs.at[2 + j], 2 + j, by_core) for j in range(2)]
    x_both = [remote(xs.at[4 + j], xs.at[6 + j], 4 + j, by_core) for j in range(2)]
    g_near = [remote(gn.at[2 + j], rc.at[j], 6 + j, by_core) for j in range(2)]
    g_far = [remote(gn.at[6 + j], rd.at[j], 8 + j, by_core) for j in range(2)]
    g_row = [remote(ac.at[j], ry.at[j], 10 + j, by_row) for j in range(2)]
    gain = gain_ref[...]

    loads[0].wait()
    for j in range(2):
        m = mid[pl.ds(j * tile, tile), :]
        inv = lax.rsqrt(jnp.mean(m * m, axis=-1, keepdims=True) + NORM_EPS)
        xs[j] = (m * inv * gain).astype(BF16)
        x_row[j].start()
        x_core[j].start()
    for load in loads[1:]:
        load.wait()

    def dn_copy(slot, at):
        return pltpu.make_async_copy(dn_st.at[slot], dn_h.at[at], dn_sem.at[slot])

    def step(s, _):
        t = tile_of(s)
        slot = s % 2

        @pl.when(s == 2)
        def _():
            x_core[0].wait_recv()

        @pl.when(s == 3)
        def _():
            x_core[1].wait_recv()

        for j in range(2):

            @pl.when(s == 4 + 2 * j)
            def _():
                x_row[j].wait_recv()
                x_both[j].start()

            @pl.when(s == 5 + 2 * j)
            def _():
                x_both[j].wait_recv()

        x = xs[t]
        gate = dot_nt(x, wg[...])
        up = dot_nt(x, wu[...])
        gh = dot_nt(cs[t], wd[...])
        sig = jax.nn.sigmoid(gate)
        act = gate * sig
        hidden = (act * up).astype(BF16)
        g_up = (gh * act).astype(BF16)
        g_gate = (gh * up * sig * (1.0 + gate * (1.0 - sig))).astype(BF16)
        hs[t] = hidden
        ggs[t] = g_gate
        gus[t] = g_up
        gn[t] = (dot(g_gate, wg[...]) + dot(g_up, wu[...])).astype(BF16)

        for j in range(2):

            @pl.when(s == 2 + j)
            def _():
                g_near[j].start()

            @pl.when(s == 5 + 2 * j)
            def _():
                g_far[j].start()

        @pl.when(s >= 2)
        def _():
            dn_copy(slot, tile_of(s - 2)).wait()

        dn_st[slot] = dot(hidden, wd[...]).astype(BF16)
        dn_copy(slot, t).start()

        for j in range(2):

            @pl.when(s == 5 + 2 * j)
            def _():
                g_far[j].wait_recv()
                ac[j] = (gn[4 + j].astype(F32) + rd[j].astype(F32)).astype(BF16)
                g_row[j].start()

        return 0

    lax.fori_loop(0, 8, step, 0)
    dn_copy(0, tile_of(6)).wait()
    dn_copy(1, tile_of(7)).wait()

    blk = gr_st.shape[1]
    count = d // blk

    def gr_copy(slot, j):
        return pltpu.make_async_copy(
            gr_st.at[slot], grads_h.at[pl.ds(pl.multiple_of(j * blk, blk), blk)], gr_sem.at[slot]
        )

    def weights(j, _):
        slot = j % 2
        cols = pl.ds(pl.multiple_of(j * blk, blk), blk)

        @pl.when(j >= 2)
        def _():
            gr_copy(slot, j - 2).wait()

        for at, lefts, rights in ((0, xs, ggs), (ff, xs, gus), (2 * ff, cs, hs)):
            acc = dot_tn(lefts[0, :, cols], rights[0])
            for t in range(1, 8):
                acc = acc + dot_tn(lefts[t, :, cols], rights[t])
            gr_st[slot, :, at : at + ff] = acc.astype(BF16)
        gr_copy(slot, j).start()
        return 0

    lax.fori_loop(0, count, weights, 0)
    gr_copy(count % 2, count - 2).wait()
    gr_copy((count + 1) % 2, count - 1).wait()

    part = jnp.zeros((1, d), F32)
    gm_out = []
    for j in range(2):
        at = pl.ds(j * tile, tile)
        g_near[j].wait_recv()
        g_row[j].wait_recv()
        grad = gn[j].astype(F32) + rc[j].astype(F32) + ry[j].astype(F32)
        m = mid[at, :]
        inv = lax.rsqrt(jnp.mean(m * m, axis=-1, keepdims=True) + NORM_EPS)
        unit = m * inv
        weighted = grad * gain
        part = part + jnp.sum(grad * unit, axis=0, keepdims=True)
        gmid = cs[j].astype(F32) + inv * (weighted - unit * jnp.mean(weighted * unit, axis=-1, keepdims=True))
        mid[at, :] = gmid
        gmb[j] = gmid.astype(BF16)
        there = gm_h.at[pl.ds(pl.multiple_of(core * rows + j * tile, tile), tile)]
        copies = [
            pltpu.make_async_copy(gmb.at[j], there, out_sem.at[1 + j]),
            remote(gmb.at[j], there, 12 + j, by_core),
        ]
        for copy in copies:
            copy.start()
        gm_out += copies
    part_ref[...] = part
    last = pltpu.make_async_copy(mid, gmid_h, out_sem.at[0])
    last.start()
    for copy in gm_out:
        copy.wait()
    last.wait()
    for group in (x_row, x_core, x_both, g_near, g_far, g_row):
        for copy in group:
            copy.wait_send()


def mlp_phase(middle, cots, wg_t, wu_t, wd, gain):
    rows, d = middle.shape
    ff = wd.shape[0]
    tile = rows // 2
    blk = 128
    hbm = pl.BlockSpec(memory_space=pltpu.HBM)
    vmem = pl.BlockSpec(memory_space=pltpu.VMEM)
    dma = pltpu.SemaphoreType.DMA
    return pl.pallas_call(
        mlp_phase_kernel,
        name="mlp_phase",
        in_specs=[hbm] * 8 + [vmem],
        out_specs=[hbm, hbm, vmem, hbm, hbm],
        out_shape=[
            sds((rows, d), F32), sds((2 * rows, d), BF16), sds((1, d), F32), sds((d, 3 * ff), BF16), sds((8, tile, d), BF16),
        ],
        scratch_shapes=[
            pltpu.VMEM((rows, d), F32), pltpu.VMEM((8, tile, d), BF16), pltpu.VMEM((8, tile, d), BF16),
            pltpu.VMEM((ff, d), BF16), pltpu.VMEM((ff, d), BF16), pltpu.VMEM((ff, d), BF16),
            pltpu.VMEM((8, tile, ff), BF16), pltpu.VMEM((8, tile, ff), BF16), pltpu.VMEM((8, tile, ff), BF16),
            pltpu.VMEM((8, tile, d), BF16), pltpu.VMEM((2, tile, d), BF16), pltpu.VMEM((2, tile, d), BF16),
            pltpu.VMEM((2, tile, d), BF16), pltpu.VMEM((2, tile, d), BF16),
            pltpu.VMEM((2, tile, d), BF16), pltpu.VMEM((2, blk, 3 * ff), BF16), pltpu.VMEM((2, tile, d), BF16),
            dma((12,)), dma((14,)), dma((14,)), dma((2,)), dma((2,)), dma((3,)),
        ],
        compiler_params=pltpu.CompilerParams(collective_id=1, has_side_effects=True, vmem_limit_bytes=62 << 20),
        cost_estimate=cost(18 * 4 * rows * d * ff, 60e6, 4 * rows * ff),
    )(middle, *cots, wg_t, wu_t, wd, gain)


def gate_back_kernel(
    gm_ref, m0, m1, s0, s1, r0, r1, gain_ref, w0, w1, gx0, gx1, gs0, gs1, lb0, lb1, gp_ref
):
    i = pl.program_id(0)

    @pl.when(i == 0)
    def _():
        lb0[...] = jnp.zeros_like(lb0)
        lb1[...] = jnp.zeros_like(lb1)
        gp_ref[...] = jnp.zeros_like(gp_ref)

    gm = gm_ref[...]
    gain = gain_ref[...]
    for m, s, r, w, gx, gs, lb in ((m0, s0, r0, w0, gx0, gs0, lb0), (m1, s1, r1, w1, gx1, gs1, lb1)):
        grad = dot_nt(gm, w[...])
        mixed = m[...]
        inv = lax.rsqrt(jnp.mean(mixed * mixed, axis=-1, keepdims=True) + GROUP_EPS)
        unit = mixed * inv
        sw = s[...]
        sig = jax.nn.sigmoid(sw)
        gs[...] = (grad * unit * gain * (sig * (1.0 + sw * (1.0 - sig)))).astype(BF16)
        dn = grad * (sw * sig)
        gp_ref[...] += jnp.sum(dn * unit, axis=0, keepdims=True)
        weighted = dn * gain
        gmix = (inv * (weighted - unit * jnp.mean(weighted * unit, axis=-1, keepdims=True))).astype(BF16)
        gx[...] = gmix
        lb[...] += dot_tn(gmix, r[...])


def gate_back(gm, mixeds, swishes, reaches, gain, weights):
    n, d = gm.shape
    dv = mixeds[0].shape[1]
    dk = reaches[0].shape[1]
    row = rows_spec(BLOCK, dv)
    return pl.pallas_call(
        gate_back_kernel,
        name="gate_back",
        grid=(n // BLOCK,),
        in_specs=[rows_spec(BLOCK, d), row, row, row, row, rows_spec(BLOCK, dk), rows_spec(BLOCK, dk)]
        + [whole((1, dv))] + [whole((dv, d))] * 2,
        out_specs=[row] * 4 + [whole((dv, dk))] * 2 + [whole((1, dv))],
        out_shape=[sds((n, dv), BF16)] * 4 + [sds((dv, dk), F32)] * 2 + [sds((1, dv), F32)],
        compiler_params=params(),
        cost_estimate=cost(2 * n * dv * (d + dk) * 2, n * (dv * 28 + d * 2), n * dv * 2),
    )(gm, *mixeds, *swishes, *reaches, gain, *weights)


def back_head_kernel(
    q_ref, k_ref, v_ref, cum_ref, dpre_ref, rank_ref, sin_ref, off_ref, gx_ref, gs_ref, enter_ref, later_ref, ru_ref,
    all_ref, grank_ref, rup_ref, bias_ref,
    ds,
):
    i = pl.program_id(0)
    dk = q_ref.shape[1]
    dv = v_ref.shape[1]

    @pl.when(i == 0)
    def _():
        ds[...] = later_ref[...]
        rup_ref[...] = jnp.zeros_like(rup_ref)
        bias_ref[...] = jnp.zeros_like(bias_ref)

    mask = triangle(True)
    ones = triangle(False).astype(F32)
    scale = dk**-0.5
    enter = enter_ref[...]
    for j in reversed(range(BLOCK // CHUNK)):
        rows = slice(j * CHUNK, (j + 1) * CHUNK)
        cum = cum_ref[rows, :]
        mid = cum[HALF - 1 : HALF]
        end = cum[CHUNK - 1 :]
        e_qd, e_kd, e_qi, e_ke = jnp.exp(cum - mid), jnp.exp(mid - cum), jnp.exp(cum), jnp.exp(end - cum)
        e_end = jnp.exp(end)
        qf = q_ref[rows, :].astype(F32) * scale
        kf = k_ref[rows, :].astype(F32)
        v = v_ref[rows, :]
        qd = (qf * e_qd).astype(BF16)
        kd = (kf * e_kd).astype(BF16)
        qi = (qf * e_qi).astype(BF16)
        ke = (kf * e_ke).astype(BF16)
        go = gx_ref[rows, :]
        state = sin_ref[j].astype(F32) + enter * jnp.exp(off_ref[j])
        state_low = state.astype(BF16)
        dstate = ds[...]
        dstate_low = dstate.astype(BF16)
        scores = jnp.where(mask, dot_nt(qd, kd), 0.0).astype(BF16)
        dscores = jnp.where(mask, dot_nt(go, v), 0.0).astype(BF16)
        d_v = dot_tn(scores, go) + dot_nt(ke, dstate_low)
        d_qd = dot(dscores, kd)
        d_qi = dot(go, state_low)
        d_kd = dot_tn(dscores, qd)
        d_ke = dot(v, dstate_low)
        d_q = scale * (d_qd * e_qd + d_qi * e_qi)
        d_k = d_kd * e_kd + d_ke * e_ke
        tail = ke.astype(F32) * d_ke
        d_cum = qd.astype(F32) * d_qd + qi.astype(F32) * d_qi - kd.astype(F32) * d_kd - tail
        d_end = jnp.sum(tail, axis=0, keepdims=True) + e_end * jnp.sum(dstate * state, axis=0, keepdims=True)
        grad_decay = exact(ones, d_cum, ((1,), (0,))) + d_end
        g_pre = grad_decay * jax.nn.sigmoid(-dpre_ref[rows, :]) * (1.0 / GATE_NORM)
        all_ref[rows, :dk] = d_q.astype(BF16)
        all_ref[rows, dk : 2 * dk] = d_k.astype(BF16)
        all_ref[rows, 2 * dk : 2 * dk + dv] = d_v.astype(BF16)
        all_ref[rows, 2 * dk + dv :] = gs_ref[rows, :]
        grank_ref[rows, :] = exact(g_pre, ru_ref[...], ((1,), (1,)))
        rup_ref[...] += exact(rank_ref[rows, :], g_pre, ((0,), (0,)))
        bias_ref[...] += jnp.sum(g_pre, axis=0, keepdims=True)
        ds[...] = dstate * e_end + dot_tn(go, qi)


def back_head(q, k, v, cum, dpre, rank, sin, off, gx, gs, enter, later, rank_cols):
    n, dk = q.shape
    dv = v.shape[1]
    rk = rank.shape[1]
    per = BLOCK // CHUNK
    last = n // BLOCK - 1

    def rev(rows, cols):
        return pl.BlockSpec((rows, cols), lambda i: (last - i, 0))

    return pl.pallas_call(
        back_head_kernel,
        name="back_head",
        grid=(n // BLOCK,),
        in_specs=[
            rev(BLOCK, dk), rev(BLOCK, dk), rev(BLOCK, dv), rev(BLOCK, dk), rev(BLOCK, dk), rev(BLOCK, rk),
            pl.BlockSpec((per, dv, dk), lambda i: (last - i, 0, 0)), pl.BlockSpec((per, 1, dk), lambda i: (last - i, 0, 0)),
            rev(BLOCK, dv), rev(BLOCK, dv), whole((dv, dk)), whole((dv, dk)), whole((rk, dk)),
        ],
        out_specs=[rev(BLOCK, 2 * dk + 2 * dv), rev(BLOCK, rk), whole((rk, dk)), whole((1, dk))],
        out_shape=[sds((n, 2 * dk + 2 * dv), BF16), sds((n, rk), F32), sds((rk, dk), F32), sds((1, dk), F32)],
        scratch_shapes=[pltpu.VMEM((dv, dk), F32)],
        compiler_params=params(),
        cost_estimate=cost(n * 128 * 128 * 40, n * 6000, n * dk * 6),
    )(q, k, v, cum, dpre, rank, sin, off, gx, gs, enter, later, rank_cols)


def hop(value, axis, bit):
    return lax.ppermute(value, axis, [(i, i ^ bit) for i in range(lax.axis_size(axis))])


def wide_bits():
    count, bits, bit = lax.axis_size("wide"), [], 1
    while bit < count:
        bits.append(bit)
        bit *= 2
    return bits


def scan_states(mult, state, backward):
    place = {"narrow": lax.axis_index("narrow"), "wide": lax.axis_index("wide")}
    heads, dv, dk = state.shape
    pre_m, pre_s = jnp.ones_like(mult), jnp.zeros_like(state)
    tot_m, tot_s = mult, state
    for axis, bit in [("narrow", 2)] + [("wide", b) for b in wide_bits()]:
        packed = jnp.concatenate(
            [tot_s, jnp.broadcast_to(tot_m, (heads, 16, dk))], axis=1
        ).astype(BF16)
        other = hop(packed, axis, bit).astype(F32)
        if axis == "narrow":
            other = other[::-1]
        oth_s, oth_m = other[:, :dv], other[:, dv : dv + 1]
        is_set = (place[axis] & bit) != 0
        mine_later = jnp.logical_not(is_set) if backward else is_set
        new_s = oth_s * pre_m + pre_s
        new_m = oth_m * pre_m
        sum_later = oth_s * tot_m + tot_s
        sum_first = tot_s * oth_m + oth_s
        pre_s = jnp.where(mine_later, new_s, pre_s)
        pre_m = jnp.where(mine_later, new_m, pre_m)
        tot_s = jnp.where(mine_later, sum_later, sum_first)
        tot_m = tot_m * oth_m
    return pre_s


def scatter_rows(value, bits):
    count = lax.axis_size("wide")
    place = lax.axis_index("wide")
    rows, cols = value.shape[0] // count, value.shape[1]
    order = sorted(bits, reverse=True)
    value = value.reshape((2,) * len(bits) + (rows, cols))
    left = list(order)
    for bit in bits:
        dim = left.index(bit)
        mine = jnp.where((place & bit) != 0, 1, 0)
        keep = lax.dynamic_index_in_dim(value, mine, dim, False)
        send = lax.dynamic_index_in_dim(value, 1 - mine, dim, False)
        got = hop(send.astype(BF16), "wide", bit)
        value = keep.astype(F32) + got.astype(F32)
        left.pop(dim)
        if left:
            value = value.astype(BF16)
    return value


def sum_everywhere(value):
    for axis, bit in [("narrow", 1), ("narrow", 2)] + [("wide", b) for b in wide_bits()]:
        value = value + hop(value, axis, bit)
    return value


def norm_back(grad, values, inv, gain):
    unit = values * inv
    weighted = grad * gain
    part = jnp.sum(grad * unit, axis=0, keepdims=True)
    return inv * (weighted - unit * jnp.mean(weighted * unit, axis=-1, keepdims=True)), part


def shards(
    tokens, cotangent, flags, norm_gain, query_weight, key_weight, value_weight, swish_weight, rank_down, rank_up,
    decay_bias, group_gain, output_weight, mlp_gain, mlp_gate, mlp_up, mlp_down,
):
    own_rows = tokens.shape[0]
    place = lax.axis_index("narrow")
    core = place & 1
    second = (place & 2) != 0
    wide_odd = (lax.axis_index("wide") & 1) != 0
    dk = query_weight.shape[1]
    dv = value_weight.shape[1]
    d = tokens.shape[1]

    def in_order(mine, other):
        return jnp.where(
            core == 0, jnp.concatenate([mine, other]), jnp.concatenate([other, mine])
        )

    def from_row_partner(value):
        half = value.shape[0] // 2
        piece = lax.dynamic_slice_in_dim(value, jnp.where(wide_odd, half, 0), half, 0)
        first = hop(piece, "narrow", 2)
        relayed = hop(first, "wide", 1)
        return jnp.where(
            wide_odd, jnp.concatenate([relayed, first]), jnp.concatenate([first, relayed])
        )

    def head_cols(index):
        ru = lax.dynamic_slice_in_dim(rank_up, index * dk, dk, 1).astype(F32)
        bias = lax.dynamic_slice_in_dim(decay_bias, index * dk, dk, 0).astype(F32)
        return ru, bias.reshape(1, dk)

    restart = 1.0 - flags[0].astype(F32)
    restart = jnp.where(second, 1.0, restart)
    norm_gain_f = norm_gain.astype(F32)
    mlp_gain_f = mlp_gain.astype(F32)
    gain_row = group_gain.astype(F32).reshape(1, dv)

    inputs = tokens.astype(F32)
    inv_one = lax.rsqrt(jnp.mean(inputs * inputs, axis=-1, keepdims=True) + NORM_EPS)
    normed = (inputs * inv_one * norm_gain_f).astype(BF16)
    normed_two = hop(normed, "narrow", 1)
    rows_all = in_order(normed, normed_two)

    w_own = jnp.concatenate([query_weight, key_weight, value_weight, swish_weight], axis=1)
    w_other = from_row_partner(w_own)
    out_other = from_row_partner(output_weight)
    cot_late, w_other, out_other = lax.optimization_barrier((cotangent, w_other, out_other))
    cot_y = hop(cot_late, "narrow", 2)
    cot_c = hop(cotangent, "narrow", 1)
    cot_d = hop(cot_y, "narrow", 1)

    ru_own, bias_own = head_cols(place)
    ru_oth, bias_oth = head_cols(place ^ 2)
    weights_out = (output_weight, out_other)
    one = forward_head(rows_all, w_own, rank_down, ru_own, bias_own, dk, dv)
    two = forward_head(rows_all, w_other, rank_down, ru_oth, bias_oth, dk, dv)
    (q, k, v, s, cum, dpre, rank_pre, base, reach, sin, off, state, mult) = zip(one, two)
    rank_pre = rank_pre[0]
    mults = restart * jnp.stack(mult)
    enter = restart * scan_states(mults, jnp.stack(state), False)
    enter_low = enter.astype(BF16)
    mixed0, mixed1, gated0, gated1, term = gate_out(
        base, reach, s, (enter_low[0], enter_low[1]), gain_row, weights_out
    )
    own_term = lax.dynamic_slice_in_dim(term, core * own_rows, own_rows, 0)
    send_term = lax.dynamic_slice_in_dim(term, (1 - core) * own_rows, own_rows, 0)
    middle = inputs + (own_term.astype(F32) + hop(send_term, "narrow", 1).astype(F32))
    grad_middle, gm_all, mlp_gain_part, mlp_w_grads, dns = mlp_phase(
        middle, (cotangent, cot_c, cot_y, cot_d), mlp_gate.T, mlp_up.T, mlp_down, mlp_gain_f.reshape(1, d)
    )
    bits = wide_bits()
    mlp_w = scatter_rows(mlp_w_grads, bits)

    def gather_sum(parts):
        own, by_core, by_y, by_both = parts
        across = by_y.astype(F32) + hop(by_both, "narrow", 1).astype(F32)
        near = own.astype(F32) + hop(by_core, "narrow", 1).astype(F32)
        return near + hop(across.astype(BF16), "narrow", 2).astype(F32)

    gx0, gx1, gs0, gs1, lb0, lb1, group_part = gate_back(
        gm_all, (mixed0, mixed1), s, reach, gain_row, weights_out
    )
    later = scan_states(mults, restart * jnp.stack([lb0, lb1]), True)
    dns = dns.reshape(4, own_rows, d)
    result = (middle + gather_sum((dns[0], dns[1], dns[2], dns[3]))).astype(BF16)

    all0, gr0, rup0, gb0 = back_head(
        q[0], k[0], v[0], cum[0], dpre[0], rank_pre, sin[0], off[0], gx0, gs0, enter[0], later[0], ru_own
    )
    all1, gr1, rup1, gb1 = back_head(
        q[1], k[1], v[1], cum[1], dpre[1], rank_pre, sin[1], off[1], gx1, gs1, enter[1], later[1], ru_oth
    )
    grad_rank = (gr0 + gr1).astype(BF16)
    total = dot_nt(all0, w_own) + dot_nt(all1, w_other) + dot_nt(grad_rank, rank_down)
    total = total.astype(BF16)
    own_total = lax.dynamic_slice_in_dim(total, core * own_rows, own_rows, 0)
    send_total = lax.dynamic_slice_in_dim(total, (1 - core) * own_rows, own_rows, 0)
    grad_normed = own_total.astype(F32) + hop(send_total, "narrow", 1).astype(F32)
    grad_input, norm_gain_part = norm_back(grad_normed, inputs, inv_one, norm_gain_f)
    input_grad = grad_middle + grad_input

    def over_y(mine, other):
        return (mine + hop(other.astype(BF16), "narrow", 2).astype(F32)).astype(BF16)

    qkvs = over_y(dot_tn(rows_all, all0), dot_tn(rows_all, all1))
    outs = over_y(dot_tn(gm_all, gated0), dot_tn(gm_all, gated1))
    qkvs = scatter_rows(qkvs, bits)
    outs = scatter_rows(outs, bits)
    grad_rank_down = dot_tn(rows_all, grad_rank)

    def spread(mine, other, width):
        zero = jnp.zeros((mine.shape[0], width), F32)
        zero = lax.dynamic_update_slice_in_dim(zero, mine, place * dk, 1)
        return lax.dynamic_update_slice_in_dim(zero, other, (place ^ 2) * dk, 1)

    qk = rank_up.shape[1]
    rank = rank_up.shape[0]
    small = [
        norm_gain_part,
        mlp_gain_part,
        group_part,
        grad_rank_down.T,
        spread(rup0, rup1, qk),
        spread(gb0, gb1, qk),
    ]
    flat = jnp.concatenate([jnp.reshape(part, (-1, dk)) for part in small])
    flat = sum_everywhere(flat)
    parts, at = [], 0
    for part in small:
        size = part.size // dk
        parts.append(flat[at : at + size].reshape(part.shape))
        at += size
    ff = mlp_gate.shape[1]
    return (
        result,
        input_grad,
        parts[0].reshape(d),
        qkvs[:, :dk],
        qkvs[:, dk : 2 * dk],
        qkvs[:, 2 * dk : 2 * dk + dv],
        qkvs[:, 2 * dk + dv :],
        parts[3].reshape(rank, d).T,
        parts[4].reshape(rank, qk),
        parts[5].reshape(qk),
        parts[2].reshape(dv),
        outs.T,
        parts[1].reshape(d),
        mlp_w[:, :ff],
        mlp_w[:, ff : 2 * ff],
        mlp_w[:, 2 * ff :].T,
    )


def solution(mesh):
    rows, cols = P(("wide", "narrow"), None), P(None, "narrow")
    both = P("wide", "narrow")
    in_specs = (
        rows, rows, P("wide"), P(), cols, cols, cols, cols, P(), P(), P(), P(), P("narrow", None), P(), cols, cols,
        P("narrow", None),
    )
    out_specs = (
        rows, rows, P(), both, both, both, both, P(), P(), P(), P(), P("narrow", "wide"), P(), both, both,
        P("narrow", "wide"),
    )
    return jax.shard_map(shards, mesh=mesh, in_specs=in_specs, out_specs=out_specs, check_vma=False)
```

```python
import itertools

import jax
import jax.numpy as jnp
from jax import lax
from jax.experimental import pallas as pl
from jax.experimental.pallas import tpu as pltpu
from jax.sharding import PartitionSpec as P

NORM_EPS = 1e-06
GROUP_EPS = 1e-05
GATE_NORM = 16.0
HIGHEST_PREC = lax.Precision.HIGHEST
MESH = pl.DeviceIdType.MESH
CHUNK = 128
HALF = CHUNK // 2
BLOCK = 256
F32 = jnp.float32
BF16 = jnp.bfloat16


def dot(a, b):
    return lax.dot_general(a, b, (((1,), (0,)), ((), ())), preferred_element_type=F32)


def dot_nt(a, b):
    return lax.dot_general(a, b, (((1,), (1,)), ((), ())), preferred_element_type=F32)


def dot_tn(a, b):
    return lax.dot_general(a, b, (((0,), (0,)), ((), ())), preferred_element_type=F32)


def exact(a, b, dims):
    return lax.dot_general(
        a, b, (dims, ((), ())), precision=HIGHEST_PREC, preferred_element_type=F32
    )


def sds(shape, dtype):
    return jax.ShapeDtypeStruct(shape, dtype)


def params(mib=48):
    return pltpu.CompilerParams(vmem_limit_bytes=mib << 20)


def cost(flops, nbytes, trans=0):
    return pl.CostEstimate(flops=int(flops), bytes_accessed=int(nbytes), transcendentals=int(trans))


def whole(shape):
    return pl.BlockSpec(shape, lambda i: (0,) * len(shape), pipeline_mode=pl.Buffered(1))


def rows_spec(rows, cols):
    return pl.BlockSpec((rows, cols), lambda i: (i, 0))


def triangle(lower):
    r = lax.broadcasted_iota(jnp.int32, (CHUNK, CHUNK), 0)
    c = lax.broadcasted_iota(jnp.int32, (CHUNK, CHUNK), 1)
    return r >= c if lower else r <= c


def forward_head_kernel(
    x_ref, w_ref, rd_ref, ru_ref, bias_ref,
    q_ref, k_ref, v_ref, s_ref, cum_ref, dpre_ref, rank_ref, base_ref, reach_ref, sin_ref, off_ref,
    state_ref, mult_ref,
    st, off,
):
    i = pl.program_id(0)
    dk = q_ref.shape[1]
    dv = v_ref.shape[1]

    @pl.when(i == 0)
    def _():
        st[...] = jnp.zeros_like(st)
        off[...] = jnp.zeros_like(off)

    x = x_ref[...]
    proj = dot(x, w_ref[...])
    rank = dot(x, rd_ref[...])
    dpre = exact(rank, ru_ref[...], ((1,), (0,))) + bias_ref[...]
    dlog = jax.nn.log_sigmoid(dpre) * (1.0 / GATE_NORM)
    k_low = proj[:, :dk].astype(BF16)
    v_low = proj[:, dk : dk + dv].astype(BF16)
    q_low = proj[:, dk + dv : 2 * dk + dv].astype(BF16)
    q_ref[...] = q_low
    k_ref[...] = k_low
    v_ref[...] = v_low
    s_ref[...] = proj[:, 2 * dk + dv :]
    rank_ref[...] = rank
    dpre_ref[...] = dpre
    mask = triangle(True)
    ones = mask.astype(F32)
    scale = dk**-0.5
    for j in range(BLOCK // CHUNK):
        rows = slice(j * CHUNK, (j + 1) * CHUNK)
        cum = exact(ones, dlog[rows], ((1,), (0,)))
        mid = cum[HALF - 1 : HALF]
        end = cum[CHUNK - 1 :]
        qf = q_low[rows].astype(F32) * scale
        kf = k_low[rows].astype(F32)
        v = v_low[rows]
        qd = (qf * jnp.exp(cum - mid)).astype(BF16)
        kd = (kf * jnp.exp(mid - cum)).astype(BF16)
        qi = (qf * jnp.exp(cum)).astype(BF16)
        ke = (kf * jnp.exp(end - cum)).astype(BF16)
        scores = jnp.where(mask, dot_nt(qd, kd), 0.0).astype(BF16)
        state = st[...]
        state_low = state.astype(BF16)
        offset = off[...]
        base_ref[rows, :] = dot(scores, v) + dot_nt(qi, state_low)
        reach_ref[rows, :] = (qf * jnp.exp(cum + offset)).astype(BF16)
        cum_ref[rows, :] = cum
        sin_ref[j] = state_low
        off_ref[j] = offset
        st[...] = state * jnp.exp(end) + dot_tn(v, ke)
        off[...] = offset + end
    state_ref[...] = st[...]
    mult_ref[...] = jnp.exp(off[...])


def forward_head(x, w, rank_down, rank_cols, bias_cols, dk, dv):
    n, d = x.shape
    rank = rank_down.shape[1]
    per = BLOCK // CHUNK
    return pl.pallas_call(
        forward_head_kernel,
        name="forward_head",
        grid=(n // BLOCK,),
        in_specs=[
            rows_spec(BLOCK, d), whole(w.shape), whole(rank_down.shape), whole(rank_cols.shape), whole(bias_cols.shape),
        ],
        out_specs=[
            rows_spec(BLOCK, dk), rows_spec(BLOCK, dk), rows_spec(BLOCK, dv), rows_spec(BLOCK, dv),
            rows_spec(BLOCK, dk), rows_spec(BLOCK, dk), rows_spec(BLOCK, rank), rows_spec(BLOCK, dv), rows_spec(BLOCK, dk),
            pl.BlockSpec((per, dv, dk), lambda i: (i, 0, 0)), pl.BlockSpec((per, 1, dk), lambda i: (i, 0, 0)),
            whole((dv, dk)), whole((1, dk)),
        ],
        out_shape=[
            sds((n, dk), BF16), sds((n, dk), BF16), sds((n, dv), BF16), sds((n, dv), F32),
            sds((n, dk), F32), sds((n, dk), F32), sds((n, rank), F32), sds((n, dv), F32), sds((n, dk), BF16),
            sds((n // CHUNK, dv, dk), BF16), sds((n // CHUNK, 1, dk), F32),
            sds((dv, dk), F32), sds((1, dk), F32),
        ],
        scratch_shapes=[pltpu.VMEM((dv, dk), F32), pltpu.VMEM((1, dk), F32)],
        compiler_params=params(),
        cost_estimate=cost(2 * n * d * (2 * dk + 2 * dv) * 1.5, n * d * 2 + n * 4000, n * dk * 6),
    )(x, w, rank_down, rank_cols, bias_cols)


def gate_out_kernel(b0, b1, r0, r1, s0, s1, e0, e1, gain_ref, w0, w1, m0, m1, g0, g1, out_ref):
    total = None
    gain = gain_ref[...]
    for b, r, s, e, w, m, g in ((b0, r0, s0, e0, w0, m0, g0), (b1, r1, s1, e1, w1, m1, g1)):
        mixed = b[...] + dot_nt(r[...], e[...])
        inv = lax.rsqrt(jnp.mean(mixed * mixed, axis=-1, keepdims=True) + GROUP_EPS)
        sw = s[...]
        gated = (mixed * inv * gain * (sw * jax.nn.sigmoid(sw))).astype(BF16)
        m[...] = mixed
        g[...] = gated
        part = dot(gated, w[...])
        total = part if total is None else total + part
    out_ref[...] = total.astype(BF16)


def gate_out(bases, reaches, swishes, enters, gain, weights):
    n, dv = bases[0].shape
    dk = reaches[0].shape[1]
    d = weights[0].shape[1]
    row = rows_spec(BLOCK, dv)
    return pl.pallas_call(
        gate_out_kernel,
        name="gate_out",
        grid=(n // BLOCK,),
        in_specs=[row, row, rows_spec(BLOCK, dk), rows_spec(BLOCK, dk), row, row]
        + [whole((dv, dk))] * 2 + [whole((1, dv))] + [whole((dv, d))] * 2,
        out_specs=[row, row, row, row, rows_spec(BLOCK, d)],
        out_shape=[sds((n, dv), F32)] * 2 + [sds((n, dv), BF16)] * 2 + [sds((n, d), BF16)],
        compiler_params=params(),
        cost_estimate=cost(2 * n * dv * (d + dk) * 2, n * (dv * 28 + d * 2), n * dv * 2),
    )(*bases, *reaches, *swishes, *enters, gain, *weights)


def tile_of(step):
    return jnp.where((step == 5) | (step == 6), 11 - step, step)


def mlp_phase_kernel(
    mid_h, c0_h, c1_h, c2_h, c3_h, wg_h, wu_h, wd_h, gain_ref,
    gmid_h, gm_h, part_ref, gg_h, gu_h, gd_h, near_h, far_h,
    mid, xs, cs, wg, wu, wd, hs, ggs, gus, gn, rc, rd, ac, ry, dn, dnr, gr_st, gmb,
    load_sem, send_sem, recv_sem, gr_sem, out_sem,
):
    tile = xs.shape[1]
    rows = 2 * tile
    d = xs.shape[2]
    ff = hs.shape[2]
    wide, place = lax.axis_index("wide"), lax.axis_index("narrow")
    core = place % 2
    by_core = (wide, place + 1 - 2 * core)
    by_row = (wide, (place + 2) % 4)

    loads = [pltpu.make_async_copy(mid_h, mid, load_sem.at[0])]
    for i, (src, dst) in enumerate(((wg_h, wg), (wu_h, wu), (wd_h, wd))):
        loads.append(pltpu.make_async_copy(src, dst, load_sem.at[1 + i]))
    for i, src in enumerate((c0_h, c1_h, c2_h, c3_h)):
        for j in range(2):
            loads.append(
                pltpu.make_async_copy(src.at[pl.ds(j * tile, tile)], cs.at[2 * i + j], load_sem.at[4 + 2 * i + j])
            )
    for load in loads:
        load.start()

    barrier = pltpu.get_barrier_semaphore()
    for other in (by_core, by_row):
        pl.semaphore_signal(barrier, 1, device_id=other, device_id_type=MESH)
    pl.semaphore_wait(barrier, 2)

    def remote(src, dst, index, target):
        return pltpu.make_async_remote_copy(
            src, dst, send_sem.at[index], recv_sem.at[index], device_id=target, device_id_type=MESH
        )

    x_row = [remote(xs.at[j], xs.at[4 + j], j, by_row) for j in range(2)]
    x_core = [remote(xs.at[j], xs.at[2 + j], 2 + j, by_core) for j in range(2)]
    x_both = [remote(xs.at[4 + j], xs.at[6 + j], 4 + j, by_core) for j in range(2)]
    g_near = [remote(gn.at[2 + j], rc.at[j], 6 + j, by_core) for j in range(2)]
    g_far = [remote(gn.at[6 + j], rd.at[j], 8 + j, by_core) for j in range(2)]
    g_row = [remote(ac.at[j], ry.at[j], 10 + j, by_row) for j in range(2)]
    d_in = [remote(dn.at[(2, 3, 6, 7)[j]], dnr.at[j], 14 + j, by_core) for j in range(4)]
    gain = gain_ref[...]

    loads[0].wait()
    for j in range(2):
        m = mid[pl.ds(j * tile, tile), :]
        inv = lax.rsqrt(jnp.mean(m * m, axis=-1, keepdims=True) + NORM_EPS)
        xs[j] = (m * inv * gain).astype(BF16)
        x_row[j].start()
        x_core[j].start()
    for load in loads[1:]:
        load.wait()

    def step(s, _):
        t = tile_of(s)

        @pl.when(s == 2)
        def _():
            x_core[0].wait_recv()

        @pl.when(s == 3)
        def _():
            x_core[1].wait_recv()

        for j in range(2):

            @pl.when(s == 4 + 2 * j)
            def _():
                x_row[j].wait_recv()
                x_both[j].start()

            @pl.when(s == 5 + 2 * j)
            def _():
                x_both[j].wait_recv()

        x = xs[t]
        gate = dot_nt(x, wg[...])
        up = dot_nt(x, wu[...])
        gh = dot_nt(cs[t], wd[...])
        sig = jax.nn.sigmoid(gate)
        act = gate * sig
        hidden = (act * up).astype(BF16)
        g_up = (gh * act).astype(BF16)
        g_gate = (gh * up * sig * (1.0 + gate * (1.0 - sig))).astype(BF16)
        hs[t] = hidden
        ggs[t] = g_gate
        gus[t] = g_up
        gn[t] = (dot(g_gate, wg[...]) + dot(g_up, wu[...])).astype(BF16)

        for j in range(2):

            @pl.when(s == 2 + j)
            def _():
                g_near[j].start()

            @pl.when(s == 5 + 2 * j)
            def _():
                g_far[j].start()

        dn[t] = dot(hidden, wd[...]).astype(BF16)

        for j in range(2):

            @pl.when(s == 5 + 2 * j)
            def _():
                g_far[j].wait_recv()
                ac[j] = (gn[4 + j].astype(F32) + rd[j].astype(F32)).astype(BF16)
                g_row[j].start()

        return 0

    lax.fori_loop(0, 8, step, 0)
    for copy in d_in:
        copy.start()

    blk = gr_st.shape[2]
    count = d // blk

    def gr_copies(slot, j):
        at = pl.ds(pl.multiple_of(j * blk, blk), blk)
        return [
            pltpu.make_async_copy(gr_st.at[slot, i], dst.at[at], gr_sem.at[slot, i])
            for i, dst in enumerate((gg_h, gu_h, gd_h))
        ]

    def weights(j, _):
        slot = j % 2
        cols = pl.ds(pl.multiple_of(j * blk, blk), blk)

        @pl.when(j >= 2)
        def _():
            for copy in gr_copies(slot, j - 2):
                copy.wait()

        for i, lefts, rights in ((0, xs, ggs), (1, xs, gus), (2, cs, hs)):
            acc = dot_tn(lefts[0, :, cols], rights[0])
            for t in range(1, 8):
                acc = acc + dot_tn(lefts[t, :, cols], rights[t])
            gr_st[slot, i] = acc.astype(BF16)
        for copy in gr_copies(slot, j):
            copy.start()
        return 0

    lax.fori_loop(0, count, weights, 0)
    for j in (count - 2, count - 1):
        for copy in gr_copies(j % 2, j):
            copy.wait()
    sums = []
    for j in range(2):
        d_in[j].wait_recv()
        d_in[2 + j].wait_recv()
        for at, extra, out in ((j, j, near_h), (4 + j, 2 + j, far_h)):
            dn[at] = (dn[at].astype(F32) + dnr[extra].astype(F32)).astype(BF16)
            sums.append(pltpu.make_async_copy(dn.at[at], out.at[pl.ds(j * tile, tile)], out_sem.at[3 + len(sums)]))
            sums[-1].start()

    part = jnp.zeros((1, d), F32)
    gm_out = []
    for j in range(2):
        at = pl.ds(j * tile, tile)
        g_near[j].wait_recv()
        g_row[j].wait_recv()
        grad = gn[j].astype(F32) + rc[j].astype(F32) + ry[j].astype(F32)
        m = mid[at, :]
        inv = lax.rsqrt(jnp.mean(m * m, axis=-1, keepdims=True) + NORM_EPS)
        unit = m * inv
        weighted = grad * gain
        part = part + jnp.sum(grad * unit, axis=0, keepdims=True)
        gmid = cs[j].astype(F32) + inv * (weighted - unit * jnp.mean(weighted * unit, axis=-1, keepdims=True))
        mid[at, :] = gmid
        gmb[j] = gmid.astype(BF16)
        there = gm_h.at[pl.ds(pl.multiple_of(core * rows + j * tile, tile), tile)]
        copies = [
            pltpu.make_async_copy(gmb.at[j], there, out_sem.at[1 + j]),
            remote(gmb.at[j], there, 12 + j, by_core),
        ]
        for copy in copies:
            copy.start()
        gm_out += copies
    part_ref[...] = part
    last = pltpu.make_async_copy(mid, gmid_h, out_sem.at[0])
    last.start()
    for copy in gm_out:
        copy.wait()
    last.wait()
    for copy in sums:
        copy.wait()
    for group in (d_in, x_row, x_core, x_both, g_near, g_far, g_row):
        for copy in group:
            copy.wait_send()


def mlp_phase(middle, cots, wg_t, wu_t, wd, gain):
    rows, d = middle.shape
    ff = wd.shape[0]
    tile = rows // 2
    blk = 128
    hbm = pl.BlockSpec(memory_space=pltpu.HBM)
    vmem = pl.BlockSpec(memory_space=pltpu.VMEM)
    dma = pltpu.SemaphoreType.DMA
    return pl.pallas_call(
        mlp_phase_kernel,
        name="mlp_phase",
        in_specs=[hbm] * 8 + [vmem],
        out_specs=[hbm, hbm, vmem] + [hbm] * 5,
        out_shape=[sds((rows, d), F32), sds((2 * rows, d), BF16), sds((1, d), F32)]
        + [sds((d, ff), BF16)] * 3 + [sds((rows, d), BF16)] * 2,
        scratch_shapes=[
            pltpu.VMEM((rows, d), F32), pltpu.VMEM((8, tile, d), BF16), pltpu.VMEM((8, tile, d), BF16),
            pltpu.VMEM((ff, d), BF16), pltpu.VMEM((ff, d), BF16), pltpu.VMEM((ff, d), BF16),
            pltpu.VMEM((8, tile, ff), BF16), pltpu.VMEM((8, tile, ff), BF16), pltpu.VMEM((8, tile, ff), BF16),
            pltpu.VMEM((8, tile, d), BF16), pltpu.VMEM((2, tile, d), BF16), pltpu.VMEM((2, tile, d), BF16),
            pltpu.VMEM((2, tile, d), BF16), pltpu.VMEM((2, tile, d), BF16),
            pltpu.VMEM((8, tile, d), BF16), pltpu.VMEM((4, tile, d), BF16),
            pltpu.VMEM((2, 3, blk, ff), BF16), pltpu.VMEM((2, tile, d), BF16),
            dma((12,)), dma((18,)), dma((18,)), dma((2, 3)), dma((7,)),
        ],
        compiler_params=pltpu.CompilerParams(collective_id=1, has_side_effects=True, vmem_limit_bytes=62 << 20),
        cost_estimate=cost(18 * 4 * rows * d * ff, 60e6, 4 * rows * ff),
    )(middle, *cots, wg_t, wu_t, wd, gain)


class Wires:
    def __init__(self, send_sem, recv_sem):
        self.send_sem, self.recv_sem, self.used, self.all = send_sem, recv_sem, 0, []

    def copy(self, src, dst, target):
        made = pltpu.make_async_remote_copy(
            src,
            dst,
            self.send_sem.at[self.used],
            self.recv_sem.at[self.used],
            device_id=target,
            device_id_type=MESH,
        )
        self.used += 1
        self.all.append(made)
        return made

    def drain(self):
        for made in self.all:
            made.wait_send()


class Places:
    def __init__(self, wide_count):
        self.wide, self.place = lax.axis_index("wide"), lax.axis_index("narrow")
        self.core = self.place % 2
        self.second = self.place // 2
        self.by_core = (self.wide, self.place + 1 - 2 * self.core)
        self.by_row = (self.wide, (self.place + 2) % 4)
        self.bits = []
        bit = 1
        while bit < wide_count:
            self.bits.append(bit)
            bit *= 2

    def has(self, bit):
        return (self.wide // bit) % 2

    def across(self, bit):
        return (self.wide + bit - 2 * bit * self.has(bit), self.place)

    def meet(self):
        barrier = pltpu.get_barrier_semaphore()
        others = [self.by_core, self.by_row] + [self.across(bit) for bit in self.bits]
        for other in others:
            pl.semaphore_signal(barrier, 1, device_id=other, device_id_type=MESH)
        pl.semaphore_wait(barrier, len(others))


class Scan:
    def __init__(self, where, wires, tot_s, tot_m, pre_s, pre_m, out, into, backward):
        self.tot_s, self.tot_m, self.pre_s, self.pre_m = tot_s, tot_m, pre_s, pre_m
        self.out, self.into = out, into
        self.steps = []
        for i, bit in enumerate([0] + where.bits):
            target = where.across(bit) if bit else where.by_row
            is_set = where.has(bit) if bit else where.second
            later = (1 - is_set if backward else is_set) > 0
            self.steps.append((wires.copy(out.at[i], into.at[i], target), later, bit == 0))
        pre_s[...] = jnp.zeros_like(pre_s)
        pre_m[...] = jnp.ones_like(pre_m)

    def begin(self, i=0):
        self.at = i
        dv = self.tot_s.shape[1]
        for h in range(2):
            self.out[i, h, :dv, :] = self.tot_s[h].astype(BF16)
            self.out[i, h, dv:, :] = jnp.broadcast_to(self.tot_m[h], (16, self.tot_m.shape[2])).astype(BF16)
        self.steps[i][0].start()

    def advance(self):
        self.finish(self.at)
        if self.at + 1 < len(self.steps):
            self.begin(self.at + 1)
            return True
        return False

    def finish(self, i):
        copy, later, swapped = self.steps[i]
        copy.wait_recv()
        dv = self.tot_s.shape[1]
        for h in range(2):
            g = 1 - h if swapped else h
            oth_s = self.into[i, g, :dv, :].astype(F32)
            oth_m = self.into[i, g, dv : dv + 1, :].astype(F32)
            pre_s, pre_m, tot_s, tot_m = self.pre_s[h], self.pre_m[h], self.tot_s[h], self.tot_m[h]
            self.pre_s[h] = jnp.where(later, oth_s * pre_m + pre_s, pre_s)
            self.pre_m[h] = jnp.where(later, oth_m * pre_m, pre_m)
            self.tot_s[h] = jnp.where(later, oth_s * tot_m + tot_s, tot_s * oth_m + oth_s)
            self.tot_m[h] = tot_m * oth_m


class Scatter:
    def __init__(self, where, wires, source, keep, order, recvs):
        self.recvs, self.steps = recvs, []
        left = sorted(where.bits, reverse=True)
        held, first = source, keep
        for bit, recv in zip(order, recvs):
            dim = left.index(bit)
            mine = where.has(bit)
            other = held.at[(slice(None),) * dim + (1 - mine,)]
            self.steps.append((wires.copy(other, recv, where.across(bit)), first if first is not None else held, dim, mine, first is not None))
            left.pop(dim)
            held, first = recv, None

    def begin(self, i=0):
        self.at = i
        self.steps[i][0].start()

    def advance(self):
        if self.at + 1 < len(self.steps):
            self.finish(self.at)
            self.begin(self.at + 1)

    def result(self):
        while self.at + 1 < len(self.steps):
            self.advance()
        return self.finish(self.at)

    def finish(self, i):
        copy, held, dim, mine, picked = self.steps[i]
        copy.wait_recv()
        recv = self.recvs[i]
        last = i == len(self.steps) - 1
        for at in itertools.product(range(2), repeat=len(recv.shape) - 2):
            source = at if picked else at[:dim] + (mine,) + at[dim:]
            total = recv[at].astype(F32) + held[source].astype(F32)
            if last:
                return total
            recv[at] = total.astype(BF16)
        return None


class Everywhere:
    def __init__(self, where, wires, values, recvs):
        self.values, self.recvs = values, recvs
        targets = [where.by_core, where.by_row] + [where.across(bit) for bit in where.bits]
        self.steps = [wires.copy(values.at[i], recvs.at[i], target) for i, target in enumerate(targets)]

    def begin(self, i=0):
        self.at = i
        self.steps[i].start()

    def advance(self):
        if self.at + 1 < len(self.steps):
            self.finish(self.at)
            self.begin(self.at + 1)

    def result(self):
        while self.at + 1 < len(self.steps):
            self.advance()
        self.finish(self.at)
        return self.values[len(self.steps)]

    def finish(self, i):
        self.steps[i].wait_recv()
        self.values[i + 1] = self.values[i] + self.recvs[i]


def bit_index(w, bits):
    return tuple((w // bit) % 2 for bit in sorted(bits, reverse=True))


def back_phase_kernel(
    bits,
    gm_h, mx_h, s_h, r_h, gt_h, rows_h, q_h, k_h, v_h, cum_h, dpre_h, rank_h, sin_h, w_h, wo_h, g_h, gmid_h, tok_h,
    off_ref, enter_ref, mult_ref, ru_ref, rd_ref, ggain_ref, ngain_ref, mpart_ref, restart_ref,
    in_h, gate_o, up_o, down_o, wout_o, k_o, v_o, q_o, s_o, rdown_o, rup_o, bias_o, mgain_o, group_o, ngain_o,
    gm, mx, sw, reach, gated, rows, q, k, v, cum, dpre, rank, sin, w, wo, keep, mrecv, gmid, tok,
    gx, al, grank, ds, lb_m, pre_s, pre_m, sc_out, sc_in, osv, osy, osr, kv, kvy, kvr, tb, tr, sm, smr, ng, ngr,
    load_sem, send_sem, recv_sem, out_sem,
):
    count, d = rows.shape
    half = count // 2
    dk, dv = q.shape[2], v.shape[2]
    where = Places(2 ** len(bits))
    wires = Wires(send_sem, recv_sem)
    loads = []

    def load(src, dst):
        copy = pltpu.make_async_copy(src, dst, load_sem.at[len(loads)])
        loads.append(copy)
        copy.start()
        return copy

    orders = (bits, bits[1:] + bits[:1], bits)
    first = [load(gm_h, gm)]
    for h in range(2):
        first += [load(wo_h[h], wo.at[h]), load(mx_h[h], mx.at[h]), load(s_h[h], sw.at[h]), load(r_h[h], reach.at[h])]
    second = [load(gt_h[h], gated.at[h]) for h in range(2)] + [load(rows_h, rows)]
    third = []
    for i in range(3):
        left = sorted(bits, reverse=True)
        dim = left.index(orders[i][0])
        third.append(load(g_h[i].at[(slice(None),) * dim + (where.has(orders[i][0]),)], keep[i]))
    fourth = [load(rank_h, rank)]
    for h in range(2):
        for src, dst in ((q_h, q), (k_h, k), (v_h, v), (cum_h, cum), (dpre_h, dpre), (sin_h, sin), (w_h, w)):
            fourth.append(load(src[h], dst.at[h]))
    fifth = [load(gmid_h, gmid), load(tok_h, tok)]

    where.meet()
    mlp = [Scatter(where, wires, g_h[i], keep[i], orders[i], mrecv[i]) for i in range(3)]
    scan = Scan(where, wires, ds, lb_m, pre_s, pre_m, sc_out, sc_in, True)
    os_y = wires.copy(osv.at[1], osy, where.by_row)
    os_s = Scatter(where, wires, osv.at[0], None, bits[1:] + bits[:1], osr)
    kv_y = wires.copy(kv.at[1], kvy, where.by_row)
    kv_s = Scatter(where, wires, kv.at[0], None, bits, kvr)
    tots = [wires.copy(tb.at[j], tr.at[j], where.by_core) for j in range(2)]
    every = Everywhere(where, wires, sm, smr)
    every_n = Everywhere(where, wires, ng, ngr)
    n_bits = len(bits)
    for part in mlp:
        part.begin()

    blk = half // 2
    gain = ggain_ref[...]
    ds[...] = jnp.zeros_like(ds)
    sm[0] = jnp.zeros_like(sm[0])
    ng[0] = jnp.zeros_like(ng[0])
    for copy in first:
        copy.wait()

    def gate_step(i, part):
        at = pl.ds(pl.multiple_of(i * blk, blk), blk)
        g = gm[at, :]
        for h in range(2):
            grad = dot_nt(g, wo[h])
            mixed = mx[h, at, :]
            inv = lax.rsqrt(jnp.mean(mixed * mixed, axis=-1, keepdims=True) + GROUP_EPS)
            unit = mixed * inv
            s = sw[h, at, :]
            sig = jax.nn.sigmoid(s)
            al[h, at, 2 * dk + dv :] = (grad * unit * gain * (sig * (1.0 + s * (1.0 - sig)))).astype(BF16)
            dn = grad * (s * sig)
            part = part + jnp.sum(dn * unit, axis=0, keepdims=True)
            weighted = dn * gain
            gmix = (inv * (weighted - unit * jnp.mean(weighted * unit, axis=-1, keepdims=True))).astype(BF16)
            gx[h, at, :] = gmix
            ds[h] += dot_tn(gmix, reach[h, at, :])
        return part

    group_part = lax.fori_loop(0, 4, gate_step, jnp.zeros((1, dv), F32))
    for h in range(2):
        ds[h] = ds[h] * restart_ref[...]
        lb_m[h] = mult_ref[h]
    scan.begin()

    size = 256
    per = size // osv.shape[-2]

    def put(ref, h, j, lanes, value):
        rows_each = ref.shape[-2]
        for p in range(per):
            ref[(h,) + bit_index(j * per + p, bits) + (slice(None), lanes)] = value[p * rows_each : (p + 1) * rows_each]

    def out_step(j, _):
        cols = pl.ds(pl.multiple_of(j * size, size), size)
        for h in (1, 0):
            put(osv, h, j, slice(0, dv), dot_tn(gm[:, cols], gated[h]).astype(BF16))
        return 0

    def swish_step(j, _):
        cols = pl.ds(pl.multiple_of(j * size, size), size)
        for h in (1, 0):
            put(osv, h, j, slice(dv, 2 * dv), dot_tn(rows[:, cols], al[h, :, 2 * dk + dv :]).astype(BF16))
        return 0

    for copy in second:
        copy.wait()
    lax.fori_loop(0, d // size, out_step, 0)
    scan.advance()
    lax.fori_loop(0, d // size, swish_step, 0)
    os_y.start()
    for copy in third:
        copy.wait()
    while scan.advance():
        if scan.at == n_bits:
            mlp[1].advance()
            mlp[0].advance()
    for copy in fourth:
        copy.wait()

    ds[...] = pre_s[...]
    chunks = count // CHUNK
    mask = triangle(True)
    ones = triangle(False).astype(F32)
    scale = dk**-0.5
    rk = rank.shape[1]

    def back_step(step, carry):
        c = chunks - 1 - step
        at = pl.ds(pl.multiple_of(c * CHUNK, CHUNK), CHUNK)
        grs, new = None, []
        for h in range(2):
            ch = cum[h, at, :]
            mid = ch[HALF - 1 : HALF]
            end = ch[CHUNK - 1 :]
            e_qd, e_kd, e_qi, e_ke = jnp.exp(ch - mid), jnp.exp(mid - ch), jnp.exp(ch), jnp.exp(end - ch)
            e_end = jnp.exp(end)
            qf = q[h, at, :].astype(F32) * scale
            kf = k[h, at, :].astype(F32)
            vc = v[h, at, :]
            qd = (qf * e_qd).astype(BF16)
            kd = (kf * e_kd).astype(BF16)
            qi = (qf * e_qi).astype(BF16)
            ke = (kf * e_ke).astype(BF16)
            go = gx[h, at, :]
            state = sin[h, c].astype(F32) + enter_ref[h] * jnp.exp(off_ref[h, c])
            state_low = state.astype(BF16)
            dstate = ds[h]
            dstate_low = dstate.astype(BF16)
            scores = jnp.where(mask, dot_nt(qd, kd), 0.0).astype(BF16)
            dscores = jnp.where(mask, dot_nt(go, vc), 0.0).astype(BF16)
            d_v = dot_tn(scores, go) + dot_nt(ke, dstate_low)
            d_qd = dot(dscores, kd)
            d_qi = dot(go, state_low)
            d_kd = dot_tn(dscores, qd)
            d_ke = dot(vc, dstate_low)
            d_q = scale * (d_qd * e_qd + d_qi * e_qi)
            d_k = d_kd * e_kd + d_ke * e_ke
            tail = ke.astype(F32) * d_ke
            d_cum = qd.astype(F32) * d_qd + qi.astype(F32) * d_qi - kd.astype(F32) * d_kd - tail
            d_end = jnp.sum(tail, axis=0, keepdims=True) + e_end * jnp.sum(dstate * state, axis=0, keepdims=True)
            grad_decay = exact(ones, d_cum, ((1,), (0,))) + d_end
            g_pre = grad_decay * jax.nn.sigmoid(-dpre[h, at, :]) * (1.0 / GATE_NORM)
            al[h, at, :dk] = d_k.astype(BF16)
            al[h, at, dk : dk + dv] = d_v.astype(BF16)
            al[h, at, dk + dv : 2 * dk + dv] = d_q.astype(BF16)
            gr = exact(g_pre, ru_ref[h], ((1,), (1,)))
            grs = gr if grs is None else grs + gr
            new.append(carry[2 * h] + exact(rank[at, :], g_pre, ((0,), (0,))))
            new.append(carry[2 * h + 1] + jnp.sum(g_pre, axis=0, keepdims=True))
            ds[h] = dstate * e_end + dot_tn(go, qi)
        grank[at, :] = grs.astype(BF16)
        return tuple(new)

    zero = (jnp.zeros((rk, dk), F32), jnp.zeros((1, dk), F32))
    rup0, gb0, rup1, gb1 = lax.fori_loop(0, chunks, back_step, zero + zero)
    for i in (1, 0, 2):
        mlp[i].advance()

    def kvq_step(h):
        def step(j, _):
            cols = pl.ds(pl.multiple_of(j * size, size), size)
            put(kv, h, j, slice(None), dot_tn(rows[:, cols], al[h, :, : 2 * dk + dv]).astype(BF16))
            return 0

        lax.fori_loop(0, d // size, step, 0)

    kvq_step(1)
    kv_y.start()

    def add_row(ref, extra):
        for at in itertools.product(range(2), repeat=n_bits):
            ref[(0,) + at] = (ref[(0,) + at].astype(F32) + extra[at].astype(F32)).astype(BF16)

    os_y.wait_recv()
    add_row(osv, osy)
    os_s.begin()

    def total_step(i, _):
        b = jnp.where(i < 2, 2 - 2 * where.core + i, 2 * where.core + i - 2)
        at = pl.ds(pl.multiple_of(b * blk, blk), blk)
        total = dot_nt(al[0, at, :], w[0]) + dot_nt(al[1, at, :], w[1]) + dot_nt(grank[at, :], rd_ref[...])
        for j in range(2):

            @pl.when(i == j)
            def _():
                tb[j] = total.astype(BF16)
                tots[j].start()

            @pl.when(i == 2 + j)
            def _():
                tb[2 + j] = total.astype(BF16)

        return 0

    lax.fori_loop(0, 4, total_step, 0)

    sm[0, 0:rk, :] = dot_tn(grank[...], rows[...])
    at0 = pl.ds(pl.multiple_of(where.place * dk, dk), dk)
    at1 = pl.ds(pl.multiple_of(((where.place + 2) % 4) * dk, dk), dk)
    sm[0, rk : 2 * rk, at0] = rup0
    sm[0, rk : 2 * rk, at1] = rup1
    sm[0, 2 * rk : 2 * rk + 1, at0] = gb0
    sm[0, 2 * rk : 2 * rk + 1, at1] = gb1
    sm[0, 2 * rk + 1 : 2 * rk + 2, :] = mpart_ref[...]
    sm[0, 2 * rk + 2 : 2 * rk + 3, :dv] = group_part
    every.begin()
    kvq_step(0)
    every.advance()

    for copy in fifth:
        copy.wait()
    ngain = ngain_ref[...]
    part = jnp.zeros((1, d), F32)
    for j in range(2):
        at = pl.ds(j * blk, blk)
        tots[j].wait_recv()
        grad = tb[2 + j].astype(F32) + tr[j].astype(F32)
        x = tok[at, :].astype(F32)
        inv = lax.rsqrt(jnp.mean(x * x, axis=-1, keepdims=True) + NORM_EPS)
        unit = x * inv
        weighted = grad * ngain
        part = part + jnp.sum(grad * unit, axis=0, keepdims=True)
        gmid[at, :] = gmid[at, :] + inv * (weighted - unit * jnp.mean(weighted * unit, axis=-1, keepdims=True))
    done = pltpu.make_async_copy(gmid, in_h, out_sem.at[0])
    done.start()
    ng[0, 0:1, :] = part
    every_n.begin()

    outs = (gate_o, up_o, down_o)
    kv_y.wait_recv()
    add_row(kv, kvy)
    kv_s.begin()
    for i in (1, 0):
        outs[i][...] = jnp.transpose(mlp[i].result())
    mlp[2].advance()
    every.advance()
    every_n.advance()
    for _ in range(n_bits - 1):
        os_s.advance()
        every_n.advance()
        kv_s.advance()
        every.advance()
    outs[2][...] = jnp.transpose(mlp[2].result())
    total = os_s.result()
    wout_o[...] = jnp.transpose(total[:, :dv])
    s_o[...] = total[:, dv:]
    every_n.advance()
    total = kv_s.result()
    k_o[...] = total[:, :dk]
    v_o[...] = total[:, dk : dk + dv]
    q_o[...] = total[:, dk + dv :]
    small = every.result()
    rdown_o[...] = small[:rk]
    rup_o[...] = small[rk : 2 * rk, : rup_o.shape[1]]
    bias_o[...] = small[2 * rk : 2 * rk + 1, : bias_o.shape[1]]
    mgain_o[...] = small[2 * rk + 1 : 2 * rk + 2]
    group_o[...] = small[2 * rk + 2 : 2 * rk + 3, :dv]
    ngain_o[...] = every_n.result()[:1]
    done.wait()
    wires.drain()


def back_phase(
    gm, mx, s, reach, gated, rows, q, k, v, cum, dpre, rank, sin, w, wo, grads, gmid, tokens,
    off, enter, mult, ru, rd, ggain, ngain, mpart, restart,
):
    bits = wide_bits()
    count, d = rows.shape
    half = count // 2
    dk, dv, rk = q[0].shape[1], v[0].shape[1], rank.shape[1]
    ff = grads[0].shape[-1]
    each = d // 2 ** len(bits)
    n_bits, chunks = len(bits), count // CHUNK
    hbm = pl.BlockSpec(memory_space=pltpu.HBM)
    vmem = pl.BlockSpec(memory_space=pltpu.VMEM)
    dma = pltpu.SemaphoreType.DMA
    v_ = pltpu.VMEM

    def shape(lead, cols):
        return (2,) * lead + (each, cols)

    def falls(cols):
        return [v_(shape(n_bits - 1 - i, cols), BF16) for i in range(n_bits)]

    pair, three = [hbm] * 2, [hbm] * 3
    kvq = 2 * dk + dv
    small = 2 * rk + 8
    scratch = [
        v_((count, d), BF16), v_((2, count, dv), F32), v_((2, count, dv), F32), v_((2, count, dk), BF16),
        v_((2, count, dv), BF16), v_((count, d), BF16), v_((2, count, dk), BF16), v_((2, count, dk), BF16),
        v_((2, count, dv), BF16), v_((2, count, dk), F32), v_((2, count, dk), F32), v_((count, rk), F32),
        v_((2, chunks, dv, dk), BF16), v_((2, d, kvq + dv), BF16), v_((2, dv, d), BF16),
        [v_(shape(n_bits - 1, ff), BF16)] * 3, [falls(ff)] * 3, v_((half, d), F32), v_((half, d), BF16),
        v_((2, count, dv), BF16), v_((2, count, kvq + dv), BF16), v_((count, rk), BF16),
        v_((2, dv, dk), F32), v_((2, 1, dk), F32), v_((2, dv, dk), F32), v_((2, 1, dk), F32),
        v_((n_bits + 1, 2, dv + 16, dk), BF16), v_((n_bits + 1, 2, dv + 16, dk), BF16),
        v_((2,) + shape(n_bits, 2 * dv), BF16), v_(shape(n_bits, 2 * dv), BF16), falls(2 * dv),
        v_((2,) + shape(n_bits, kvq), BF16), v_(shape(n_bits, kvq), BF16), falls(kvq),
        v_((4, half // 2, d), BF16), v_((2, half // 2, d), BF16),
        v_((n_bits + 3, small, d), F32), v_((n_bits + 2, small, d), F32),
        v_((n_bits + 3, 8, d), F32), v_((n_bits + 2, 8, d), F32),
        dma((48,)), dma((64,)), dma((64,)), dma((1,)),
    ]
    out_shape = [
        sds((half, d), F32), sds((ff, each), F32), sds((ff, each), F32), sds((ff, each), F32), sds((dv, each), F32),
        sds((each, dk), F32), sds((each, dv), F32), sds((each, dk), F32), sds((each, dv), F32),
        sds((rk, d), F32), sds((rk, 4 * dk), F32), sds((1, 4 * dk), F32), sds((1, d), F32), sds((1, dv), F32), sds((1, d), F32),
    ]
    operands = (
        gm, mx, s, reach, gated, rows, q, k, v, cum, dpre, rank, sin, w, wo, grads, gmid, tokens,
        off, enter, mult, ru, rd, ggain, ngain, mpart, restart,
    )
    flat, tree = jax.tree.flatten(operands)
    n_vmem = len(jax.tree.leaves(operands[18:]))
    flat_scratch, scratch_tree = jax.tree.flatten(scratch, is_leaf=lambda x: not isinstance(x, list))
    n_in, n_out = len(flat), len(out_shape)

    def kernel(*refs):
        ins = jax.tree.unflatten(tree, refs[:n_in])
        rest = jax.tree.unflatten(scratch_tree, refs[n_in + n_out :])
        back_phase_kernel(bits, *ins, *refs[n_in : n_in + n_out], *rest)

    return pl.pallas_call(
        kernel,
        name="back_phase",
        in_specs=[hbm] * (n_in - n_vmem) + [vmem] * n_vmem,
        out_specs=[hbm] + [vmem] * (n_out - 1),
        out_shape=out_shape,
        scratch_shapes=flat_scratch,
        compiler_params=pltpu.CompilerParams(collective_id=2, has_side_effects=True, vmem_limit_bytes=62 << 20),
        cost_estimate=cost(40e9, 60e6, 1e6),
    )(*flat)


def hop(value, axis, bit):
    return lax.ppermute(value, axis, [(i, i ^ bit) for i in range(lax.axis_size(axis))])


def wide_bits():
    count, bits, bit = lax.axis_size("wide"), [], 1
    while bit < count:
        bits.append(bit)
        bit *= 2
    return bits


def scan_states(mult, state, backward):
    place = {"narrow": lax.axis_index("narrow"), "wide": lax.axis_index("wide")}
    heads, dv, dk = state.shape
    pre_m, pre_s = jnp.ones_like(mult), jnp.zeros_like(state)
    tot_m, tot_s = mult, state
    for axis, bit in [("narrow", 2)] + [("wide", b) for b in wide_bits()]:
        packed = jnp.concatenate(
            [tot_s, jnp.broadcast_to(tot_m, (heads, 16, dk))], axis=1
        ).astype(BF16)
        other = hop(packed, axis, bit).astype(F32)
        if axis == "narrow":
            other = other[::-1]
        oth_s, oth_m = other[:, :dv], other[:, dv : dv + 1]
        is_set = (place[axis] & bit) != 0
        mine_later = jnp.logical_not(is_set) if backward else is_set
        new_s = oth_s * pre_m + pre_s
        new_m = oth_m * pre_m
        sum_later = oth_s * tot_m + tot_s
        sum_first = tot_s * oth_m + oth_s
        pre_s = jnp.where(mine_later, new_s, pre_s)
        pre_m = jnp.where(mine_later, new_m, pre_m)
        tot_s = jnp.where(mine_later, sum_later, sum_first)
        tot_m = tot_m * oth_m
    return pre_s


def shards(
    tokens, cotangent, flags, norm_gain, query_weight, key_weight, value_weight, swish_weight, rank_down, rank_up,
    decay_bias, group_gain, output_weight, mlp_gain, mlp_gate, mlp_up, mlp_down,
):
    own_rows = tokens.shape[0]
    place = lax.axis_index("narrow")
    core = place & 1
    second = (place & 2) != 0
    wide_odd = (lax.axis_index("wide") & 1) != 0
    dk = query_weight.shape[1]
    dv = value_weight.shape[1]
    d = tokens.shape[1]

    def in_order(mine, other):
        return jnp.where(
            core == 0, jnp.concatenate([mine, other]), jnp.concatenate([other, mine])
        )

    def from_row_partner(value):
        half = value.shape[0] // 2
        piece = lax.dynamic_slice_in_dim(value, jnp.where(wide_odd, half, 0), half, 0)
        first = hop(piece, "narrow", 2)
        relayed = hop(first, "wide", 1)
        return jnp.where(
            wide_odd, jnp.concatenate([relayed, first]), jnp.concatenate([first, relayed])
        )

    def head_cols(index):
        ru = lax.dynamic_slice_in_dim(rank_up, index * dk, dk, 1).astype(F32)
        bias = lax.dynamic_slice_in_dim(decay_bias, index * dk, dk, 0).astype(F32)
        return ru, bias.reshape(1, dk)

    restart = 1.0 - flags[0].astype(F32)
    restart = jnp.where(second, 1.0, restart)
    norm_gain_f = norm_gain.astype(F32)
    mlp_gain_f = mlp_gain.astype(F32)
    gain_row = group_gain.astype(F32).reshape(1, dv)

    inputs = tokens.astype(F32)
    inv_one = lax.rsqrt(jnp.mean(inputs * inputs, axis=-1, keepdims=True) + NORM_EPS)
    normed = (inputs * inv_one * norm_gain_f).astype(BF16)
    normed_two = hop(normed, "narrow", 1)
    rows_all = in_order(normed, normed_two)

    w_own = jnp.concatenate([key_weight, value_weight, query_weight, swish_weight], axis=1)
    w_other = from_row_partner(w_own)
    out_other = from_row_partner(output_weight)
    cot_late, w_other, out_other = lax.optimization_barrier((cotangent, w_other, out_other))
    cot_y = hop(cot_late, "narrow", 2)
    cot_c = hop(cotangent, "narrow", 1)
    cot_d = hop(cot_y, "narrow", 1)

    ru_own, bias_own = head_cols(place)
    ru_oth, bias_oth = head_cols(place ^ 2)
    weights_out = (output_weight, out_other)
    one = forward_head(rows_all, w_own, rank_down, ru_own, bias_own, dk, dv)
    two = forward_head(rows_all, w_other, rank_down, ru_oth, bias_oth, dk, dv)
    (q, k, v, s, cum, dpre, rank_pre, base, reach, sin, off, state, mult) = zip(one, two)
    rank_pre = rank_pre[0]
    mults = restart * jnp.stack(mult)
    enter = restart * scan_states(mults, jnp.stack(state), False)
    enter_low = enter.astype(BF16)
    mixed0, mixed1, gated0, gated1, term = gate_out(
        base, reach, s, (enter_low[0], enter_low[1]), gain_row, weights_out
    )
    own_term = lax.dynamic_slice_in_dim(term, core * own_rows, own_rows, 0)
    send_term = lax.dynamic_slice_in_dim(term, (1 - core) * own_rows, own_rows, 0)
    middle = inputs + (own_term.astype(F32) + hop(send_term, "narrow", 1).astype(F32))
    grad_middle, gm_all, mlp_gain_part, gate_g, up_g, down_g, near, far = mlp_phase(
        middle, (cotangent, cot_c, cot_y, cot_d), mlp_gate.T, mlp_up.T, mlp_down, mlp_gain_f.reshape(1, d)
    )
    result = (middle + (near.astype(F32) + hop(far, "narrow", 2).astype(F32))).astype(BF16)
    bits = wide_bits()
    split = (2,) * len(bits) + (d // 2 ** len(bits), -1)
    input_grad, gate_t, up_t, down_t, out_t, k_g, v_g, q_g, s_g, rdown_t, rup_g, bias_g, mgain_g, group_g, ngain = back_phase(
        gm_all, (mixed0, mixed1), s, reach, (gated0, gated1), rows_all, q, k, v, cum, dpre, rank_pre, sin,
        (w_own, w_other), weights_out, tuple(g.reshape(split) for g in (gate_g, up_g, down_g)), grad_middle, tokens,
        jnp.stack(off), enter, mults, jnp.stack([ru_own, ru_oth]), rank_down, gain_row, norm_gain_f.reshape(1, d),
        mlp_gain_part, jnp.full((1, dk), restart, F32),
    )
    return (
        result,
        input_grad,
        ngain[0],
        q_g,
        k_g,
        v_g,
        s_g,
        rdown_t.T,
        rup_g,
        bias_g[0],
        group_g[0],
        out_t,
        mgain_g[0],
        gate_t.T,
        up_t.T,
        down_t,
    )


def solution(mesh):
    rows, cols = P(("wide", "narrow"), None), P(None, "narrow")
    both = P("wide", "narrow")
    in_specs = (
        rows, rows, P("wide"), P(), cols, cols, cols, cols, P(), P(), P(), P(), P("narrow", None), P(), cols, cols,
        P("narrow", None),
    )
    out_specs = (
        rows, rows, P(), both, both, both, both, P(), P(), P(), P(), P("narrow", "wide"), P(), both, both,
        P("narrow", "wide"),
    )
    return jax.shard_map(shards, mesh=mesh, in_specs=in_specs, out_specs=out_specs, check_vma=False)
```

```python
import functools
import itertools

import jax
import jax.numpy as jnp
from jax import lax
from jax.experimental import pallas as pl
from jax.experimental.pallas import tpu as pltpu
from jax.sharding import PartitionSpec as P

NORM_EPS = 1e-06
GROUP_EPS = 1e-05
GATE_NORM = 16.0
HIGHEST_PREC = lax.Precision.HIGHEST
MESH = pl.DeviceIdType.MESH
CHUNK = 128
HALF = CHUNK // 2
BLOCK = 256
F32 = jnp.float32
BF16 = jnp.bfloat16


def dot(a, b):
    return lax.dot_general(a, b, (((1,), (0,)), ((), ())), preferred_element_type=F32)


def dot_nt(a, b):
    return lax.dot_general(a, b, (((1,), (1,)), ((), ())), preferred_element_type=F32)


def dot_tn(a, b):
    return lax.dot_general(a, b, (((0,), (0,)), ((), ())), preferred_element_type=F32)


def exact(a, b, dims):
    return lax.dot_general(
        a, b, (dims, ((), ())), precision=HIGHEST_PREC, preferred_element_type=F32
    )


def sds(shape, dtype):
    return jax.ShapeDtypeStruct(shape, dtype)


def params(mib=48):
    return pltpu.CompilerParams(vmem_limit_bytes=mib << 20)


def cost(flops, nbytes, trans=0):
    return pl.CostEstimate(flops=int(flops), bytes_accessed=int(nbytes), transcendentals=int(trans))


def whole(shape):
    return pl.BlockSpec(shape, lambda i: (0,) * len(shape), pipeline_mode=pl.Buffered(1))


def rows_spec(rows, cols):
    return pl.BlockSpec((rows, cols), lambda i: (i, 0))


def triangle(lower):
    r = lax.broadcasted_iota(jnp.int32, (CHUNK, CHUNK), 0)
    c = lax.broadcasted_iota(jnp.int32, (CHUNK, CHUNK), 1)
    return r >= c if lower else r <= c


class Wires:
    def __init__(self, send_sem, recv_sem):
        self.send_sem, self.recv_sem, self.used, self.all = send_sem, recv_sem, 0, []

    def copy(self, src, dst, target):
        made = pltpu.make_async_remote_copy(
            src,
            dst,
            self.send_sem.at[self.used],
            self.recv_sem.at[self.used],
            device_id=target,
            device_id_type=MESH,
        )
        self.used += 1
        self.all.append(made)
        return made

    def drain(self):
        for made in self.all:
            made.wait_send()


class Places:
    def __init__(self, wide_count):
        self.wide, self.place = lax.axis_index("wide"), lax.axis_index("narrow")
        self.core = self.place % 2
        self.second = self.place // 2
        self.by_core = (self.wide, self.place + 1 - 2 * self.core)
        self.by_row = (self.wide, (self.place + 2) % 4)
        self.bits = []
        bit = 1
        while bit < wide_count:
            self.bits.append(bit)
            bit *= 2

    def has(self, bit):
        return (self.wide // bit) % 2

    def across(self, bit):
        return (self.wide + bit - 2 * bit * self.has(bit), self.place)

    def meet(self):
        barrier = pltpu.get_barrier_semaphore()
        others = [self.by_core, self.by_row] + [self.across(bit) for bit in self.bits]
        for other in others:
            pl.semaphore_signal(barrier, 1, device_id=other, device_id_type=MESH)
        pl.semaphore_wait(barrier, len(others))


class Scan:
    def __init__(self, where, wires, tot_s, tot_m, pre_s, pre_m, out, into, backward):
        self.tot_s, self.tot_m, self.pre_s, self.pre_m = tot_s, tot_m, pre_s, pre_m
        self.out, self.into = out, into
        self.steps = []
        for i, bit in enumerate([0] + where.bits):
            target = where.across(bit) if bit else where.by_row
            is_set = where.has(bit) if bit else where.second
            later = (1 - is_set if backward else is_set) > 0
            self.steps.append((wires.copy(out.at[i], into.at[i], target), later, bit == 0))
        pre_s[...] = jnp.zeros_like(pre_s)
        pre_m[...] = jnp.ones_like(pre_m)

    def begin(self, i=0):
        self.at = i
        dv = self.tot_s.shape[1]
        for h in range(2):
            self.out[i, h, :dv, :] = self.tot_s[h].astype(BF16)
            self.out[i, h, dv:, :] = jnp.broadcast_to(self.tot_m[h], (16, self.tot_m.shape[2])).astype(BF16)
        self.steps[i][0].start()

    def advance(self):
        self.finish(self.at)
        if self.at + 1 < len(self.steps):
            self.begin(self.at + 1)
            return True
        return False

    def finish(self, i):
        copy, later, swapped = self.steps[i]
        copy.wait_recv()
        dv = self.tot_s.shape[1]
        for h in range(2):
            g = 1 - h if swapped else h
            oth_s = self.into[i, g, :dv, :].astype(F32)
            oth_m = self.into[i, g, dv : dv + 1, :].astype(F32)
            pre_s, pre_m, tot_s, tot_m = self.pre_s[h], self.pre_m[h], self.tot_s[h], self.tot_m[h]
            self.pre_s[h] = jnp.where(later, oth_s * pre_m + pre_s, pre_s)
            self.pre_m[h] = jnp.where(later, oth_m * pre_m, pre_m)
            self.tot_s[h] = jnp.where(later, oth_s * tot_m + tot_s, tot_s * oth_m + oth_s)
            self.tot_m[h] = tot_m * oth_m


class Scatter:
    def __init__(self, where, wires, source, keep, order, recvs):
        self.recvs, self.steps = recvs, []
        left = sorted(where.bits, reverse=True)
        held, first = source, keep
        for bit, recv in zip(order, recvs):
            dim = left.index(bit)
            mine = where.has(bit)
            other = held.at[(slice(None),) * dim + (1 - mine,)]
            self.steps.append((wires.copy(other, recv, where.across(bit)), first if first is not None else held, dim, mine, first is not None))
            left.pop(dim)
            held, first = recv, None

    def begin(self, i=0):
        self.at = i
        self.steps[i][0].start()

    def advance(self):
        if self.at + 1 < len(self.steps):
            self.finish(self.at)
            self.begin(self.at + 1)

    def result(self):
        while self.at + 1 < len(self.steps):
            self.advance()
        return self.finish(self.at)

    def finish(self, i):
        copy, held, dim, mine, picked = self.steps[i]
        copy.wait_recv()
        recv = self.recvs[i]
        last = i == len(self.steps) - 1
        for at in itertools.product(range(2), repeat=len(recv.shape) - 2):
            source = at if picked else at[:dim] + (mine,) + at[dim:]
            total = recv[at].astype(F32) + held[source].astype(F32)
            if last:
                return total
            recv[at] = total.astype(BF16)
        return None


class Everywhere:
    def __init__(self, where, wires, values, recvs):
        self.values, self.recvs = values, recvs
        targets = [where.by_core, where.by_row] + [where.across(bit) for bit in where.bits]
        self.steps = [wires.copy(values.at[i], recvs.at[i], target) for i, target in enumerate(targets)]

    def begin(self, i=0):
        self.at = i
        self.steps[i].start()

    def advance(self):
        if self.at + 1 < len(self.steps):
            self.finish(self.at)
            self.begin(self.at + 1)

    def result(self):
        while self.at + 1 < len(self.steps):
            self.advance()
        self.finish(self.at)
        return self.values[len(self.steps)]

    def finish(self, i):
        self.steps[i].wait_recv()
        self.values[i + 1] = self.values[i] + self.recvs[i]


def bit_index(w, bits):
    return tuple((w // bit) % 2 for bit in sorted(bits, reverse=True))


def front_phase_kernel(
    bits,
    tok_h, cot_h, kw_h, vw_h, qw_h, sw_h, wo_h, rd_ref, ru_ref, bias_ref, ggain_ref, ngain_ref, restart_ref,
    mid_h, rows_h, q_h, k_h, v_h, s_h, cum_h, dpre_h, rank_h, reach_h, sin_h, mx_h, gated_h, w_h, wo2_h, c1_h, c2_h, c3_h,
    off_o, enter_o, mult_o,
    tok, rows, w, wo, q, k, v, sw, cum, dpre, rank, reach, sin, mx, gated, tb, tr, mid, st, off,
    tot_s, tot_m, pre_s, pre_m, sc_out, sc_in,
    load_sem, send_sem, recv_sem, out_sem,
):
    count, d = rows.shape
    half = count // 2
    blk = half // 2
    dk, dv = q.shape[2], v.shape[2]
    kv = dk + dv
    where = Places(2 ** len(bits))
    wires = Wires(send_sem, recv_sem)
    loads, stores = [], []

    def load(src, dst):
        copy = pltpu.make_async_copy(src, dst, load_sem.at[len(loads)])
        loads.append(copy)
        copy.start()
        return copy

    def store(src, dst):
        copy = pltpu.make_async_copy(src, dst, out_sem.at[len(stores)])
        stores.append(copy)
        copy.start()

    load_tok = load(tok_h, tok)
    load_kv = [load(kw_h, w.at[0, :, pl.ds(0, dk)]), load(vw_h, w.at[0, :, pl.ds(dk, dv)])]
    load_qs = [load(qw_h, w.at[0, :, pl.ds(kv, dk)]), load(sw_h, w.at[0, :, pl.ds(kv + dk, dv)])]
    load_wo = load(wo_h, wo.at[0])

    where.meet()

    odd = where.has(1)
    over_x = where.across(1)
    quarter = d // 4

    def weight_pieces(cols):
        made = []
        for i in range(2):
            near = pl.ds(pl.multiple_of(odd * 2 * quarter + i * quarter, quarter), quarter)
            made.append(
                (
                    wires.copy(w.at[0, near, cols], w.at[1, near, cols], where.by_row),
                    wires.copy(w.at[1, near, cols], w.at[1, near, cols], over_x),
                )
            )
        return made

    kv_in = weight_pieces(pl.ds(0, kv))
    qs_in = weight_pieces(pl.ds(kv, kv))
    near = pl.ds(pl.multiple_of(odd * (dv // 2), dv // 2), dv // 2)
    wo_in = [
        wires.copy(wo.at[0, near], wo.at[1, near], where.by_row),
        wires.copy(wo.at[1, near], wo.at[1, near], over_x),
    ]
    cot_row, cot_both = [], []
    for i in range(2):
        at = pl.ds(i * blk, blk)
        cot_row.append(wires.copy(cot_h.at[at], c2_h.at[at], where.by_row))
        cot_both.append(wires.copy(c2_h.at[at], c3_h.at[at], where.by_core))
    cot_core = wires.copy(cot_h, c1_h, where.by_core)
    row_out = []
    for i in range(2):
        at = pl.ds(pl.multiple_of(where.core * half + i * blk, blk), blk)
        row_out.append(wires.copy(rows.at[at], rows.at[at], where.by_core))
    terms = [wires.copy(tb.at[j], tr.at[j], where.by_core) for j in range(2)]
    scan = Scan(where, wires, tot_s, tot_m, pre_s, pre_m, sc_out, sc_in, False)

    for copy in load_kv:
        copy.wait()
    for piece in kv_in:
        piece[0].start()
    load_tok.wait()
    ngain = ngain_ref[...]
    for i in range(2):
        x = tok[pl.ds(i * blk, blk), :].astype(F32)
        inv = lax.rsqrt(jnp.mean(x * x, axis=-1, keepdims=True) + NORM_EPS)
        rows[pl.ds(pl.multiple_of(where.core * half + i * blk, blk), blk), :] = (x * inv * ngain).astype(BF16)
        row_out[i].start()
    for copy in load_qs:
        copy.wait()
    load_wo.wait()
    for copy in row_out:
        copy.wait_recv()
    cot_core.start()
    store(rows, rows_h)

    mask = triangle(True)
    ones = mask.astype(F32)
    scale = dk**-0.5
    blocks = count // BLOCK
    per = BLOCK // CHUNK

    def first_step(i, _):
        h, b = i // blocks, i % blocks
        at = pl.ds(pl.multiple_of(b * BLOCK, BLOCK), BLOCK)
        for p in range(2):

            @pl.when(i == blocks - 2 + p)
            def _():
                kv_in[p][0].wait_recv()
                kv_in[p][1].start()

            @pl.when(i == 2 * blocks - 2 + p)
            def _():
                qs_in[p][0].wait_recv()
                qs_in[p][1].start()

        @pl.when(i == blocks - 1)
        def _():
            for piece in qs_in:
                piece[0].start()
            cot_row[0].start()

        @pl.when(i == blocks)
        def _():
            for piece in kv_in:
                piece[1].wait_recv()

        @pl.when(b == 0)
        def _():
            st[...] = jnp.zeros_like(st)
            off[...] = jnp.zeros_like(off)

        x = rows[at, :]

        @pl.when(i < blocks)
        def _():
            rank[at, :] = dot(x, rd_ref[...])

        proj = dot(x, w[h, :, :kv])
        pre = exact(rank[at, :], ru_ref[h], ((1,), (0,))) + bias_ref[h]
        dlog = jax.nn.log_sigmoid(pre) * (1.0 / GATE_NORM)
        k_low = proj[:, :dk].astype(BF16)
        v_low = proj[:, dk:].astype(BF16)
        k[h, at, :] = k_low
        v[h, at, :] = v_low
        dpre[h, at, :] = pre
        for j in range(per):
            part = slice(j * CHUNK, (j + 1) * CHUNK)
            c = b * per + j
            ch = exact(ones, dlog[part], ((1,), (0,)))
            end = ch[CHUNK - 1 :]
            ke = (k_low[part].astype(F32) * jnp.exp(end - ch)).astype(BF16)
            state = st[...]
            offset = off[...]
            cum[h, pl.ds(pl.multiple_of(c * CHUNK, CHUNK), CHUNK), :] = ch
            sin[h, c] = state.astype(BF16)
            off_o[h, c] = offset
            st[...] = state * jnp.exp(end) + dot_tn(v_low[part], ke)
            off[...] = offset + end

        @pl.when(b == blocks - 1)
        def _():
            tot_s[h] = st[...]
            mult = restart_ref[...] * jnp.exp(off[...])
            tot_m[h] = mult
            mult_o[h] = mult

        return 0

    lax.fori_loop(0, 2 * blocks, first_step, 0)
    scan.begin()
    wo_in[0].start()
    cot_row[1].start()
    for src, dst in ((k, k_h), (v, v_h), (cum, cum_h), (dpre, dpre_h), (rank, rank_h), (sin, sin_h)):
        store(src, dst)

    def second_step(i, _):
        h, b = i // blocks, i % blocks
        at = pl.ds(pl.multiple_of(b * BLOCK, BLOCK), BLOCK)

        @pl.when(i == blocks)
        def _():
            for piece in qs_in:
                piece[1].wait_recv()

        for n in range(min(len(bits), 3)):

            @pl.when(i == 2 + 3 * n)
            def _():
                scan.advance()

        @pl.when(i == 2 * blocks - 1)
        def _():
            wo_in[0].wait_recv()
            wo_in[1].start()

        proj = dot(rows[at, :], w[h, :, kv:])
        q_low = proj[:, :dk].astype(BF16)
        q[h, at, :] = q_low
        sw[h, at, :] = proj[:, dk:]
        for j in range(per):
            part = slice(j * CHUNK, (j + 1) * CHUNK)
            c = b * per + j
            this = pl.ds(pl.multiple_of(c * CHUNK, CHUNK), CHUNK)
            ch = cum[h, this, :]
            mid_row = ch[HALF - 1 : HALF]
            qf = q_low[part].astype(F32) * scale
            kf = k[h, this, :].astype(F32)
            qd = (qf * jnp.exp(ch - mid_row)).astype(BF16)
            kd = (kf * jnp.exp(mid_row - ch)).astype(BF16)
            qi = (qf * jnp.exp(ch)).astype(BF16)
            scores = jnp.where(mask, dot_nt(qd, kd), 0.0).astype(BF16)
            mx[h, this, :] = dot(scores, v[h, this, :]) + dot_nt(qi, sin[h, c])
            reach[h, this, :] = (qf * jnp.exp(ch + off_o[h, c])).astype(BF16)
        return 0

    lax.fori_loop(0, 2 * blocks, second_step, 0)
    for src, dst in ((q, q_h), (sw, s_h), (reach, reach_h), (w, w_h)):
        store(src, dst)
    while scan.advance():
        pass
    for h in range(2):
        enter_o[h] = restart_ref[...] * pre_s[h]
    wo_in[1].wait_recv()
    store(wo, wo2_h)
    gain = ggain_ref[...]

    def gate_step(i, _):
        b = jnp.where(i < 2, 2 - 2 * where.core + i, 2 * where.core + i - 2)
        at = pl.ds(pl.multiple_of(b * blk, blk), blk)
        total = None
        for h in range(2):
            mixed = mx[h, at, :] + dot_nt(reach[h, at, :], enter_o[h].astype(BF16))
            inv = lax.rsqrt(jnp.mean(mixed * mixed, axis=-1, keepdims=True) + GROUP_EPS)
            s = sw[h, at, :]
            g = (mixed * inv * gain * (s * jax.nn.sigmoid(s))).astype(BF16)
            mx[h, at, :] = mixed
            gated[h, at, :] = g
            part = dot(g, wo[h])
            total = part if total is None else total + part
        for j in range(2):

            @pl.when(i == j)
            def _():
                tb[j] = total.astype(BF16)
                terms[j].start()

            @pl.when(i == 2 + j)
            def _():
                mid[pl.ds(j * blk, blk), :] = tok[pl.ds(j * blk, blk), :].astype(F32) + total

        return 0

    lax.fori_loop(0, 4, gate_step, 0)
    for i in range(2):
        cot_row[i].wait_recv()
        cot_both[i].start()
    for src, dst in ((mx, mx_h), (gated, gated_h)):
        store(src, dst)
    for j in range(2):
        at = pl.ds(j * blk, blk)
        terms[j].wait_recv()
        mid[at, :] += tr[j].astype(F32)
    store(mid, mid_h)
    cot_core.wait_recv()
    for copy in cot_both:
        copy.wait_recv()
    for copy in stores:
        copy.wait()
    wires.drain()


def front_phase(tokens, cotangent, kw, vw, qw, sw, wo, rd, ru, bias, ggain, ngain, restart):
    bits = wide_bits()
    half, d = tokens.shape
    count = 2 * half
    dk, dv, rk = kw.shape[1], vw.shape[1], rd.shape[1]
    chunks, n_bits = count // CHUNK, len(bits)
    hbm = pl.BlockSpec(memory_space=pltpu.HBM)
    vmem = pl.BlockSpec(memory_space=pltpu.VMEM)
    dma = pltpu.SemaphoreType.DMA
    v_ = pltpu.VMEM
    out_shape = [
        sds((half, d), F32), sds((count, d), BF16), sds((2, count, dk), BF16), sds((2, count, dk), BF16),
        sds((2, count, dv), BF16), sds((2, count, dv), F32), sds((2, count, dk), F32), sds((2, count, dk), F32),
        sds((count, rk), F32), sds((2, count, dk), BF16), sds((2, chunks, dv, dk), BF16), sds((2, count, dv), F32),
        sds((2, count, dv), BF16), sds((2, d, 2 * dk + 2 * dv), BF16), sds((2, dv, d), BF16),
        sds((half, d), BF16), sds((half, d), BF16), sds((half, d), BF16),
        sds((2, chunks, 1, dk), F32), sds((2, dv, dk), F32), sds((2, 1, dk), F32),
    ]
    scratch = [
        v_((half, d), BF16), v_((count, d), BF16), v_((2, d, 2 * dk + 2 * dv), BF16), v_((2, dv, d), BF16),
        v_((2, count, dk), BF16), v_((2, count, dk), BF16), v_((2, count, dv), BF16), v_((2, count, dv), F32),
        v_((2, count, dk), F32), v_((2, count, dk), F32), v_((count, rk), F32), v_((2, count, dk), BF16),
        v_((2, chunks, dv, dk), BF16), v_((2, count, dv), F32), v_((2, count, dv), BF16),
        v_((2, half // 2, d), BF16), v_((2, half // 2, d), BF16), v_((half, d), F32), v_((dv, dk), F32), v_((1, dk), F32),
        v_((2, dv, dk), F32), v_((2, 1, dk), F32), v_((2, dv, dk), F32), v_((2, 1, dk), F32),
        v_((n_bits + 1, 2, dv + 16, dk), BF16), v_((n_bits + 1, 2, dv + 16, dk), BF16),
        dma((8,)), dma((32,)), dma((32,)), dma((20,)),
    ]
    return pl.pallas_call(
        functools.partial(front_phase_kernel, bits),
        name="front_phase",
        in_specs=[hbm] * 7 + [vmem] * 6,
        out_specs=[hbm] * 18 + [vmem] * 3,
        out_shape=out_shape,
        scratch_shapes=scratch,
        compiler_params=pltpu.CompilerParams(collective_id=3, has_side_effects=True, vmem_limit_bytes=60 << 20),
        cost_estimate=cost(12e9, 60e6, 1e6),
    )(tokens, cotangent, kw, vw, qw, sw, wo, rd, ru, bias, ggain, ngain, restart)


def tile_of(step):
    return jnp.where((step == 5) | (step == 6), 11 - step, step)


def mlp_phase_kernel(
    mid_h, c0_h, c1_h, c2_h, c3_h, wg_h, wu_h, wd_h, gain_ref,
    gmid_h, gm_h, part_ref, gg_h, gu_h, gd_h, near_h, far_h,
    mid, xs, cs, wg, wu, wd, hs, ggs, gus, gn, rc, rd, ac, ry, dn, dnr, gr_st, gmb,
    load_sem, send_sem, recv_sem, gr_sem, out_sem,
):
    tile = xs.shape[1]
    rows = 2 * tile
    d = xs.shape[2]
    ff = hs.shape[2]
    wide, place = lax.axis_index("wide"), lax.axis_index("narrow")
    core = place % 2
    by_core = (wide, place + 1 - 2 * core)
    by_row = (wide, (place + 2) % 4)

    loads = [pltpu.make_async_copy(mid_h, mid, load_sem.at[0])]
    for i, (src, dst) in enumerate(((wg_h, wg), (wu_h, wu), (wd_h, wd))):
        loads.append(pltpu.make_async_copy(src, dst, load_sem.at[1 + i]))
    for i, src in enumerate((c0_h, c1_h, c2_h, c3_h)):
        for j in range(2):
            loads.append(
                pltpu.make_async_copy(src.at[pl.ds(j * tile, tile)], cs.at[2 * i + j], load_sem.at[4 + 2 * i + j])
            )
    for load in loads:
        load.start()

    barrier = pltpu.get_barrier_semaphore()
    for other in (by_core, by_row):
        pl.semaphore_signal(barrier, 1, device_id=other, device_id_type=MESH)
    pl.semaphore_wait(barrier, 2)

    def remote(src, dst, index, target):
        return pltpu.make_async_remote_copy(
            src, dst, send_sem.at[index], recv_sem.at[index], device_id=target, device_id_type=MESH
        )

    x_row = [remote(xs.at[j], xs.at[4 + j], j, by_row) for j in range(2)]
    x_core = [remote(xs.at[j], xs.at[2 + j], 2 + j, by_core) for j in range(2)]
    x_both = [remote(xs.at[4 + j], xs.at[6 + j], 4 + j, by_core) for j in range(2)]
    g_near = [remote(gn.at[2 + j], rc.at[j], 6 + j, by_core) for j in range(2)]
    g_far = [remote(gn.at[6 + j], rd.at[j], 8 + j, by_core) for j in range(2)]
    g_row = [remote(ac.at[j], ry.at[j], 10 + j, by_row) for j in range(2)]
    d_in = [remote(dn.at[(2, 3, 6, 7)[j]], dnr.at[j], 14 + j, by_core) for j in range(4)]
    gain = gain_ref[...]

    loads[0].wait()
    for j in range(2):
        m = mid[pl.ds(j * tile, tile), :]
        inv = lax.rsqrt(jnp.mean(m * m, axis=-1, keepdims=True) + NORM_EPS)
        xs[j] = (m * inv * gain).astype(BF16)
        x_row[j].start()
        x_core[j].start()
    for load in loads[1:]:
        load.wait()

    def step(s, _):
        t = tile_of(s)

        @pl.when(s == 2)
        def _():
            x_core[0].wait_recv()

        @pl.when(s == 3)
        def _():
            x_core[1].wait_recv()

        for j in range(2):

            @pl.when(s == 4 + 2 * j)
            def _():
                x_row[j].wait_recv()
                x_both[j].start()

            @pl.when(s == 5 + 2 * j)
            def _():
                x_both[j].wait_recv()

        x = xs[t]
        gate = dot_nt(x, wg[...])
        up = dot_nt(x, wu[...])
        gh = dot_nt(cs[t], wd[...])
        sig = jax.nn.sigmoid(gate)
        act = gate * sig
        hidden = (act * up).astype(BF16)
        g_up = (gh * act).astype(BF16)
        g_gate = (gh * up * sig * (1.0 + gate * (1.0 - sig))).astype(BF16)
        hs[t] = hidden
        ggs[t] = g_gate
        gus[t] = g_up
        gn[t] = (dot(g_gate, wg[...]) + dot(g_up, wu[...])).astype(BF16)

        for j in range(2):

            @pl.when(s == 2 + j)
            def _():
                g_near[j].start()

            @pl.when(s == 5 + 2 * j)
            def _():
                g_far[j].start()

        dn[t] = dot(hidden, wd[...]).astype(BF16)

        for j in range(2):

            @pl.when(s == 5 + 2 * j)
            def _():
                g_far[j].wait_recv()
                ac[j] = (gn[4 + j].astype(F32) + rd[j].astype(F32)).astype(BF16)
                g_row[j].start()

        return 0

    lax.fori_loop(0, 8, step, 0)
    for copy in d_in:
        copy.start()

    blk = gr_st.shape[2]
    count = d // blk

    def gr_copies(slot, j):
        at = pl.ds(pl.multiple_of(j * blk, blk), blk)
        return [
            pltpu.make_async_copy(gr_st.at[slot, i], dst.at[at], gr_sem.at[slot, i])
            for i, dst in enumerate((gg_h, gu_h, gd_h))
        ]

    def weights(j, _):
        slot = j % 2
        cols = pl.ds(pl.multiple_of(j * blk, blk), blk)

        @pl.when(j >= 2)
        def _():
            for copy in gr_copies(slot, j - 2):
                copy.wait()

        for i, lefts, rights in ((0, xs, ggs), (1, xs, gus), (2, cs, hs)):
            acc = dot_tn(lefts[0, :, cols], rights[0])
            for t in range(1, 8):
                acc = acc + dot_tn(lefts[t, :, cols], rights[t])
            gr_st[slot, i] = acc.astype(BF16)
        for copy in gr_copies(slot, j):
            copy.start()
        return 0

    lax.fori_loop(0, count, weights, 0)
    for j in (count - 2, count - 1):
        for copy in gr_copies(j % 2, j):
            copy.wait()
    sums = []
    for j in range(2):
        d_in[j].wait_recv()
        d_in[2 + j].wait_recv()
        for at, extra, out in ((j, j, near_h), (4 + j, 2 + j, far_h)):
            dn[at] = (dn[at].astype(F32) + dnr[extra].astype(F32)).astype(BF16)
            sums.append(pltpu.make_async_copy(dn.at[at], out.at[pl.ds(j * tile, tile)], out_sem.at[3 + len(sums)]))
            sums[-1].start()

    part = jnp.zeros((1, d), F32)
    gm_out = []
    for j in range(2):
        at = pl.ds(j * tile, tile)
        g_near[j].wait_recv()
        g_row[j].wait_recv()
        grad = gn[j].astype(F32) + rc[j].astype(F32) + ry[j].astype(F32)
        m = mid[at, :]
        inv = lax.rsqrt(jnp.mean(m * m, axis=-1, keepdims=True) + NORM_EPS)
        unit = m * inv
        weighted = grad * gain
        part = part + jnp.sum(grad * unit, axis=0, keepdims=True)
        gmid = cs[j].astype(F32) + inv * (weighted - unit * jnp.mean(weighted * unit, axis=-1, keepdims=True))
        mid[at, :] = gmid
        gmb[j] = gmid.astype(BF16)
        there = gm_h.at[pl.ds(pl.multiple_of(core * rows + j * tile, tile), tile)]
        copies = [
            pltpu.make_async_copy(gmb.at[j], there, out_sem.at[1 + j]),
            remote(gmb.at[j], there, 12 + j, by_core),
        ]
        for copy in copies:
            copy.start()
        gm_out += copies
    part_ref[...] = part
    last = pltpu.make_async_copy(mid, gmid_h, out_sem.at[0])
    last.start()
    for copy in gm_out:
        copy.wait()
    last.wait()
    for copy in sums:
        copy.wait()
    for group in (d_in, x_row, x_core, x_both, g_near, g_far, g_row):
        for copy in group:
            copy.wait_send()


def mlp_phase(middle, cots, wg_t, wu_t, wd, gain):
    rows, d = middle.shape
    ff = wd.shape[0]
    tile = rows // 2
    blk = 128
    hbm = pl.BlockSpec(memory_space=pltpu.HBM)
    vmem = pl.BlockSpec(memory_space=pltpu.VMEM)
    dma = pltpu.SemaphoreType.DMA
    return pl.pallas_call(
        mlp_phase_kernel,
        name="mlp_phase",
        in_specs=[hbm] * 8 + [vmem],
        out_specs=[hbm, hbm, vmem] + [hbm] * 5,
        out_shape=[sds((rows, d), F32), sds((2 * rows, d), BF16), sds((1, d), F32)]
        + [sds((d, ff), BF16)] * 3 + [sds((rows, d), BF16)] * 2,
        scratch_shapes=[
            pltpu.VMEM((rows, d), F32), pltpu.VMEM((8, tile, d), BF16), pltpu.VMEM((8, tile, d), BF16),
            pltpu.VMEM((ff, d), BF16), pltpu.VMEM((ff, d), BF16), pltpu.VMEM((ff, d), BF16),
            pltpu.VMEM((8, tile, ff), BF16), pltpu.VMEM((8, tile, ff), BF16), pltpu.VMEM((8, tile, ff), BF16),
            pltpu.VMEM((8, tile, d), BF16), pltpu.VMEM((2, tile, d), BF16), pltpu.VMEM((2, tile, d), BF16),
            pltpu.VMEM((2, tile, d), BF16), pltpu.VMEM((2, tile, d), BF16),
            pltpu.VMEM((8, tile, d), BF16), pltpu.VMEM((4, tile, d), BF16),
            pltpu.VMEM((2, 3, blk, ff), BF16), pltpu.VMEM((2, tile, d), BF16),
            dma((12,)), dma((18,)), dma((18,)), dma((2, 3)), dma((7,)),
        ],
        compiler_params=pltpu.CompilerParams(collective_id=1, has_side_effects=True, vmem_limit_bytes=62 << 20),
        cost_estimate=cost(18 * 4 * rows * d * ff, 60e6, 4 * rows * ff),
    )(middle, *cots, wg_t, wu_t, wd, gain)


def back_phase_kernel(
    bits,
    gm_h, mx_h, s_h, r_h, gt_h, rows_h, q_h, k_h, v_h, cum_h, dpre_h, rank_h, sin_h, w_h, wo_h, g_h, gmid_h, tok_h,
    off_ref, enter_ref, mult_ref, ru_ref, rd_ref, ggain_ref, ngain_ref, mpart_ref, restart_ref,
    in_h, gate_o, up_o, down_o, wout_o, k_o, v_o, q_o, s_o, rdown_o, rup_o, bias_o, mgain_o, group_o, ngain_o,
    gm, mx, sw, reach, gated, rows, q, k, v, cum, dpre, rank, sin, w, wo, keep, mrecv, gmid, tok,
    gx, al, grank, ds, lb_m, pre_s, pre_m, sc_out, sc_in, osv, osy, osr, kv, kvy, kvr, tb, tr, sm, smr, ng, ngr,
    load_sem, send_sem, recv_sem, out_sem,
):
    count, d = rows.shape
    half = count // 2
    dk, dv = q.shape[2], v.shape[2]
    where = Places(2 ** len(bits))
    wires = Wires(send_sem, recv_sem)
    loads = []

    def load(src, dst):
        copy = pltpu.make_async_copy(src, dst, load_sem.at[len(loads)])
        loads.append(copy)
        copy.start()
        return copy

    orders = (bits, bits[1:] + bits[:1], bits)
    first = [load(gm_h, gm), load(wo_h, wo), load(mx_h, mx), load(s_h, sw), load(r_h, reach)]
    second = [load(gt_h, gated), load(rows_h, rows)]
    third = []
    for i in range(3):
        left = sorted(bits, reverse=True)
        dim = left.index(orders[i][0])
        third.append(load(g_h[i].at[(slice(None),) * dim + (where.has(orders[i][0]),)], keep[i]))
    fourth = [load(rank_h, rank)]
    for src, dst in ((q_h, q), (k_h, k), (v_h, v), (cum_h, cum), (dpre_h, dpre), (sin_h, sin), (w_h, w)):
        fourth.append(load(src, dst))
    fifth = [load(gmid_h, gmid), load(tok_h, tok)]

    where.meet()
    mlp = [Scatter(where, wires, g_h[i], keep[i], orders[i], mrecv[i]) for i in range(3)]
    scan = Scan(where, wires, ds, lb_m, pre_s, pre_m, sc_out, sc_in, True)
    os_y = wires.copy(osv.at[1], osy, where.by_row)
    os_s = Scatter(where, wires, osv.at[0], None, bits[1:] + bits[:1], osr)
    kv_y = wires.copy(kv.at[1], kvy, where.by_row)
    kv_s = Scatter(where, wires, kv.at[0], None, bits, kvr)
    tots = [wires.copy(tb.at[j], tr.at[j], where.by_core) for j in range(2)]
    every = Everywhere(where, wires, sm, smr)
    every_n = Everywhere(where, wires, ng, ngr)
    n_bits = len(bits)
    for part in mlp:
        part.begin()

    blk = half // 2
    gain = ggain_ref[...]
    ds[...] = jnp.zeros_like(ds)
    sm[0] = jnp.zeros_like(sm[0])
    ng[0] = jnp.zeros_like(ng[0])
    for copy in first:
        copy.wait()

    def gate_step(i, part):
        at = pl.ds(pl.multiple_of(i * blk, blk), blk)
        g = gm[at, :]
        for h in range(2):
            grad = dot_nt(g, wo[h])
            mixed = mx[h, at, :]
            inv = lax.rsqrt(jnp.mean(mixed * mixed, axis=-1, keepdims=True) + GROUP_EPS)
            unit = mixed * inv
            s = sw[h, at, :]
            sig = jax.nn.sigmoid(s)
            al[h, at, 2 * dk + dv :] = (grad * unit * gain * (sig * (1.0 + s * (1.0 - sig)))).astype(BF16)
            dn = grad * (s * sig)
            part = part + jnp.sum(dn * unit, axis=0, keepdims=True)
            weighted = dn * gain
            gmix = (inv * (weighted - unit * jnp.mean(weighted * unit, axis=-1, keepdims=True))).astype(BF16)
            gx[h, at, :] = gmix
            ds[h] += dot_tn(gmix, reach[h, at, :])
        return part

    group_part = lax.fori_loop(0, 4, gate_step, jnp.zeros((1, dv), F32))
    for h in range(2):
        ds[h] = ds[h] * restart_ref[...]
        lb_m[h] = mult_ref[h]
    scan.begin()

    size = 256
    per = size // osv.shape[-2]

    def put(ref, h, j, lanes, value):
        rows_each = ref.shape[-2]
        for p in range(per):
            ref[(h,) + bit_index(j * per + p, bits) + (slice(None), lanes)] = value[p * rows_each : (p + 1) * rows_each]

    def out_step(j, _):
        cols = pl.ds(pl.multiple_of(j * size, size), size)
        for h in (1, 0):
            put(osv, h, j, slice(0, dv), dot_tn(gm[:, cols], gated[h]).astype(BF16))
        return 0

    def swish_step(j, _):
        cols = pl.ds(pl.multiple_of(j * size, size), size)
        for h in (1, 0):
            put(osv, h, j, slice(dv, 2 * dv), dot_tn(rows[:, cols], al[h, :, 2 * dk + dv :]).astype(BF16))
        return 0

    for copy in second:
        copy.wait()
    lax.fori_loop(0, d // size, out_step, 0)
    scan.advance()
    lax.fori_loop(0, d // size, swish_step, 0)
    os_y.start()
    for copy in third:
        copy.wait()
    while scan.advance():
        if scan.at == n_bits:
            mlp[1].advance()
            mlp[0].advance()
    for copy in fourth:
        copy.wait()

    ds[...] = pre_s[...]
    chunks = count // CHUNK
    mask = triangle(True)
    ones = triangle(False).astype(F32)
    scale = dk**-0.5
    rk = rank.shape[1]

    def back_step(step, carry):
        c = chunks - 1 - step
        at = pl.ds(pl.multiple_of(c * CHUNK, CHUNK), CHUNK)
        grs, new = None, []
        for h in range(2):
            ch = cum[h, at, :]
            mid = ch[HALF - 1 : HALF]
            end = ch[CHUNK - 1 :]
            e_qd, e_kd, e_qi, e_ke = jnp.exp(ch - mid), jnp.exp(mid - ch), jnp.exp(ch), jnp.exp(end - ch)
            e_end = jnp.exp(end)
            qf = q[h, at, :].astype(F32) * scale
            kf = k[h, at, :].astype(F32)
            vc = v[h, at, :]
            qd = (qf * e_qd).astype(BF16)
            kd = (kf * e_kd).astype(BF16)
            qi = (qf * e_qi).astype(BF16)
            ke = (kf * e_ke).astype(BF16)
            go = gx[h, at, :]
            state = sin[h, c].astype(F32) + enter_ref[h] * jnp.exp(off_ref[h, c])
            state_low = state.astype(BF16)
            dstate = ds[h]
            dstate_low = dstate.astype(BF16)
            scores = jnp.where(mask, dot_nt(qd, kd), 0.0).astype(BF16)
            dscores = jnp.where(mask, dot_nt(go, vc), 0.0).astype(BF16)
            d_v = dot_tn(scores, go) + dot_nt(ke, dstate_low)
            d_qd = dot(dscores, kd)
            d_qi = dot(go, state_low)
            d_kd = dot_tn(dscores, qd)
            d_ke = dot(vc, dstate_low)
            d_q = scale * (d_qd * e_qd + d_qi * e_qi)
            d_k = d_kd * e_kd + d_ke * e_ke
            tail = ke.astype(F32) * d_ke
            d_cum = qd.astype(F32) * d_qd + qi.astype(F32) * d_qi - kd.astype(F32) * d_kd - tail
            d_end = jnp.sum(tail, axis=0, keepdims=True) + e_end * jnp.sum(dstate * state, axis=0, keepdims=True)
            grad_decay = exact(ones, d_cum, ((1,), (0,))) + d_end
            g_pre = grad_decay * jax.nn.sigmoid(-dpre[h, at, :]) * (1.0 / GATE_NORM)
            al[h, at, :dk] = d_k.astype(BF16)
            al[h, at, dk : dk + dv] = d_v.astype(BF16)
            al[h, at, dk + dv : 2 * dk + dv] = d_q.astype(BF16)
            gr = exact(g_pre, ru_ref[h], ((1,), (1,)))
            grs = gr if grs is None else grs + gr
            new.append(carry[2 * h] + exact(rank[at, :], g_pre, ((0,), (0,))))
            new.append(carry[2 * h + 1] + jnp.sum(g_pre, axis=0, keepdims=True))
            ds[h] = dstate * e_end + dot_tn(go, qi)
        grank[at, :] = grs.astype(BF16)
        return tuple(new)

    zero = (jnp.zeros((rk, dk), F32), jnp.zeros((1, dk), F32))
    rup0, gb0, rup1, gb1 = lax.fori_loop(0, chunks, back_step, zero + zero)
    for i in (1, 0, 2):
        mlp[i].advance()

    def kvq_step(h):
        def step(j, _):
            cols = pl.ds(pl.multiple_of(j * size, size), size)
            put(kv, h, j, slice(None), dot_tn(rows[:, cols], al[h, :, : 2 * dk + dv]).astype(BF16))
            return 0

        lax.fori_loop(0, d // size, step, 0)

    kvq_step(1)
    kv_y.start()

    def add_row(ref, extra):
        for at in itertools.product(range(2), repeat=n_bits):
            ref[(0,) + at] = (ref[(0,) + at].astype(F32) + extra[at].astype(F32)).astype(BF16)

    os_y.wait_recv()
    add_row(osv, osy)
    os_s.begin()

    def total_step(i, _):
        b = jnp.where(i < 2, 2 - 2 * where.core + i, 2 * where.core + i - 2)
        at = pl.ds(pl.multiple_of(b * blk, blk), blk)
        total = dot_nt(al[0, at, :], w[0]) + dot_nt(al[1, at, :], w[1]) + dot_nt(grank[at, :], rd_ref[...])
        for j in range(2):

            @pl.when(i == j)
            def _():
                tb[j] = total.astype(BF16)
                tots[j].start()

            @pl.when(i == 2 + j)
            def _():
                tb[2 + j] = total.astype(BF16)

        return 0

    lax.fori_loop(0, 4, total_step, 0)

    sm[0, 0:rk, :] = dot_tn(grank[...], rows[...])
    at0 = pl.ds(pl.multiple_of(where.place * dk, dk), dk)
    at1 = pl.ds(pl.multiple_of(((where.place + 2) % 4) * dk, dk), dk)
    sm[0, rk : 2 * rk, at0] = rup0
    sm[0, rk : 2 * rk, at1] = rup1
    sm[0, 2 * rk : 2 * rk + 1, at0] = gb0
    sm[0, 2 * rk : 2 * rk + 1, at1] = gb1
    sm[0, 2 * rk + 1 : 2 * rk + 2, :] = mpart_ref[...]
    sm[0, 2 * rk + 2 : 2 * rk + 3, :dv] = group_part
    every.begin()
    kvq_step(0)
    every.advance()

    for copy in fifth:
        copy.wait()
    ngain = ngain_ref[...]
    part = jnp.zeros((1, d), F32)
    for j in range(2):
        at = pl.ds(j * blk, blk)
        tots[j].wait_recv()
        grad = tb[2 + j].astype(F32) + tr[j].astype(F32)
        x = tok[at, :].astype(F32)
        inv = lax.rsqrt(jnp.mean(x * x, axis=-1, keepdims=True) + NORM_EPS)
        unit = x * inv
        weighted = grad * ngain
        part = part + jnp.sum(grad * unit, axis=0, keepdims=True)
        gmid[at, :] = gmid[at, :] + inv * (weighted - unit * jnp.mean(weighted * unit, axis=-1, keepdims=True))
    done = pltpu.make_async_copy(gmid, in_h, out_sem.at[0])
    done.start()
    ng[0, 0:1, :] = part
    every_n.begin()

    outs = (gate_o, up_o, down_o)
    kv_y.wait_recv()
    add_row(kv, kvy)
    kv_s.begin()
    for i in (1, 0):
        outs[i][...] = jnp.transpose(mlp[i].result())
    mlp[2].advance()
    every.advance()
    every_n.advance()
    for _ in range(n_bits - 1):
        os_s.advance()
        every_n.advance()
        kv_s.advance()
        every.advance()
    outs[2][...] = jnp.transpose(mlp[2].result())
    total = os_s.result()
    wout_o[...] = jnp.transpose(total[:, :dv])
    s_o[...] = total[:, dv:]
    every_n.advance()
    total = kv_s.result()
    k_o[...] = total[:, :dk]
    v_o[...] = total[:, dk : dk + dv]
    q_o[...] = total[:, dk + dv :]
    small = every.result()
    rdown_o[...] = small[:rk]
    rup_o[...] = small[rk : 2 * rk, : rup_o.shape[1]]
    bias_o[...] = small[2 * rk : 2 * rk + 1, : bias_o.shape[1]]
    mgain_o[...] = small[2 * rk + 1 : 2 * rk + 2]
    group_o[...] = small[2 * rk + 2 : 2 * rk + 3, :dv]
    ngain_o[...] = every_n.result()[:1]
    done.wait()
    wires.drain()


def back_phase(
    gm, mx, s, reach, gated, rows, q, k, v, cum, dpre, rank, sin, w, wo, grads, gmid, tokens,
    off, enter, mult, ru, rd, ggain, ngain, mpart, restart,
):
    bits = wide_bits()
    count, d = rows.shape
    half = count // 2
    dk, dv, rk = q.shape[2], v.shape[2], rank.shape[1]
    ff = grads[0].shape[-1]
    each = d // 2 ** len(bits)
    n_bits, chunks = len(bits), count // CHUNK
    hbm = pl.BlockSpec(memory_space=pltpu.HBM)
    vmem = pl.BlockSpec(memory_space=pltpu.VMEM)
    dma = pltpu.SemaphoreType.DMA
    v_ = pltpu.VMEM

    def shape(lead, cols):
        return (2,) * lead + (each, cols)

    def falls(cols):
        return [v_(shape(n_bits - 1 - i, cols), BF16) for i in range(n_bits)]

    pair, three = [hbm] * 2, [hbm] * 3
    kvq = 2 * dk + dv
    small = 2 * rk + 8
    scratch = [
        v_((count, d), BF16), v_((2, count, dv), F32), v_((2, count, dv), F32), v_((2, count, dk), BF16),
        v_((2, count, dv), BF16), v_((count, d), BF16), v_((2, count, dk), BF16), v_((2, count, dk), BF16),
        v_((2, count, dv), BF16), v_((2, count, dk), F32), v_((2, count, dk), F32), v_((count, rk), F32),
        v_((2, chunks, dv, dk), BF16), v_((2, d, kvq + dv), BF16), v_((2, dv, d), BF16),
        [v_(shape(n_bits - 1, ff), BF16)] * 3, [falls(ff)] * 3, v_((half, d), F32), v_((half, d), BF16),
        v_((2, count, dv), BF16), v_((2, count, kvq + dv), BF16), v_((count, rk), BF16),
        v_((2, dv, dk), F32), v_((2, 1, dk), F32), v_((2, dv, dk), F32), v_((2, 1, dk), F32),
        v_((n_bits + 1, 2, dv + 16, dk), BF16), v_((n_bits + 1, 2, dv + 16, dk), BF16),
        v_((2,) + shape(n_bits, 2 * dv), BF16), v_(shape(n_bits, 2 * dv), BF16), falls(2 * dv),
        v_((2,) + shape(n_bits, kvq), BF16), v_(shape(n_bits, kvq), BF16), falls(kvq),
        v_((4, half // 2, d), BF16), v_((2, half // 2, d), BF16),
        v_((n_bits + 3, small, d), F32), v_((n_bits + 2, small, d), F32),
        v_((n_bits + 3, 8, d), F32), v_((n_bits + 2, 8, d), F32),
        dma((48,)), dma((64,)), dma((64,)), dma((1,)),
    ]
    out_shape = [
        sds((half, d), F32), sds((ff, each), F32), sds((ff, each), F32), sds((ff, each), F32), sds((dv, each), F32),
        sds((each, dk), F32), sds((each, dv), F32), sds((each, dk), F32), sds((each, dv), F32),
        sds((rk, d), F32), sds((rk, 4 * dk), F32), sds((1, 4 * dk), F32), sds((1, d), F32), sds((1, dv), F32), sds((1, d), F32),
    ]
    operands = (
        gm, mx, s, reach, gated, rows, q, k, v, cum, dpre, rank, sin, w, wo, grads, gmid, tokens,
        off, enter, mult, ru, rd, ggain, ngain, mpart, restart,
    )
    flat, tree = jax.tree.flatten(operands)
    n_vmem = len(jax.tree.leaves(operands[18:]))
    flat_scratch, scratch_tree = jax.tree.flatten(scratch, is_leaf=lambda x: not isinstance(x, list))
    n_in, n_out = len(flat), len(out_shape)

    def kernel(*refs):
        ins = jax.tree.unflatten(tree, refs[:n_in])
        rest = jax.tree.unflatten(scratch_tree, refs[n_in + n_out :])
        back_phase_kernel(bits, *ins, *refs[n_in : n_in + n_out], *rest)

    return pl.pallas_call(
        kernel,
        name="back_phase",
        in_specs=[hbm] * (n_in - n_vmem) + [vmem] * n_vmem,
        out_specs=[hbm] + [vmem] * (n_out - 1),
        out_shape=out_shape,
        scratch_shapes=flat_scratch,
        compiler_params=pltpu.CompilerParams(collective_id=2, has_side_effects=True, vmem_limit_bytes=62 << 20),
        cost_estimate=cost(40e9, 60e6, 1e6),
    )(*flat)


def hop(value, axis, bit):
    return lax.ppermute(value, axis, [(i, i ^ bit) for i in range(lax.axis_size(axis))])


def wide_bits():
    count, bits, bit = lax.axis_size("wide"), [], 1
    while bit < count:
        bits.append(bit)
        bit *= 2
    return bits


def shards(
    tokens, cotangent, flags, norm_gain, query_weight, key_weight, value_weight, swish_weight, rank_down, rank_up,
    decay_bias, group_gain, output_weight, mlp_gain, mlp_gate, mlp_up, mlp_down,
):
    place = lax.axis_index("narrow")
    dk, dv, d = query_weight.shape[1], value_weight.shape[1], tokens.shape[1]
    restart = jnp.where((place & 2) != 0, 1.0, 1.0 - flags[0].astype(F32))
    restart = jnp.full((1, dk), restart, F32)
    norm_gain_f = norm_gain.astype(F32).reshape(1, d)
    mlp_gain_f = mlp_gain.astype(F32).reshape(1, d)
    gain_row = group_gain.astype(F32).reshape(1, dv)

    def both_heads(value):
        return jnp.stack([lax.dynamic_slice_in_dim(value, head * dk, dk, 1) for head in (place, place ^ 2)]).astype(F32)

    ru = both_heads(rank_up)
    bias = both_heads(decay_bias.reshape(1, -1))
    (
        middle, rows_all, q, k, v, s, cum, dpre, rank_pre, reach, sin, mixed, gated, w, weights_out, cot_c, cot_y, cot_d,
        off, enter, mults,
    ) = front_phase(
        tokens, cotangent, key_weight, value_weight, query_weight, swish_weight, output_weight, rank_down, ru, bias,
        gain_row, norm_gain_f, restart,
    )
    grad_middle, gm_all, mlp_gain_part, gate_g, up_g, down_g, near, far = mlp_phase(
        middle, (cotangent, cot_c, cot_y, cot_d), mlp_gate.T, mlp_up.T, mlp_down, mlp_gain_f
    )
    result = (middle + (near.astype(F32) + hop(far, "narrow", 2).astype(F32))).astype(BF16)
    bits = wide_bits()
    split = (2,) * len(bits) + (d // 2 ** len(bits), -1)
    input_grad, gate_t, up_t, down_t, out_t, k_g, v_g, q_g, s_g, rdown_t, rup_g, bias_g, mgain_g, group_g, ngain = back_phase(
        gm_all, mixed, s, reach, gated, rows_all, q, k, v, cum, dpre, rank_pre, sin,
        w, weights_out, tuple(g.reshape(split) for g in (gate_g, up_g, down_g)), grad_middle, tokens,
        off, enter, mults, ru, rank_down, gain_row, norm_gain_f, mlp_gain_part, restart,
    )
    return (
        result,
        input_grad,
        ngain[0],
        q_g,
        k_g,
        v_g,
        s_g,
        rdown_t.T,
        rup_g,
        bias_g[0],
        group_g[0],
        out_t,
        mgain_g[0],
        gate_t.T,
        up_t.T,
        down_t,
    )


def solution(mesh):
    rows, cols = P(("wide", "narrow"), None), P(None, "narrow")
    both = P("wide", "narrow")
    in_specs = (
        rows, rows, P("wide"), P(), cols, cols, cols, cols, P(), P(), P(), P(), P("narrow", None), P(), cols, cols,
        P("narrow", None),
    )
    out_specs = (
        rows, rows, P(), both, both, both, both, P(), P(), P(), P(), P("narrow", "wide"), P(), both, both,
        P("narrow", "wide"),
    )
    return jax.shard_map(shards, mesh=mesh, in_specs=in_specs, out_specs=out_specs, check_vma=False)
```

```python
import functools
import itertools

import jax
import jax.numpy as jnp
from jax import lax
from jax.experimental import pallas as pl
from jax.experimental.pallas import tpu as pltpu
from jax.sharding import PartitionSpec as P

NORM_EPS = 1e-06
GROUP_EPS = 1e-05
GATE_NORM = 16.0
HIGHEST_PREC = lax.Precision.HIGHEST
MESH = pl.DeviceIdType.MESH
CHUNK = 128
HALF = CHUNK // 2
BLOCK = 256
F32 = jnp.float32
BF16 = jnp.bfloat16


def dot(a, b):
    return lax.dot_general(a, b, (((1,), (0,)), ((), ())), preferred_element_type=F32)


def dot_nt(a, b):
    return lax.dot_general(a, b, (((1,), (1,)), ((), ())), preferred_element_type=F32)


def dot_tn(a, b):
    return lax.dot_general(a, b, (((0,), (0,)), ((), ())), preferred_element_type=F32)


def exact(a, b, dims):
    return lax.dot_general(
        a, b, (dims, ((), ())), precision=HIGHEST_PREC, preferred_element_type=F32
    )


def sds(shape, dtype):
    return jax.ShapeDtypeStruct(shape, dtype)


def params(mib=48):
    return pltpu.CompilerParams(vmem_limit_bytes=mib << 20)


def cost(flops, nbytes, trans=0):
    return pl.CostEstimate(flops=int(flops), bytes_accessed=int(nbytes), transcendentals=int(trans))


def whole(shape):
    return pl.BlockSpec(shape, lambda i: (0,) * len(shape), pipeline_mode=pl.Buffered(1))


def rows_spec(rows, cols):
    return pl.BlockSpec((rows, cols), lambda i: (i, 0))


def triangle(lower):
    r = lax.broadcasted_iota(jnp.int32, (CHUNK, CHUNK), 0)
    c = lax.broadcasted_iota(jnp.int32, (CHUNK, CHUNK), 1)
    return r >= c if lower else r <= c


class Wires:
    def __init__(self, send_sem, recv_sem):
        self.send_sem, self.recv_sem, self.used, self.all = send_sem, recv_sem, 0, []

    def copy(self, src, dst, target):
        made = pltpu.make_async_remote_copy(
            src,
            dst,
            self.send_sem.at[self.used],
            self.recv_sem.at[self.used],
            device_id=target,
            device_id_type=MESH,
        )
        self.used += 1
        self.all.append(made)
        return made

    def drain(self):
        for made in self.all:
            made.wait_send()


class Places:
    def __init__(self, wide_count):
        self.wide, self.place = lax.axis_index("wide"), lax.axis_index("narrow")
        self.core = self.place % 2
        self.second = self.place // 2
        self.by_core = (self.wide, self.place + 1 - 2 * self.core)
        self.by_row = (self.wide, (self.place + 2) % 4)
        self.bits = []
        bit = 1
        while bit < wide_count:
            self.bits.append(bit)
            bit *= 2

    def has(self, bit):
        return (self.wide // bit) % 2

    def across(self, bit):
        return (self.wide + bit - 2 * bit * self.has(bit), self.place)

    def meet(self):
        barrier = pltpu.get_barrier_semaphore()
        others = [self.by_core, self.by_row] + [self.across(bit) for bit in self.bits]
        for other in others:
            pl.semaphore_signal(barrier, 1, device_id=other, device_id_type=MESH)
        pl.semaphore_wait(barrier, len(others))


class Scan:
    def __init__(self, where, wires, tot_s, tot_m, pre_s, pre_m, out, into, backward):
        self.tot_s, self.tot_m, self.pre_s, self.pre_m = tot_s, tot_m, pre_s, pre_m
        self.out, self.into = out, into
        self.steps = []
        for i, bit in enumerate([0] + where.bits):
            target = where.across(bit) if bit else where.by_row
            is_set = where.has(bit) if bit else where.second
            later = (1 - is_set if backward else is_set) > 0
            self.steps.append((wires.copy(out.at[i], into.at[i], target), later, bit == 0))
        pre_s[...] = jnp.zeros_like(pre_s)
        pre_m[...] = jnp.ones_like(pre_m)

    def begin(self, i=0):
        self.at = i
        dv = self.tot_s.shape[1]
        for h in range(2):
            self.out[i, h, :dv, :] = self.tot_s[h].astype(BF16)
            self.out[i, h, dv:, :] = jnp.broadcast_to(self.tot_m[h], (16, self.tot_m.shape[2])).astype(BF16)
        self.steps[i][0].start()

    def advance(self):
        self.finish(self.at)
        if self.at + 1 < len(self.steps):
            self.begin(self.at + 1)
            return True
        return False

    def finish(self, i):
        copy, later, swapped = self.steps[i]
        copy.wait_recv()
        dv = self.tot_s.shape[1]
        for h in range(2):
            g = 1 - h if swapped else h
            oth_s = self.into[i, g, :dv, :].astype(F32)
            oth_m = self.into[i, g, dv : dv + 1, :].astype(F32)
            pre_s, pre_m, tot_s, tot_m = self.pre_s[h], self.pre_m[h], self.tot_s[h], self.tot_m[h]
            self.pre_s[h] = jnp.where(later, oth_s * pre_m + pre_s, pre_s)
            self.pre_m[h] = jnp.where(later, oth_m * pre_m, pre_m)
            self.tot_s[h] = jnp.where(later, oth_s * tot_m + tot_s, tot_s * oth_m + oth_s)
            self.tot_m[h] = tot_m * oth_m


class Scatter:
    def __init__(self, where, wires, source, keep, order, recvs):
        self.recvs, self.steps, self.at = recvs, [], 0
        left = sorted(order, reverse=True)
        held, first = source, keep
        for bit, recv in zip(order, recvs):
            dim = left.index(bit)
            mine = where.has(bit)
            other = held.at[(slice(None),) * dim + (1 - mine,)]
            copy = wires.copy(other, recv, where.across(bit))
            self.steps.append((copy, held if first is None else first, dim, mine, first is not None))
            left.pop(dim)
            held, first = recv, None

    def go(self):
        self.steps[self.at][0].start()

    def land(self):
        total = self.finish(self.at)
        self.at += 1
        return total

    def advance(self):
        if self.at + 1 < len(self.steps):
            self.land()
            self.go()

    def result(self):
        while self.at + 1 < len(self.steps):
            self.advance()
        return self.land()

    def finish(self, i):
        copy, held, dim, mine, picked = self.steps[i]
        copy.wait_recv()
        recv = self.recvs[i]
        last = i == len(self.steps) - 1
        for at in itertools.product(range(2), repeat=len(recv.shape) - 2):
            source = at if picked else at[:dim] + (mine,) + at[dim:]
            total = recv[at].astype(F32) + held[source].astype(F32)
            if last:
                return total
            recv[at] = total.astype(BF16)
        return None


class Everywhere:
    def __init__(self, where, wires, values, recvs):
        self.values, self.recvs = values, recvs
        targets = [where.by_core, where.by_row] + [where.across(bit) for bit in where.bits]
        self.steps = [wires.copy(values.at[i], recvs.at[i], target) for i, target in enumerate(targets)]

    def begin(self, i=0):
        self.at = i
        self.steps[i].start()

    def advance(self):
        if self.at + 1 < len(self.steps):
            self.finish(self.at)
            self.begin(self.at + 1)

    def result(self):
        while self.at + 1 < len(self.steps):
            self.advance()
        self.finish(self.at)
        return self.values[len(self.steps)]

    def finish(self, i):
        self.steps[i].wait_recv()
        self.values[i + 1] = self.values[i] + self.recvs[i]


class Shared:
    def __init__(self, where, wires, parts, first, values, recvs, out):
        self.core, self.parts, self.first = where.core, parts, first
        self.values, self.recvs, self.out, self.at = values, recvs, out, 0
        targets = [where.by_row] + [where.across(bit) for bit in where.bits]
        self.steps = [wires.copy(parts.at[1 - where.core], first, where.by_core)]
        self.steps += [wires.copy(values.at[i], recvs.at[i], target) for i, target in enumerate(targets)]
        self.steps.append(wires.copy(out.at[where.core], out.at[where.core], where.by_core))

    def begin(self):
        self.steps[0].start()

    def advance(self):
        i, last = self.at, len(self.steps) - 1
        if i == last:
            return
        self.steps[i].wait_recv()
        if i == 0:
            total = self.parts[self.core] + self.first[...]
        else:
            total = self.values[i - 1] + self.recvs[i - 1]
        if i + 1 == last:
            self.out[self.core] = total
        else:
            self.values[i] = total
        self.at = i + 1
        self.steps[i + 1].start()

    def result(self):
        while self.at + 1 < len(self.steps):
            self.advance()
        self.steps[-1].wait_recv()
        return self.out


def bit_index(w, bits):
    return tuple((w // bit) % 2 for bit in sorted(bits, reverse=True))


def put_rows(ref, lead, j, size, bits, lanes, value):
    each = ref.shape[-2]
    for p in range(size // each):
        at = lead + bit_index(j * (size // each) + p, bits) + (slice(None), lanes)
        ref[at] = value[p * each : (p + 1) * each]


def lanes_at(start, size):
    return pl.ds(pl.multiple_of(start, size), size)


def row_places(d, dv, qk):
    return (0, d, 2 * d, 2 * d + dv, 2 * d + dv + qk)


def front_phase_kernel(
    bits,
    tok_h, cot_h, kw_h, vw_h, qw_h, sw_h, wo_h, rd_ref, ru_ref, row_ref,
    mid_h, rows_h, q_h, k_h, v_h, s_h, cum_h, dpre_h, rank_h, reach_h, sin_h, mx_h, gated_h, w_h, wo2_h, c1_h, c2_h, c3_h,
    off_o, enter_o, mult_o,
    tok, rows, w, wo, q, k, v, sw, cum, dpre, rank, reach, sin, mx, gated, tb, tr, mid, st, off,
    tot_s, tot_m, pre_s, pre_m, sc_out, sc_in,
    load_sem, send_sem, recv_sem, out_sem,
):
    count, d = rows.shape
    half = count // 2
    blk = half // 2
    dk, dv = q.shape[2], v.shape[2]
    kv = dk + dv
    where = Places(2 ** len(bits))
    wires = Wires(send_sem, recv_sem)
    loads, stores = [], []

    def load(src, dst):
        copy = pltpu.make_async_copy(src, dst, load_sem.at[len(loads)])
        loads.append(copy)
        copy.start()
        return copy

    def store(src, dst):
        copy = pltpu.make_async_copy(src, dst, out_sem.at[len(stores)])
        stores.append(copy)
        copy.start()

    load_tok = load(tok_h, tok)
    load_kv = [load(kw_h, w.at[0, :, pl.ds(0, dk)]), load(vw_h, w.at[0, :, pl.ds(dk, dv)])]
    load_qs = [load(qw_h, w.at[0, :, pl.ds(kv, dk)]), load(sw_h, w.at[0, :, pl.ds(kv + dk, dv)])]
    load_wo = load(wo_h, wo.at[0])

    where.meet()
    at_row = row_places(d, dv, 4 * dk)
    ngain = row_ref[:, at_row[0] : at_row[1]]
    gain = row_ref[:, at_row[2] : at_row[3]]
    restart = row_ref[:, at_row[4] : at_row[4] + dk]

    odd = where.has(1)
    over_x = where.across(1)
    quarter = d // 4

    def weight_pieces(cols):
        made = []
        for i in range(2):
            near = pl.ds(pl.multiple_of(odd * 2 * quarter + i * quarter, quarter), quarter)
            made.append(
                (
                    wires.copy(w.at[0, near, cols], w.at[1, near, cols], where.by_row),
                    wires.copy(w.at[1, near, cols], w.at[1, near, cols], over_x),
                )
            )
        return made

    kv_in = weight_pieces(pl.ds(0, kv))
    qs_in = weight_pieces(pl.ds(kv, kv))
    near = pl.ds(pl.multiple_of(odd * (dv // 2), dv // 2), dv // 2)
    wo_in = [
        wires.copy(wo.at[0, near], wo.at[1, near], where.by_row),
        wires.copy(wo.at[1, near], wo.at[1, near], over_x),
    ]
    cot_row, cot_both = [], []
    for i in range(2):
        at = pl.ds(i * blk, blk)
        cot_row.append(wires.copy(cot_h.at[at], c2_h.at[at], where.by_row))
        cot_both.append(wires.copy(c2_h.at[at], c3_h.at[at], where.by_core))
    cot_core = wires.copy(cot_h, c1_h, where.by_core)
    row_out = []
    for i in range(2):
        at = pl.ds(pl.multiple_of(where.core * half + i * blk, blk), blk)
        row_out.append(wires.copy(rows.at[at], rows.at[at], where.by_core))
    terms = [wires.copy(tb.at[j], tr.at[j], where.by_core) for j in range(2)]
    scan = Scan(where, wires, tot_s, tot_m, pre_s, pre_m, sc_out, sc_in, False)

    for copy in load_kv:
        copy.wait()
    for piece in kv_in:
        piece[0].start()
    load_tok.wait()
    for i in range(2):
        x = tok[pl.ds(i * blk, blk), :].astype(F32)
        inv = lax.rsqrt(jnp.mean(x * x, axis=-1, keepdims=True) + NORM_EPS)
        rows[pl.ds(pl.multiple_of(where.core * half + i * blk, blk), blk), :] = (x * inv * ngain).astype(BF16)
        row_out[i].start()
    for copy in load_qs:
        copy.wait()
    load_wo.wait()
    for copy in row_out:
        copy.wait_recv()
    cot_core.start()
    store(rows, rows_h)

    mask = triangle(True)
    ones = mask.astype(F32)
    scale = dk**-0.5
    blocks = count // BLOCK
    per = BLOCK // CHUNK

    def first_step(i, _):
        h, b = i // blocks, i % blocks
        at = pl.ds(pl.multiple_of(b * BLOCK, BLOCK), BLOCK)
        for p in range(2):

            @pl.when(i == blocks - 2 + p)
            def _():
                kv_in[p][0].wait_recv()
                kv_in[p][1].start()

            @pl.when(i == 2 * blocks - 2 + p)
            def _():
                qs_in[p][0].wait_recv()
                qs_in[p][1].start()

        @pl.when(i == blocks - 1)
        def _():
            for piece in qs_in:
                piece[0].start()
            cot_row[0].start()

        @pl.when(i == blocks)
        def _():
            for piece in kv_in:
                piece[1].wait_recv()

        @pl.when(b == 0)
        def _():
            st[...] = jnp.zeros_like(st)
            off[...] = jnp.zeros_like(off)

        x = rows[at, :]

        @pl.when(i < blocks)
        def _():
            rank[at, :] = dot_nt(x, rd_ref[...])

        proj = dot(x, w[h, :, :kv])
        head = (where.place + 2 * h) % 4
        ru = ru_ref[:, lanes_at(head * dk, dk)].astype(F32)
        bias = row_ref[:, lanes_at(at_row[3] + head * dk, dk)]
        pre = exact(rank[at, :], ru, ((1,), (0,))) + bias
        dlog = jax.nn.log_sigmoid(pre) * (1.0 / GATE_NORM)
        k_low = proj[:, :dk].astype(BF16)
        v_low = proj[:, dk:].astype(BF16)
        k[h, at, :] = k_low
        v[h, at, :] = v_low
        dpre[h, at, :] = pre
        for j in range(per):
            part = slice(j * CHUNK, (j + 1) * CHUNK)
            c = b * per + j
            ch = exact(ones, dlog[part], ((1,), (0,)))
            end = ch[CHUNK - 1 :]
            ke = (k_low[part].astype(F32) * jnp.exp(end - ch)).astype(BF16)
            state = st[...]
            offset = off[...]
            cum[h, pl.ds(pl.multiple_of(c * CHUNK, CHUNK), CHUNK), :] = ch
            sin[h, c] = state.astype(BF16)
            off_o[h, c] = offset
            st[...] = state * jnp.exp(end) + dot_tn(v_low[part], ke)
            off[...] = offset + end

        @pl.when(b == blocks - 1)
        def _():
            tot_s[h] = st[...]
            mult = restart * jnp.exp(off[...])
            tot_m[h] = mult
            mult_o[h] = mult

        return 0

    lax.fori_loop(0, 2 * blocks, first_step, 0)
    scan.begin()
    wo_in[0].start()
    cot_row[1].start()
    for src, dst in ((k, k_h), (v, v_h), (cum, cum_h), (dpre, dpre_h), (rank, rank_h), (sin, sin_h)):
        store(src, dst)

    def second_step(i, _):
        h, b = i // blocks, i % blocks
        at = pl.ds(pl.multiple_of(b * BLOCK, BLOCK), BLOCK)

        @pl.when(i == blocks)
        def _():
            for piece in qs_in:
                piece[1].wait_recv()

        for n in range(min(len(bits), 3)):

            @pl.when(i == 2 + 3 * n)
            def _():
                scan.advance()

        @pl.when(i == 2 * blocks - 1)
        def _():
            wo_in[0].wait_recv()
            wo_in[1].start()

        proj = dot(rows[at, :], w[h, :, kv:])
        q_low = proj[:, :dk].astype(BF16)
        q[h, at, :] = q_low
        sw[h, at, :] = proj[:, dk:]
        for j in range(per):
            part = slice(j * CHUNK, (j + 1) * CHUNK)
            c = b * per + j
            this = pl.ds(pl.multiple_of(c * CHUNK, CHUNK), CHUNK)
            ch = cum[h, this, :]
            mid_row = ch[HALF - 1 : HALF]
            qf = q_low[part].astype(F32) * scale
            kf = k[h, this, :].astype(F32)
            qd = (qf * jnp.exp(ch - mid_row)).astype(BF16)
            kd = (kf * jnp.exp(mid_row - ch)).astype(BF16)
            qi = (qf * jnp.exp(ch)).astype(BF16)
            scores = jnp.where(mask, dot_nt(qd, kd), 0.0).astype(BF16)
            mx[h, this, :] = dot(scores, v[h, this, :]) + dot_nt(qi, sin[h, c])
            reach[h, this, :] = (qf * jnp.exp(ch + off_o[h, c])).astype(BF16)
        return 0

    lax.fori_loop(0, 2 * blocks, second_step, 0)
    for src, dst in ((q, q_h), (sw, s_h), (reach, reach_h), (w, w_h)):
        store(src, dst)
    while scan.advance():
        pass
    for h in range(2):
        enter_o[h] = restart * pre_s[h]
    wo_in[1].wait_recv()
    store(wo, wo2_h)

    def gate_step(i, _):
        b = jnp.where(i < 2, 2 - 2 * where.core + i, 2 * where.core + i - 2)
        at = pl.ds(pl.multiple_of(b * blk, blk), blk)
        total = None
        for h in range(2):
            mixed = mx[h, at, :] + dot_nt(reach[h, at, :], enter_o[h].astype(BF16))
            inv = lax.rsqrt(jnp.mean(mixed * mixed, axis=-1, keepdims=True) + GROUP_EPS)
            s = sw[h, at, :]
            g = (mixed * inv * gain * (s * jax.nn.sigmoid(s))).astype(BF16)
            mx[h, at, :] = mixed
            gated[h, at, :] = g
            part = dot(g, wo[h])
            total = part if total is None else total + part
        for j in range(2):

            @pl.when(i == j)
            def _():
                tb[j] = total.astype(BF16)
                terms[j].start()

            @pl.when(i == 2 + j)
            def _():
                mid[pl.ds(j * blk, blk), :] = tok[pl.ds(j * blk, blk), :].astype(F32) + total

        return 0

    lax.fori_loop(0, 4, gate_step, 0)
    for i in range(2):
        cot_row[i].wait_recv()
        cot_both[i].start()
    for src, dst in ((mx, mx_h), (gated, gated_h)):
        store(src, dst)
    for j in range(2):
        at = pl.ds(j * blk, blk)
        terms[j].wait_recv()
        mid[at, :] += tr[j].astype(F32)
    store(mid, mid_h)
    cot_core.wait_recv()
    for copy in cot_both:
        copy.wait_recv()
    for copy in stores:
        copy.wait()
    wires.drain()


def front_phase(tokens, cotangent, kw, vw, qw, sw, wo, rd, ru, row):
    bits = wide_bits()
    half, d = tokens.shape
    count = 2 * half
    dk, dv, rk = kw.shape[1], vw.shape[1], rd.shape[0]
    chunks, n_bits = count // CHUNK, len(bits)
    hbm = pl.BlockSpec(memory_space=pltpu.HBM)
    vmem = pl.BlockSpec(memory_space=pltpu.VMEM)
    dma = pltpu.SemaphoreType.DMA
    v_ = pltpu.VMEM
    out_shape = [
        sds((half, d), F32), sds((count, d), BF16), sds((2, count, dk), BF16), sds((2, count, dk), BF16),
        sds((2, count, dv), BF16), sds((2, count, dv), F32), sds((2, count, dk), F32), sds((2, count, dk), F32),
        sds((count, rk), F32), sds((2, count, dk), BF16), sds((2, chunks, dv, dk), BF16), sds((2, count, dv), F32),
        sds((2, count, dv), BF16), sds((2, d, 2 * dk + 2 * dv), BF16), sds((2, dv, d), BF16),
        sds((half, d), BF16), sds((half, d), BF16), sds((half, d), BF16),
        sds((2, chunks, 1, dk), F32), sds((2, dv, dk), F32), sds((2, 1, dk), F32),
    ]
    scratch = [
        v_((half, d), BF16), v_((count, d), BF16), v_((2, d, 2 * dk + 2 * dv), BF16), v_((2, dv, d), BF16),
        v_((2, count, dk), BF16), v_((2, count, dk), BF16), v_((2, count, dv), BF16), v_((2, count, dv), F32),
        v_((2, count, dk), F32), v_((2, count, dk), F32), v_((count, rk), F32), v_((2, count, dk), BF16),
        v_((2, chunks, dv, dk), BF16), v_((2, count, dv), F32), v_((2, count, dv), BF16),
        v_((2, half // 2, d), BF16), v_((2, half // 2, d), BF16), v_((half, d), F32), v_((dv, dk), F32), v_((1, dk), F32),
        v_((2, dv, dk), F32), v_((2, 1, dk), F32), v_((2, dv, dk), F32), v_((2, 1, dk), F32),
        v_((n_bits + 1, 2, dv + 16, dk), BF16), v_((n_bits + 1, 2, dv + 16, dk), BF16),
        dma((8,)), dma((32,)), dma((32,)), dma((20,)),
    ]
    return pl.pallas_call(
        functools.partial(front_phase_kernel, bits),
        name="front_phase",
        in_specs=[hbm] * 7 + [vmem] * 3,
        out_specs=[hbm] * 18 + [vmem] * 3,
        out_shape=out_shape,
        scratch_shapes=scratch,
        compiler_params=pltpu.CompilerParams(collective_id=3, has_side_effects=True, vmem_limit_bytes=60 << 20),
        cost_estimate=cost(12e9, 60e6, 1e6),
    )(tokens, cotangent, kw, vw, qw, sw, wo, rd, ru, row)


def tile_of(step):
    return jnp.where((step == 5) | (step == 6), 11 - step, step)


def mlp_phase_kernel(
    bits,
    mid_h, c0_h, c1_h, c2_h, c3_h, wg_h, wu_h, wd_h, row_ref,
    gmid_h, gm_h, part_ref, gg_h, gu_h, gd_h, near_h, far_h,
    mid, xs, cs, wg, wu, wd, hs, ggs, gus, gn, rc, rd, ac, ry, dn, dnr, gmb, sum_g, sum_u, sum_d, got_g, got_u,
    load_sem, send_sem, recv_sem, out_sem,
):
    tile = xs.shape[0] // 8
    rows = 2 * tile
    d = xs.shape[1]

    def rows_of(t):
        return lanes_at(t * tile, tile)

    where = Places(2 ** len(bits))
    wires = Wires(send_sem, recv_sem)
    by_core, by_row = where.by_core, where.by_row

    loads = [pltpu.make_async_copy(mid_h, mid, load_sem.at[0])]
    for i, (src, dst) in enumerate(((wg_h, wg), (wu_h, wu), (wd_h, wd))):
        loads.append(pltpu.make_async_copy(src, dst, load_sem.at[1 + i]))
    for i, src in enumerate((c0_h, c1_h, c2_h, c3_h)):
        for j in range(2):
            loads.append(
                pltpu.make_async_copy(src.at[pl.ds(j * tile, tile)], cs.at[rows_of(2 * i + j)], load_sem.at[4 + 2 * i + j])
            )
    for load in loads:
        load.start()
    stores = []

    def store(src, dst):
        copy = pltpu.make_async_copy(src, dst, out_sem.at[len(stores)])
        stores.append(copy)
        copy.start()

    where.meet()
    x_row = [wires.copy(xs.at[rows_of(j)], xs.at[rows_of(4 + j)], by_row) for j in range(2)]
    x_core = [wires.copy(xs.at[rows_of(j)], xs.at[rows_of(2 + j)], by_core) for j in range(2)]
    x_both = [wires.copy(xs.at[rows_of(4 + j)], xs.at[rows_of(6 + j)], by_core) for j in range(2)]
    g_near = [wires.copy(gn.at[2 + j], rc.at[j], by_core) for j in range(2)]
    g_far = [wires.copy(gn.at[6 + j], rd.at[j], by_core) for j in range(2)]
    g_row = [wires.copy(ac.at[j], ry.at[j], by_row) for j in range(2)]
    d_in = [wires.copy(dn.at[(2, 3, 6, 7)[j]], dnr.at[j], by_core) for j in range(4)]
    left = sorted(bits, reverse=True)

    def first_hop(total, got, bit):
        dim, mine = left.index(bit), where.has(bit)
        mids = (slice(None),) * (dim - 1)
        copies = [
            wires.copy(total.at[(top,) + mids + (1 - mine,)], got.at[top], where.across(bit)) for top in range(2)
        ]

        def finish():
            for copy in copies:
                copy.wait_recv()
            for at in itertools.product(range(2), repeat=len(bits) - 1):
                own = at[:dim] + (mine,) + at[dim:]
                got[at] = (got[at].astype(F32) + total[own].astype(F32)).astype(BF16)

        return copies, finish

    hop_g, end_g = first_hop(sum_g, got_g, bits[0])
    hop_u, end_u = first_hop(sum_u, got_u, bits[1])
    gain = row_ref[:, d : 2 * d]

    loads[0].wait()
    for j in range(2):
        m = mid[pl.ds(j * tile, tile), :]
        inv = lax.rsqrt(jnp.mean(m * m, axis=-1, keepdims=True) + NORM_EPS)
        xs[rows_of(j), :] = (m * inv * gain).astype(BF16)
        x_row[j].start()
        x_core[j].start()
    for load in loads[1:]:
        load.wait()

    def step(s, _):
        t = tile_of(s)
        at = rows_of(t)

        @pl.when(s == 2)
        def _():
            x_core[0].wait_recv()

        @pl.when(s == 3)
        def _():
            x_core[1].wait_recv()

        for j in range(2):

            @pl.when(s == 4 + 2 * j)
            def _():
                x_row[j].wait_recv()
                x_both[j].start()

            @pl.when(s == 5 + 2 * j)
            def _():
                x_both[j].wait_recv()

        x = xs[at, :]
        gate = dot_nt(x, wg[...])
        up = dot_nt(x, wu[...])
        gh = dot_nt(cs[at, :], wd[...])
        sig = jax.nn.sigmoid(gate)
        act = gate * sig
        hidden = (act * up).astype(BF16)
        g_up = (gh * act).astype(BF16)
        g_gate = (gh * up * sig * (1.0 + gate * (1.0 - sig))).astype(BF16)
        hs[at, :] = hidden
        ggs[at, :] = g_gate
        gus[at, :] = g_up
        gn[t] = (dot(g_gate, wg[...]) + dot(g_up, wu[...])).astype(BF16)

        for j in range(2):

            @pl.when(s == 2 + j)
            def _():
                g_near[j].start()

            @pl.when(s == 5 + 2 * j)
            def _():
                g_far[j].start()

        dn[t] = dot(hidden, wd[...]).astype(BF16)

        for j in range(2):

            @pl.when(s == 5 + 2 * j)
            def _():
                g_far[j].wait_recv()
                ac[j] = (gn[4 + j].astype(F32) + rd[j].astype(F32)).astype(BF16)
                g_row[j].start()

        return 0

    lax.fori_loop(0, 8, step, 0)
    for copy in d_in:
        copy.start()

    size = 256
    count = d // size

    def weight_grad(lefts, rights, total, copies):
        def step(j, _):
            cols = lanes_at(j * size, size)
            acc = dot_tn(lefts[:, cols], rights[...])
            put_rows(total, (), j, size, bits, slice(None), acc.astype(BF16))
            for top, copy in enumerate(copies):

                @pl.when(j == (top + 1) * count // 2 - 1)
                def _():
                    copy.start()

            return 0

        lax.fori_loop(0, count, step, 0)

    part = jnp.zeros((1, d), F32)

    def final(j, part):
        at = pl.ds(j * tile, tile)
        g_near[j].wait_recv()
        g_row[j].wait_recv()
        grad = gn[j].astype(F32) + rc[j].astype(F32) + ry[j].astype(F32)
        m = mid[at, :]
        inv = lax.rsqrt(jnp.mean(m * m, axis=-1, keepdims=True) + NORM_EPS)
        unit = m * inv
        weighted = grad * gain
        part = part + jnp.sum(grad * unit, axis=0, keepdims=True)
        gmid = cs[rows_of(j), :].astype(F32) + inv * (weighted - unit * jnp.mean(weighted * unit, axis=-1, keepdims=True))
        mid[at, :] = gmid
        gmb[j] = gmid.astype(BF16)
        there = gm_h.at[lanes_at(where.core * rows + j * tile, tile)]
        store(gmb.at[j], there)
        store(mid.at[at], gmid_h.at[at])
        gm_out[j].start()
        return part

    gm_out = []
    for j in range(2):
        there = gm_h.at[lanes_at(where.core * rows + j * tile, tile)]
        gm_out.append(wires.copy(gmb.at[j], there, by_core))

    weight_grad(xs, ggs, sum_g, hop_g)
    weight_grad(xs, gus, sum_u, hop_u)
    part = final(0, part)
    weight_grad(cs, hs, sum_d, [])
    store(sum_d, gd_h)
    for j in range(2):
        d_in[j].wait_recv()
        d_in[2 + j].wait_recv()
        for at, extra, out in ((j, j, near_h), (4 + j, 2 + j, far_h)):
            dn[at] = (dn[at].astype(F32) + dnr[extra].astype(F32)).astype(BF16)
            store(dn.at[at], out.at[pl.ds(j * tile, tile)])
    end_g()
    store(got_g, gg_h)
    part_ref[...] = final(1, part)
    end_u()
    store(got_u, gu_h)
    for copy in gm_out:
        copy.wait_recv()
    for copy in stores:
        copy.wait()
    wires.drain()


def mlp_phase(middle, cots, wg_t, wu_t, wd, row):
    bits = wide_bits()
    rows, d = middle.shape
    ff = wd.shape[0]
    tile = rows // 2
    hbm = pl.BlockSpec(memory_space=pltpu.HBM)
    vmem = pl.BlockSpec(memory_space=pltpu.VMEM)
    dma = pltpu.SemaphoreType.DMA
    v_ = pltpu.VMEM
    block = (d // 2 ** len(bits), ff)
    full, part = (2,) * len(bits) + block, (2,) * (len(bits) - 1) + block
    return pl.pallas_call(
        functools.partial(mlp_phase_kernel, bits),
        name="mlp_phase",
        in_specs=[hbm] * 8 + [vmem],
        out_specs=[hbm, hbm, vmem] + [hbm] * 5,
        out_shape=[sds((rows, d), F32), sds((2 * rows, d), BF16), sds((1, d), F32)]
        + [sds(part, BF16), sds(part, BF16), sds(full, BF16)] + [sds((rows, d), BF16)] * 2,
        scratch_shapes=[
            v_((rows, d), F32), v_((8 * tile, d), BF16), v_((8 * tile, d), BF16),
            v_((ff, d), BF16), v_((ff, d), BF16), v_((ff, d), BF16),
            v_((8 * tile, ff), BF16), v_((8 * tile, ff), BF16), v_((8 * tile, ff), BF16),
            v_((8, tile, d), BF16), v_((2, tile, d), BF16), v_((2, tile, d), BF16),
            v_((2, tile, d), BF16), v_((2, tile, d), BF16), v_((8, tile, d), BF16), v_((4, tile, d), BF16),
            v_((2, tile, d), BF16), v_(full, BF16), v_(full, BF16), v_(full, BF16), v_(part, BF16), v_(part, BF16),
            dma((12,)), dma((24,)), dma((24,)), dma((12,)),
        ],
        compiler_params=pltpu.CompilerParams(collective_id=1, has_side_effects=True, vmem_limit_bytes=63 << 20),
        cost_estimate=cost(18 * 4 * rows * d * ff, 60e6, 4 * rows * ff),
    )(middle, *cots, wg_t, wu_t, wd, row)


def back_phase_kernel(
    bits,
    gm_h, mx_h, s_h, r_h, gt_h, rows_h, q_h, k_h, v_h, cum_h, dpre_h, rank_h, sin_h, w_h, wo_h, g_h, gmid_h, tok_h, far_h,
    off_ref, enter_ref, mult_ref, ru_ref, rd_ref, row_ref, mpart_ref,
    in_h, fr_h, gate_o, up_o, down_o, wout_o, k_o, v_o, q_o, s_o, rdown_o, rup_o, bias_o, mgain_o, group_o, ngain_o,
    gm, mx, sw, reach, gated, rows, q, k, v, cum, dpre, rank, sin, w, wo, held, mrecv, gmid, tok,
    gx, al, grank, ds, lb_m, pre_s, pre_m, sc_out, sc_in, osv, osy, osr, kva, kvay, kvar, kvb, kvbr, kvbo, tb, tr,
    sm, smf, smv, smr, smo, ng, ngr,
    load_sem, send_sem, recv_sem, out_sem,
):
    count, d = rows.shape
    half = count // 2
    dk, dv = q.shape[2], v.shape[2]
    where = Places(2 ** len(bits))
    wires = Wires(send_sem, recv_sem)
    loads = []

    def load(src, dst):
        copy = pltpu.make_async_copy(src, dst, load_sem.at[len(loads)])
        loads.append(copy)
        copy.start()
        return copy

    orders = (bits[1:], bits[:1] + bits[2:], bits)
    third = [load(g_h[0], held[0]), load(g_h[1], held[1])]
    first = [load(gm_h, gm), load(wo_h, wo), load(mx_h, mx), load(s_h, sw), load(r_h, reach)]
    second = [load(gt_h, gated), load(rows_h, rows)]
    dim = sorted(bits, reverse=True).index(bits[0])
    keep = load(g_h[2].at[(slice(None),) * dim + (where.has(bits[0]),)], held[2])
    fourth = [load(rank_h, rank)]
    for src, dst in ((q_h, q), (k_h, k), (v_h, v), (cum_h, cum), (dpre_h, dpre), (sin_h, sin), (w_h, w)):
        fourth.append(load(src, dst))
    fifth = [load(gmid_h, gmid), load(tok_h, tok)]

    where.meet()
    mlp = [
        Scatter(where, wires, held[0], None, orders[0], mrecv[0]),
        Scatter(where, wires, held[1], None, orders[1], mrecv[1]),
        Scatter(where, wires, g_h[2], held[2], orders[2], mrecv[2]),
    ]
    scan = Scan(where, wires, ds, lb_m, pre_s, pre_m, sc_out, sc_in, True)
    os_y = wires.copy(osv.at[1], osy, where.by_row)
    os_s = Scatter(where, wires, osv.at[0], None, bits, osr)
    kva_y = wires.copy(kva.at[1], kvay, where.by_row)
    kva_s = Scatter(where, wires, kva.at[0], None, bits, kvar)
    kvb_s = [Scatter(where, wires, kvb.at[h], None, bits, kvbr[h]) for h in range(2)]
    kvb_y = wires.copy(kvbo.at[0], kvbo.at[1], where.by_row)
    tots = [wires.copy(tb.at[j], tr.at[j], where.by_core) for j in range(2)]
    far = []
    for j in range(2):
        at = pl.ds(j * (half // 2), half // 2)
        far.append(wires.copy(far_h.at[at], fr_h.at[at], where.by_row))
    every = Shared(where, wires, sm, smf, smv, smr, smo)
    every_n = Everywhere(where, wires, ng, ngr)
    n_bits = len(bits)
    at_row = row_places(d, dv, 4 * dk)
    ngain = row_ref[:, at_row[0] : at_row[1]]
    gain = row_ref[:, at_row[2] : at_row[3]]
    restart = row_ref[:, at_row[4] : at_row[4] + dk]
    far[0].start()
    for copy in third:
        copy.wait()
    mlp[1].go()
    mlp[0].go()

    blk = half // 2
    ds[...] = jnp.zeros_like(ds)
    sm[...] = jnp.zeros_like(sm)
    for copy in first:
        copy.wait()

    def gate_step(i, part):
        at = pl.ds(pl.multiple_of(i * blk, blk), blk)
        g = gm[at, :]
        for h in range(2):
            grad = dot_nt(g, wo[h])
            mixed = mx[h, at, :]
            inv = lax.rsqrt(jnp.mean(mixed * mixed, axis=-1, keepdims=True) + GROUP_EPS)
            unit = mixed * inv
            s = sw[h, at, :]
            sig = jax.nn.sigmoid(s)
            al[h, at, 2 * dk + dv :] = (grad * unit * gain * (sig * (1.0 + s * (1.0 - sig)))).astype(BF16)
            dn = grad * (s * sig)
            part = part + jnp.sum(dn * unit, axis=0, keepdims=True)
            weighted = dn * gain
            gmix = (inv * (weighted - unit * jnp.mean(weighted * unit, axis=-1, keepdims=True))).astype(BF16)
            gx[h, at, :] = gmix
            ds[h] += dot_tn(gmix, reach[h, at, :])
        return part

    group_part = lax.fori_loop(0, 4, gate_step, jnp.zeros((1, dv), F32))
    for h in range(2):
        ds[h] = ds[h] * restart
        lb_m[h] = mult_ref[h]
    scan.begin()

    size = 256

    def out_step(j, _):
        cols = pl.ds(pl.multiple_of(j * size, size), size)
        for h in (1, 0):
            value = dot_tn(gm[:, cols], gated[h]).astype(BF16)
            put_rows(osv, (h,), j, size, bits, slice(0, dv), value)
        return 0

    def swish_step(j, _):
        cols = pl.ds(pl.multiple_of(j * size, size), size)
        for h in (1, 0):
            value = dot_tn(rows[:, cols], al[h, :, 2 * dk + dv :]).astype(BF16)
            put_rows(osv, (h,), j, size, bits, slice(dv, 2 * dv), value)
        return 0

    for copy in second:
        copy.wait()
    lax.fori_loop(0, d // size, out_step, 0)
    lax.fori_loop(0, d // size, swish_step, 0)
    scan.advance()
    os_y.start()
    scan.advance()
    keep.wait()
    mlp[2].go()
    while scan.advance():
        pass
    mlp[0].advance()
    mlp[1].advance()
    for copy in fourth:
        copy.wait()

    ds[...] = pre_s[...]
    chunks = count // CHUNK
    mask = triangle(True)
    ones = triangle(False).astype(F32)
    scale = dk**-0.5
    rk = rank.shape[1]

    def add_row(ref, extra):
        for at in itertools.product(range(2), repeat=n_bits):
            ref[(0,) + at] = (ref[(0,) + at].astype(F32) + extra[at].astype(F32)).astype(BF16)

    def back_step(step, carry):
        c = chunks - 1 - step

        @pl.when(step == chunks // 2)
        def _():
            mlp[2].advance()

        @pl.when(step == chunks - 3)
        def _():
            os_y.wait_recv()
            add_row(osv, osy)
            os_s.go()

        at = pl.ds(pl.multiple_of(c * CHUNK, CHUNK), CHUNK)
        grs, new = None, []
        for h in range(2):
            ch = cum[h, at, :]
            mid = ch[HALF - 1 : HALF]
            end = ch[CHUNK - 1 :]
            e_qd, e_kd, e_qi, e_ke = jnp.exp(ch - mid), jnp.exp(mid - ch), jnp.exp(ch), jnp.exp(end - ch)
            e_end = jnp.exp(end)
            qf = q[h, at, :].astype(F32) * scale
            kf = k[h, at, :].astype(F32)
            vc = v[h, at, :]
            qd = (qf * e_qd).astype(BF16)
            kd = (kf * e_kd).astype(BF16)
            qi = (qf * e_qi).astype(BF16)
            ke = (kf * e_ke).astype(BF16)
            go = gx[h, at, :]
            ru = ru_ref[:, lanes_at(((where.place + 2 * h) % 4) * dk, dk)].astype(F32)
            state = sin[h, c].astype(F32) + enter_ref[h] * jnp.exp(off_ref[h, c])
            state_low = state.astype(BF16)
            dstate = ds[h]
            dstate_low = dstate.astype(BF16)
            scores = jnp.where(mask, dot_nt(qd, kd), 0.0).astype(BF16)
            dscores = jnp.where(mask, dot_nt(go, vc), 0.0).astype(BF16)
            d_v = dot_tn(scores, go) + dot_nt(ke, dstate_low)
            d_qd = dot(dscores, kd)
            d_qi = dot(go, state_low)
            d_kd = dot_tn(dscores, qd)
            d_ke = dot(vc, dstate_low)
            d_q = scale * (d_qd * e_qd + d_qi * e_qi)
            d_k = d_kd * e_kd + d_ke * e_ke
            tail = ke.astype(F32) * d_ke
            d_cum = qd.astype(F32) * d_qd + qi.astype(F32) * d_qi - kd.astype(F32) * d_kd - tail
            d_end = jnp.sum(tail, axis=0, keepdims=True) + e_end * jnp.sum(dstate * state, axis=0, keepdims=True)
            grad_decay = exact(ones, d_cum, ((1,), (0,))) + d_end
            g_pre = grad_decay * jax.nn.sigmoid(-dpre[h, at, :]) * (1.0 / GATE_NORM)
            al[h, at, :dk] = d_k.astype(BF16)
            al[h, at, dk : dk + dv] = d_v.astype(BF16)
            al[h, at, dk + dv : 2 * dk + dv] = d_q.astype(BF16)
            gr = exact(g_pre, ru, ((1,), (1,)))
            grs = gr if grs is None else grs + gr
            new.append(carry[2 * h] + exact(rank[at, :], g_pre, ((0,), (0,))))
            new.append(carry[2 * h + 1] + jnp.sum(g_pre, axis=0, keepdims=True))
            ds[h] = dstate * e_end + dot_tn(go, qi)
        grank[at, :] = grs.astype(BF16)
        return tuple(new)

    zero = (jnp.zeros((rk, dk), F32), jnp.zeros((1, dk), F32))
    rup0, gb0, rup1, gb1 = lax.fori_loop(0, chunks, back_step, zero + zero)
    def kvq_step(ref, h, low):
        def step(j, _):
            cols = lanes_at(j * size, size)
            value = dot_tn(rows[:, cols], al[h, :, low : low + size]).astype(BF16)
            put_rows(ref, (h,), j, size, bits, slice(None), value)
            return 0

        lax.fori_loop(0, d // size, step, 0)

    kvq_step(kva, 1, 0)
    kva_y.start()
    for h in range(2):
        kvq_step(kvb, h, size)
        kvb_s[h].go()
    mlp[2].advance()
    os_s.advance()

    def total_step(i, _):
        b = jnp.where(i < 2, 2 - 2 * where.core + i, 2 * where.core + i - 2)
        at = pl.ds(pl.multiple_of(b * blk, blk), blk)
        total = dot_nt(al[0, at, :], w[0]) + dot_nt(al[1, at, :], w[1]) + dot(grank[at, :], rd_ref[...])
        for j in range(2):

            @pl.when(i == j)
            def _():
                tb[j] = total.astype(BF16)
                tots[j].start()

            @pl.when(i == 2 + j)
            def _():
                tb[2 + j] = total.astype(BF16)

        return 0

    lax.fori_loop(0, 4, total_step, 0)

    qk = 4 * dk
    sm[0] = dot_tn(grank[...], rows[...])
    at0 = where.place * dk
    at1 = ((where.place + 2) % 4) * dk
    sm[1, :, lanes_at(at0, dk)] = rup0
    sm[1, :, lanes_at(at1, dk)] = rup1
    sm[1, 0:1, lanes_at(qk + at0, dk)] = gb0
    sm[1, 0:1, lanes_at(qk + at1, dk)] = gb1
    sm[1, 1:2, qk : qk + dv] = group_part
    for i in range(d // qk):
        sm[1, 2 + i : 3 + i, qk : 2 * qk] = mpart_ref[:, i * qk : (i + 1) * qk]
    every.begin()
    kvq_step(kva, 0, 0)
    every.advance()

    for copy in fifth:
        copy.wait()
    part = jnp.zeros((1, d), F32)
    for j in range(2):
        at = pl.ds(j * blk, blk)
        tots[j].wait_recv()
        grad = tb[2 + j].astype(F32) + tr[j].astype(F32)
        x = tok[at, :].astype(F32)
        inv = lax.rsqrt(jnp.mean(x * x, axis=-1, keepdims=True) + NORM_EPS)
        unit = x * inv
        weighted = grad * ngain
        part = part + jnp.sum(grad * unit, axis=0, keepdims=True)
        gmid[at, :] = gmid[at, :] + inv * (weighted - unit * jnp.mean(weighted * unit, axis=-1, keepdims=True))
    done = pltpu.make_async_copy(gmid, in_h, out_sem.at[0])
    done.start()
    for i in range(8):
        ng[0, i : i + 1, :] = part[:, i * (d // 8) : (i + 1) * (d // 8)]
    every_n.begin()

    kva_y.wait_recv()
    far[1].start()
    add_row(kva, kvay)
    kva_s.go()
    for part in kvb_s:
        part.advance()
    os_s.advance()
    every.advance()
    every_n.advance()
    for i, out in ((0, gate_o), (1, up_o)):
        out[...] = jnp.transpose(mlp[i].result())
    for i in range(n_bits - 1):
        kva_s.advance()
        if i < n_bits - 2:
            for part in kvb_s:
                part.advance()
        every.advance()
        every_n.advance()
    kvbo[0] = kvb_s[1].result().astype(BF16)
    kvb_y.start()
    down_o[...] = jnp.transpose(mlp[2].result())
    total = os_s.result()
    wout_o[...] = jnp.transpose(total[:, :dv])
    s_o[...] = total[:, dv:]
    every.advance()
    every_n.advance()
    first_half = kva_s.result()
    last_half = kvb_s[0].result()
    kvb_y.wait_recv()
    last_half = last_half + kvbo[1].astype(F32)
    k_o[...] = first_half[:, :dk]
    v_o[:, : size - dk] = first_half[:, dk:]
    v_o[:, size - dk :] = last_half[:, : dk + dv - size]
    q_o[...] = last_half[:, dk + dv - size :]
    small = every.result()
    rdown_o[...] = small[0]
    rup_o[...] = small[1, :, :qk]
    bias_o[...] = small[1, 0:1, qk : 2 * qk]
    group_o[...] = small[1, 1:2, qk : qk + dv]
    for i in range(d // qk):
        mgain_o[:, i * qk : (i + 1) * qk] = small[1, 2 + i : 3 + i, qk : 2 * qk]
    whole_n = every_n.result()
    for i in range(8):
        ngain_o[:, i * (d // 8) : (i + 1) * (d // 8)] = whole_n[i : i + 1, :]
    for copy in far:
        copy.wait_recv()
    done.wait()
    wires.drain()


def back_phase(
    gm, mx, s, reach, gated, rows, q, k, v, cum, dpre, rank, sin, w, wo, grads, gmid, tokens, far,
    off, enter, mult, ru, rd, row, mpart,
):
    bits = wide_bits()
    count, d = rows.shape
    half = count // 2
    dk, dv, rk = q.shape[2], v.shape[2], rank.shape[1]
    ff = grads[0].shape[-1]
    each = d // 2 ** len(bits)
    n_bits, chunks = len(bits), count // CHUNK
    hbm = pl.BlockSpec(memory_space=pltpu.HBM)
    vmem = pl.BlockSpec(memory_space=pltpu.VMEM)
    dma = pltpu.SemaphoreType.DMA
    v_ = pltpu.VMEM

    def shape(lead, cols):
        return (2,) * lead + (each, cols)

    def falls(cols):
        return [v_(shape(n_bits - 1 - i, cols), BF16) for i in range(n_bits)]

    pair, three = [hbm] * 2, [hbm] * 3
    kvq = 2 * dk + dv
    scratch = [
        v_((count, d), BF16), v_((2, count, dv), F32), v_((2, count, dv), F32), v_((2, count, dk), BF16),
        v_((2, count, dv), BF16), v_((count, d), BF16), v_((2, count, dk), BF16), v_((2, count, dk), BF16),
        v_((2, count, dv), BF16), v_((2, count, dk), F32), v_((2, count, dk), F32), v_((count, rk), F32),
        v_((2, chunks, dv, dk), BF16), v_((2, d, kvq + dv), BF16), v_((2, dv, d), BF16),
        [v_(shape(n_bits - 1, ff), BF16)] * 3, [falls(ff)[1:], falls(ff)[1:], falls(ff)], v_((half, d), F32), v_((half, d), BF16),
        v_((2, count, dv), BF16), v_((2, count, kvq + dv), BF16), v_((count, rk), BF16),
        v_((2, dv, dk), F32), v_((2, 1, dk), F32), v_((2, dv, dk), F32), v_((2, 1, dk), F32),
        v_((n_bits + 1, 2, dv + 16, dk), BF16), v_((n_bits + 1, 2, dv + 16, dk), BF16),
        v_((2,) + shape(n_bits, 2 * dv), BF16), v_(shape(n_bits, 2 * dv), BF16), falls(2 * dv),
        v_((2,) + shape(n_bits, 256), BF16), v_(shape(n_bits, 256), BF16), falls(256),
        v_((2,) + shape(n_bits, 256), BF16), [falls(256), falls(256)], v_((2, each, 256), BF16),
        v_((4, half // 2, d), BF16), v_((2, half // 2, d), BF16),
        v_((2, rk, d), F32), v_((rk, d), F32), v_((n_bits + 1, rk, d), F32), v_((n_bits + 1, rk, d), F32), v_((2, rk, d), F32),
        v_((n_bits + 3, 8, d // 8), F32), v_((n_bits + 2, 8, d // 8), F32),
        dma((24,)), dma((80,)), dma((80,)), dma((1,)),
    ]
    out_shape = [
        sds((half, d), F32), sds((half, d), BF16), sds((ff, each), F32), sds((ff, each), F32), sds((ff, each), F32), sds((dv, each), F32),
        sds((each, dk), F32), sds((each, dv), F32), sds((each, dk), F32), sds((each, dv), F32),
        sds((rk, d), F32), sds((rk, 4 * dk), F32), sds((1, 4 * dk), F32), sds((1, d), F32), sds((1, dv), F32), sds((1, d), F32),
    ]
    operands = (
        gm, mx, s, reach, gated, rows, q, k, v, cum, dpre, rank, sin, w, wo, grads, gmid, tokens, far,
        off, enter, mult, ru, rd, row, mpart,
    )
    flat, tree = jax.tree.flatten(operands)
    n_vmem = len(jax.tree.leaves(operands[19:]))
    flat_scratch, scratch_tree = jax.tree.flatten(scratch, is_leaf=lambda x: not isinstance(x, list))
    n_in, n_out = len(flat), len(out_shape)

    def kernel(*refs):
        ins = jax.tree.unflatten(tree, refs[:n_in])
        rest = jax.tree.unflatten(scratch_tree, refs[n_in + n_out :])
        back_phase_kernel(bits, *ins, *refs[n_in : n_in + n_out], *rest)

    return pl.pallas_call(
        kernel,
        name="back_phase",
        in_specs=[hbm] * (n_in - n_vmem) + [vmem] * n_vmem,
        out_specs=[hbm, hbm] + [vmem] * (n_out - 2),
        out_shape=out_shape,
        scratch_shapes=flat_scratch,
        compiler_params=pltpu.CompilerParams(collective_id=2, has_side_effects=True, vmem_limit_bytes=62 << 20),
        cost_estimate=cost(40e9, 60e6, 1e6),
    )(*flat)


def finish_kernel(count, mid_ref, near_ref, far_ref, grad_ref, *refs):
    res_ref, in_ref = refs[count : count + 2]
    res_ref[...] = (mid_ref[...] + (near_ref[...].astype(F32) + far_ref[...].astype(F32))).astype(BF16)
    in_ref[...] = grad_ref[...]

    @pl.when(pl.program_id(0) == 0)
    def _():
        for src, dst in zip(refs[:count], refs[count + 2 :]):
            dst[...] = src[...]


def finish(middle, near, far, grad, smalls):
    rows, d = middle.shape
    blk = rows // 4
    row = rows_spec(blk, d)
    wholes = [pl.BlockSpec(v.shape, lambda i: (0, 0)) for v in smalls]
    return pl.pallas_call(
        functools.partial(finish_kernel, len(smalls)),
        name="finish",
        grid=(4,),
        in_specs=[row] * 4 + wholes,
        out_specs=[row] * 2 + wholes,
        out_shape=[sds((rows, d), BF16), sds((rows, d), F32)] + [sds(v.shape, v.dtype) for v in smalls],
        compiler_params=params(62),
    )(middle, near, far, grad, *smalls)


def wide_bits():
    count, bits, bit = lax.axis_size("wide"), [], 1
    while bit < count:
        bits.append(bit)
        bit *= 2
    return bits


def shards(
    tokens, cotangent, flags, norm_gain, query_weight, key_weight, value_weight, swish_weight, rank_down, rank_up,
    decay_bias, group_gain, output_weight, mlp_gain, mlp_gate, mlp_up, mlp_down,
):
    place = lax.axis_index("narrow")
    dk, dv, d = query_weight.shape[1], value_weight.shape[1], tokens.shape[1]
    restart = jnp.where((place & 2) != 0, 1.0, 1.0 - flags[0].astype(F32))
    parts = [part.astype(F32) for part in (norm_gain, mlp_gain, group_gain, decay_bias)]
    row = jnp.concatenate(parts + [jnp.full((dk,), restart, F32)]).reshape(1, -1)
    rd = rank_down.T
    (
        middle, rows_all, q, k, v, s, cum, dpre, rank_pre, reach, sin, mixed, gated, w, weights_out, cot_c, cot_y, cot_d,
        off, enter, mults,
    ) = front_phase(
        tokens, cotangent, key_weight, value_weight, query_weight, swish_weight, output_weight, rd, rank_up, row
    )
    grad_middle, gm_all, mlp_gain_part, gate_g, up_g, down_g, near, far = mlp_phase(
        middle, (cotangent, cot_c, cot_y, cot_d), mlp_gate.T, mlp_up.T, mlp_down, row
    )
    input_grad, far_sum, *smalls = back_phase(
        gm_all, mixed, s, reach, gated, rows_all, q, k, v, cum, dpre, rank_pre, sin,
        w, weights_out, (gate_g, up_g, down_g), grad_middle, tokens, far, off, enter, mults, rank_up, rd, row,
        mlp_gain_part,
    )
    result, input_grad, *smalls = finish(middle, near, far_sum, input_grad, smalls)
    gate_t, up_t, down_t, out_t, k_g, v_g, q_g, s_g, rdown_t, rup_g, bias_g, mgain_g, group_g, ngain = smalls
    return (
        result,
        input_grad,
        ngain[0],
        q_g,
        k_g,
        v_g,
        s_g,
        rdown_t.T,
        rup_g,
        bias_g[0],
        group_g[0],
        out_t,
        mgain_g[0],
        gate_t.T,
        up_t.T,
        down_t,
    )


def solution(mesh):
    rows, cols = P(("wide", "narrow"), None), P(None, "narrow")
    both = P("wide", "narrow")
    in_specs = (
        rows, rows, P("wide"), P(), cols, cols, cols, cols, P(), P(), P(), P(), P("narrow", None), P(), cols, cols,
        P("narrow", None),
    )
    out_specs = (
        rows, rows, P(), both, both, both, both, P(), P(), P(), P(), P("narrow", "wide"), P(), both, both,
        P("narrow", "wide"),
    )
    return jax.shard_map(shards, mesh=mesh, in_specs=in_specs, out_specs=out_specs, check_vma=False)
```

```python
import functools
import itertools

import jax
import jax.numpy as jnp
from jax import lax
from jax.experimental import pallas as pl
from jax.experimental.pallas import tpu as pltpu
from jax.sharding import PartitionSpec as P

NORM_EPS = 1e-06
GROUP_EPS = 1e-05
GATE_NORM = 16.0
HIGHEST_PREC = lax.Precision.HIGHEST
MESH = pl.DeviceIdType.MESH
CHUNK = 128
HALF = CHUNK // 2
BLOCK = 256
F32 = jnp.float32
BF16 = jnp.bfloat16


def dot(a, b):
    return lax.dot_general(a, b, (((1,), (0,)), ((), ())), preferred_element_type=F32)


def dot_nt(a, b):
    return lax.dot_general(a, b, (((1,), (1,)), ((), ())), preferred_element_type=F32)


def dot_tn(a, b):
    return lax.dot_general(a, b, (((0,), (0,)), ((), ())), preferred_element_type=F32)


def exact(a, b, dims):
    return lax.dot_general(
        a, b, (dims, ((), ())), precision=HIGHEST_PREC, preferred_element_type=F32
    )


def sds(shape, dtype):
    return jax.ShapeDtypeStruct(shape, dtype)


def params(mib=48):
    return pltpu.CompilerParams(vmem_limit_bytes=mib << 20)


def cost(flops, nbytes, trans=0):
    return pl.CostEstimate(flops=int(flops), bytes_accessed=int(nbytes), transcendentals=int(trans))


def whole(shape):
    return pl.BlockSpec(shape, lambda i: (0,) * len(shape), pipeline_mode=pl.Buffered(1))


def rows_spec(rows, cols):
    return pl.BlockSpec((rows, cols), lambda i: (i, 0))


def triangle(lower):
    r = lax.broadcasted_iota(jnp.int32, (CHUNK, CHUNK), 0)
    c = lax.broadcasted_iota(jnp.int32, (CHUNK, CHUNK), 1)
    return r >= c if lower else r <= c


class Wires:
    def __init__(self, send_sem, recv_sem):
        self.send_sem, self.recv_sem, self.used, self.all = send_sem, recv_sem, 0, []

    def copy(self, src, dst, target):
        made = pltpu.make_async_remote_copy(
            src,
            dst,
            self.send_sem.at[self.used],
            self.recv_sem.at[self.used],
            device_id=target,
            device_id_type=MESH,
        )
        self.used += 1
        self.all.append(made)
        return made

    def drain(self):
        for made in self.all:
            made.wait_send()


class Places:
    def __init__(self, wide_count):
        self.wide, self.place = lax.axis_index("wide"), lax.axis_index("narrow")
        self.core = self.place % 2
        self.second = self.place // 2
        self.by_core = (self.wide, self.place + 1 - 2 * self.core)
        self.by_row = (self.wide, (self.place + 2) % 4)
        self.bits = []
        bit = 1
        while bit < wide_count:
            self.bits.append(bit)
            bit *= 2

    def has(self, bit):
        return (self.wide // bit) % 2

    def across(self, bit):
        return (self.wide + bit - 2 * bit * self.has(bit), self.place)

    def meet(self):
        barrier = pltpu.get_barrier_semaphore()
        others = [self.by_core, self.by_row] + [self.across(bit) for bit in self.bits]
        for other in others:
            pl.semaphore_signal(barrier, 1, device_id=other, device_id_type=MESH)
        pl.semaphore_wait(barrier, len(others))


class Scan:
    def __init__(self, where, wires, tot_s, tot_m, pre_s, pre_m, out, into, backward):
        self.tot_s, self.tot_m, self.pre_s, self.pre_m = tot_s, tot_m, pre_s, pre_m
        self.out, self.into, self.at, self.order = out, into, 0, (0, 1)
        self.steps = []
        for i, bit in enumerate([0] + where.bits):
            target = where.across(bit) if bit else where.by_row
            is_set = where.has(bit) if bit else where.second
            later = (1 - is_set if backward else is_set) > 0
            copies = [wires.copy(out.at[i, h], into.at[i, h], target) for h in range(2)]
            self.steps.append((copies, later, bit == 0))
        pre_s[...] = jnp.zeros_like(pre_s)
        pre_m[...] = jnp.ones_like(pre_m)

    def send(self, i, h):
        dv = self.tot_s.shape[1]
        self.out[i, h, :dv, :] = self.tot_s[h].astype(BF16)
        self.out[i, h, dv:, :] = jnp.broadcast_to(self.tot_m[h], (16, self.tot_m.shape[2])).astype(BF16)
        self.steps[i][0][h].start()

    def begin(self):
        for h in range(2):
            self.send(0, h)

    def advance(self):
        i, more = self.at, self.at + 1 < len(self.steps)
        copies, later, swapped = self.steps[i]
        dv = self.tot_s.shape[1]
        heads = []
        for g in self.order:
            h = 1 - g if swapped else g
            heads.append(h)
            copies[g].wait_recv()
            oth_s = self.into[i, g, :dv, :].astype(F32)
            oth_m = self.into[i, g, dv : dv + 1, :].astype(F32)
            pre_s, pre_m, tot_s, tot_m = self.pre_s[h], self.pre_m[h], self.tot_s[h], self.tot_m[h]
            if more:
                self.tot_s[h] = jnp.where(later, oth_s * tot_m + tot_s, tot_s * oth_m + oth_s)
                self.tot_m[h] = tot_m * oth_m
                self.send(i + 1, h)
            self.pre_s[h] = jnp.where(later, oth_s * pre_m + pre_s, pre_s)
            self.pre_m[h] = jnp.where(later, oth_m * pre_m, pre_m)
        self.order = tuple(heads)
        self.at = i + 1
        return more


class Scatter:
    def __init__(self, where, wires, source, keep, order, recvs):
        self.recvs, self.steps, self.at = recvs, [], 0
        left = sorted(order, reverse=True)
        held, first = source, keep
        for bit, recv in zip(order, recvs):
            dim = left.index(bit)
            mine = where.has(bit)
            other = held.at[(slice(None),) * dim + (1 - mine,)]
            copy = wires.copy(other, recv, where.across(bit))
            self.steps.append((copy, held if first is None else first, dim, mine, first is not None))
            left.pop(dim)
            held, first = recv, None

    def go(self):
        self.steps[self.at][0].start()

    def land(self):
        total = self.finish(self.at)
        self.at += 1
        return total

    def advance(self):
        if self.at + 1 < len(self.steps):
            self.land()
            self.go()

    def result(self):
        while self.at + 1 < len(self.steps):
            self.advance()
        return self.land()

    def finish(self, i):
        copy, held, dim, mine, picked = self.steps[i]
        copy.wait_recv()
        recv = self.recvs[i]
        last = i == len(self.steps) - 1
        for at in itertools.product(range(2), repeat=len(recv.shape) - 2):
            source = at if picked else at[:dim] + (mine,) + at[dim:]
            total = recv[at].astype(F32) + held[source].astype(F32)
            if last:
                return total
            recv[at] = total.astype(BF16)
        return None


class Everywhere:
    def __init__(self, where, wires, values, recvs):
        self.values, self.recvs = values, recvs
        targets = [where.by_core, where.by_row] + [where.across(bit) for bit in where.bits]
        self.steps = [wires.copy(values.at[i], recvs.at[i], target) for i, target in enumerate(targets)]

    def begin(self, i=0):
        self.at = i
        self.steps[i].start()

    def advance(self):
        if self.at + 1 < len(self.steps):
            self.finish(self.at)
            self.begin(self.at + 1)

    def result(self):
        while self.at + 1 < len(self.steps):
            self.advance()
        self.finish(self.at)
        return self.values[len(self.steps)]

    def finish(self, i):
        self.steps[i].wait_recv()
        self.values[i + 1] = self.values[i] + self.recvs[i]


class Shared:
    def __init__(self, where, wires, parts, first, values, recvs, out):
        self.core, self.parts, self.first = where.core, parts, first
        self.values, self.recvs, self.out, self.at = values, recvs, out, 0
        targets = [where.by_row] + [where.across(bit) for bit in where.bits]
        self.steps = [wires.copy(parts.at[1 - where.core], first, where.by_core)]
        self.steps += [wires.copy(values.at[i], recvs.at[i], target) for i, target in enumerate(targets)]
        self.steps.append(wires.copy(out.at[where.core], out.at[where.core], where.by_core))

    def begin(self):
        self.steps[0].start()

    def advance(self):
        i, last = self.at, len(self.steps) - 1
        if i == last:
            return
        self.steps[i].wait_recv()
        if i == 0:
            total = self.parts[self.core] + self.first[...]
        else:
            total = self.values[i - 1] + self.recvs[i - 1]
        if i + 1 == last:
            self.out[self.core] = total
        else:
            self.values[i] = total
        self.at = i + 1
        self.steps[i + 1].start()

    def result(self):
        while self.at + 1 < len(self.steps):
            self.advance()
        self.steps[-1].wait_recv()
        return self.out


def bit_index(w, bits):
    return tuple((w // bit) % 2 for bit in sorted(bits, reverse=True))


def put_rows(ref, lead, j, size, bits, lanes, value):
    each = ref.shape[-2]
    for p in range(size // each):
        at = lead + bit_index(j * (size // each) + p, bits) + (slice(None), lanes)
        ref[at] = value[p * each : (p + 1) * each]


def lanes_at(start, size):
    return pl.ds(pl.multiple_of(start, size), size)


def row_places(d, dv, qk):
    return (0, d, 2 * d, 2 * d + dv, 2 * d + dv + qk)


def front_phase_kernel(
    bits,
    tok_h, cot_h, kw_h, vw_h, qw_h, sw_h, wo_h, rd_ref, ru_ref, row_ref,
    mid_h, rows_h, q_h, k_h, v_h, s_h, cum_h, dpre_h, rank_h, reach_h, sin_h, mx_h, gated_h, w_h, wo2_h, c1_h, c2_h, c3_h,
    off_o, enter_o, mult_o,
    tok, rows, w, wo, q, k, v, sw, cum, dpre, rank, reach, sin, mx, gated, tb, tr, mid, st, off,
    tot_s, tot_m, pre_s, pre_m, sc_out, sc_in,
    load_sem, send_sem, recv_sem, out_sem,
):
    count, d = rows.shape
    half = count // 2
    blk = half // 2
    dk, dv = q.shape[2], v.shape[2]
    kv = dk + dv
    where = Places(2 ** len(bits))
    wires = Wires(send_sem, recv_sem)
    loads, stores = [], []

    def load(src, dst):
        copy = pltpu.make_async_copy(src, dst, load_sem.at[len(loads)])
        loads.append(copy)
        copy.start()
        return copy

    def store(src, dst):
        copy = pltpu.make_async_copy(src, dst, out_sem.at[len(stores)])
        stores.append(copy)
        copy.start()

    load_tok = load(tok_h, tok)
    load_kv = [load(kw_h, w.at[0, :, pl.ds(0, dk)]), load(vw_h, w.at[0, :, pl.ds(dk, dv)])]
    load_qs = [load(qw_h, w.at[0, :, pl.ds(kv, dk)]), load(sw_h, w.at[0, :, pl.ds(kv + dk, dv)])]
    load_wo = load(wo_h, wo.at[0])

    where.meet()
    at_row = row_places(d, dv, 4 * dk)
    ngain = row_ref[:, at_row[0] : at_row[1]]
    gain = row_ref[:, at_row[2] : at_row[3]]
    restart = row_ref[:, at_row[4] : at_row[4] + dk]

    odd = where.has(1)
    over_x = where.across(1)
    quarter = d // 4

    def weight_pieces(cols):
        made = []
        for i in range(2):
            near = pl.ds(pl.multiple_of(odd * 2 * quarter + i * quarter, quarter), quarter)
            made.append(
                (
                    wires.copy(w.at[0, near, cols], w.at[1, near, cols], where.by_row),
                    wires.copy(w.at[1, near, cols], w.at[1, near, cols], over_x),
                )
            )
        return made

    kv_in = weight_pieces(pl.ds(0, kv))
    qs_in = weight_pieces(pl.ds(kv, kv))
    near = pl.ds(pl.multiple_of(odd * (dv // 2), dv // 2), dv // 2)
    wo_in = [
        wires.copy(wo.at[0, near], wo.at[1, near], where.by_row),
        wires.copy(wo.at[1, near], wo.at[1, near], over_x),
    ]
    cot_row, cot_both = [], []
    for i in range(2):
        at = pl.ds(i * blk, blk)
        cot_row.append(wires.copy(cot_h.at[at], c2_h.at[at], where.by_row))
        cot_both.append(wires.copy(c2_h.at[at], c3_h.at[at], where.by_core))
    cot_core = wires.copy(cot_h, c1_h, where.by_core)
    row_out = []
    for i in range(2):
        at = pl.ds(pl.multiple_of(where.core * half + i * blk, blk), blk)
        row_out.append(wires.copy(rows.at[at], rows.at[at], where.by_core))
    terms = [wires.copy(tb.at[j], tr.at[j], where.by_core) for j in range(2)]
    scan = Scan(where, wires, tot_s, tot_m, pre_s, pre_m, sc_out, sc_in, False)

    for copy in load_kv:
        copy.wait()
    for piece in kv_in:
        piece[0].start()
    load_tok.wait()
    for i in range(2):
        x = tok[pl.ds(i * blk, blk), :].astype(F32)
        inv = lax.rsqrt(jnp.mean(x * x, axis=-1, keepdims=True) + NORM_EPS)
        rows[pl.ds(pl.multiple_of(where.core * half + i * blk, blk), blk), :] = (x * inv * ngain).astype(BF16)
        row_out[i].start()
    for copy in load_qs:
        copy.wait()
    load_wo.wait()
    for copy in row_out:
        copy.wait_recv()
    cot_core.start()
    store(rows, rows_h)

    mask = triangle(True)
    ones = mask.astype(F32)
    scale = dk**-0.5
    blocks = count // BLOCK
    per = BLOCK // CHUNK

    def first_step(i, _):
        h, b = i // blocks, i % blocks
        at = pl.ds(pl.multiple_of(b * BLOCK, BLOCK), BLOCK)
        for p in range(2):

            @pl.when(i == blocks - 2 + p)
            def _():
                kv_in[p][0].wait_recv()
                kv_in[p][1].start()

            @pl.when(i == 2 * blocks - 2 + p)
            def _():
                qs_in[p][0].wait_recv()
                qs_in[p][1].start()

        @pl.when(i == blocks - 1)
        def _():
            for piece in qs_in:
                piece[0].start()
            cot_row[0].start()

        @pl.when(i == blocks)
        def _():
            for piece in kv_in:
                piece[1].wait_recv()

        @pl.when(b == 0)
        def _():
            st[...] = jnp.zeros_like(st)
            off[...] = jnp.zeros_like(off)

        x = rows[at, :]

        @pl.when(i < blocks)
        def _():
            rank[at, :] = dot_nt(x, rd_ref[...])

        proj = dot(x, w[h, :, :kv])
        head = (where.place + 2 * h) % 4
        ru = ru_ref[:, lanes_at(head * dk, dk)].astype(F32)
        bias = row_ref[:, lanes_at(at_row[3] + head * dk, dk)]
        pre = exact(rank[at, :], ru, ((1,), (0,))) + bias
        dlog = jax.nn.log_sigmoid(pre) * (1.0 / GATE_NORM)
        k_low = proj[:, :dk].astype(BF16)
        v_low = proj[:, dk:].astype(BF16)
        k[h, at, :] = k_low
        v[h, at, :] = v_low
        dpre[h, at, :] = pre
        for j in range(per):
            part = slice(j * CHUNK, (j + 1) * CHUNK)
            c = b * per + j
            ch = exact(ones, dlog[part], ((1,), (0,)))
            end = ch[CHUNK - 1 :]
            ke = (k_low[part].astype(F32) * jnp.exp(end - ch)).astype(BF16)
            state = st[...]
            offset = off[...]
            cum[h, pl.ds(pl.multiple_of(c * CHUNK, CHUNK), CHUNK), :] = ch
            sin[h, c] = state.astype(BF16)
            off_o[h, c] = offset
            st[...] = state * jnp.exp(end) + dot_tn(v_low[part], ke)
            off[...] = offset + end

        @pl.when(b == blocks - 1)
        def _():
            tot_s[h] = st[...]
            mult = restart * jnp.exp(off[...])
            tot_m[h] = mult
            mult_o[h] = mult

        return 0

    lax.fori_loop(0, 2 * blocks, first_step, 0)
    scan.begin()
    wo_in[0].start()
    cot_row[1].start()
    for src, dst in ((k, k_h), (v, v_h), (cum, cum_h), (dpre, dpre_h), (rank, rank_h), (sin, sin_h)):
        store(src, dst)

    def second_step(i, _):
        h, b = i // blocks, i % blocks
        at = pl.ds(pl.multiple_of(b * BLOCK, BLOCK), BLOCK)

        @pl.when(i == blocks)
        def _():
            for piece in qs_in:
                piece[1].wait_recv()

        for n in range(min(len(bits), 3)):

            @pl.when(i == 2 + 3 * n)
            def _():
                scan.advance()

        @pl.when(i == 2 * blocks - 1)
        def _():
            wo_in[0].wait_recv()
            wo_in[1].start()

        proj = dot(rows[at, :], w[h, :, kv:])
        q_low = proj[:, :dk].astype(BF16)
        q[h, at, :] = q_low
        sw[h, at, :] = proj[:, dk:]
        for j in range(per):
            part = slice(j * CHUNK, (j + 1) * CHUNK)
            c = b * per + j
            this = pl.ds(pl.multiple_of(c * CHUNK, CHUNK), CHUNK)
            ch = cum[h, this, :]
            mid_row = ch[HALF - 1 : HALF]
            qf = q_low[part].astype(F32) * scale
            kf = k[h, this, :].astype(F32)
            qd = (qf * jnp.exp(ch - mid_row)).astype(BF16)
            kd = (kf * jnp.exp(mid_row - ch)).astype(BF16)
            qi = (qf * jnp.exp(ch)).astype(BF16)
            scores = jnp.where(mask, dot_nt(qd, kd), 0.0).astype(BF16)
            mx[h, this, :] = dot(scores, v[h, this, :]) + dot_nt(qi, sin[h, c])
            reach[h, this, :] = (qf * jnp.exp(ch + off_o[h, c])).astype(BF16)
        return 0

    lax.fori_loop(0, 2 * blocks, second_step, 0)
    for src, dst in ((q, q_h), (sw, s_h), (reach, reach_h), (w, w_h)):
        store(src, dst)
    while scan.advance():
        pass
    for h in range(2):
        enter_o[h] = restart * pre_s[h]
    wo_in[1].wait_recv()
    store(wo, wo2_h)

    def gate_step(i, _):
        b = jnp.where(i < 2, 2 - 2 * where.core + i, 2 * where.core + i - 2)
        at = pl.ds(pl.multiple_of(b * blk, blk), blk)
        total = None
        for h in range(2):
            mixed = mx[h, at, :] + dot_nt(reach[h, at, :], enter_o[h].astype(BF16))
            inv = lax.rsqrt(jnp.mean(mixed * mixed, axis=-1, keepdims=True) + GROUP_EPS)
            s = sw[h, at, :]
            g = (mixed * inv * gain * (s * jax.nn.sigmoid(s))).astype(BF16)
            mx[h, at, :] = mixed
            gated[h, at, :] = g
            part = dot(g, wo[h])
            total = part if total is None else total + part
        for j in range(2):

            @pl.when(i == j)
            def _():
                tb[j] = total.astype(BF16)
                terms[j].start()

            @pl.when(i == 2 + j)
            def _():
                mid[pl.ds(j * blk, blk), :] = tok[pl.ds(j * blk, blk), :].astype(F32) + total

        return 0

    lax.fori_loop(0, 4, gate_step, 0)
    for i in range(2):
        cot_row[i].wait_recv()
        cot_both[i].start()
    for src, dst in ((mx, mx_h), (gated, gated_h)):
        store(src, dst)
    for j in range(2):
        at = pl.ds(j * blk, blk)
        terms[j].wait_recv()
        mid[at, :] += tr[j].astype(F32)
    store(mid, mid_h)
    cot_core.wait_recv()
    for copy in cot_both:
        copy.wait_recv()
    for copy in stores:
        copy.wait()
    wires.drain()


def front_phase(tokens, cotangent, kw, vw, qw, sw, wo, rd, ru, row):
    bits = wide_bits()
    half, d = tokens.shape
    count = 2 * half
    dk, dv, rk = kw.shape[1], vw.shape[1], rd.shape[0]
    chunks, n_bits = count // CHUNK, len(bits)
    hbm = pl.BlockSpec(memory_space=pltpu.HBM)
    vmem = pl.BlockSpec(memory_space=pltpu.VMEM)
    dma = pltpu.SemaphoreType.DMA
    v_ = pltpu.VMEM
    out_shape = [
        sds((half, d), F32), sds((count, d), BF16), sds((2, count, dk), BF16), sds((2, count, dk), BF16),
        sds((2, count, dv), BF16), sds((2, count, dv), F32), sds((2, count, dk), F32), sds((2, count, dk), F32),
        sds((count, rk), F32), sds((2, count, dk), BF16), sds((2, chunks, dv, dk), BF16), sds((2, count, dv), F32),
        sds((2, count, dv), BF16), sds((2, d, 2 * dk + 2 * dv), BF16), sds((2, dv, d), BF16),
        sds((half, d), BF16), sds((half, d), BF16), sds((half, d), BF16),
        sds((2, chunks, 1, dk), F32), sds((2, dv, dk), F32), sds((2, 1, dk), F32),
    ]
    scratch = [
        v_((half, d), BF16), v_((count, d), BF16), v_((2, d, 2 * dk + 2 * dv), BF16), v_((2, dv, d), BF16),
        v_((2, count, dk), BF16), v_((2, count, dk), BF16), v_((2, count, dv), BF16), v_((2, count, dv), F32),
        v_((2, count, dk), F32), v_((2, count, dk), F32), v_((count, rk), F32), v_((2, count, dk), BF16),
        v_((2, chunks, dv, dk), BF16), v_((2, count, dv), F32), v_((2, count, dv), BF16),
        v_((2, half // 2, d), BF16), v_((2, half // 2, d), BF16), v_((half, d), F32), v_((dv, dk), F32), v_((1, dk), F32),
        v_((2, dv, dk), F32), v_((2, 1, dk), F32), v_((2, dv, dk), F32), v_((2, 1, dk), F32),
        v_((n_bits + 1, 2, dv + 16, dk), BF16), v_((n_bits + 1, 2, dv + 16, dk), BF16),
        dma((8,)), dma((48,)), dma((48,)), dma((20,)),
    ]
    return pl.pallas_call(
        functools.partial(front_phase_kernel, bits),
        name="front_phase",
        in_specs=[hbm] * 7 + [vmem] * 3,
        out_specs=[hbm] * 18 + [vmem] * 3,
        out_shape=out_shape,
        scratch_shapes=scratch,
        compiler_params=pltpu.CompilerParams(collective_id=3, has_side_effects=True, vmem_limit_bytes=60 << 20),
        cost_estimate=cost(12e9, 60e6, 1e6),
    )(tokens, cotangent, kw, vw, qw, sw, wo, rd, ru, row)


def tile_of(step):
    return jnp.where((step == 5) | (step == 6), 11 - step, step)


def mlp_phase_kernel(
    bits,
    mid_h, c0_h, c1_h, c2_h, c3_h, wg_h, wu_h, wd_h, row_ref,
    gmid_h, gm_h, part_ref, gg_h, gu_h, gd_h, near_h, far_h,
    mid, xs, cs, wg, wu, wd, hs, ggs, gus, gn, rc, rd, ac, ry, dn, dnr, gmb, sum_g, sum_u, sum_d, got_g, got_u,
    load_sem, send_sem, recv_sem, out_sem,
):
    tile = xs.shape[0] // 8
    rows = 2 * tile
    d = xs.shape[1]

    def rows_of(t):
        return lanes_at(t * tile, tile)

    where = Places(2 ** len(bits))
    wires = Wires(send_sem, recv_sem)
    by_core, by_row = where.by_core, where.by_row

    loads = [pltpu.make_async_copy(mid_h, mid, load_sem.at[0])]
    for i, (src, dst) in enumerate(((wg_h, wg), (wu_h, wu), (wd_h, wd))):
        loads.append(pltpu.make_async_copy(src, dst, load_sem.at[1 + i]))
    for i, src in enumerate((c0_h, c1_h, c2_h, c3_h)):
        for j in range(2):
            loads.append(
                pltpu.make_async_copy(src.at[pl.ds(j * tile, tile)], cs.at[rows_of(2 * i + j)], load_sem.at[4 + 2 * i + j])
            )
    for load in loads:
        load.start()
    stores = []

    def store(src, dst):
        copy = pltpu.make_async_copy(src, dst, out_sem.at[len(stores)])
        stores.append(copy)
        copy.start()

    where.meet()
    x_row = [wires.copy(xs.at[rows_of(j)], xs.at[rows_of(4 + j)], by_row) for j in range(2)]
    x_core = [wires.copy(xs.at[rows_of(j)], xs.at[rows_of(2 + j)], by_core) for j in range(2)]
    x_both = [wires.copy(xs.at[rows_of(4 + j)], xs.at[rows_of(6 + j)], by_core) for j in range(2)]
    g_near = [wires.copy(gn.at[2 + j], rc.at[j], by_core) for j in range(2)]
    g_far = [wires.copy(gn.at[6 + j], rd.at[j], by_core) for j in range(2)]
    g_row = [wires.copy(ac.at[j], ry.at[j], by_row) for j in range(2)]
    d_in = [wires.copy(dn.at[(2, 3, 6, 7)[j]], dnr.at[j], by_core) for j in range(4)]
    left = sorted(bits, reverse=True)

    def first_hop(total, got, bit):
        dim, mine = left.index(bit), where.has(bit)
        mids = (slice(None),) * (dim - 1)
        copies = [
            wires.copy(total.at[(top,) + mids + (1 - mine,)], got.at[top], where.across(bit)) for top in range(2)
        ]

        def finish():
            for copy in copies:
                copy.wait_recv()
            for at in itertools.product(range(2), repeat=len(bits) - 1):
                own = at[:dim] + (mine,) + at[dim:]
                got[at] = (got[at].astype(F32) + total[own].astype(F32)).astype(BF16)

        return copies, finish

    hop_g, end_g = first_hop(sum_g, got_g, bits[0])
    hop_u, end_u = first_hop(sum_u, got_u, bits[1])
    gain = row_ref[:, d : 2 * d]

    loads[0].wait()
    for j in range(2):
        m = mid[pl.ds(j * tile, tile), :]
        inv = lax.rsqrt(jnp.mean(m * m, axis=-1, keepdims=True) + NORM_EPS)
        xs[rows_of(j), :] = (m * inv * gain).astype(BF16)
        x_row[j].start()
        x_core[j].start()
    for load in loads[1:]:
        load.wait()

    def step(s, _):
        t = tile_of(s)
        at = rows_of(t)

        @pl.when(s == 2)
        def _():
            x_core[0].wait_recv()

        @pl.when(s == 3)
        def _():
            x_core[1].wait_recv()

        for j in range(2):

            @pl.when(s == 4 + 2 * j)
            def _():
                x_row[j].wait_recv()
                x_both[j].start()

            @pl.when(s == 5 + 2 * j)
            def _():
                x_both[j].wait_recv()

        x = xs[at, :]
        gate = dot_nt(x, wg[...])
        up = dot_nt(x, wu[...])
        gh = dot_nt(cs[at, :], wd[...])
        sig = jax.nn.sigmoid(gate)
        act = gate * sig
        hidden = (act * up).astype(BF16)
        g_up = (gh * act).astype(BF16)
        g_gate = (gh * up * sig * (1.0 + gate * (1.0 - sig))).astype(BF16)
        hs[at, :] = hidden
        ggs[at, :] = g_gate
        gus[at, :] = g_up
        gn[t] = (dot(g_gate, wg[...]) + dot(g_up, wu[...])).astype(BF16)

        for j in range(2):

            @pl.when(s == 2 + j)
            def _():
                g_near[j].start()

            @pl.when(s == 5 + 2 * j)
            def _():
                g_far[j].start()

        dn[t] = dot(hidden, wd[...]).astype(BF16)

        for j in range(2):

            @pl.when(s == 5 + 2 * j)
            def _():
                g_far[j].wait_recv()
                ac[j] = (gn[4 + j].astype(F32) + rd[j].astype(F32)).astype(BF16)
                g_row[j].start()

        return 0

    lax.fori_loop(0, 8, step, 0)
    for copy in d_in:
        copy.start()

    size = 256
    count = d // size

    def weight_grad(lefts, rights, total, copies):
        def step(j, _):
            cols = lanes_at(j * size, size)
            acc = dot_tn(lefts[:, cols], rights[...])
            put_rows(total, (), j, size, bits, slice(None), acc.astype(BF16))
            for top, copy in enumerate(copies):

                @pl.when(j == (top + 1) * count // 2 - 1)
                def _():
                    copy.start()

            return 0

        lax.fori_loop(0, count, step, 0)

    part = jnp.zeros((1, d), F32)

    def final(j, part):
        at = pl.ds(j * tile, tile)
        g_near[j].wait_recv()
        g_row[j].wait_recv()
        grad = gn[j].astype(F32) + rc[j].astype(F32) + ry[j].astype(F32)
        m = mid[at, :]
        inv = lax.rsqrt(jnp.mean(m * m, axis=-1, keepdims=True) + NORM_EPS)
        unit = m * inv
        weighted = grad * gain
        part = part + jnp.sum(grad * unit, axis=0, keepdims=True)
        gmid = cs[rows_of(j), :].astype(F32) + inv * (weighted - unit * jnp.mean(weighted * unit, axis=-1, keepdims=True))
        mid[at, :] = gmid
        gmb[j] = gmid.astype(BF16)
        there = gm_h.at[lanes_at(where.core * rows + j * tile, tile)]
        store(gmb.at[j], there)
        store(mid.at[at], gmid_h.at[at])
        gm_out[j].start()
        return part

    gm_out = []
    for j in range(2):
        there = gm_h.at[lanes_at(where.core * rows + j * tile, tile)]
        gm_out.append(wires.copy(gmb.at[j], there, by_core))

    weight_grad(xs, ggs, sum_g, hop_g)
    weight_grad(xs, gus, sum_u, hop_u)
    part = final(0, part)
    weight_grad(cs, hs, sum_d, [])
    store(sum_d, gd_h)
    for j in range(2):
        d_in[j].wait_recv()
        d_in[2 + j].wait_recv()
        for at, extra, out in ((j, j, near_h), (4 + j, 2 + j, far_h)):
            dn[at] = (dn[at].astype(F32) + dnr[extra].astype(F32)).astype(BF16)
            store(dn.at[at], out.at[pl.ds(j * tile, tile)])
    end_g()
    store(got_g, gg_h)
    part_ref[...] = final(1, part)
    end_u()
    store(got_u, gu_h)
    for copy in gm_out:
        copy.wait_recv()
    for copy in stores:
        copy.wait()
    wires.drain()


def mlp_phase(middle, cots, wg_t, wu_t, wd, row):
    bits = wide_bits()
    rows, d = middle.shape
    ff = wd.shape[0]
    tile = rows // 2
    hbm = pl.BlockSpec(memory_space=pltpu.HBM)
    vmem = pl.BlockSpec(memory_space=pltpu.VMEM)
    dma = pltpu.SemaphoreType.DMA
    v_ = pltpu.VMEM
    block = (d // 2 ** len(bits), ff)
    full, part = (2,) * len(bits) + block, (2,) * (len(bits) - 1) + block
    return pl.pallas_call(
        functools.partial(mlp_phase_kernel, bits),
        name="mlp_phase",
        in_specs=[hbm] * 8 + [vmem],
        out_specs=[hbm, hbm, vmem] + [hbm] * 5,
        out_shape=[sds((rows, d), F32), sds((2 * rows, d), BF16), sds((1, d), F32)]
        + [sds(part, BF16), sds(part, BF16), sds(full, BF16)] + [sds((rows, d), BF16)] * 2,
        scratch_shapes=[
            v_((rows, d), F32), v_((8 * tile, d), BF16), v_((8 * tile, d), BF16),
            v_((ff, d), BF16), v_((ff, d), BF16), v_((ff, d), BF16),
            v_((8 * tile, ff), BF16), v_((8 * tile, ff), BF16), v_((8 * tile, ff), BF16),
            v_((8, tile, d), BF16), v_((2, tile, d), BF16), v_((2, tile, d), BF16),
            v_((2, tile, d), BF16), v_((2, tile, d), BF16), v_((8, tile, d), BF16), v_((4, tile, d), BF16),
            v_((2, tile, d), BF16), v_(full, BF16), v_(full, BF16), v_(full, BF16), v_(part, BF16), v_(part, BF16),
            dma((12,)), dma((24,)), dma((24,)), dma((12,)),
        ],
        compiler_params=pltpu.CompilerParams(collective_id=1, has_side_effects=True, vmem_limit_bytes=63 << 20),
        cost_estimate=cost(18 * 4 * rows * d * ff, 60e6, 4 * rows * ff),
    )(middle, *cots, wg_t, wu_t, wd, row)


def back_phase_kernel(
    bits,
    gm_h, mx_h, s_h, r_h, gt_h, rows_h, q_h, k_h, v_h, cum_h, dpre_h, rank_h, sin_h, w_h, wo_h, g_h, gmid_h, tok_h, far_h,
    off_ref, enter_ref, mult_ref, ru_ref, rd_ref, row_ref, mpart_ref,
    in_h, fr_h, gate_o, up_o, down_o, wout_o, k_o, v_o, q_o, s_o, rdown_o, rup_o, bias_o, mgain_o, group_o, ngain_o,
    gm, mx, sw, reach, gated, rows, q, k, v, cum, dpre, rank, sin, w, wo, held, mrecv, gmid, tok,
    gx, al, grank, ds, lb_m, pre_s, pre_m, sc_out, sc_in, osv, osy, osr, kva, kvay, kvar, kvb, kvbr, kvbo, tb, tr,
    sm, smf, smv, smr, smo, ng, ngr,
    load_sem, send_sem, recv_sem, out_sem,
):
    count, d = rows.shape
    half = count // 2
    dk, dv = q.shape[2], v.shape[2]
    where = Places(2 ** len(bits))
    wires = Wires(send_sem, recv_sem)
    loads = []

    def load(src, dst):
        copy = pltpu.make_async_copy(src, dst, load_sem.at[len(loads)])
        loads.append(copy)
        copy.start()
        return copy

    orders = (bits[1:], bits[:1] + bits[2:], bits)
    third = [load(g_h[0], held[0]), load(g_h[1], held[1])]
    first = [load(gm_h, gm), load(wo_h, wo), load(mx_h, mx), load(s_h, sw), load(r_h, reach)]
    second = [load(gt_h, gated), load(rows_h, rows)]
    dim = sorted(bits, reverse=True).index(bits[0])
    keep = load(g_h[2].at[(slice(None),) * dim + (where.has(bits[0]),)], held[2])
    fourth = [load(rank_h, rank)]
    for src, dst in ((q_h, q), (k_h, k), (v_h, v), (cum_h, cum), (dpre_h, dpre), (sin_h, sin), (w_h, w)):
        fourth.append(load(src, dst))
    fifth = [load(gmid_h, gmid), load(tok_h, tok)]

    where.meet()
    mlp = [
        Scatter(where, wires, held[0], None, orders[0], mrecv[0]),
        Scatter(where, wires, held[1], None, orders[1], mrecv[1]),
        Scatter(where, wires, g_h[2], held[2], orders[2], mrecv[2]),
    ]
    scan = Scan(where, wires, ds, lb_m, pre_s, pre_m, sc_out, sc_in, True)
    os_y = wires.copy(osv.at[1], osy, where.by_row)
    os_s = Scatter(where, wires, osv.at[0], None, bits, osr)
    kva_y = wires.copy(kva.at[1], kvay, where.by_row)
    kva_s = Scatter(where, wires, kva.at[0], None, bits, kvar)
    kvb_s = [Scatter(where, wires, kvb.at[h], None, bits, kvbr[h]) for h in range(2)]
    kvb_y = wires.copy(kvbo.at[0], kvbo.at[1], where.by_row)
    tots = [wires.copy(tb.at[j], tr.at[j], where.by_core) for j in range(2)]
    far = []
    for j in range(4):
        at = pl.ds(j * (half // 4), half // 4)
        far.append(wires.copy(far_h.at[at], fr_h.at[at], where.by_row))
    every = Shared(where, wires, sm, smf, smv, smr, smo)
    every_n = Everywhere(where, wires, ng, ngr)
    n_bits = len(bits)
    at_row = row_places(d, dv, 4 * dk)
    ngain = row_ref[:, at_row[0] : at_row[1]]
    gain = row_ref[:, at_row[2] : at_row[3]]
    restart = row_ref[:, at_row[4] : at_row[4] + dk]
    far[0].start()
    for copy in third:
        copy.wait()
    mlp[1].go()
    mlp[0].go()

    blk = half // 2
    ds[...] = jnp.zeros_like(ds)
    sm[...] = jnp.zeros_like(sm)
    for copy in first:
        copy.wait()

    def gate_step(i, part):
        at = pl.ds(pl.multiple_of(i * blk, blk), blk)
        g = gm[at, :]
        for h in range(2):
            grad = dot_nt(g, wo[h])
            mixed = mx[h, at, :]
            inv = lax.rsqrt(jnp.mean(mixed * mixed, axis=-1, keepdims=True) + GROUP_EPS)
            unit = mixed * inv
            s = sw[h, at, :]
            sig = jax.nn.sigmoid(s)
            al[h, at, 2 * dk + dv :] = (grad * unit * gain * (sig * (1.0 + s * (1.0 - sig)))).astype(BF16)
            dn = grad * (s * sig)
            part = part + jnp.sum(dn * unit, axis=0, keepdims=True)
            weighted = dn * gain
            gmix = (inv * (weighted - unit * jnp.mean(weighted * unit, axis=-1, keepdims=True))).astype(BF16)
            gx[h, at, :] = gmix
            ds[h] += dot_tn(gmix, reach[h, at, :])
        return part

    group_part = lax.fori_loop(0, 4, gate_step, jnp.zeros((1, dv), F32))
    for h in range(2):
        ds[h] = ds[h] * restart
        lb_m[h] = mult_ref[h]
    scan.begin()

    size = 256

    def out_step(j, _):
        cols = pl.ds(pl.multiple_of(j * size, size), size)
        for h in (1, 0):
            value = dot_tn(gm[:, cols], gated[h]).astype(BF16)
            put_rows(osv, (h,), j, size, bits, slice(0, dv), value)
        return 0

    def swish_step(j, _):
        cols = pl.ds(pl.multiple_of(j * size, size), size)
        for h in (1, 0):
            value = dot_tn(rows[:, cols], al[h, :, 2 * dk + dv :]).astype(BF16)
            put_rows(osv, (h,), j, size, bits, slice(dv, 2 * dv), value)
        return 0

    for copy in second:
        copy.wait()
    lax.fori_loop(0, d // size, out_step, 0)
    lax.fori_loop(0, d // size, swish_step, 0)
    scan.advance()
    os_y.start()
    scan.advance()
    keep.wait()
    mlp[2].go()
    while scan.advance():
        pass
    mlp[0].advance()
    mlp[1].advance()
    for copy in fourth:
        copy.wait()

    ds[...] = pre_s[...]
    chunks = count // CHUNK
    mask = triangle(True)
    ones = triangle(False).astype(F32)
    scale = dk**-0.5
    rk = rank.shape[1]

    def add_row(ref, extra):
        for at in itertools.product(range(2), repeat=n_bits):
            ref[(0,) + at] = (ref[(0,) + at].astype(F32) + extra[at].astype(F32)).astype(BF16)

    def back_step(step, carry):
        c = chunks - 1 - step

        @pl.when(step == chunks // 2)
        def _():
            mlp[2].advance()

        @pl.when(step == chunks - 3)
        def _():
            os_y.wait_recv()
            add_row(osv, osy)
            os_s.go()
            far[1].start()

        at = pl.ds(pl.multiple_of(c * CHUNK, CHUNK), CHUNK)
        grs, new = None, []
        for h in range(2):
            ch = cum[h, at, :]
            mid = ch[HALF - 1 : HALF]
            end = ch[CHUNK - 1 :]
            e_qd, e_kd, e_qi, e_ke = jnp.exp(ch - mid), jnp.exp(mid - ch), jnp.exp(ch), jnp.exp(end - ch)
            e_end = jnp.exp(end)
            qf = q[h, at, :].astype(F32) * scale
            kf = k[h, at, :].astype(F32)
            vc = v[h, at, :]
            qd = (qf * e_qd).astype(BF16)
            kd = (kf * e_kd).astype(BF16)
            qi = (qf * e_qi).astype(BF16)
            ke = (kf * e_ke).astype(BF16)
            go = gx[h, at, :]
            ru = ru_ref[:, lanes_at(((where.place + 2 * h) % 4) * dk, dk)].astype(F32)
            state = sin[h, c].astype(F32) + enter_ref[h] * jnp.exp(off_ref[h, c])
            state_low = state.astype(BF16)
            dstate = ds[h]
            dstate_low = dstate.astype(BF16)
            scores = jnp.where(mask, dot_nt(qd, kd), 0.0).astype(BF16)
            dscores = jnp.where(mask, dot_nt(go, vc), 0.0).astype(BF16)
            d_v = dot_tn(scores, go) + dot_nt(ke, dstate_low)
            d_qd = dot(dscores, kd)
            d_qi = dot(go, state_low)
            d_kd = dot_tn(dscores, qd)
            d_ke = dot(vc, dstate_low)
            d_q = scale * (d_qd * e_qd + d_qi * e_qi)
            d_k = d_kd * e_kd + d_ke * e_ke
            tail = ke.astype(F32) * d_ke
            d_cum = qd.astype(F32) * d_qd + qi.astype(F32) * d_qi - kd.astype(F32) * d_kd - tail
            d_end = jnp.sum(tail, axis=0, keepdims=True) + e_end * jnp.sum(dstate * state, axis=0, keepdims=True)
            grad_decay = exact(ones, d_cum, ((1,), (0,))) + d_end
            g_pre = grad_decay * jax.nn.sigmoid(-dpre[h, at, :]) * (1.0 / GATE_NORM)
            al[h, at, :dk] = d_k.astype(BF16)
            al[h, at, dk : dk + dv] = d_v.astype(BF16)
            al[h, at, dk + dv : 2 * dk + dv] = d_q.astype(BF16)
            gr = exact(g_pre, ru, ((1,), (1,)))
            grs = gr if grs is None else grs + gr
            new.append(carry[2 * h] + exact(rank[at, :], g_pre, ((0,), (0,))))
            new.append(carry[2 * h + 1] + jnp.sum(g_pre, axis=0, keepdims=True))
            ds[h] = dstate * e_end + dot_tn(go, qi)
        grank[at, :] = grs.astype(BF16)
        return tuple(new)

    zero = (jnp.zeros((rk, dk), F32), jnp.zeros((1, dk), F32))
    rup0, gb0, rup1, gb1 = lax.fori_loop(0, chunks, back_step, zero + zero)
    qk = 4 * dk
    sm[0] = dot_tn(grank[...], rows[...])
    at0 = where.place * dk
    at1 = ((where.place + 2) % 4) * dk
    sm[1, :, lanes_at(at0, dk)] = rup0
    sm[1, :, lanes_at(at1, dk)] = rup1
    sm[1, 0:1, lanes_at(qk + at0, dk)] = gb0
    sm[1, 0:1, lanes_at(qk + at1, dk)] = gb1
    sm[1, 1:2, qk : qk + dv] = group_part
    for i in range(d // qk):
        sm[1, 2 + i : 3 + i, qk : 2 * qk] = mpart_ref[:, i * qk : (i + 1) * qk]
    every.begin()
    def kvq_step(ref, h, low):
        def step(j, _):
            cols = lanes_at(j * size, size)
            value = dot_tn(rows[:, cols], al[h, :, low : low + size]).astype(BF16)
            put_rows(ref, (h,), j, size, bits, slice(None), value)
            return 0

        lax.fori_loop(0, d // size, step, 0)

    kvq_step(kva, 1, 0)
    kva_y.start()
    for h in range(2):
        kvq_step(kvb, h, size)
        kvb_s[h].go()
    mlp[2].advance()
    os_s.advance()

    def total_step(i, _):
        b = jnp.where(i < 2, 2 - 2 * where.core + i, 2 * where.core + i - 2)
        at = pl.ds(pl.multiple_of(b * blk, blk), blk)
        total = dot_nt(al[0, at, :], w[0]) + dot_nt(al[1, at, :], w[1]) + dot(grank[at, :], rd_ref[...])
        for j in range(2):

            @pl.when(i == j)
            def _():
                tb[j] = total.astype(BF16)
                tots[j].start()

            @pl.when(i == 2 + j)
            def _():
                tb[2 + j] = total.astype(BF16)

        return 0

    every.advance()
    lax.fori_loop(0, 4, total_step, 0)

    kvq_step(kva, 0, 0)
    every.advance()

    for copy in fifth:
        copy.wait()
    part = jnp.zeros((1, d), F32)
    for j in range(2):
        at = pl.ds(j * blk, blk)
        tots[j].wait_recv()
        grad = tb[2 + j].astype(F32) + tr[j].astype(F32)
        x = tok[at, :].astype(F32)
        inv = lax.rsqrt(jnp.mean(x * x, axis=-1, keepdims=True) + NORM_EPS)
        unit = x * inv
        weighted = grad * ngain
        part = part + jnp.sum(grad * unit, axis=0, keepdims=True)
        gmid[at, :] = gmid[at, :] + inv * (weighted - unit * jnp.mean(weighted * unit, axis=-1, keepdims=True))
    done = pltpu.make_async_copy(gmid, in_h, out_sem.at[0])
    done.start()
    for i in range(8):
        ng[0, i : i + 1, :] = part[:, i * (d // 8) : (i + 1) * (d // 8)]
    every_n.begin()

    kva_y.wait_recv()
    far[2].start()
    far[3].start()
    add_row(kva, kvay)
    kva_s.go()
    for part in kvb_s:
        part.advance()
    os_s.advance()
    every.advance()
    every_n.advance()
    for i, out in ((0, gate_o), (1, up_o)):
        out[...] = jnp.transpose(mlp[i].result())
    for i in range(n_bits - 1):
        kva_s.advance()
        if i < n_bits - 2:
            for part in kvb_s:
                part.advance()
        every.advance()
        every_n.advance()
    kvbo[0] = kvb_s[1].result().astype(BF16)
    kvb_y.start()
    down_o[...] = jnp.transpose(mlp[2].result())
    total = os_s.result()
    wout_o[...] = jnp.transpose(total[:, :dv])
    s_o[...] = total[:, dv:]
    every.advance()
    every_n.advance()
    first_half = kva_s.result()
    last_half = kvb_s[0].result()
    kvb_y.wait_recv()
    last_half = last_half + kvbo[1].astype(F32)
    k_o[...] = first_half[:, :dk]
    v_o[:, : size - dk] = first_half[:, dk:]
    v_o[:, size - dk :] = last_half[:, : dk + dv - size]
    q_o[...] = last_half[:, dk + dv - size :]
    small = every.result()
    rdown_o[...] = small[0]
    rup_o[...] = small[1, :, :qk]
    bias_o[...] = small[1, 0:1, qk : 2 * qk]
    group_o[...] = small[1, 1:2, qk : qk + dv]
    for i in range(d // qk):
        mgain_o[:, i * qk : (i + 1) * qk] = small[1, 2 + i : 3 + i, qk : 2 * qk]
    whole_n = every_n.result()
    for i in range(8):
        ngain_o[:, i * (d // 8) : (i + 1) * (d // 8)] = whole_n[i : i + 1, :]
    for copy in far:
        copy.wait_recv()
    done.wait()
    wires.drain()


def back_phase(
    gm, mx, s, reach, gated, rows, q, k, v, cum, dpre, rank, sin, w, wo, grads, gmid, tokens, far,
    off, enter, mult, ru, rd, row, mpart,
):
    bits = wide_bits()
    count, d = rows.shape
    half = count // 2
    dk, dv, rk = q.shape[2], v.shape[2], rank.shape[1]
    ff = grads[0].shape[-1]
    each = d // 2 ** len(bits)
    n_bits, chunks = len(bits), count // CHUNK
    hbm = pl.BlockSpec(memory_space=pltpu.HBM)
    vmem = pl.BlockSpec(memory_space=pltpu.VMEM)
    dma = pltpu.SemaphoreType.DMA
    v_ = pltpu.VMEM

    def shape(lead, cols):
        return (2,) * lead + (each, cols)

    def falls(cols):
        return [v_(shape(n_bits - 1 - i, cols), BF16) for i in range(n_bits)]

    pair, three = [hbm] * 2, [hbm] * 3
    kvq = 2 * dk + dv
    scratch = [
        v_((count, d), BF16), v_((2, count, dv), F32), v_((2, count, dv), F32), v_((2, count, dk), BF16),
        v_((2, count, dv), BF16), v_((count, d), BF16), v_((2, count, dk), BF16), v_((2, count, dk), BF16),
        v_((2, count, dv), BF16), v_((2, count, dk), F32), v_((2, count, dk), F32), v_((count, rk), F32),
        v_((2, chunks, dv, dk), BF16), v_((2, d, kvq + dv), BF16), v_((2, dv, d), BF16),
        [v_(shape(n_bits - 1, ff), BF16)] * 3, [falls(ff)[1:], falls(ff)[1:], falls(ff)], v_((half, d), F32), v_((half, d), BF16),
        v_((2, count, dv), BF16), v_((2, count, kvq + dv), BF16), v_((count, rk), BF16),
        v_((2, dv, dk), F32), v_((2, 1, dk), F32), v_((2, dv, dk), F32), v_((2, 1, dk), F32),
        v_((n_bits + 1, 2, dv + 16, dk), BF16), v_((n_bits + 1, 2, dv + 16, dk), BF16),
        v_((2,) + shape(n_bits, 2 * dv), BF16), v_(shape(n_bits, 2 * dv), BF16), falls(2 * dv),
        v_((2,) + shape(n_bits, 256), BF16), v_(shape(n_bits, 256), BF16), falls(256),
        v_((2,) + shape(n_bits, 256), BF16), [falls(256), falls(256)], v_((2, each, 256), BF16),
        v_((4, half // 2, d), BF16), v_((2, half // 2, d), BF16),
        v_((2, rk, d), F32), v_((rk, d), F32), v_((n_bits + 1, rk, d), F32), v_((n_bits + 1, rk, d), F32), v_((2, rk, d), F32),
        v_((n_bits + 3, 8, d // 8), F32), v_((n_bits + 2, 8, d // 8), F32),
        dma((24,)), dma((96,)), dma((96,)), dma((1,)),
    ]
    out_shape = [
        sds((half, d), F32), sds((half, d), BF16), sds((ff, each), F32), sds((ff, each), F32), sds((ff, each), F32), sds((dv, each), F32),
        sds((each, dk), F32), sds((each, dv), F32), sds((each, dk), F32), sds((each, dv), F32),
        sds((rk, d), F32), sds((rk, 4 * dk), F32), sds((1, 4 * dk), F32), sds((1, d), F32), sds((1, dv), F32), sds((1, d), F32),
    ]
    operands = (
        gm, mx, s, reach, gated, rows, q, k, v, cum, dpre, rank, sin, w, wo, grads, gmid, tokens, far,
        off, enter, mult, ru, rd, row, mpart,
    )
    flat, tree = jax.tree.flatten(operands)
    n_vmem = len(jax.tree.leaves(operands[19:]))
    flat_scratch, scratch_tree = jax.tree.flatten(scratch, is_leaf=lambda x: not isinstance(x, list))
    n_in, n_out = len(flat), len(out_shape)

    def kernel(*refs):
        ins = jax.tree.unflatten(tree, refs[:n_in])
        rest = jax.tree.unflatten(scratch_tree, refs[n_in + n_out :])
        back_phase_kernel(bits, *ins, *refs[n_in : n_in + n_out], *rest)

    return pl.pallas_call(
        kernel,
        name="back_phase",
        in_specs=[hbm] * (n_in - n_vmem) + [vmem] * n_vmem,
        out_specs=[hbm, hbm] + [vmem] * (n_out - 2),
        out_shape=out_shape,
        scratch_shapes=flat_scratch,
        compiler_params=pltpu.CompilerParams(collective_id=2, has_side_effects=True, vmem_limit_bytes=62 << 20),
        cost_estimate=cost(40e9, 60e6, 1e6),
    )(*flat)


def finish_kernel(count, mid_ref, near_ref, far_ref, grad_ref, *refs):
    res_ref, in_ref = refs[count : count + 2]
    res_ref[...] = (mid_ref[...] + (near_ref[...].astype(F32) + far_ref[...].astype(F32))).astype(BF16)
    in_ref[...] = grad_ref[...]

    @pl.when(pl.program_id(0) == 0)
    def _():
        for src, dst in zip(refs[:count], refs[count + 2 :]):
            dst[...] = src[...]


def finish(middle, near, far, grad, smalls):
    rows, d = middle.shape
    blk = rows // 4
    row = rows_spec(blk, d)
    wholes = [pl.BlockSpec(v.shape, lambda i: (0, 0)) for v in smalls]
    return pl.pallas_call(
        functools.partial(finish_kernel, len(smalls)),
        name="finish",
        grid=(4,),
        in_specs=[row] * 4 + wholes,
        out_specs=[row] * 2 + wholes,
        out_shape=[sds((rows, d), BF16), sds((rows, d), F32)] + [sds(v.shape, v.dtype) for v in smalls],
        compiler_params=params(62),
    )(middle, near, far, grad, *smalls)


def wide_bits():
    count, bits, bit = lax.axis_size("wide"), [], 1
    while bit < count:
        bits.append(bit)
        bit *= 2
    return bits


def shards(
    tokens, cotangent, flags, norm_gain, query_weight, key_weight, value_weight, swish_weight, rank_down, rank_up,
    decay_bias, group_gain, output_weight, mlp_gain, mlp_gate, mlp_up, mlp_down,
):
    place = lax.axis_index("narrow")
    dk, dv, d = query_weight.shape[1], value_weight.shape[1], tokens.shape[1]
    restart = jnp.where((place & 2) != 0, 1.0, 1.0 - flags[0].astype(F32))
    parts = [part.astype(F32) for part in (norm_gain, mlp_gain, group_gain, decay_bias)]
    row = jnp.concatenate(parts + [jnp.full((dk,), restart, F32)]).reshape(1, -1)
    rd = rank_down.T
    (
        middle, rows_all, q, k, v, s, cum, dpre, rank_pre, reach, sin, mixed, gated, w, weights_out, cot_c, cot_y, cot_d,
        off, enter, mults,
    ) = front_phase(
        tokens, cotangent, key_weight, value_weight, query_weight, swish_weight, output_weight, rd, rank_up, row
    )
    grad_middle, gm_all, mlp_gain_part, gate_g, up_g, down_g, near, far = mlp_phase(
        middle, (cotangent, cot_c, cot_y, cot_d), mlp_gate.T, mlp_up.T, mlp_down, row
    )
    input_grad, far_sum, *smalls = back_phase(
        gm_all, mixed, s, reach, gated, rows_all, q, k, v, cum, dpre, rank_pre, sin,
        w, weights_out, (gate_g, up_g, down_g), grad_middle, tokens, far, off, enter, mults, rank_up, rd, row,
        mlp_gain_part,
    )
    result, input_grad, *smalls = finish(middle, near, far_sum, input_grad, smalls)
    gate_t, up_t, down_t, out_t, k_g, v_g, q_g, s_g, rdown_t, rup_g, bias_g, mgain_g, group_g, ngain = smalls
    return (
        result,
        input_grad,
        ngain[0],
        q_g,
        k_g,
        v_g,
        s_g,
        rdown_t.T,
        rup_g,
        bias_g[0],
        group_g[0],
        out_t,
        mgain_g[0],
        gate_t.T,
        up_t.T,
        down_t,
    )


def solution(mesh):
    rows, cols = P(("wide", "narrow"), None), P(None, "narrow")
    both = P("wide", "narrow")
    in_specs = (
        rows, rows, P("wide"), P(), cols, cols, cols, cols, P(), P(), P(), P(), P("narrow", None), P(), cols, cols,
        P("narrow", None),
    )
    out_specs = (
        rows, rows, P(), both, both, both, both, P(), P(), P(), P(), P("narrow", "wide"), P(), both, both,
        P("narrow", "wide"),
    )
    return jax.shard_map(shards, mesh=mesh, in_specs=in_specs, out_specs=out_specs, check_vma=False)
```

```python
import functools
import itertools

import jax
import jax.numpy as jnp
from jax import lax
from jax.experimental import pallas as pl
from jax.experimental.pallas import tpu as pltpu
from jax.sharding import PartitionSpec as P

NORM_EPS = 1e-06
GROUP_EPS = 1e-05
GATE_NORM = 16.0
HIGHEST_PREC = lax.Precision.HIGHEST
MESH = pl.DeviceIdType.MESH
CHUNK = 128
HALF = CHUNK // 2
BLOCK = 256
F32 = jnp.float32
BF16 = jnp.bfloat16


def dot(a, b):
    return lax.dot_general(a, b, (((1,), (0,)), ((), ())), preferred_element_type=F32)


def dot_nt(a, b):
    return lax.dot_general(a, b, (((1,), (1,)), ((), ())), preferred_element_type=F32)


def dot_tn(a, b):
    return lax.dot_general(a, b, (((0,), (0,)), ((), ())), preferred_element_type=F32)


def exact(a, b, dims):
    return lax.dot_general(
        a, b, (dims, ((), ())), precision=HIGHEST_PREC, preferred_element_type=F32
    )


def sds(shape, dtype):
    return jax.ShapeDtypeStruct(shape, dtype)


def params(mib=48):
    return pltpu.CompilerParams(vmem_limit_bytes=mib << 20)


def cost(flops, nbytes, trans=0):
    return pl.CostEstimate(flops=int(flops), bytes_accessed=int(nbytes), transcendentals=int(trans))


def whole(shape):
    return pl.BlockSpec(shape, lambda i: (0,) * len(shape), pipeline_mode=pl.Buffered(1))


def rows_spec(rows, cols):
    return pl.BlockSpec((rows, cols), lambda i: (i, 0))


def triangle(lower):
    r = lax.broadcasted_iota(jnp.int32, (CHUNK, CHUNK), 0)
    c = lax.broadcasted_iota(jnp.int32, (CHUNK, CHUNK), 1)
    return r >= c if lower else r <= c


class Wires:
    def __init__(self, send_sem, recv_sem):
        self.send_sem, self.recv_sem, self.used, self.all = send_sem, recv_sem, 0, []

    def copy(self, src, dst, target):
        made = pltpu.make_async_remote_copy(
            src,
            dst,
            self.send_sem.at[self.used],
            self.recv_sem.at[self.used],
            device_id=target,
            device_id_type=MESH,
        )
        self.used += 1
        self.all.append(made)
        return made

    def drain(self):
        for made in self.all:
            made.wait_send()


class Places:
    def __init__(self, wide_count):
        self.wide, self.place = lax.axis_index("wide"), lax.axis_index("narrow")
        self.core = self.place % 2
        self.second = self.place // 2
        self.by_core = (self.wide, self.place + 1 - 2 * self.core)
        self.by_row = (self.wide, (self.place + 2) % 4)
        self.bits = []
        bit = 1
        while bit < wide_count:
            self.bits.append(bit)
            bit *= 2

    def has(self, bit):
        return (self.wide // bit) % 2

    def across(self, bit):
        return (self.wide + bit - 2 * bit * self.has(bit), self.place)

    def meet(self):
        barrier = pltpu.get_barrier_semaphore()
        others = [self.by_core, self.by_row] + [self.across(bit) for bit in self.bits]
        for other in others:
            pl.semaphore_signal(barrier, 1, device_id=other, device_id_type=MESH)
        pl.semaphore_wait(barrier, len(others))


class Scan:
    def __init__(self, where, wires, tot_s, tot_m, pre_s, pre_m, out, into, backward):
        self.tot_s, self.tot_m, self.pre_s, self.pre_m = tot_s, tot_m, pre_s, pre_m
        self.out, self.into, self.at, self.order = out, into, 0, (0, 1)
        self.steps = []
        for i, bit in enumerate([0] + where.bits):
            target = where.across(bit) if bit else where.by_row
            is_set = where.has(bit) if bit else where.second
            later = (1 - is_set if backward else is_set) > 0
            copies = [wires.copy(out.at[i, h], into.at[i, h], target) for h in range(2)]
            self.steps.append((copies, later, bit == 0))
        pre_s[...] = jnp.zeros_like(pre_s)
        pre_m[...] = jnp.ones_like(pre_m)

    def send(self, i, h):
        dv = self.tot_s.shape[1]
        self.out[i, h, :dv, :] = self.tot_s[h].astype(BF16)
        self.out[i, h, dv:, :] = jnp.broadcast_to(self.tot_m[h], (16, self.tot_m.shape[2])).astype(BF16)
        self.steps[i][0][h].start()

    def begin(self):
        for h in range(2):
            self.send(0, h)

    def advance(self):
        i, more = self.at, self.at + 1 < len(self.steps)
        copies, later, swapped = self.steps[i]
        dv = self.tot_s.shape[1]
        heads = []
        for g in self.order:
            h = 1 - g if swapped else g
            heads.append(h)
            copies[g].wait_recv()
            oth_s = self.into[i, g, :dv, :].astype(F32)
            oth_m = self.into[i, g, dv : dv + 1, :].astype(F32)
            pre_s, pre_m, tot_s, tot_m = self.pre_s[h], self.pre_m[h], self.tot_s[h], self.tot_m[h]
            if more:
                self.tot_s[h] = jnp.where(later, oth_s * tot_m + tot_s, tot_s * oth_m + oth_s)
                self.tot_m[h] = tot_m * oth_m
                self.send(i + 1, h)
            self.pre_s[h] = jnp.where(later, oth_s * pre_m + pre_s, pre_s)
            self.pre_m[h] = jnp.where(later, oth_m * pre_m, pre_m)
        self.order = tuple(heads)
        self.at = i + 1
        return more


class Scatter:
    def __init__(self, where, wires, source, keep, order, recvs):
        self.recvs, self.steps, self.at = recvs, [], 0
        left = sorted(order, reverse=True)
        held, first = source, keep
        for bit, recv in zip(order, recvs):
            dim = left.index(bit)
            mine = where.has(bit)
            other = held.at[(slice(None),) * dim + (1 - mine,)]
            copy = wires.copy(other, recv, where.across(bit))
            self.steps.append((copy, held if first is None else first, dim, mine, first is not None))
            left.pop(dim)
            held, first = recv, None

    def go(self):
        self.steps[self.at][0].start()

    def land(self):
        total = self.finish(self.at)
        self.at += 1
        return total

    def advance(self):
        if self.at + 1 < len(self.steps):
            self.land()
            self.go()

    def result(self):
        while self.at + 1 < len(self.steps):
            self.advance()
        return self.land()

    def finish(self, i):
        copy, held, dim, mine, picked = self.steps[i]
        copy.wait_recv()
        recv = self.recvs[i]
        last = i == len(self.steps) - 1
        for at in itertools.product(range(2), repeat=len(recv.shape) - 2):
            source = at if picked else at[:dim] + (mine,) + at[dim:]
            total = recv[at].astype(F32) + held[source].astype(F32)
            if last:
                return total
            recv[at] = total.astype(BF16)
        return None


class Everywhere:
    def __init__(self, where, wires, values, recvs):
        self.values, self.recvs = values, recvs
        targets = [where.by_core, where.by_row] + [where.across(bit) for bit in where.bits]
        self.steps = [wires.copy(values.at[i], recvs.at[i], target) for i, target in enumerate(targets)]

    def begin(self, i=0):
        self.at = i
        self.steps[i].start()

    def advance(self):
        if self.at + 1 < len(self.steps):
            self.finish(self.at)
            self.begin(self.at + 1)

    def result(self):
        while self.at + 1 < len(self.steps):
            self.advance()
        self.finish(self.at)
        return self.values[len(self.steps)]

    def finish(self, i):
        self.steps[i].wait_recv()
        self.values[i + 1] = self.values[i] + self.recvs[i]


class Shared:
    def __init__(self, where, wires, parts, first, values, recvs, out):
        self.core, self.parts, self.first = where.core, parts, first
        self.values, self.recvs, self.out, self.at = values, recvs, out, 0
        targets = [where.by_row] + [where.across(bit) for bit in where.bits]
        self.steps = [wires.copy(parts.at[1 - where.core], first, where.by_core)]
        self.steps += [wires.copy(values.at[i], recvs.at[i], target) for i, target in enumerate(targets)]
        self.steps.append(wires.copy(out.at[where.core], out.at[where.core], where.by_core))

    def begin(self):
        self.steps[0].start()

    def advance(self):
        i, last = self.at, len(self.steps) - 1
        if i == last:
            return
        self.steps[i].wait_recv()
        if i == 0:
            total = self.parts[self.core] + self.first[...]
        else:
            total = self.values[i - 1] + self.recvs[i - 1]
        if i + 1 == last:
            self.out[self.core] = total
        else:
            self.values[i] = total
        self.at = i + 1
        self.steps[i + 1].start()

    def result(self):
        while self.at + 1 < len(self.steps):
            self.advance()
        self.steps[-1].wait_recv()
        return self.out


def bit_index(w, bits):
    return tuple((w // bit) % 2 for bit in sorted(bits, reverse=True))


def put_rows(ref, lead, j, size, bits, lanes, value):
    each = ref.shape[-2]
    for p in range(size // each):
        at = lead + bit_index(j * (size // each) + p, bits) + (slice(None), lanes)
        ref[at] = value[p * each : (p + 1) * each]


def lanes_at(start, size):
    return pl.ds(pl.multiple_of(start, size), size)


def row_places(d, dv, qk):
    return (0, d, 2 * d, 2 * d + dv, 2 * d + dv + qk)


def front_phase_kernel(
    bits,
    tok_h, cot_h, kw_h, vw_h, qw_h, sw_h, wo_h, rd_ref, ru_ref, row_ref,
    mid_h, rows_h, q_h, k_h, v_h, s_h, cum_h, dpre_h, rank_h, reach_h, sin_h, mx_h, gated_h, w_h, wo2_h, c1_h, c2_h, c3_h,
    off_o, enter_o, mult_o,
    tok, rows, w, wo, q, k, v, sw, cum, dpre, rank, reach, sin, mx, gated, tb, tr, mid, st, off,
    tot_s, tot_m, pre_s, pre_m, sc_out, sc_in,
    load_sem, send_sem, recv_sem, out_sem,
):
    count, d = rows.shape
    half = count // 2
    blk = half // 2
    dk, dv = q.shape[2], v.shape[2]
    kv = dk + dv
    where = Places(2 ** len(bits))
    wires = Wires(send_sem, recv_sem)
    loads, stores = [], []

    def load(src, dst):
        copy = pltpu.make_async_copy(src, dst, load_sem.at[len(loads)])
        loads.append(copy)
        copy.start()
        return copy

    def store(src, dst):
        copy = pltpu.make_async_copy(src, dst, out_sem.at[len(stores)])
        stores.append(copy)
        copy.start()

    load_tok = load(tok_h, tok)
    load_kv = [load(kw_h, w.at[0, :, pl.ds(0, dk)]), load(vw_h, w.at[0, :, pl.ds(dk, dv)])]
    load_qs = [load(qw_h, w.at[0, :, pl.ds(kv, dk)]), load(sw_h, w.at[0, :, pl.ds(kv + dk, dv)])]
    load_wo = load(wo_h, wo.at[0])

    where.meet()
    at_row = row_places(d, dv, 4 * dk)
    ngain = row_ref[:, at_row[0] : at_row[1]]
    gain = row_ref[:, at_row[2] : at_row[3]]
    restart = row_ref[:, at_row[4] : at_row[4] + dk]

    first_bit, second_bit = where.bits[0], where.bits[1]
    over_a, over_b = where.across(first_bit), where.across(second_bit)
    spot_a, spot_b = where.has(first_bit), where.has(second_bit)

    class Quarters:
        def __init__(self, ref, cols):
            quarter = ref.shape[1] // 4

            def part(of_a, of_b, low, size):
                at = pl.ds(pl.multiple_of((of_a + 2 * of_b) * quarter + low, size), size)
                return (at,) if cols is None else (at, cols)

            mine = part(spot_a, spot_b, 0, quarter)
            from_a = part(1 - spot_a, spot_b, 0, quarter // 2)
            from_b = part(spot_a, 1 - spot_b, quarter // 2, quarter // 2)
            got = ref.at[(1,) + mine]
            self.row = wires.copy(ref.at[(0,) + mine], got, where.by_row)
            self.near = [wires.copy(got, got, over_a), wires.copy(got, got, over_b)]
            self.far = [
                wires.copy(ref.at[(1,) + from_a], ref.at[(1,) + from_a], over_b),
                wires.copy(ref.at[(1,) + from_b], ref.at[(1,) + from_b], over_a),
            ]

        def start(self):
            self.row.start()

        def relay(self):
            self.row.wait_recv()
            for copy in self.near:
                copy.start()

        def forward(self):
            for copy in self.near:
                copy.wait_recv()
            for copy in self.far:
                copy.start()

        def done(self):
            for copy in self.far:
                copy.wait_recv()

    kv_in = Quarters(w, pl.ds(0, kv))
    qs_in = Quarters(w, pl.ds(kv, kv))
    wo_in = Quarters(wo, None)
    cot_row, cot_both = [], []
    for i in range(2):
        at = pl.ds(i * blk, blk)
        cot_row.append(wires.copy(cot_h.at[at], c2_h.at[at], where.by_row))
        cot_both.append(wires.copy(c2_h.at[at], c3_h.at[at], where.by_core))
    cot_core = wires.copy(cot_h, c1_h, where.by_core)
    row_out = []
    for i in range(2):
        at = pl.ds(pl.multiple_of(where.core * half + i * blk, blk), blk)
        row_out.append(wires.copy(rows.at[at], rows.at[at], where.by_core))
    terms = [wires.copy(tb.at[j], tr.at[j], where.by_core) for j in range(2)]
    scan = Scan(where, wires, tot_s, tot_m, pre_s, pre_m, sc_out, sc_in, False)

    for copy in load_kv:
        copy.wait()
    kv_in.start()
    load_tok.wait()
    for i in range(2):
        x = tok[pl.ds(i * blk, blk), :].astype(F32)
        inv = lax.rsqrt(jnp.mean(x * x, axis=-1, keepdims=True) + NORM_EPS)
        rows[pl.ds(pl.multiple_of(where.core * half + i * blk, blk), blk), :] = (x * inv * ngain).astype(BF16)
        row_out[i].start()
    for copy in load_qs:
        copy.wait()
    qs_in.start()
    load_wo.wait()
    wo_in.start()
    for copy in row_out:
        copy.wait_recv()
    cot_core.start()
    store(rows, rows_h)

    mask = triangle(True)
    ones = mask.astype(F32)
    scale = dk**-0.5
    blocks = count // BLOCK
    per = BLOCK // CHUNK

    def first_step(h, i, _):
        b = i
        at = pl.ds(pl.multiple_of(b * BLOCK, BLOCK), BLOCK)
        if h == 0:

            @pl.when(i == 2)
            def _():
                kv_in.relay()

            @pl.when(i == blocks - 1)
            def _():
                qs_in.relay()

        @pl.when(b == 0)
        def _():
            st[...] = jnp.zeros_like(st)
            off[...] = jnp.zeros_like(off)

        x = rows[at, :]

        if h == 0:
            rank[at, :] = dot_nt(x, rd_ref[...])

        proj = dot(x, w[h, :, :kv])
        head = (where.place + 2 * h) % 4
        ru = ru_ref[:, lanes_at(head * dk, dk)].astype(F32)
        bias = row_ref[:, lanes_at(at_row[3] + head * dk, dk)]
        pre = exact(rank[at, :], ru, ((1,), (0,))) + bias
        dlog = jax.nn.log_sigmoid(pre) * (1.0 / GATE_NORM)
        k_low = proj[:, :dk].astype(BF16)
        v_low = proj[:, dk:].astype(BF16)
        k[h, at, :] = k_low
        v[h, at, :] = v_low
        dpre[h, at, :] = pre
        for j in range(per):
            part = slice(j * CHUNK, (j + 1) * CHUNK)
            c = b * per + j
            ch = exact(ones, dlog[part], ((1,), (0,)))
            end = ch[CHUNK - 1 :]
            ke = (k_low[part].astype(F32) * jnp.exp(end - ch)).astype(BF16)
            state = st[...]
            offset = off[...]
            cum[h, pl.ds(pl.multiple_of(c * CHUNK, CHUNK), CHUNK), :] = ch
            sin[h, c] = state.astype(BF16)
            off_o[h, c] = offset
            st[...] = state * jnp.exp(end) + dot_tn(v_low[part], ke)
            off[...] = offset + end

        @pl.when(b == blocks - 1)
        def _():
            tot_s[h] = st[...]
            mult = restart * jnp.exp(off[...])
            tot_m[h] = mult
            mult_o[h] = mult

        return 0

    def second_step(h, i, _):
        b = i
        at = pl.ds(pl.multiple_of(b * BLOCK, BLOCK), BLOCK)
        proj = dot(rows[at, :], w[h, :, kv:])
        q_low = proj[:, :dk].astype(BF16)
        q[h, at, :] = q_low
        sw[h, at, :] = proj[:, dk:]
        for j in range(per):
            part = slice(j * CHUNK, (j + 1) * CHUNK)
            c = b * per + j
            this = pl.ds(pl.multiple_of(c * CHUNK, CHUNK), CHUNK)
            ch = cum[h, this, :]
            mid_row = ch[HALF - 1 : HALF]
            qf = q_low[part].astype(F32) * scale
            kf = k[h, this, :].astype(F32)
            qd = (qf * jnp.exp(ch - mid_row)).astype(BF16)
            kd = (kf * jnp.exp(mid_row - ch)).astype(BF16)
            qi = (qf * jnp.exp(ch)).astype(BF16)
            scores = jnp.where(mask, dot_nt(qd, kd), 0.0).astype(BF16)
            mx[h, this, :] = dot(scores, v[h, this, :]) + dot_nt(qi, sin[h, c])
            reach[h, this, :] = (qf * jnp.exp(ch + off_o[h, c])).astype(BF16)
        return 0

    lax.fori_loop(0, blocks, functools.partial(first_step, 0), 0)
    kv_in.forward()
    cot_row[0].start()
    lax.fori_loop(0, blocks, functools.partial(second_step, 0), 0)
    kv_in.done()
    qs_in.forward()
    wo_in.relay()
    lax.fori_loop(0, blocks, functools.partial(first_step, 1), 0)
    scan.begin()
    cot_row[1].start()
    for src, dst in ((k, k_h), (v, v_h), (cum, cum_h), (dpre, dpre_h), (rank, rank_h), (sin, sin_h)):
        store(src, dst)
    qs_in.done()
    wo_in.forward()
    lax.fori_loop(0, blocks, functools.partial(second_step, 1), 0)
    for src, dst in ((q, q_h), (sw, s_h), (reach, reach_h), (w, w_h)):
        store(src, dst)
    while scan.advance():
        pass
    for h in range(2):
        enter_o[h] = restart * pre_s[h]
    wo_in.done()
    store(wo, wo2_h)

    def gate_step(i, _):
        b = jnp.where(i < 2, 2 - 2 * where.core + i, 2 * where.core + i - 2)
        at = pl.ds(pl.multiple_of(b * blk, blk), blk)
        total = None
        for h in range(2):
            mixed = mx[h, at, :] + dot_nt(reach[h, at, :], enter_o[h].astype(BF16))
            inv = lax.rsqrt(jnp.mean(mixed * mixed, axis=-1, keepdims=True) + GROUP_EPS)
            s = sw[h, at, :]
            g = (mixed * inv * gain * (s * jax.nn.sigmoid(s))).astype(BF16)
            mx[h, at, :] = mixed
            gated[h, at, :] = g
            part = dot(g, wo[h])
            total = part if total is None else total + part
        for j in range(2):

            @pl.when(i == j)
            def _():
                tb[j] = total.astype(BF16)
                terms[j].start()

            @pl.when(i == 2 + j)
            def _():
                mid[pl.ds(j * blk, blk), :] = tok[pl.ds(j * blk, blk), :].astype(F32) + total

        return 0

    lax.fori_loop(0, 4, gate_step, 0)
    for i in range(2):
        cot_row[i].wait_recv()
        cot_both[i].start()
    for src, dst in ((mx, mx_h), (gated, gated_h)):
        store(src, dst)
    for j in range(2):
        at = pl.ds(j * blk, blk)
        terms[j].wait_recv()
        mid[at, :] += tr[j].astype(F32)
    store(mid, mid_h)
    cot_core.wait_recv()
    for copy in cot_both:
        copy.wait_recv()
    for copy in stores:
        copy.wait()
    wires.drain()


def front_phase(tokens, cotangent, kw, vw, qw, sw, wo, rd, ru, row):
    bits = wide_bits()
    half, d = tokens.shape
    count = 2 * half
    dk, dv, rk = kw.shape[1], vw.shape[1], rd.shape[0]
    chunks, n_bits = count // CHUNK, len(bits)
    hbm = pl.BlockSpec(memory_space=pltpu.HBM)
    vmem = pl.BlockSpec(memory_space=pltpu.VMEM)
    dma = pltpu.SemaphoreType.DMA
    v_ = pltpu.VMEM
    out_shape = [
        sds((half, d), F32), sds((count, d), BF16), sds((2, count, dk), BF16), sds((2, count, dk), BF16),
        sds((2, count, dv), BF16), sds((2, count, dv), F32), sds((2, count, dk), F32), sds((2, count, dk), F32),
        sds((count, rk), F32), sds((2, count, dk), BF16), sds((2, chunks, dv, dk), BF16), sds((2, count, dv), F32),
        sds((2, count, dv), BF16), sds((2, d, 2 * dk + 2 * dv), BF16), sds((2, dv, d), BF16),
        sds((half, d), BF16), sds((half, d), BF16), sds((half, d), BF16),
        sds((2, chunks, 1, dk), F32), sds((2, dv, dk), F32), sds((2, 1, dk), F32),
    ]
    scratch = [
        v_((half, d), BF16), v_((count, d), BF16), v_((2, d, 2 * dk + 2 * dv), BF16), v_((2, dv, d), BF16),
        v_((2, count, dk), BF16), v_((2, count, dk), BF16), v_((2, count, dv), BF16), v_((2, count, dv), F32),
        v_((2, count, dk), F32), v_((2, count, dk), F32), v_((count, rk), F32), v_((2, count, dk), BF16),
        v_((2, chunks, dv, dk), BF16), v_((2, count, dv), F32), v_((2, count, dv), BF16),
        v_((2, half // 2, d), BF16), v_((2, half // 2, d), BF16), v_((half, d), F32), v_((dv, dk), F32), v_((1, dk), F32),
        v_((2, dv, dk), F32), v_((2, 1, dk), F32), v_((2, dv, dk), F32), v_((2, 1, dk), F32),
        v_((n_bits + 1, 2, dv + 16, dk), BF16), v_((n_bits + 1, 2, dv + 16, dk), BF16),
        dma((8,)), dma((48,)), dma((48,)), dma((20,)),
    ]
    return pl.pallas_call(
        functools.partial(front_phase_kernel, bits),
        name="front_phase",
        in_specs=[hbm] * 7 + [vmem] * 3,
        out_specs=[hbm] * 18 + [vmem] * 3,
        out_shape=out_shape,
        scratch_shapes=scratch,
        compiler_params=pltpu.CompilerParams(collective_id=3, has_side_effects=True, vmem_limit_bytes=60 << 20),
        cost_estimate=cost(12e9, 60e6, 1e6),
    )(tokens, cotangent, kw, vw, qw, sw, wo, rd, ru, row)


def tile_of(step):
    return jnp.where((step == 5) | (step == 6), 11 - step, step)


def mlp_phase_kernel(
    bits,
    mid_h, c0_h, c1_h, c2_h, c3_h, wg_h, wu_h, wd_h, row_ref,
    gmid_h, gm_h, part_ref, gg_h, gu_h, gd_h, near_h, far_h,
    mid, xs, cs, wg, wu, wd, hs, ggs, gus, gn, rc, rd, ac, ry, dn, dnr, gmb, sum_g, sum_u, sum_d, got_g, got_u,
    load_sem, send_sem, recv_sem, out_sem,
):
    tile = xs.shape[0] // 8
    rows = 2 * tile
    d = xs.shape[1]

    def rows_of(t):
        return lanes_at(t * tile, tile)

    where = Places(2 ** len(bits))
    wires = Wires(send_sem, recv_sem)
    by_core, by_row = where.by_core, where.by_row

    loads = [pltpu.make_async_copy(mid_h, mid, load_sem.at[0])]
    for i, (src, dst) in enumerate(((wg_h, wg), (wu_h, wu), (wd_h, wd))):
        loads.append(pltpu.make_async_copy(src, dst, load_sem.at[1 + i]))
    for i, src in enumerate((c0_h, c1_h, c2_h, c3_h)):
        for j in range(2):
            loads.append(
                pltpu.make_async_copy(src.at[pl.ds(j * tile, tile)], cs.at[rows_of(2 * i + j)], load_sem.at[4 + 2 * i + j])
            )
    for load in loads:
        load.start()
    stores = []

    def store(src, dst):
        copy = pltpu.make_async_copy(src, dst, out_sem.at[len(stores)])
        stores.append(copy)
        copy.start()

    where.meet()
    x_row = [wires.copy(xs.at[rows_of(j)], xs.at[rows_of(4 + j)], by_row) for j in range(2)]
    x_core = [wires.copy(xs.at[rows_of(j)], xs.at[rows_of(2 + j)], by_core) for j in range(2)]
    x_both = [wires.copy(xs.at[rows_of(4 + j)], xs.at[rows_of(6 + j)], by_core) for j in range(2)]
    g_near = [wires.copy(gn.at[2 + j], rc.at[j], by_core) for j in range(2)]
    g_far = [wires.copy(gn.at[6 + j], rd.at[j], by_core) for j in range(2)]
    g_row = [wires.copy(ac.at[j], ry.at[j], by_row) for j in range(2)]
    d_in = [wires.copy(dn.at[(2, 3, 6, 7)[j]], dnr.at[j], by_core) for j in range(4)]
    left = sorted(bits, reverse=True)

    def first_hop(total, got, bit):
        dim, mine = left.index(bit), where.has(bit)
        mids = (slice(None),) * (dim - 1)
        copies = [
            wires.copy(total.at[(top,) + mids + (1 - mine,)], got.at[top], where.across(bit)) for top in range(2)
        ]

        def finish():
            for copy in copies:
                copy.wait_recv()
            for at in itertools.product(range(2), repeat=len(bits) - 1):
                own = at[:dim] + (mine,) + at[dim:]
                got[at] = (got[at].astype(F32) + total[own].astype(F32)).astype(BF16)

        return copies, finish

    hop_g, end_g = first_hop(sum_g, got_g, bits[0])
    hop_u, end_u = first_hop(sum_u, got_u, bits[1])
    gain = row_ref[:, d : 2 * d]

    loads[0].wait()
    for j in range(2):
        m = mid[pl.ds(j * tile, tile), :]
        inv = lax.rsqrt(jnp.mean(m * m, axis=-1, keepdims=True) + NORM_EPS)
        xs[rows_of(j), :] = (m * inv * gain).astype(BF16)
        x_row[j].start()
        x_core[j].start()
    for load in loads[1:]:
        load.wait()

    def step(s, _):
        t = tile_of(s)
        at = rows_of(t)

        @pl.when(s == 2)
        def _():
            x_core[0].wait_recv()

        @pl.when(s == 3)
        def _():
            x_core[1].wait_recv()

        for j in range(2):

            @pl.when(s == 4 + 2 * j)
            def _():
                x_row[j].wait_recv()
                x_both[j].start()

            @pl.when(s == 5 + 2 * j)
            def _():
                x_both[j].wait_recv()

        x = xs[at, :]
        gate = dot_nt(x, wg[...])
        up = dot_nt(x, wu[...])
        gh = dot_nt(cs[at, :], wd[...])
        sig = jax.nn.sigmoid(gate)
        act = gate * sig
        hidden = (act * up).astype(BF16)
        g_up = (gh * act).astype(BF16)
        g_gate = (gh * up * sig * (1.0 + gate * (1.0 - sig))).astype(BF16)
        hs[at, :] = hidden
        ggs[at, :] = g_gate
        gus[at, :] = g_up
        gn[t] = (dot(g_gate, wg[...]) + dot(g_up, wu[...])).astype(BF16)

        for j in range(2):

            @pl.when(s == 2 + j)
            def _():
                g_near[j].start()

            @pl.when(s == 5 + 2 * j)
            def _():
                g_far[j].start()

        dn[t] = dot(hidden, wd[...]).astype(BF16)

        for j in range(2):

            @pl.when(s == 5 + 2 * j)
            def _():
                g_far[j].wait_recv()
                ac[j] = (gn[4 + j].astype(F32) + rd[j].astype(F32)).astype(BF16)
                g_row[j].start()

        return 0

    lax.fori_loop(0, 8, step, 0)
    for copy in d_in:
        copy.start()

    size = 256
    count = d // size

    def weight_grad(lefts, rights, total, copies):
        def step(j, _):
            cols = lanes_at(j * size, size)
            acc = dot_tn(lefts[:, cols], rights[...])
            put_rows(total, (), j, size, bits, slice(None), acc.astype(BF16))
            for top, copy in enumerate(copies):

                @pl.when(j == (top + 1) * count // 2 - 1)
                def _():
                    copy.start()

            return 0

        lax.fori_loop(0, count, step, 0)

    part = jnp.zeros((1, d), F32)

    def final(j, part):
        at = pl.ds(j * tile, tile)
        g_near[j].wait_recv()
        g_row[j].wait_recv()
        grad = gn[j].astype(F32) + rc[j].astype(F32) + ry[j].astype(F32)
        m = mid[at, :]
        inv = lax.rsqrt(jnp.mean(m * m, axis=-1, keepdims=True) + NORM_EPS)
        unit = m * inv
        weighted = grad * gain
        part = part + jnp.sum(grad * unit, axis=0, keepdims=True)
        gmid = cs[rows_of(j), :].astype(F32) + inv * (weighted - unit * jnp.mean(weighted * unit, axis=-1, keepdims=True))
        mid[at, :] = gmid
        gmb[j] = gmid.astype(BF16)
        there = gm_h.at[lanes_at(where.core * rows + j * tile, tile)]
        store(gmb.at[j], there)
        store(mid.at[at], gmid_h.at[at])
        gm_out[j].start()
        return part

    gm_out = []
    for j in range(2):
        there = gm_h.at[lanes_at(where.core * rows + j * tile, tile)]
        gm_out.append(wires.copy(gmb.at[j], there, by_core))

    weight_grad(xs, ggs, sum_g, hop_g)
    weight_grad(xs, gus, sum_u, hop_u)
    part = final(0, part)
    weight_grad(cs, hs, sum_d, [])
    store(sum_d, gd_h)
    for j in range(2):
        d_in[j].wait_recv()
        d_in[2 + j].wait_recv()
        for at, extra, out in ((j, j, near_h), (4 + j, 2 + j, far_h)):
            dn[at] = (dn[at].astype(F32) + dnr[extra].astype(F32)).astype(BF16)
            store(dn.at[at], out.at[pl.ds(j * tile, tile)])
    end_g()
    store(got_g, gg_h)
    part_ref[...] = final(1, part)
    end_u()
    store(got_u, gu_h)
    for copy in gm_out:
        copy.wait_recv()
    for copy in stores:
        copy.wait()
    wires.drain()


def mlp_phase(middle, cots, wg_t, wu_t, wd, row):
    bits = wide_bits()
    rows, d = middle.shape
    ff = wd.shape[0]
    tile = rows // 2
    hbm = pl.BlockSpec(memory_space=pltpu.HBM)
    vmem = pl.BlockSpec(memory_space=pltpu.VMEM)
    dma = pltpu.SemaphoreType.DMA
    v_ = pltpu.VMEM
    block = (d // 2 ** len(bits), ff)
    full, part = (2,) * len(bits) + block, (2,) * (len(bits) - 1) + block
    return pl.pallas_call(
        functools.partial(mlp_phase_kernel, bits),
        name="mlp_phase",
        in_specs=[hbm] * 8 + [vmem],
        out_specs=[hbm, hbm, vmem] + [hbm] * 5,
        out_shape=[sds((rows, d), F32), sds((2 * rows, d), BF16), sds((1, d), F32)]
        + [sds(part, BF16), sds(part, BF16), sds(full, BF16)] + [sds((rows, d), BF16)] * 2,
        scratch_shapes=[
            v_((rows, d), F32), v_((8 * tile, d), BF16), v_((8 * tile, d), BF16),
            v_((ff, d), BF16), v_((ff, d), BF16), v_((ff, d), BF16),
            v_((8 * tile, ff), BF16), v_((8 * tile, ff), BF16), v_((8 * tile, ff), BF16),
            v_((8, tile, d), BF16), v_((2, tile, d), BF16), v_((2, tile, d), BF16),
            v_((2, tile, d), BF16), v_((2, tile, d), BF16), v_((8, tile, d), BF16), v_((4, tile, d), BF16),
            v_((2, tile, d), BF16), v_(full, BF16), v_(full, BF16), v_(full, BF16), v_(part, BF16), v_(part, BF16),
            dma((12,)), dma((24,)), dma((24,)), dma((12,)),
        ],
        compiler_params=pltpu.CompilerParams(collective_id=1, has_side_effects=True, vmem_limit_bytes=63 << 20),
        cost_estimate=cost(18 * 4 * rows * d * ff, 60e6, 4 * rows * ff),
    )(middle, *cots, wg_t, wu_t, wd, row)


def back_phase_kernel(
    bits,
    gm_h, mx_h, s_h, r_h, gt_h, rows_h, q_h, k_h, v_h, cum_h, dpre_h, rank_h, sin_h, w_h, wo_h, g_h, gmid_h, tok_h, far_h,
    off_ref, enter_ref, mult_ref, ru_ref, rd_ref, row_ref, mpart_ref,
    in_h, fr_h, gate_o, up_o, down_o, wout_o, k_o, v_o, q_o, s_o, rdown_o, rup_o, bias_o, mgain_o, group_o, ngain_o,
    gm, mx, sw, reach, gated, rows, q, k, v, cum, dpre, rank, sin, w, wo, held, mrecv, gmid, tok,
    gx, al, grank, ds, lb_m, pre_s, pre_m, sc_out, sc_in, osv, osy, osr, kva, kvay, kvar, kvb, kvbr, kvbo, tb, tr,
    sm, smf, smv, smr, smo, ng, ngr,
    load_sem, send_sem, recv_sem, out_sem,
):
    count, d = rows.shape
    half = count // 2
    dk, dv = q.shape[2], v.shape[2]
    where = Places(2 ** len(bits))
    wires = Wires(send_sem, recv_sem)
    loads = []

    def load(src, dst):
        copy = pltpu.make_async_copy(src, dst, load_sem.at[len(loads)])
        loads.append(copy)
        copy.start()
        return copy

    orders = (bits[1:], bits[:1] + bits[2:], bits)
    third = [load(g_h[0], held[0]), load(g_h[1], held[1])]
    first = [load(gm_h, gm), load(wo_h, wo), load(mx_h, mx), load(s_h, sw), load(r_h, reach)]
    second = [load(gt_h, gated), load(rows_h, rows)]
    dim = sorted(bits, reverse=True).index(bits[0])
    keep = load(g_h[2].at[(slice(None),) * dim + (where.has(bits[0]),)], held[2])
    fourth = [load(rank_h, rank)]
    for src, dst in ((q_h, q), (k_h, k), (v_h, v), (cum_h, cum), (dpre_h, dpre), (sin_h, sin), (w_h, w)):
        fourth.append(load(src, dst))
    fifth = [load(gmid_h, gmid), load(tok_h, tok)]

    where.meet()
    mlp = [
        Scatter(where, wires, held[0], None, orders[0], mrecv[0]),
        Scatter(where, wires, held[1], None, orders[1], mrecv[1]),
        Scatter(where, wires, g_h[2], held[2], orders[2], mrecv[2]),
    ]
    scan = Scan(where, wires, ds, lb_m, pre_s, pre_m, sc_out, sc_in, True)
    os_y = wires.copy(osv.at[1], osy, where.by_row)
    os_s = Scatter(where, wires, osv.at[0], None, bits, osr)
    kva_y = wires.copy(kva.at[1], kvay, where.by_row)
    kva_s = Scatter(where, wires, kva.at[0], None, bits, kvar)
    kvb_s = [Scatter(where, wires, kvb.at[h], None, bits, kvbr[h]) for h in range(2)]
    kvb_y = wires.copy(kvbo.at[0], kvbo.at[1], where.by_row)
    tots = [wires.copy(tb.at[j], tr.at[j], where.by_core) for j in range(2)]
    far = []
    for j in range(4):
        at = pl.ds(j * (half // 4), half // 4)
        far.append(wires.copy(far_h.at[at], fr_h.at[at], where.by_row))
    every = Shared(where, wires, sm, smf, smv, smr, smo)
    every_n = Everywhere(where, wires, ng, ngr)
    n_bits = len(bits)
    at_row = row_places(d, dv, 4 * dk)
    ngain = row_ref[:, at_row[0] : at_row[1]]
    gain = row_ref[:, at_row[2] : at_row[3]]
    restart = row_ref[:, at_row[4] : at_row[4] + dk]
    far[0].start()
    for copy in third:
        copy.wait()
    mlp[1].go()
    mlp[0].go()

    blk = half // 2
    ds[...] = jnp.zeros_like(ds)
    sm[...] = jnp.zeros_like(sm)
    for copy in first:
        copy.wait()

    def gate_step(i, part):
        at = pl.ds(pl.multiple_of(i * blk, blk), blk)
        g = gm[at, :]
        for h in range(2):
            grad = dot_nt(g, wo[h])
            mixed = mx[h, at, :]
            inv = lax.rsqrt(jnp.mean(mixed * mixed, axis=-1, keepdims=True) + GROUP_EPS)
            unit = mixed * inv
            s = sw[h, at, :]
            sig = jax.nn.sigmoid(s)
            al[h, at, 2 * dk + dv :] = (grad * unit * gain * (sig * (1.0 + s * (1.0 - sig)))).astype(BF16)
            dn = grad * (s * sig)
            part = part + jnp.sum(dn * unit, axis=0, keepdims=True)
            weighted = dn * gain
            gmix = (inv * (weighted - unit * jnp.mean(weighted * unit, axis=-1, keepdims=True))).astype(BF16)
            gx[h, at, :] = gmix
            ds[h] += dot_tn(gmix, reach[h, at, :])
        return part

    group_part = lax.fori_loop(0, 4, gate_step, jnp.zeros((1, dv), F32))
    for h in range(2):
        ds[h] = ds[h] * restart
        lb_m[h] = mult_ref[h]
    scan.begin()

    size = 256

    def out_step(j, _):
        cols = pl.ds(pl.multiple_of(j * size, size), size)
        for h in (1, 0):
            value = dot_tn(gm[:, cols], gated[h]).astype(BF16)
            put_rows(osv, (h,), j, size, bits, slice(0, dv), value)
        return 0

    def swish_step(j, _):
        cols = pl.ds(pl.multiple_of(j * size, size), size)
        for h in (1, 0):
            value = dot_tn(rows[:, cols], al[h, :, 2 * dk + dv :]).astype(BF16)
            put_rows(osv, (h,), j, size, bits, slice(dv, 2 * dv), value)
        return 0

    for copy in second:
        copy.wait()
    lax.fori_loop(0, d // size, out_step, 0)
    lax.fori_loop(0, d // size, swish_step, 0)
    scan.advance()
    os_y.start()
    scan.advance()
    keep.wait()
    mlp[2].go()
    while scan.advance():
        pass
    mlp[0].advance()
    mlp[1].advance()
    for copy in fourth:
        copy.wait()

    ds[...] = pre_s[...]
    chunks = count // CHUNK
    mask = triangle(True)
    ones = triangle(False).astype(F32)
    scale = dk**-0.5
    rk = rank.shape[1]

    def add_row(ref, extra):
        for at in itertools.product(range(2), repeat=n_bits):
            ref[(0,) + at] = (ref[(0,) + at].astype(F32) + extra[at].astype(F32)).astype(BF16)

    def back_step(step, carry):
        c = chunks - 1 - step

        @pl.when(step == chunks // 2)
        def _():
            mlp[2].advance()

        @pl.when(step == chunks - 3)
        def _():
            os_y.wait_recv()
            add_row(osv, osy)
            os_s.go()
            far[1].start()

        at = pl.ds(pl.multiple_of(c * CHUNK, CHUNK), CHUNK)
        grs, new = None, []
        for h in range(2):
            ch = cum[h, at, :]
            mid = ch[HALF - 1 : HALF]
            end = ch[CHUNK - 1 :]
            e_qd, e_kd, e_qi, e_ke = jnp.exp(ch - mid), jnp.exp(mid - ch), jnp.exp(ch), jnp.exp(end - ch)
            e_end = jnp.exp(end)
            qf = q[h, at, :].astype(F32) * scale
            kf = k[h, at, :].astype(F32)
            vc = v[h, at, :]
            qd = (qf * e_qd).astype(BF16)
            kd = (kf * e_kd).astype(BF16)
            qi = (qf * e_qi).astype(BF16)
            ke = (kf * e_ke).astype(BF16)
            go = gx[h, at, :]
            ru = ru_ref[:, lanes_at(((where.place + 2 * h) % 4) * dk, dk)].astype(F32)
            state = sin[h, c].astype(F32) + enter_ref[h] * jnp.exp(off_ref[h, c])
            state_low = state.astype(BF16)
            dstate = ds[h]
            dstate_low = dstate.astype(BF16)
            scores = jnp.where(mask, dot_nt(qd, kd), 0.0).astype(BF16)
            dscores = jnp.where(mask, dot_nt(go, vc), 0.0).astype(BF16)
            d_v = dot_tn(scores, go) + dot_nt(ke, dstate_low)
            d_qd = dot(dscores, kd)
            d_qi = dot(go, state_low)
            d_kd = dot_tn(dscores, qd)
            d_ke = dot(vc, dstate_low)
            d_q = scale * (d_qd * e_qd + d_qi * e_qi)
            d_k = d_kd * e_kd + d_ke * e_ke
            tail = ke.astype(F32) * d_ke
            d_cum = qd.astype(F32) * d_qd + qi.astype(F32) * d_qi - kd.astype(F32) * d_kd - tail
            d_end = jnp.sum(tail, axis=0, keepdims=True) + e_end * jnp.sum(dstate * state, axis=0, keepdims=True)
            grad_decay = exact(ones, d_cum, ((1,), (0,))) + d_end
            g_pre = grad_decay * jax.nn.sigmoid(-dpre[h, at, :]) * (1.0 / GATE_NORM)
            al[h, at, :dk] = d_k.astype(BF16)
            al[h, at, dk : dk + dv] = d_v.astype(BF16)
            al[h, at, dk + dv : 2 * dk + dv] = d_q.astype(BF16)
            gr = exact(g_pre, ru, ((1,), (1,)))
            grs = gr if grs is None else grs + gr
            new.append(carry[2 * h] + exact(rank[at, :], g_pre, ((0,), (0,))))
            new.append(carry[2 * h + 1] + jnp.sum(g_pre, axis=0, keepdims=True))
            ds[h] = dstate * e_end + dot_tn(go, qi)
        grank[at, :] = grs.astype(BF16)
        return tuple(new)

    zero = (jnp.zeros((rk, dk), F32), jnp.zeros((1, dk), F32))
    rup0, gb0, rup1, gb1 = lax.fori_loop(0, chunks, back_step, zero + zero)
    qk = 4 * dk
    sm[0] = dot_tn(grank[...], rows[...])
    at0 = where.place * dk
    at1 = ((where.place + 2) % 4) * dk
    sm[1, :, lanes_at(at0, dk)] = rup0
    sm[1, :, lanes_at(at1, dk)] = rup1
    sm[1, 0:1, lanes_at(qk + at0, dk)] = gb0
    sm[1, 0:1, lanes_at(qk + at1, dk)] = gb1
    sm[1, 1:2, qk : qk + dv] = group_part
    for i in range(d // qk):
        sm[1, 2 + i : 3 + i, qk : 2 * qk] = mpart_ref[:, i * qk : (i + 1) * qk]
    every.begin()
    def kvq_step(ref, h, low):
        def step(j, _):
            cols = lanes_at(j * size, size)
            value = dot_tn(rows[:, cols], al[h, :, low : low + size]).astype(BF16)
            put_rows(ref, (h,), j, size, bits, slice(None), value)
            return 0

        lax.fori_loop(0, d // size, step, 0)

    kvq_step(kva, 1, 0)
    kva_y.start()
    for h in range(2):
        kvq_step(kvb, h, size)
        kvb_s[h].go()
    mlp[2].advance()
    os_s.advance()

    def total_step(i, _):
        b = jnp.where(i < 2, 2 - 2 * where.core + i, 2 * where.core + i - 2)
        at = pl.ds(pl.multiple_of(b * blk, blk), blk)
        total = dot_nt(al[0, at, :], w[0]) + dot_nt(al[1, at, :], w[1]) + dot(grank[at, :], rd_ref[...])
        for j in range(2):

            @pl.when(i == j)
            def _():
                tb[j] = total.astype(BF16)
                tots[j].start()

            @pl.when(i == 2 + j)
            def _():
                tb[2 + j] = total.astype(BF16)

        return 0

    every.advance()
    lax.fori_loop(0, 4, total_step, 0)

    kvq_step(kva, 0, 0)
    every.advance()

    for copy in fifth:
        copy.wait()
    part = jnp.zeros((1, d), F32)
    for j in range(2):
        at = pl.ds(j * blk, blk)
        tots[j].wait_recv()
        grad = tb[2 + j].astype(F32) + tr[j].astype(F32)
        x = tok[at, :].astype(F32)
        inv = lax.rsqrt(jnp.mean(x * x, axis=-1, keepdims=True) + NORM_EPS)
        unit = x * inv
        weighted = grad * ngain
        part = part + jnp.sum(grad * unit, axis=0, keepdims=True)
        gmid[at, :] = gmid[at, :] + inv * (weighted - unit * jnp.mean(weighted * unit, axis=-1, keepdims=True))
    done = pltpu.make_async_copy(gmid, in_h, out_sem.at[0])
    done.start()
    for i in range(8):
        ng[0, i : i + 1, :] = part[:, i * (d // 8) : (i + 1) * (d // 8)]
    every_n.begin()

    kva_y.wait_recv()
    far[2].start()
    far[3].start()
    add_row(kva, kvay)
    kva_s.go()
    for part in kvb_s:
        part.advance()
    os_s.advance()
    every.advance()
    every_n.advance()
    for i, out in ((0, gate_o), (1, up_o)):
        out[...] = jnp.transpose(mlp[i].result())
    for i in range(n_bits - 1):
        kva_s.advance()
        if i < n_bits - 2:
            for part in kvb_s:
                part.advance()
        every.advance()
        every_n.advance()
    kvbo[0] = kvb_s[1].result().astype(BF16)
    kvb_y.start()
    down_o[...] = jnp.transpose(mlp[2].result())
    total = os_s.result()
    wout_o[...] = jnp.transpose(total[:, :dv])
    s_o[...] = total[:, dv:]
    every.advance()
    every_n.advance()
    first_half = kva_s.result()
    last_half = kvb_s[0].result()
    kvb_y.wait_recv()
    last_half = last_half + kvbo[1].astype(F32)
    k_o[...] = first_half[:, :dk]
    v_o[:, : size - dk] = first_half[:, dk:]
    v_o[:, size - dk :] = last_half[:, : dk + dv - size]
    q_o[...] = last_half[:, dk + dv - size :]
    small = every.result()
    rdown_o[...] = small[0]
    rup_o[...] = small[1, :, :qk]
    bias_o[...] = small[1, 0:1, qk : 2 * qk]
    group_o[...] = small[1, 1:2, qk : qk + dv]
    for i in range(d // qk):
        mgain_o[:, i * qk : (i + 1) * qk] = small[1, 2 + i : 3 + i, qk : 2 * qk]
    whole_n = every_n.result()
    for i in range(8):
        ngain_o[:, i * (d // 8) : (i + 1) * (d // 8)] = whole_n[i : i + 1, :]
    for copy in far:
        copy.wait_recv()
    done.wait()
    wires.drain()


def back_phase(
    gm, mx, s, reach, gated, rows, q, k, v, cum, dpre, rank, sin, w, wo, grads, gmid, tokens, far,
    off, enter, mult, ru, rd, row, mpart,
):
    bits = wide_bits()
    count, d = rows.shape
    half = count // 2
    dk, dv, rk = q.shape[2], v.shape[2], rank.shape[1]
    ff = grads[0].shape[-1]
    each = d // 2 ** len(bits)
    n_bits, chunks = len(bits), count // CHUNK
    hbm = pl.BlockSpec(memory_space=pltpu.HBM)
    vmem = pl.BlockSpec(memory_space=pltpu.VMEM)
    dma = pltpu.SemaphoreType.DMA
    v_ = pltpu.VMEM

    def shape(lead, cols):
        return (2,) * lead + (each, cols)

    def falls(cols):
        return [v_(shape(n_bits - 1 - i, cols), BF16) for i in range(n_bits)]

    pair, three = [hbm] * 2, [hbm] * 3
    kvq = 2 * dk + dv
    scratch = [
        v_((count, d), BF16), v_((2, count, dv), F32), v_((2, count, dv), F32), v_((2, count, dk), BF16),
        v_((2, count, dv), BF16), v_((count, d), BF16), v_((2, count, dk), BF16), v_((2, count, dk), BF16),
        v_((2, count, dv), BF16), v_((2, count, dk), F32), v_((2, count, dk), F32), v_((count, rk), F32),
        v_((2, chunks, dv, dk), BF16), v_((2, d, kvq + dv), BF16), v_((2, dv, d), BF16),
        [v_(shape(n_bits - 1, ff), BF16)] * 3, [falls(ff)[1:], falls(ff)[1:], falls(ff)], v_((half, d), F32), v_((half, d), BF16),
        v_((2, count, dv), BF16), v_((2, count, kvq + dv), BF16), v_((count, rk), BF16),
        v_((2, dv, dk), F32), v_((2, 1, dk), F32), v_((2, dv, dk), F32), v_((2, 1, dk), F32),
        v_((n_bits + 1, 2, dv + 16, dk), BF16), v_((n_bits + 1, 2, dv + 16, dk), BF16),
        v_((2,) + shape(n_bits, 2 * dv), BF16), v_(shape(n_bits, 2 * dv), BF16), falls(2 * dv),
        v_((2,) + shape(n_bits, 256), BF16), v_(shape(n_bits, 256), BF16), falls(256),
        v_((2,) + shape(n_bits, 256), BF16), [falls(256), falls(256)], v_((2, each, 256), BF16),
        v_((4, half // 2, d), BF16), v_((2, half // 2, d), BF16),
        v_((2, rk, d), F32), v_((rk, d), F32), v_((n_bits + 1, rk, d), F32), v_((n_bits + 1, rk, d), F32), v_((2, rk, d), F32),
        v_((n_bits + 3, 8, d // 8), F32), v_((n_bits + 2, 8, d // 8), F32),
        dma((24,)), dma((96,)), dma((96,)), dma((1,)),
    ]
    out_shape = [
        sds((half, d), F32), sds((half, d), BF16), sds((ff, each), F32), sds((ff, each), F32), sds((ff, each), F32), sds((dv, each), F32),
        sds((each, dk), F32), sds((each, dv), F32), sds((each, dk), F32), sds((each, dv), F32),
        sds((rk, d), F32), sds((rk, 4 * dk), F32), sds((1, 4 * dk), F32), sds((1, d), F32), sds((1, dv), F32), sds((1, d), F32),
    ]
    operands = (
        gm, mx, s, reach, gated, rows, q, k, v, cum, dpre, rank, sin, w, wo, grads, gmid, tokens, far,
        off, enter, mult, ru, rd, row, mpart,
    )
    flat, tree = jax.tree.flatten(operands)
    n_vmem = len(jax.tree.leaves(operands[19:]))
    flat_scratch, scratch_tree = jax.tree.flatten(scratch, is_leaf=lambda x: not isinstance(x, list))
    n_in, n_out = len(flat), len(out_shape)

    def kernel(*refs):
        ins = jax.tree.unflatten(tree, refs[:n_in])
        rest = jax.tree.unflatten(scratch_tree, refs[n_in + n_out :])
        back_phase_kernel(bits, *ins, *refs[n_in : n_in + n_out], *rest)

    return pl.pallas_call(
        kernel,
        name="back_phase",
        in_specs=[hbm] * (n_in - n_vmem) + [vmem] * n_vmem,
        out_specs=[hbm, hbm] + [vmem] * (n_out - 2),
        out_shape=out_shape,
        scratch_shapes=flat_scratch,
        compiler_params=pltpu.CompilerParams(collective_id=2, has_side_effects=True, vmem_limit_bytes=62 << 20),
        cost_estimate=cost(40e9, 60e6, 1e6),
    )(*flat)


def finish_kernel(count, mid_ref, near_ref, far_ref, grad_ref, *refs):
    res_ref, in_ref = refs[count : count + 2]
    res_ref[...] = (mid_ref[...] + (near_ref[...].astype(F32) + far_ref[...].astype(F32))).astype(BF16)
    in_ref[...] = grad_ref[...]

    @pl.when(pl.program_id(0) == 0)
    def _():
        for src, dst in zip(refs[:count], refs[count + 2 :]):
            dst[...] = src[...]


def finish(middle, near, far, grad, smalls):
    rows, d = middle.shape
    blk = rows // 4
    row = rows_spec(blk, d)
    wholes = [pl.BlockSpec(v.shape, lambda i: (0, 0)) for v in smalls]
    return pl.pallas_call(
        functools.partial(finish_kernel, len(smalls)),
        name="finish",
        grid=(4,),
        in_specs=[row] * 4 + wholes,
        out_specs=[row] * 2 + wholes,
        out_shape=[sds((rows, d), BF16), sds((rows, d), F32)] + [sds(v.shape, v.dtype) for v in smalls],
        compiler_params=params(62),
    )(middle, near, far, grad, *smalls)


def wide_bits():
    count, bits, bit = lax.axis_size("wide"), [], 1
    while bit < count:
        bits.append(bit)
        bit *= 2
    return bits


def shards(
    tokens, cotangent, flags, norm_gain, query_weight, key_weight, value_weight, swish_weight, rank_down, rank_up,
    decay_bias, group_gain, output_weight, mlp_gain, mlp_gate, mlp_up, mlp_down,
):
    place = lax.axis_index("narrow")
    dk, dv, d = query_weight.shape[1], value_weight.shape[1], tokens.shape[1]
    restart = jnp.where((place & 2) != 0, 1.0, 1.0 - flags[0].astype(F32))
    parts = [part.astype(F32) for part in (norm_gain, mlp_gain, group_gain, decay_bias)]
    row = jnp.concatenate(parts + [jnp.full((dk,), restart, F32)]).reshape(1, -1)
    rd = rank_down.T
    (
        middle, rows_all, q, k, v, s, cum, dpre, rank_pre, reach, sin, mixed, gated, w, weights_out, cot_c, cot_y, cot_d,
        off, enter, mults,
    ) = front_phase(
        tokens, cotangent, key_weight, value_weight, query_weight, swish_weight, output_weight, rd, rank_up, row
    )
    grad_middle, gm_all, mlp_gain_part, gate_g, up_g, down_g, near, far = mlp_phase(
        middle, (cotangent, cot_c, cot_y, cot_d), mlp_gate.T, mlp_up.T, mlp_down, row
    )
    input_grad, far_sum, *smalls = back_phase(
        gm_all, mixed, s, reach, gated, rows_all, q, k, v, cum, dpre, rank_pre, sin,
        w, weights_out, (gate_g, up_g, down_g), grad_middle, tokens, far, off, enter, mults, rank_up, rd, row,
        mlp_gain_part,
    )
    result, input_grad, *smalls = finish(middle, near, far_sum, input_grad, smalls)
    gate_t, up_t, down_t, out_t, k_g, v_g, q_g, s_g, rdown_t, rup_g, bias_g, mgain_g, group_g, ngain = smalls
    return (
        result,
        input_grad,
        ngain[0],
        q_g,
        k_g,
        v_g,
        s_g,
        rdown_t.T,
        rup_g,
        bias_g[0],
        group_g[0],
        out_t,
        mgain_g[0],
        gate_t.T,
        up_t.T,
        down_t,
    )


def solution(mesh):
    rows, cols = P(("wide", "narrow"), None), P(None, "narrow")
    both = P("wide", "narrow")
    in_specs = (
        rows, rows, P("wide"), P(), cols, cols, cols, cols, P(), P(), P(), P(), P("narrow", None), P(), cols, cols,
        P("narrow", None),
    )
    out_specs = (
        rows, rows, P(), both, both, both, both, P(), P(), P(), P(), P("narrow", "wide"), P(), both, both,
        P("narrow", "wide"),
    )
    return jax.shard_map(shards, mesh=mesh, in_specs=in_specs, out_specs=out_specs, check_vma=False)
```

```python
import functools
import itertools

import jax
import jax.numpy as jnp
from jax import lax
from jax.experimental import pallas as pl
from jax.experimental.pallas import tpu as pltpu
from jax.sharding import PartitionSpec as P

NORM_EPS = 1e-06
GROUP_EPS = 1e-05
GATE_NORM = 16.0
HIGHEST_PREC = lax.Precision.HIGHEST
MESH = pl.DeviceIdType.MESH
CHUNK = 128
HALF = CHUNK // 2
BLOCK = 256
F32 = jnp.float32
BF16 = jnp.bfloat16


def dot(a, b):
    return lax.dot_general(a, b, (((1,), (0,)), ((), ())), preferred_element_type=F32)


def dot_nt(a, b):
    return lax.dot_general(a, b, (((1,), (1,)), ((), ())), preferred_element_type=F32)


def dot_tn(a, b):
    return lax.dot_general(a, b, (((0,), (0,)), ((), ())), preferred_element_type=F32)


def exact(a, b, dims):
    return lax.dot_general(
        a, b, (dims, ((), ())), precision=HIGHEST_PREC, preferred_element_type=F32
    )


def sds(shape, dtype):
    return jax.ShapeDtypeStruct(shape, dtype)


def params(mib=48):
    return pltpu.CompilerParams(vmem_limit_bytes=mib << 20)


def cost(flops, nbytes, trans=0):
    return pl.CostEstimate(flops=int(flops), bytes_accessed=int(nbytes), transcendentals=int(trans))


def whole(shape):
    return pl.BlockSpec(shape, lambda i: (0,) * len(shape), pipeline_mode=pl.Buffered(1))


def rows_spec(rows, cols):
    return pl.BlockSpec((rows, cols), lambda i: (i, 0))


def triangle(lower):
    r = lax.broadcasted_iota(jnp.int32, (CHUNK, CHUNK), 0)
    c = lax.broadcasted_iota(jnp.int32, (CHUNK, CHUNK), 1)
    return r >= c if lower else r <= c


class Wires:
    def __init__(self, send_sem, recv_sem):
        self.send_sem, self.recv_sem, self.used, self.all = send_sem, recv_sem, 0, []

    def copy(self, src, dst, target):
        made = pltpu.make_async_remote_copy(
            src,
            dst,
            self.send_sem.at[self.used],
            self.recv_sem.at[self.used],
            device_id=target,
            device_id_type=MESH,
        )
        self.used += 1
        self.all.append(made)
        return made

    def drain(self):
        for made in self.all:
            made.wait_send()


class Places:
    def __init__(self, wide_count):
        self.wide, self.place = lax.axis_index("wide"), lax.axis_index("narrow")
        self.core = self.place % 2
        self.second = self.place // 2
        self.by_core = (self.wide, self.place + 1 - 2 * self.core)
        self.by_row = (self.wide, (self.place + 2) % 4)
        self.bits = []
        bit = 1
        while bit < wide_count:
            self.bits.append(bit)
            bit *= 2

    def has(self, bit):
        return (self.wide // bit) % 2

    def across(self, bit):
        return (self.wide + bit - 2 * bit * self.has(bit), self.place)

    def meet(self):
        barrier = pltpu.get_barrier_semaphore()
        others = [self.by_core, self.by_row] + [self.across(bit) for bit in self.bits]
        for other in others:
            pl.semaphore_signal(barrier, 1, device_id=other, device_id_type=MESH)
        pl.semaphore_wait(barrier, len(others))


class Scan:
    def __init__(self, where, wires, tot_s, tot_m, pre_s, pre_m, out, into, backward):
        self.tot_s, self.tot_m, self.pre_s, self.pre_m = tot_s, tot_m, pre_s, pre_m
        self.out, self.into, self.at, self.order = out, into, 0, (0, 1)
        self.steps = []
        for i, bit in enumerate([0] + where.bits):
            target = where.across(bit) if bit else where.by_row
            is_set = where.has(bit) if bit else where.second
            later = (1 - is_set if backward else is_set) > 0
            copies = [wires.copy(out.at[i, h], into.at[i, h], target) for h in range(2)]
            self.steps.append((copies, later, bit == 0))
        pre_s[...] = jnp.zeros_like(pre_s)
        pre_m[...] = jnp.ones_like(pre_m)

    def send(self, i, h):
        dv = self.tot_s.shape[1]
        self.out[i, h, :dv, :] = self.tot_s[h].astype(BF16)
        self.out[i, h, dv:, :] = jnp.broadcast_to(self.tot_m[h], (16, self.tot_m.shape[2])).astype(BF16)
        self.steps[i][0][h].start()

    def begin(self):
        for h in range(2):
            self.send(0, h)

    def advance(self):
        i, more = self.at, self.at + 1 < len(self.steps)
        copies, later, swapped = self.steps[i]
        dv = self.tot_s.shape[1]
        heads = []
        for g in self.order:
            h = 1 - g if swapped else g
            heads.append(h)
            copies[g].wait_recv()
            oth_s = self.into[i, g, :dv, :].astype(F32)
            oth_m = self.into[i, g, dv : dv + 1, :].astype(F32)
            pre_s, pre_m, tot_s, tot_m = self.pre_s[h], self.pre_m[h], self.tot_s[h], self.tot_m[h]
            if more:
                self.tot_s[h] = jnp.where(later, oth_s * tot_m + tot_s, tot_s * oth_m + oth_s)
                self.tot_m[h] = tot_m * oth_m
                self.send(i + 1, h)
            self.pre_s[h] = jnp.where(later, oth_s * pre_m + pre_s, pre_s)
            self.pre_m[h] = jnp.where(later, oth_m * pre_m, pre_m)
        self.order = tuple(heads)
        self.at = i + 1
        return more


class Scatter:
    def __init__(self, where, wires, source, keep, order, recvs):
        self.recvs, self.steps, self.at = recvs, [], 0
        left = sorted(order, reverse=True)
        held, first = source, keep
        for bit, recv in zip(order, recvs):
            dim = left.index(bit)
            mine = where.has(bit)
            other = held.at[(slice(None),) * dim + (1 - mine,)]
            copy = wires.copy(other, recv, where.across(bit))
            self.steps.append((copy, held if first is None else first, dim, mine, first is not None))
            left.pop(dim)
            held, first = recv, None

    def go(self):
        self.steps[self.at][0].start()

    def land(self):
        total = self.finish(self.at)
        self.at += 1
        return total

    def advance(self):
        if self.at + 1 < len(self.steps):
            self.land()
            self.go()

    def result(self):
        while self.at + 1 < len(self.steps):
            self.advance()
        return self.land()

    def finish(self, i):
        copy, held, dim, mine, picked = self.steps[i]
        copy.wait_recv()
        recv = self.recvs[i]
        last = i == len(self.steps) - 1
        for at in itertools.product(range(2), repeat=len(recv.shape) - 2):
            source = at if picked else at[:dim] + (mine,) + at[dim:]
            total = recv[at].astype(F32) + held[source].astype(F32)
            if last:
                return total
            recv[at] = total.astype(BF16)
        return None


class Everywhere:
    def __init__(self, where, wires, values, recvs):
        self.values, self.recvs = values, recvs
        targets = [where.by_core, where.by_row] + [where.across(bit) for bit in where.bits]
        self.steps = [wires.copy(values.at[i], recvs.at[i], target) for i, target in enumerate(targets)]

    def begin(self, i=0):
        self.at = i
        self.steps[i].start()

    def advance(self):
        if self.at + 1 < len(self.steps):
            self.finish(self.at)
            self.begin(self.at + 1)

    def result(self):
        while self.at + 1 < len(self.steps):
            self.advance()
        self.finish(self.at)
        return self.values[len(self.steps)]

    def finish(self, i):
        self.steps[i].wait_recv()
        self.values[i + 1] = self.values[i] + self.recvs[i]


class Shared:
    def __init__(self, where, wires, parts, first, values, recvs, out):
        self.core, self.parts, self.first = where.core, parts, first
        self.values, self.recvs, self.out, self.at = values, recvs, out, 0
        targets = [where.by_row] + [where.across(bit) for bit in where.bits]
        self.steps = [wires.copy(parts.at[1 - where.core], first, where.by_core)]
        self.steps += [wires.copy(values.at[i], recvs.at[i], target) for i, target in enumerate(targets)]
        self.steps.append(wires.copy(out.at[where.core], out.at[where.core], where.by_core))

    def begin(self):
        self.steps[0].start()

    def advance(self):
        i, last = self.at, len(self.steps) - 1
        if i == last:
            return
        self.steps[i].wait_recv()
        if i == 0:
            total = self.parts[self.core] + self.first[...]
        else:
            total = self.values[i - 1] + self.recvs[i - 1]
        if i + 1 == last:
            self.out[self.core] = total
        else:
            self.values[i] = total
        self.at = i + 1
        self.steps[i + 1].start()

    def result(self):
        while self.at + 1 < len(self.steps):
            self.advance()
        self.steps[-1].wait_recv()
        return self.out


def bit_index(w, bits):
    return tuple((w // bit) % 2 for bit in sorted(bits, reverse=True))


def put_rows(ref, lead, j, size, bits, lanes, value):
    each = ref.shape[-2]
    for p in range(size // each):
        at = lead + bit_index(j * (size // each) + p, bits) + (slice(None), lanes)
        ref[at] = value[p * each : (p + 1) * each]


def lanes_at(start, size):
    return pl.ds(pl.multiple_of(start, size), size)


def row_places(d, dv, qk):
    return (0, d, 2 * d, 2 * d + dv, 2 * d + dv + qk)


def front_phase_kernel(
    bits,
    tok_h, cot_h, kw_h, vw_h, qw_h, sw_h, wo_h, rd_ref, ru_ref, row_ref,
    mid_h, rows_h, q_h, k_h, v_h, s_h, cum_h, dpre_h, rank_h, reach_h, sin_h, mx_h, gated_h, w_h, wo2_h, c1_h, c2_h, c3_h,
    off_o, enter_o, mult_o,
    tok, rows, w, wo, q, k, v, sw, cum, dpre, rank, reach, sin, mx, gated, tb, tr, mid, st, off,
    tot_s, tot_m, pre_s, pre_m, sc_out, sc_in,
    load_sem, send_sem, recv_sem, out_sem,
):
    count, d = rows.shape
    half = count // 2
    blk = half // 2
    dk, dv = q.shape[2], v.shape[2]
    kv = dk + dv
    where = Places(2 ** len(bits))
    wires = Wires(send_sem, recv_sem)
    loads, stores = [], []

    def load(src, dst):
        copy = pltpu.make_async_copy(src, dst, load_sem.at[len(loads)])
        loads.append(copy)
        copy.start()
        return copy

    def store(src, dst):
        copy = pltpu.make_async_copy(src, dst, out_sem.at[len(stores)])
        stores.append(copy)
        copy.start()

    load_tok = load(tok_h, tok)
    load_kv = [load(kw_h, w.at[0, :, pl.ds(0, dk)]), load(vw_h, w.at[0, :, pl.ds(dk, dv)])]
    load_qs = [load(qw_h, w.at[0, :, pl.ds(kv, dk)]), load(sw_h, w.at[0, :, pl.ds(kv + dk, dv)])]
    load_wo = load(wo_h, wo.at[0])

    where.meet()
    at_row = row_places(d, dv, 4 * dk)
    ngain = row_ref[:, at_row[0] : at_row[1]]
    gain = row_ref[:, at_row[2] : at_row[3]]
    restart = row_ref[:, at_row[4] : at_row[4] + dk]

    first_bit, second_bit = where.bits[0], where.bits[1]
    over_a, over_b = where.across(first_bit), where.across(second_bit)
    spot_a, spot_b = where.has(first_bit), where.has(second_bit)

    class Quarters:
        def __init__(self, ref, cols):
            quarter = ref.shape[1] // 4

            def part(of_a, of_b, low, size):
                at = pl.ds(pl.multiple_of((of_a + 2 * of_b) * quarter + low, size), size)
                return (at,) if cols is None else (at, cols)

            mine = part(spot_a, spot_b, 0, quarter)
            from_a = part(1 - spot_a, spot_b, 0, quarter // 2)
            from_b = part(spot_a, 1 - spot_b, quarter // 2, quarter // 2)
            got = ref.at[(1,) + mine]
            self.row = wires.copy(ref.at[(0,) + mine], got, where.by_row)
            self.near = [wires.copy(got, got, over_a), wires.copy(got, got, over_b)]
            self.far = [
                wires.copy(ref.at[(1,) + from_a], ref.at[(1,) + from_a], over_b),
                wires.copy(ref.at[(1,) + from_b], ref.at[(1,) + from_b], over_a),
            ]

        def start(self):
            self.row.start()

        def relay(self):
            self.row.wait_recv()
            for copy in self.near:
                copy.start()

        def forward(self):
            for copy in self.near:
                copy.wait_recv()
            for copy in self.far:
                copy.start()

        def done(self):
            for copy in self.far:
                copy.wait_recv()

    kv_in = Quarters(w, pl.ds(0, kv))
    qs_in = Quarters(w, pl.ds(kv, kv))
    wo_in = Quarters(wo, None)
    cot_row, cot_both = [], []
    for i in range(2):
        at = pl.ds(i * blk, blk)
        cot_row.append(wires.copy(cot_h.at[at], c2_h.at[at], where.by_row))
        cot_both.append(wires.copy(c2_h.at[at], c3_h.at[at], where.by_core))
    cot_core = wires.copy(cot_h, c1_h, where.by_core)
    row_out = []
    for i in range(2):
        at = pl.ds(pl.multiple_of(where.core * half + i * blk, blk), blk)
        row_out.append(wires.copy(rows.at[at], rows.at[at], where.by_core))
    terms = [wires.copy(tb.at[j], tr.at[j], where.by_core) for j in range(2)]
    scan = Scan(where, wires, tot_s, tot_m, pre_s, pre_m, sc_out, sc_in, False)

    for copy in load_kv:
        copy.wait()
    kv_in.start()
    load_tok.wait()
    for i in range(2):
        x = tok[pl.ds(i * blk, blk), :].astype(F32)
        inv = lax.rsqrt(jnp.mean(x * x, axis=-1, keepdims=True) + NORM_EPS)
        rows[pl.ds(pl.multiple_of(where.core * half + i * blk, blk), blk), :] = (x * inv * ngain).astype(BF16)
        row_out[i].start()
    for copy in load_qs:
        copy.wait()
    qs_in.start()
    load_wo.wait()
    wo_in.start()
    for copy in row_out:
        copy.wait_recv()
    cot_core.start()
    store(rows, rows_h)

    mask = triangle(True)
    ones = mask.astype(F32)
    scale = dk**-0.5
    blocks = count // BLOCK
    per = BLOCK // CHUNK

    def first_step(h, i, _):
        b = i
        at = pl.ds(pl.multiple_of(b * BLOCK, BLOCK), BLOCK)
        if h == 0:

            @pl.when(i == 2)
            def _():
                kv_in.relay()

            @pl.when(i == blocks - 1)
            def _():
                qs_in.relay()

        @pl.when(b == 0)
        def _():
            st[...] = jnp.zeros_like(st)
            off[...] = jnp.zeros_like(off)

        x = rows[at, :]

        if h == 0:
            rank[at, :] = dot_nt(x, rd_ref[...])

        proj = dot(x, w[h, :, :kv])
        head = (where.place + 2 * h) % 4
        ru = ru_ref[:, lanes_at(head * dk, dk)].astype(F32)
        bias = row_ref[:, lanes_at(at_row[3] + head * dk, dk)]
        pre = exact(rank[at, :], ru, ((1,), (0,))) + bias
        dlog = jax.nn.log_sigmoid(pre) * (1.0 / GATE_NORM)
        k_low = proj[:, :dk].astype(BF16)
        v_low = proj[:, dk:].astype(BF16)
        k[h, at, :] = k_low
        v[h, at, :] = v_low
        dpre[h, at, :] = pre
        for j in range(per):
            part = slice(j * CHUNK, (j + 1) * CHUNK)
            c = b * per + j
            ch = exact(ones, dlog[part], ((1,), (0,)))
            end = ch[CHUNK - 1 :]
            ke = (k_low[part].astype(F32) * jnp.exp(end - ch)).astype(BF16)
            state = st[...]
            offset = off[...]
            cum[h, pl.ds(pl.multiple_of(c * CHUNK, CHUNK), CHUNK), :] = ch
            sin[h, c] = state.astype(BF16)
            off_o[h, c] = offset
            st[...] = state * jnp.exp(end) + dot_tn(v_low[part], ke)
            off[...] = offset + end

        @pl.when(b == blocks - 1)
        def _():
            tot_s[h] = st[...]
            mult = restart * jnp.exp(off[...])
            tot_m[h] = mult
            mult_o[h] = mult

        return 0

    def second_step(h, i, _):
        b = i
        at = pl.ds(pl.multiple_of(b * BLOCK, BLOCK), BLOCK)
        proj = dot(rows[at, :], w[h, :, kv:])
        q_low = proj[:, :dk].astype(BF16)
        q[h, at, :] = q_low
        sw[h, at, :] = proj[:, dk:]
        for j in range(per):
            part = slice(j * CHUNK, (j + 1) * CHUNK)
            c = b * per + j
            this = pl.ds(pl.multiple_of(c * CHUNK, CHUNK), CHUNK)
            ch = cum[h, this, :]
            mid_row = ch[HALF - 1 : HALF]
            qf = q_low[part].astype(F32) * scale
            kf = k[h, this, :].astype(F32)
            qd = (qf * jnp.exp(ch - mid_row)).astype(BF16)
            kd = (kf * jnp.exp(mid_row - ch)).astype(BF16)
            qi = (qf * jnp.exp(ch)).astype(BF16)
            scores = jnp.where(mask, dot_nt(qd, kd), 0.0).astype(BF16)
            mx[h, this, :] = dot(scores, v[h, this, :]) + dot_nt(qi, sin[h, c])
            reach[h, this, :] = (qf * jnp.exp(ch + off_o[h, c])).astype(BF16)
        return 0

    lax.fori_loop(0, blocks, functools.partial(first_step, 0), 0)
    kv_in.forward()
    cot_row[0].start()
    lax.fori_loop(0, blocks, functools.partial(second_step, 0), 0)
    kv_in.done()
    qs_in.forward()
    wo_in.relay()
    lax.fori_loop(0, blocks, functools.partial(first_step, 1), 0)
    scan.begin()
    cot_row[1].start()
    for src, dst in ((k, k_h), (v, v_h), (cum, cum_h), (dpre, dpre_h), (rank, rank_h), (sin, sin_h)):
        store(src, dst)
    qs_in.done()
    wo_in.forward()
    lax.fori_loop(0, blocks, functools.partial(second_step, 1), 0)
    for src, dst in ((q, q_h), (sw, s_h), (reach, reach_h), (w, w_h)):
        store(src, dst)
    while scan.advance():
        pass
    for h in range(2):
        enter_o[h] = restart * pre_s[h]
    wo_in.done()
    store(wo, wo2_h)

    def gate_step(i, _):
        b = jnp.where(i < 2, 2 - 2 * where.core + i, 2 * where.core + i - 2)
        at = pl.ds(pl.multiple_of(b * blk, blk), blk)
        total = None
        for h in range(2):
            mixed = mx[h, at, :] + dot_nt(reach[h, at, :], enter_o[h].astype(BF16))
            inv = lax.rsqrt(jnp.mean(mixed * mixed, axis=-1, keepdims=True) + GROUP_EPS)
            s = sw[h, at, :]
            g = (mixed * inv * gain * (s * jax.nn.sigmoid(s))).astype(BF16)
            mx[h, at, :] = mixed
            gated[h, at, :] = g
            part = dot(g, wo[h])
            total = part if total is None else total + part
        for j in range(2):

            @pl.when(i == j)
            def _():
                tb[j] = total.astype(BF16)
                terms[j].start()

            @pl.when(i == 2 + j)
            def _():
                mid[pl.ds(j * blk, blk), :] = tok[pl.ds(j * blk, blk), :].astype(F32) + total

        return 0

    lax.fori_loop(0, 4, gate_step, 0)
    for i in range(2):
        cot_row[i].wait_recv()
        cot_both[i].start()
    for src, dst in ((mx, mx_h), (gated, gated_h)):
        store(src, dst)
    for j in range(2):
        at = pl.ds(j * blk, blk)
        terms[j].wait_recv()
        mid[at, :] += tr[j].astype(F32)
    store(mid, mid_h)
    cot_core.wait_recv()
    for copy in cot_both:
        copy.wait_recv()
    for copy in stores:
        copy.wait()
    wires.drain()


def front_phase(tokens, cotangent, kw, vw, qw, sw, wo, rd, ru, row):
    bits = wide_bits()
    half, d = tokens.shape
    count = 2 * half
    dk, dv, rk = kw.shape[1], vw.shape[1], rd.shape[0]
    chunks, n_bits = count // CHUNK, len(bits)
    hbm = pl.BlockSpec(memory_space=pltpu.HBM)
    vmem = pl.BlockSpec(memory_space=pltpu.VMEM)
    dma = pltpu.SemaphoreType.DMA
    v_ = pltpu.VMEM
    out_shape = [
        sds((half, d), F32), sds((count, d), BF16), sds((2, count, dk), BF16), sds((2, count, dk), BF16),
        sds((2, count, dv), BF16), sds((2, count, dv), F32), sds((2, count, dk), F32), sds((2, count, dk), F32),
        sds((count, rk), F32), sds((2, count, dk), BF16), sds((2, chunks, dv, dk), BF16), sds((2, count, dv), F32),
        sds((2, count, dv), BF16), sds((2, d, 2 * dk + 2 * dv), BF16), sds((2, dv, d), BF16),
        sds((half, d), BF16), sds((half, d), BF16), sds((half, d), BF16),
        sds((2, chunks, 1, dk), F32), sds((2, dv, dk), F32), sds((2, 1, dk), F32),
    ]
    scratch = [
        v_((half, d), BF16), v_((count, d), BF16), v_((2, d, 2 * dk + 2 * dv), BF16), v_((2, dv, d), BF16),
        v_((2, count, dk), BF16), v_((2, count, dk), BF16), v_((2, count, dv), BF16), v_((2, count, dv), F32),
        v_((2, count, dk), F32), v_((2, count, dk), F32), v_((count, rk), F32), v_((2, count, dk), BF16),
        v_((2, chunks, dv, dk), BF16), v_((2, count, dv), F32), v_((2, count, dv), BF16),
        v_((2, half // 2, d), BF16), v_((2, half // 2, d), BF16), v_((half, d), F32), v_((dv, dk), F32), v_((1, dk), F32),
        v_((2, dv, dk), F32), v_((2, 1, dk), F32), v_((2, dv, dk), F32), v_((2, 1, dk), F32),
        v_((n_bits + 1, 2, dv + 16, dk), BF16), v_((n_bits + 1, 2, dv + 16, dk), BF16),
        dma((8,)), dma((48,)), dma((48,)), dma((20,)),
    ]
    return pl.pallas_call(
        functools.partial(front_phase_kernel, bits),
        name="front_phase",
        in_specs=[hbm] * 7 + [vmem] * 3,
        out_specs=[hbm] * 18 + [vmem] * 3,
        out_shape=out_shape,
        scratch_shapes=scratch,
        compiler_params=pltpu.CompilerParams(collective_id=3, has_side_effects=True, vmem_limit_bytes=60 << 20),
        cost_estimate=cost(12e9, 60e6, 1e6),
    )(tokens, cotangent, kw, vw, qw, sw, wo, rd, ru, row)


def tile_of(step):
    return jnp.where((step == 5) | (step == 6), 11 - step, step)


def mlp_phase_kernel(
    bits,
    mid_h, c0_h, c1_h, c2_h, c3_h, wg_h, wu_h, wd_h, row_ref,
    gmid_h, gm_h, part_ref, gg_h, gu_h, gd_h, near_h, far_h,
    mid, xs, cs, wg, wu, wd, hs, ggs, gus, gn, rc, rd, ac, ry, dn, dnr, gmb, sum_g, sum_u, sum_d, got_g, got_u,
    load_sem, send_sem, recv_sem, out_sem,
):
    tile = xs.shape[0] // 8
    rows = 2 * tile
    d = xs.shape[1]

    def rows_of(t):
        return lanes_at(t * tile, tile)

    where = Places(2 ** len(bits))
    wires = Wires(send_sem, recv_sem)
    by_core, by_row = where.by_core, where.by_row

    loads = [pltpu.make_async_copy(mid_h, mid, load_sem.at[0])]
    for i, (src, dst) in enumerate(((wg_h, wg), (wu_h, wu), (wd_h, wd))):
        loads.append(pltpu.make_async_copy(src, dst, load_sem.at[1 + i]))
    for i, src in enumerate((c0_h, c1_h, c2_h, c3_h)):
        for j in range(2):
            loads.append(
                pltpu.make_async_copy(src.at[pl.ds(j * tile, tile)], cs.at[rows_of(2 * i + j)], load_sem.at[4 + 2 * i + j])
            )
    for load in loads:
        load.start()
    stores = []

    def store(src, dst):
        copy = pltpu.make_async_copy(src, dst, out_sem.at[len(stores)])
        stores.append(copy)
        copy.start()

    where.meet()
    x_row = [wires.copy(xs.at[rows_of(j)], xs.at[rows_of(4 + j)], by_row) for j in range(2)]
    x_core = [wires.copy(xs.at[rows_of(j)], xs.at[rows_of(2 + j)], by_core) for j in range(2)]
    x_both = [wires.copy(xs.at[rows_of(4 + j)], xs.at[rows_of(6 + j)], by_core) for j in range(2)]
    g_near = [wires.copy(gn.at[2 + j], rc.at[j], by_core) for j in range(2)]
    g_far = [wires.copy(gn.at[6 + j], rd.at[j], by_core) for j in range(2)]
    g_row = [wires.copy(ac.at[j], ry.at[j], by_row) for j in range(2)]
    d_in = [wires.copy(dn.at[(2, 3, 6, 7)[j]], dnr.at[j], by_core) for j in range(4)]
    left = sorted(bits, reverse=True)

    def first_hop(total, got, bit):
        dim, mine = left.index(bit), where.has(bit)
        mids = (slice(None),) * (dim - 1)
        copies = [
            wires.copy(total.at[(top,) + mids + (1 - mine,)], got.at[top], where.across(bit)) for top in range(2)
        ]

        def finish():
            for copy in copies:
                copy.wait_recv()
            for at in itertools.product(range(2), repeat=len(bits) - 1):
                own = at[:dim] + (mine,) + at[dim:]
                got[at] = (got[at].astype(F32) + total[own].astype(F32)).astype(BF16)

        return copies, finish

    hop_g, end_g = first_hop(sum_g, got_g, bits[0])
    hop_u, end_u = first_hop(sum_u, got_u, bits[1])
    gain = row_ref[:, d : 2 * d]

    loads[0].wait()
    for j in range(2):
        m = mid[pl.ds(j * tile, tile), :]
        inv = lax.rsqrt(jnp.mean(m * m, axis=-1, keepdims=True) + NORM_EPS)
        xs[rows_of(j), :] = (m * inv * gain).astype(BF16)
        x_row[j].start()
        x_core[j].start()
    for load in loads[1:6]:
        load.wait()

    def step(s, _):
        t = tile_of(s)
        at = rows_of(t)

        @pl.when(s == 2)
        def _():
            for load in loads[6:]:
                load.wait()
            x_core[0].wait_recv()

        @pl.when(s == 3)
        def _():
            x_core[1].wait_recv()

        for j in range(2):

            @pl.when(s == 4 + 2 * j)
            def _():
                x_row[j].wait_recv()
                x_both[j].start()

            @pl.when(s == 5 + 2 * j)
            def _():
                x_both[j].wait_recv()

        x = xs[at, :]
        gate = dot_nt(x, wg[...])
        up = dot_nt(x, wu[...])
        gh = dot_nt(cs[at, :], wd[...])
        sig = jax.nn.sigmoid(gate)
        act = gate * sig
        hidden = (act * up).astype(BF16)
        g_up = (gh * act).astype(BF16)
        g_gate = (gh * up * sig * (1.0 + gate * (1.0 - sig))).astype(BF16)
        hs[at, :] = hidden
        ggs[at, :] = g_gate
        gus[at, :] = g_up
        gn[t] = (dot(g_gate, wg[...]) + dot(g_up, wu[...])).astype(BF16)

        for j in range(2):

            @pl.when(s == 2 + j)
            def _():
                g_near[j].start()

            @pl.when(s == 5 + 2 * j)
            def _():
                g_far[j].start()

        dn[t] = dot(hidden, wd[...]).astype(BF16)

        for j in range(2):

            @pl.when(s == 5 + 2 * j)
            def _():
                g_far[j].wait_recv()
                ac[j] = (gn[4 + j].astype(F32) + rd[j].astype(F32)).astype(BF16)
                g_row[j].start()

        return 0

    lax.fori_loop(0, 8, step, 0)
    for copy in d_in:
        copy.start()

    size = 256
    count = d // size

    def weight_grad(lefts, rights, total, copies):
        def step(j, _):
            cols = lanes_at(j * size, size)
            acc = dot_tn(lefts[:, cols], rights[...])
            put_rows(total, (), j, size, bits, slice(None), acc.astype(BF16))
            for top, copy in enumerate(copies):

                @pl.when(j == (top + 1) * count // 2 - 1)
                def _():
                    copy.start()

            return 0

        lax.fori_loop(0, count, step, 0)

    part = jnp.zeros((1, d), F32)

    def final(j, part):
        at = pl.ds(j * tile, tile)
        g_near[j].wait_recv()
        g_row[j].wait_recv()
        grad = gn[j].astype(F32) + rc[j].astype(F32) + ry[j].astype(F32)
        m = mid[at, :]
        inv = lax.rsqrt(jnp.mean(m * m, axis=-1, keepdims=True) + NORM_EPS)
        unit = m * inv
        weighted = grad * gain
        part = part + jnp.sum(grad * unit, axis=0, keepdims=True)
        gmid = cs[rows_of(j), :].astype(F32) + inv * (weighted - unit * jnp.mean(weighted * unit, axis=-1, keepdims=True))
        mid[at, :] = gmid
        gmb[j] = gmid.astype(BF16)
        there = gm_h.at[lanes_at(where.core * rows + j * tile, tile)]
        store(gmb.at[j], there)
        store(mid.at[at], gmid_h.at[at])
        gm_out[j].start()
        return part

    gm_out = []
    for j in range(2):
        there = gm_h.at[lanes_at(where.core * rows + j * tile, tile)]
        gm_out.append(wires.copy(gmb.at[j], there, by_core))

    weight_grad(xs, ggs, sum_g, hop_g)
    weight_grad(xs, gus, sum_u, hop_u)
    part = final(0, part)
    weight_grad(cs, hs, sum_d, [])
    store(sum_d, gd_h)
    for j in range(2):
        d_in[j].wait_recv()
        d_in[2 + j].wait_recv()
        for at, extra, out in ((j, j, near_h), (4 + j, 2 + j, far_h)):
            dn[at] = (dn[at].astype(F32) + dnr[extra].astype(F32)).astype(BF16)
            store(dn.at[at], out.at[pl.ds(j * tile, tile)])
    end_g()
    store(got_g, gg_h)
    part_ref[...] = final(1, part)
    end_u()
    store(got_u, gu_h)
    for copy in gm_out:
        copy.wait_recv()
    for copy in stores:
        copy.wait()
    wires.drain()


def mlp_phase(middle, cots, wg_t, wu_t, wd, row):
    bits = wide_bits()
    rows, d = middle.shape
    ff = wd.shape[0]
    tile = rows // 2
    hbm = pl.BlockSpec(memory_space=pltpu.HBM)
    vmem = pl.BlockSpec(memory_space=pltpu.VMEM)
    dma = pltpu.SemaphoreType.DMA
    v_ = pltpu.VMEM
    block = (d // 2 ** len(bits), ff)
    full, part = (2,) * len(bits) + block, (2,) * (len(bits) - 1) + block
    return pl.pallas_call(
        functools.partial(mlp_phase_kernel, bits),
        name="mlp_phase",
        in_specs=[hbm] * 8 + [vmem],
        out_specs=[hbm, hbm, vmem] + [hbm] * 5,
        out_shape=[sds((rows, d), F32), sds((2 * rows, d), BF16), sds((1, d), F32)]
        + [sds(part, BF16), sds(part, BF16), sds(full, BF16)] + [sds((rows, d), BF16)] * 2,
        scratch_shapes=[
            v_((rows, d), F32), v_((8 * tile, d), BF16), v_((8 * tile, d), BF16),
            v_((ff, d), BF16), v_((ff, d), BF16), v_((ff, d), BF16),
            v_((8 * tile, ff), BF16), v_((8 * tile, ff), BF16), v_((8 * tile, ff), BF16),
            v_((8, tile, d), BF16), v_((2, tile, d), BF16), v_((2, tile, d), BF16),
            v_((2, tile, d), BF16), v_((2, tile, d), BF16), v_((8, tile, d), BF16), v_((4, tile, d), BF16),
            v_((2, tile, d), BF16), v_(full, BF16), v_(full, BF16), v_(full, BF16), v_(part, BF16), v_(part, BF16),
            dma((12,)), dma((24,)), dma((24,)), dma((12,)),
        ],
        compiler_params=pltpu.CompilerParams(collective_id=1, has_side_effects=True, vmem_limit_bytes=63 << 20),
        cost_estimate=cost(18 * 4 * rows * d * ff, 60e6, 4 * rows * ff),
    )(middle, *cots, wg_t, wu_t, wd, row)


def back_phase_kernel(
    bits,
    gm_h, mx_h, s_h, r_h, gt_h, rows_h, q_h, k_h, v_h, cum_h, dpre_h, rank_h, sin_h, w_h, wo_h, g_h, gmid_h, tok_h, far_h,
    off_ref, enter_ref, mult_ref, ru_ref, rd_ref, row_ref, mpart_ref,
    in_h, fr_h, gate_o, up_o, down_o, wout_o, k_o, v_o, q_o, s_o, rdown_o, rup_o, bias_o, mgain_o, group_o, ngain_o,
    gm, mx, sw, reach, gated, rows, q, k, v, cum, dpre, rank, sin, w, wo, held, mrecv, gmid, tok,
    gx, al, grank, ds, lb_m, pre_s, pre_m, sc_out, sc_in, osv, osy, osr, kva, kvay, kvar, kvb, kvbr, kvbo, tb, tr,
    sm, smf, smv, smr, smo, ng, ngr,
    load_sem, send_sem, recv_sem, out_sem,
):
    count, d = rows.shape
    half = count // 2
    dk, dv = q.shape[2], v.shape[2]
    where = Places(2 ** len(bits))
    wires = Wires(send_sem, recv_sem)
    loads = []

    def load(src, dst):
        copy = pltpu.make_async_copy(src, dst, load_sem.at[len(loads)])
        loads.append(copy)
        copy.start()
        return copy

    orders = (bits[1:], bits[:1] + bits[2:], bits)
    third = [load(g_h[0], held[0]), load(g_h[1], held[1])]
    first = [load(gm_h, gm), load(wo_h, wo), load(mx_h, mx), load(s_h, sw), load(r_h, reach)]
    second = [load(gt_h, gated), load(rows_h, rows)]
    dim = sorted(bits, reverse=True).index(bits[0])
    keep = load(g_h[2].at[(slice(None),) * dim + (where.has(bits[0]),)], held[2])
    fourth = [load(rank_h, rank)]
    for src, dst in ((q_h, q), (k_h, k), (v_h, v), (cum_h, cum), (dpre_h, dpre), (sin_h, sin), (w_h, w)):
        fourth.append(load(src, dst))
    fifth = [load(gmid_h, gmid), load(tok_h, tok)]

    where.meet()
    mlp = [
        Scatter(where, wires, held[0], None, orders[0], mrecv[0]),
        Scatter(where, wires, held[1], None, orders[1], mrecv[1]),
        Scatter(where, wires, g_h[2], held[2], orders[2], mrecv[2]),
    ]
    scan = Scan(where, wires, ds, lb_m, pre_s, pre_m, sc_out, sc_in, True)
    os_y = wires.copy(osv.at[1], osy, where.by_row)
    os_s = Scatter(where, wires, osv.at[0], None, bits, osr)
    kva_y = wires.copy(kva.at[1], kvay, where.by_row)
    kva_s = Scatter(where, wires, kva.at[0], None, bits, kvar)
    kvb_s = [Scatter(where, wires, kvb.at[h], None, bits, kvbr[h]) for h in range(2)]
    kvb_y = wires.copy(kvbo.at[0], kvbo.at[1], where.by_row)
    tots = [wires.copy(tb.at[j], tr.at[j], where.by_core) for j in range(2)]
    far = []
    for j in range(4):
        at = pl.ds(j * (half // 4), half // 4)
        far.append(wires.copy(far_h.at[at], fr_h.at[at], where.by_row))
    every = Shared(where, wires, sm, smf, smv, smr, smo)
    every_n = Everywhere(where, wires, ng, ngr)
    n_bits = len(bits)
    at_row = row_places(d, dv, 4 * dk)
    ngain = row_ref[:, at_row[0] : at_row[1]]
    gain = row_ref[:, at_row[2] : at_row[3]]
    restart = row_ref[:, at_row[4] : at_row[4] + dk]
    far[0].start()
    for copy in third:
        copy.wait()
    mlp[1].go()
    mlp[0].go()

    blk = half // 2
    ds[...] = jnp.zeros_like(ds)
    sm[...] = jnp.zeros_like(sm)
    for copy in first:
        copy.wait()

    def gate_step(i, part):
        at = pl.ds(pl.multiple_of(i * blk, blk), blk)
        g = gm[at, :]
        for h in range(2):
            grad = dot_nt(g, wo[h])
            mixed = mx[h, at, :]
            inv = lax.rsqrt(jnp.mean(mixed * mixed, axis=-1, keepdims=True) + GROUP_EPS)
            unit = mixed * inv
            s = sw[h, at, :]
            sig = jax.nn.sigmoid(s)
            al[h, at, 2 * dk + dv :] = (grad * unit * gain * (sig * (1.0 + s * (1.0 - sig)))).astype(BF16)
            dn = grad * (s * sig)
            part = part + jnp.sum(dn * unit, axis=0, keepdims=True)
            weighted = dn * gain
            gmix = (inv * (weighted - unit * jnp.mean(weighted * unit, axis=-1, keepdims=True))).astype(BF16)
            gx[h, at, :] = gmix
            ds[h] += dot_tn(gmix, reach[h, at, :])
        return part

    group_part = lax.fori_loop(0, 4, gate_step, jnp.zeros((1, dv), F32))
    for h in range(2):
        ds[h] = ds[h] * restart
        lb_m[h] = mult_ref[h]
    scan.begin()

    size = 256

    def out_step(j, _):
        cols = pl.ds(pl.multiple_of(j * size, size), size)
        for h in (1, 0):
            value = dot_tn(gm[:, cols], gated[h]).astype(BF16)
            put_rows(osv, (h,), j, size, bits, slice(0, dv), value)
        return 0

    def swish_step(j, _):
        cols = pl.ds(pl.multiple_of(j * size, size), size)
        for h in (1, 0):
            value = dot_tn(rows[:, cols], al[h, :, 2 * dk + dv :]).astype(BF16)
            put_rows(osv, (h,), j, size, bits, slice(dv, 2 * dv), value)
        return 0

    for copy in second:
        copy.wait()
    lax.fori_loop(0, d // size, out_step, 0)
    lax.fori_loop(0, d // size, swish_step, 0)
    scan.advance()
    os_y.start()
    scan.advance()
    keep.wait()
    mlp[2].go()
    while scan.advance():
        pass
    mlp[0].advance()
    mlp[1].advance()
    for copy in fourth:
        copy.wait()

    ds[...] = pre_s[...]
    chunks = count // CHUNK
    mask = triangle(True)
    ones = triangle(False).astype(F32)
    scale = dk**-0.5
    rk = rank.shape[1]

    def add_row(ref, extra):
        for at in itertools.product(range(2), repeat=n_bits):
            ref[(0,) + at] = (ref[(0,) + at].astype(F32) + extra[at].astype(F32)).astype(BF16)

    def back_step(step, carry):
        c = chunks - 1 - step

        @pl.when(step == chunks // 2)
        def _():
            mlp[2].advance()

        @pl.when(step == chunks - 3)
        def _():
            os_y.wait_recv()
            add_row(osv, osy)
            os_s.go()
            far[1].start()

        at = pl.ds(pl.multiple_of(c * CHUNK, CHUNK), CHUNK)
        grs, new = None, []
        for h in range(2):
            ch = cum[h, at, :]
            mid = ch[HALF - 1 : HALF]
            end = ch[CHUNK - 1 :]
            e_qd, e_kd, e_qi, e_ke = jnp.exp(ch - mid), jnp.exp(mid - ch), jnp.exp(ch), jnp.exp(end - ch)
            e_end = jnp.exp(end)
            qf = q[h, at, :].astype(F32) * scale
            kf = k[h, at, :].astype(F32)
            vc = v[h, at, :]
            qd = (qf * e_qd).astype(BF16)
            kd = (kf * e_kd).astype(BF16)
            qi = (qf * e_qi).astype(BF16)
            ke = (kf * e_ke).astype(BF16)
            go = gx[h, at, :]
            ru = ru_ref[:, lanes_at(((where.place + 2 * h) % 4) * dk, dk)].astype(F32)
            state = sin[h, c].astype(F32) + enter_ref[h] * jnp.exp(off_ref[h, c])
            state_low = state.astype(BF16)
            dstate = ds[h]
            dstate_low = dstate.astype(BF16)
            scores = jnp.where(mask, dot_nt(qd, kd), 0.0).astype(BF16)
            dscores = jnp.where(mask, dot_nt(go, vc), 0.0).astype(BF16)
            d_v = dot_tn(scores, go) + dot_nt(ke, dstate_low)
            d_qd = dot(dscores, kd)
            d_qi = dot(go, state_low)
            d_kd = dot_tn(dscores, qd)
            d_ke = dot(vc, dstate_low)
            d_q = scale * (d_qd * e_qd + d_qi * e_qi)
            d_k = d_kd * e_kd + d_ke * e_ke
            tail = ke.astype(F32) * d_ke
            d_cum = qd.astype(F32) * d_qd + qi.astype(F32) * d_qi - kd.astype(F32) * d_kd - tail
            d_end = jnp.sum(tail, axis=0, keepdims=True) + e_end * jnp.sum(dstate * state, axis=0, keepdims=True)
            grad_decay = exact(ones, d_cum, ((1,), (0,))) + d_end
            g_pre = grad_decay * jax.nn.sigmoid(-dpre[h, at, :]) * (1.0 / GATE_NORM)
            al[h, at, :dk] = d_k.astype(BF16)
            al[h, at, dk : dk + dv] = d_v.astype(BF16)
            al[h, at, dk + dv : 2 * dk + dv] = d_q.astype(BF16)
            gr = exact(g_pre, ru, ((1,), (1,)))
            grs = gr if grs is None else grs + gr
            new.append(carry[2 * h] + exact(rank[at, :], g_pre, ((0,), (0,))))
            new.append(carry[2 * h + 1] + jnp.sum(g_pre, axis=0, keepdims=True))
            ds[h] = dstate * e_end + dot_tn(go, qi)
        grank[at, :] = grs.astype(BF16)
        return tuple(new)

    zero = (jnp.zeros((rk, dk), F32), jnp.zeros((1, dk), F32))
    rup0, gb0, rup1, gb1 = lax.fori_loop(0, chunks, back_step, zero + zero)
    qk = 4 * dk
    sm[0] = dot_tn(grank[...], rows[...])
    at0 = where.place * dk
    at1 = ((where.place + 2) % 4) * dk
    sm[1, :, lanes_at(at0, dk)] = rup0
    sm[1, :, lanes_at(at1, dk)] = rup1
    sm[1, 0:1, lanes_at(qk + at0, dk)] = gb0
    sm[1, 0:1, lanes_at(qk + at1, dk)] = gb1
    sm[1, 1:2, qk : qk + dv] = group_part
    for i in range(d // qk):
        sm[1, 2 + i : 3 + i, qk : 2 * qk] = mpart_ref[:, i * qk : (i + 1) * qk]
    every.begin()
    def kvq_step(ref, h, low):
        def step(j, _):
            cols = lanes_at(j * size, size)
            value = dot_tn(rows[:, cols], al[h, :, low : low + size]).astype(BF16)
            put_rows(ref, (h,), j, size, bits, slice(None), value)
            return 0

        lax.fori_loop(0, d // size, step, 0)

    kvq_step(kva, 1, 0)
    kva_y.start()
    for h in range(2):
        kvq_step(kvb, h, size)
        kvb_s[h].go()
    mlp[2].advance()
    os_s.advance()

    def total_step(i, _):
        b = jnp.where(i < 2, 2 - 2 * where.core + i, 2 * where.core + i - 2)
        at = pl.ds(pl.multiple_of(b * blk, blk), blk)
        total = dot_nt(al[0, at, :], w[0]) + dot_nt(al[1, at, :], w[1]) + dot(grank[at, :], rd_ref[...])
        for j in range(2):

            @pl.when(i == j)
            def _():
                tb[j] = total.astype(BF16)
                tots[j].start()

            @pl.when(i == 2 + j)
            def _():
                tb[2 + j] = total.astype(BF16)

        return 0

    every.advance()
    lax.fori_loop(0, 4, total_step, 0)

    kvq_step(kva, 0, 0)
    every.advance()

    for copy in fifth:
        copy.wait()
    part = jnp.zeros((1, d), F32)
    for j in range(2):
        at = pl.ds(j * blk, blk)
        tots[j].wait_recv()
        grad = tb[2 + j].astype(F32) + tr[j].astype(F32)
        x = tok[at, :].astype(F32)
        inv = lax.rsqrt(jnp.mean(x * x, axis=-1, keepdims=True) + NORM_EPS)
        unit = x * inv
        weighted = grad * ngain
        part = part + jnp.sum(grad * unit, axis=0, keepdims=True)
        gmid[at, :] = gmid[at, :] + inv * (weighted - unit * jnp.mean(weighted * unit, axis=-1, keepdims=True))
    done = pltpu.make_async_copy(gmid, in_h, out_sem.at[0])
    done.start()
    for i in range(8):
        ng[0, i : i + 1, :] = part[:, i * (d // 8) : (i + 1) * (d // 8)]
    every_n.begin()

    kva_y.wait_recv()
    far[2].start()
    far[3].start()
    add_row(kva, kvay)
    kva_s.go()
    for part in kvb_s:
        part.advance()
    os_s.advance()
    every.advance()
    every_n.advance()
    for i, out in ((0, gate_o), (1, up_o)):
        out[...] = jnp.transpose(mlp[i].result())
    for i in range(n_bits - 1):
        kva_s.advance()
        if i < n_bits - 2:
            for part in kvb_s:
                part.advance()
        every.advance()
        every_n.advance()
    kvbo[0] = kvb_s[1].result().astype(BF16)
    kvb_y.start()
    down_o[...] = jnp.transpose(mlp[2].result())
    total = os_s.result()
    wout_o[...] = jnp.transpose(total[:, :dv])
    s_o[...] = total[:, dv:]
    every.advance()
    every_n.advance()
    first_half = kva_s.result()
    last_half = kvb_s[0].result()
    kvb_y.wait_recv()
    last_half = last_half + kvbo[1].astype(F32)
    k_o[...] = first_half[:, :dk]
    v_o[:, : size - dk] = first_half[:, dk:]
    v_o[:, size - dk :] = last_half[:, : dk + dv - size]
    q_o[...] = last_half[:, dk + dv - size :]
    small = every.result()
    rdown_o[...] = small[0]
    rup_o[...] = small[1, :, :qk]
    bias_o[...] = small[1, 0:1, qk : 2 * qk]
    group_o[...] = small[1, 1:2, qk : qk + dv]
    for i in range(d // qk):
        mgain_o[:, i * qk : (i + 1) * qk] = small[1, 2 + i : 3 + i, qk : 2 * qk]
    whole_n = every_n.result()
    for i in range(8):
        ngain_o[:, i * (d // 8) : (i + 1) * (d // 8)] = whole_n[i : i + 1, :]
    for copy in far:
        copy.wait_recv()
    done.wait()
    wires.drain()


def back_phase(
    gm, mx, s, reach, gated, rows, q, k, v, cum, dpre, rank, sin, w, wo, grads, gmid, tokens, far,
    off, enter, mult, ru, rd, row, mpart,
):
    bits = wide_bits()
    count, d = rows.shape
    half = count // 2
    dk, dv, rk = q.shape[2], v.shape[2], rank.shape[1]
    ff = grads[0].shape[-1]
    each = d // 2 ** len(bits)
    n_bits, chunks = len(bits), count // CHUNK
    hbm = pl.BlockSpec(memory_space=pltpu.HBM)
    vmem = pl.BlockSpec(memory_space=pltpu.VMEM)
    dma = pltpu.SemaphoreType.DMA
    v_ = pltpu.VMEM

    def shape(lead, cols):
        return (2,) * lead + (each, cols)

    def falls(cols):
        return [v_(shape(n_bits - 1 - i, cols), BF16) for i in range(n_bits)]

    pair, three = [hbm] * 2, [hbm] * 3
    kvq = 2 * dk + dv
    scratch = [
        v_((count, d), BF16), v_((2, count, dv), F32), v_((2, count, dv), F32), v_((2, count, dk), BF16),
        v_((2, count, dv), BF16), v_((count, d), BF16), v_((2, count, dk), BF16), v_((2, count, dk), BF16),
        v_((2, count, dv), BF16), v_((2, count, dk), F32), v_((2, count, dk), F32), v_((count, rk), F32),
        v_((2, chunks, dv, dk), BF16), v_((2, d, kvq + dv), BF16), v_((2, dv, d), BF16),
        [v_(shape(n_bits - 1, ff), BF16)] * 3, [falls(ff)[1:], falls(ff)[1:], falls(ff)], v_((half, d), F32), v_((half, d), BF16),
        v_((2, count, dv), BF16), v_((2, count, kvq + dv), BF16), v_((count, rk), BF16),
        v_((2, dv, dk), F32), v_((2, 1, dk), F32), v_((2, dv, dk), F32), v_((2, 1, dk), F32),
        v_((n_bits + 1, 2, dv + 16, dk), BF16), v_((n_bits + 1, 2, dv + 16, dk), BF16),
        v_((2,) + shape(n_bits, 2 * dv), BF16), v_(shape(n_bits, 2 * dv), BF16), falls(2 * dv),
        v_((2,) + shape(n_bits, 256), BF16), v_(shape(n_bits, 256), BF16), falls(256),
        v_((2,) + shape(n_bits, 256), BF16), [falls(256), falls(256)], v_((2, each, 256), BF16),
        v_((4, half // 2, d), BF16), v_((2, half // 2, d), BF16),
        v_((2, rk, d), F32), v_((rk, d), F32), v_((n_bits + 1, rk, d), F32), v_((n_bits + 1, rk, d), F32), v_((2, rk, d), F32),
        v_((n_bits + 3, 8, d // 8), F32), v_((n_bits + 2, 8, d // 8), F32),
        dma((24,)), dma((96,)), dma((96,)), dma((1,)),
    ]
    out_shape = [
        sds((half, d), F32), sds((half, d), BF16), sds((ff, each), F32), sds((ff, each), F32), sds((ff, each), F32), sds((dv, each), F32),
        sds((each, dk), F32), sds((each, dv), F32), sds((each, dk), F32), sds((each, dv), F32),
        sds((rk, d), F32), sds((rk, 4 * dk), F32), sds((1, 4 * dk), F32), sds((1, d), F32), sds((1, dv), F32), sds((1, d), F32),
    ]
    operands = (
        gm, mx, s, reach, gated, rows, q, k, v, cum, dpre, rank, sin, w, wo, grads, gmid, tokens, far,
        off, enter, mult, ru, rd, row, mpart,
    )
    flat, tree = jax.tree.flatten(operands)
    n_vmem = len(jax.tree.leaves(operands[19:]))
    flat_scratch, scratch_tree = jax.tree.flatten(scratch, is_leaf=lambda x: not isinstance(x, list))
    n_in, n_out = len(flat), len(out_shape)

    def kernel(*refs):
        ins = jax.tree.unflatten(tree, refs[:n_in])
        rest = jax.tree.unflatten(scratch_tree, refs[n_in + n_out :])
        back_phase_kernel(bits, *ins, *refs[n_in : n_in + n_out], *rest)

    return pl.pallas_call(
        kernel,
        name="back_phase",
        in_specs=[hbm] * (n_in - n_vmem) + [vmem] * n_vmem,
        out_specs=[hbm, hbm] + [vmem] * (n_out - 2),
        out_shape=out_shape,
        scratch_shapes=flat_scratch,
        compiler_params=pltpu.CompilerParams(collective_id=2, has_side_effects=True, vmem_limit_bytes=62 << 20),
        cost_estimate=cost(40e9, 60e6, 1e6),
    )(*flat)


def finish_kernel(count, mid_ref, near_ref, far_ref, grad_ref, *refs):
    res_ref, in_ref = refs[count : count + 2]
    res_ref[...] = (mid_ref[...] + (near_ref[...].astype(F32) + far_ref[...].astype(F32))).astype(BF16)
    in_ref[...] = grad_ref[...]

    @pl.when(pl.program_id(0) == 0)
    def _():
        for src, dst in zip(refs[:count], refs[count + 2 :]):
            dst[...] = src[...]


def finish(middle, near, far, grad, smalls):
    rows, d = middle.shape
    blk = rows // 2
    row = rows_spec(blk, d)
    wholes = [pl.BlockSpec(v.shape, lambda i: (0, 0)) for v in smalls]
    return pl.pallas_call(
        functools.partial(finish_kernel, len(smalls)),
        name="finish",
        grid=(2,),
        in_specs=[row] * 4 + wholes,
        out_specs=[row] * 2 + wholes,
        out_shape=[sds((rows, d), BF16), sds((rows, d), F32)] + [sds(v.shape, v.dtype) for v in smalls],
        compiler_params=params(62),
    )(middle, near, far, grad, *smalls)


def wide_bits():
    count, bits, bit = lax.axis_size("wide"), [], 1
    while bit < count:
        bits.append(bit)
        bit *= 2
    return bits


def shards(
    tokens, cotangent, flags, norm_gain, query_weight, key_weight, value_weight, swish_weight, rank_down, rank_up,
    decay_bias, group_gain, output_weight, mlp_gain, mlp_gate, mlp_up, mlp_down,
):
    place = lax.axis_index("narrow")
    dk, dv, d = query_weight.shape[1], value_weight.shape[1], tokens.shape[1]
    restart = jnp.where((place & 2) != 0, 1.0, 1.0 - flags[0].astype(F32))
    parts = [part.astype(F32) for part in (norm_gain, mlp_gain, group_gain, decay_bias)]
    parts.append(jnp.full((dk,), restart, F32))
    total, at = sum(part.size for part in parts), 0
    row = jnp.zeros((1, total), F32)
    for part in parts:
        row = row + jnp.pad(part.reshape(1, -1), ((0, 0), (at, total - at - part.size)))
        at += part.size
    rd = rank_down.T
    (
        middle, rows_all, q, k, v, s, cum, dpre, rank_pre, reach, sin, mixed, gated, w, weights_out, cot_c, cot_y, cot_d,
        off, enter, mults,
    ) = front_phase(
        tokens, cotangent, key_weight, value_weight, query_weight, swish_weight, output_weight, rd, rank_up, row
    )
    grad_middle, gm_all, mlp_gain_part, gate_g, up_g, down_g, near, far = mlp_phase(
        middle, (cotangent, cot_c, cot_y, cot_d), mlp_gate.T, mlp_up.T, mlp_down, row
    )
    input_grad, far_sum, *smalls = back_phase(
        gm_all, mixed, s, reach, gated, rows_all, q, k, v, cum, dpre, rank_pre, sin,
        w, weights_out, (gate_g, up_g, down_g), grad_middle, tokens, far, off, enter, mults, rank_up, rd, row,
        mlp_gain_part,
    )
    result, input_grad, *smalls = finish(middle, near, far_sum, input_grad, smalls)
    gate_t, up_t, down_t, out_t, k_g, v_g, q_g, s_g, rdown_t, rup_g, bias_g, mgain_g, group_g, ngain = smalls
    return (
        result,
        input_grad,
        ngain[0],
        q_g,
        k_g,
        v_g,
        s_g,
        rdown_t.T,
        rup_g,
        bias_g[0],
        group_g[0],
        out_t,
        mgain_g[0],
        gate_t.T,
        up_t.T,
        down_t,
    )


def solution(mesh):
    rows, cols = P(("wide", "narrow"), None), P(None, "narrow")
    both = P("wide", "narrow")
    in_specs = (
        rows, rows, P("wide"), P(), cols, cols, cols, cols, P(), P(), P(), P(), P("narrow", None), P(), cols, cols,
        P("narrow", None),
    )
    out_specs = (
        rows, rows, P(), both, both, both, both, P(), P(), P(), P(), P("narrow", "wide"), P(), both, both,
        P("narrow", "wide"),
    )
    return jax.shard_map(shards, mesh=mesh, in_specs=in_specs, out_specs=out_specs, check_vma=False)
```
